32 devices in a mesh: dp: 4 (over y, x), tensor: 8 (over z, core).
Axes of the slice: x: 2, y: 2, z: 4, core: 2. Of those that a mesh axis runs over, the one named last changes fastest.
Arguments:
- tokens: bfloat16 [8192, 1152], P(('dp', 'tensor')), may hold values from -6 to 6
- picture_ids: int32 [8192], P('dp'), may hold values from 0 to 21, as said below
- ln1_gain: bfloat16 [1152], replicated, may hold values from 0.25 to 1.75
- ln1_bias: bfloat16 [1152], replicated, may hold values from -1.75 to 1.75
- q_weight: bfloat16 [1152, 1152], P(None, 'tensor'), may hold values from -0.1875 to 0.1875
- q_bias: bfloat16 [1152], P('tensor'), may hold values from -3 to 3
- k_weight: bfloat16 [1152, 1152], P(None, 'tensor'), may hold values from -0.1875 to 0.1875
- v_weight: bfloat16 [1152, 1152], P(None, 'tensor'), may hold values from -0.1875 to 0.1875
- v_bias: bfloat16 [1152], P('tensor'), may hold values from -3 to 3
- o_weight: bfloat16 [1152, 1152], P('tensor'), may hold values from -2.5 to 2.5
- o_bias: bfloat16 [1152], replicated, may hold values from -1.75 to 1.75
- ln2_gain: bfloat16 [1152], replicated, may hold values from 0.25 to 1.75
- ln2_bias: bfloat16 [1152], replicated, may hold values from -1.75 to 1.75
- fc1_weight: bfloat16 [1152, 4304], P(None, 'tensor'), may hold values from -0.1875 to 0.1875
- fc1_bias: bfloat16 [4304], P('tensor'), may hold values from -3 to 3
- fc2_weight: bfloat16 [4304, 1152], P('tensor'), may hold values from -0.09375 to 0.09375
- fc2_bias: bfloat16 [1152], replicated, may hold values from -1.75 to 1.75
- out_grad: bfloat16 [8192, 1152], P(('dp', 'tensor')), may hold values from -6 to 6
Outputs:
- output: bfloat16 [8192, 1152], P(('dp', 'tensor'))
- grad_tokens: float32 [8192, 1152], P(('dp', 'tensor'))
- grad_ln1_gain: float32 [1152], replicated
- grad_ln1_bias: float32 [1152], replicated
- grad_q_weight: float32 [1152, 1152], P(None, 'tensor')
- grad_q_bias: float32 [1152], P('tensor')
- grad_k_weight: float32 [1152, 1152], P(None, 'tensor')
- grad_v_weight: float32 [1152, 1152], P(None, 'tensor')
- grad_v_bias: float32 [1152], P('tensor')
- grad_o_weight: float32 [1152, 1152], P('tensor')
- grad_o_bias: float32 [1152], replicated
- grad_ln2_gain: float32 [1152], replicated
- grad_ln2_bias: float32 [1152], replicated
- grad_fc1_weight: float32 [1152, 4304], P(None, 'tensor')
- grad_fc1_bias: float32 [4304], P('tensor')
- grad_fc2_weight: float32 [4304, 1152], P('tensor')
- grad_fc2_bias: float32 [1152], replicated
The draws below stay inside these ranges and needn't reach their ends.
Inputs may be any that keep to these rules, and one draw needn't show every extreme that they name: `picture_ids`: each packed row of 2048 tokens (rows begin at multiples of 2048) holds whole pictures numbered 21, 20, 19 ... in order, each of 100 to 1024 tokens, followed by one or more padding tokens numbered 0; one of a row's first two pictures has exactly 1024 tokens.
All inputs are finite; a program needn't handle non-finite values.
Results may differ from the reference program's by a relative error of at most 0.024.
Values may be sent and summed in bfloat16 or wider, within the bound.
A program may use at most 128 MiB of HBM per device.

```python
import jax
import jax.numpy as jnp
from jax import lax

H = 16
HD = 72
D = 1152
FF = 4304
LEN = 2048
PMAX = 1024
PMIN = 100
PICS = 21
TOKENS = 8192


def draw_picture_ids(key, part):
    rows_total = TOKENS // LEN
    size_key, slot_key = jax.random.split(jax.random.fold_in(key, 11))
    pic_sizes = jax.random.randint(size_key, (rows_total, PICS), PMIN, PMAX + 1)
    chosen_slot = jax.random.randint(slot_key, (rows_total, 1), 0, 2)
    slot_index = jnp.arange(PICS)[None, :]
    pic_sizes = jnp.where(slot_index == chosen_slot, PMAX, pic_sizes)
    pic_ends = jnp.cumsum(pic_sizes, axis=1)
    filled = jnp.max(jnp.where(pic_ends <= LEN - 1, pic_ends, 0), axis=1, keepdims=True)
    positions = jnp.arange(LEN)[None, :]
    number = jnp.sum((pic_ends[:, None, :] <= positions[:, :, None]).astype(jnp.int32), axis=2)
    pic_ids = jnp.where(positions < filled, PICS - number, 0)
    return pic_ids.reshape(-1).astype(jnp.int32)


def steps_of(key, dims, cuts, least, high):
    gain, own = 1.0, jax.random.fold_in(key, 6)
    for position, blocks in cuts:
        draws = jnp.exp(jax.random.uniform(jax.random.fold_in(own, position), (blocks,), jnp.float32, least / len(cuts), high / len(cuts)))
        gain = gain * jnp.repeat(draws, dims[position] // blocks).reshape([-1 if axis == position else 1 for axis in range(len(dims))])
    return gain


def gaussian(stream_key, shape, deviation, bound, pieces=(), dtype=jnp.bfloat16):
    values = deviation * jax.random.normal(stream_key, shape, jnp.float32)
    if pieces:
        values = values * steps_of(stream_key, shape, pieces, -0.22, 0.18)
    return jnp.clip(values, -bound, bound).astype(dtype)


def setup_inputs(seed: int = 0) -> dict:
    splits = jax.random.split(jax.random.key(seed), 19)
    return {
        "tokens": gaussian(splits[0], (TOKENS, D), 1.0, 6.0, ((0, 32),)),
        "picture_ids": draw_picture_ids(jax.random.fold_in(splits[18], 71), 0),
        "ln1_gain": jnp.clip(1.0 + 0.15 * jax.random.normal(splits[2], (D,), jnp.float32), 0.25, 1.75).astype(jnp.bfloat16),
        "ln1_bias": gaussian(splits[3], (D,), 0.3, 1.75),
        "q_weight": gaussian(splits[4], (D, D), D ** -0.5, 0.1875, ((1, 8),)),
        "q_bias": gaussian(splits[5], (D,), 0.5, 3.0, ((0, 8),)),
        "k_weight": gaussian(splits[6], (D, D), D ** -0.5, 0.1875, ((1, 8),)),
        "v_weight": gaussian(splits[7], (D, D), D ** -0.5, 0.1875, ((1, 8),)),
        "v_bias": gaussian(splits[8], (D,), 0.5, 3.0, ((0, 8),)),
        "o_weight": gaussian(splits[9], (D, D), (max(D * 6 // PMAX, 1)) ** -0.5, 2.5, ((0, 8),)),
        "o_bias": gaussian(splits[10], (D,), 0.3, 1.75),
        "ln2_gain": jnp.clip(1.0 + 0.15 * jax.random.normal(splits[11], (D,), jnp.float32), 0.25, 1.75).astype(jnp.bfloat16),
        "ln2_bias": gaussian(splits[12], (D,), 0.3, 1.75),
        "fc1_weight": gaussian(splits[13], (D, FF), D ** -0.5, 0.1875, ((1, 8),)),
        "fc1_bias": gaussian(splits[14], (FF,), 0.5, 3.0, ((0, 8),)),
        "fc2_weight": gaussian(splits[15], (FF, D), FF ** -0.5, 0.09375, ((0, 8),)),
        "fc2_bias": gaussian(splits[16], (D,), 0.3, 1.75),
        "out_grad": gaussian(splits[17], (TOKENS, D), 1.0, 6.0, ((0, 32),)),
    }


@jax.custom_vjp
def low(v):
    return lax.optimization_barrier(v.astype(jnp.bfloat16)).astype(jnp.float32)

@jax.custom_vjp
def low_back(v):
    return v

def low_keep(v):
    return (low(v), None)

def low_pass(kept, grad):
    return (grad,)

def back_keep(v):
    return (v, None)

def back_low(kept, grad):
    return (low(grad),)
low.defvjp(low_keep, low_pass)
low_back.defvjp(back_keep, back_low)
NORM_EPS = 1e-06
NEG_FILL = -1e+30
HIGHEST_PREC = lax.Precision.HIGHEST

def product(left, right):
    return jnp.dot(left, right, precision=HIGHEST_PREC, preferred_element_type=jnp.float32)

def layer_norm(values, norm_gain, norm_bias):
    average = lax.optimization_barrier(jnp.mean(values, axis=-1, keepdims=True))
    centred = values - average
    variance = lax.optimization_barrier(jnp.mean(centred * centred, axis=-1, keepdims=True))
    return centred * lax.rsqrt(variance + NORM_EPS) * norm_gain + norm_bias

def row_forward(weights, tok_row, ids_row):
    ln1_gain, ln1_bias, q_weight, q_bias, k_weight, v_weight, v_bias, o_weight, o_bias, ln2_gain, ln2_bias, fc1_weight, fc1_bias, fc2_weight, fc2_bias = weights
    valid_mask = (ids_row > 0).astype(jnp.float32)[:, None]
    norm1 = low(layer_norm(tok_row, ln1_gain, ln1_bias))
    queries = low(low_back(product(norm1, q_weight) + q_bias))
    key_rows = low(low_back(product(norm1, k_weight)))
    value_rows = low(low_back(product(norm1, v_weight) + v_bias))
    query_heads = queries.reshape(LEN, H, HD)
    key_heads = key_rows.reshape(LEN, H, HD)
    value_heads = value_rows.reshape(LEN, H, HD)
    raw_scores = jnp.einsum('qhd,khd->hqk', query_heads, key_heads, precision=HIGHEST_PREC)
    allowed = (ids_row[:, None] == ids_row[None, :]) & (ids_row[None, :] > 0)
    score_scale = HD ** (-0.5)
    scores = low_back(jnp.where(allowed[None], raw_scores * score_scale, NEG_FILL))
    attn_probs = low(jax.nn.softmax(scores, axis=-1))
    attended = jnp.einsum('hqk,khd->qhd', attn_probs, value_heads, precision=HIGHEST_PREC)
    attended = low(low_back(attended.reshape(LEN, D)))
    attn_sum = low_back(product(attended, o_weight))
    residual = tok_row + attn_sum + o_bias
    norm2 = low(layer_norm(residual, ln2_gain, ln2_bias))
    pre_act = low_back(product(norm2, fc1_weight) + fc1_bias)
    hidden = low(jax.nn.gelu(pre_act, approximate=True))
    branch = low_back(product(hidden, fc2_weight))
    return valid_mask * (residual + branch + fc2_bias)

def reference(tokens, picture_ids, ln1_gain, ln1_bias, q_weight, q_bias, k_weight, v_weight, v_bias, o_weight, o_bias, ln2_gain, ln2_bias, fc1_weight, fc1_bias, fc2_weight, fc2_bias, out_grad):
    weights = tuple((item.astype(jnp.float32) for item in (ln1_gain, ln1_bias, q_weight, q_bias, k_weight, v_weight, v_bias, o_weight, o_bias, ln2_gain, ln2_bias, fc1_weight, fc1_bias, fc2_weight, fc2_bias)))
    rows_total = tokens.shape[0] // LEN
    tok_rows = tokens.astype(jnp.float32).reshape(rows_total, LEN, D)
    id_rows = picture_ids.reshape(rows_total, LEN)
    row_step = jax.checkpoint(row_forward)

    def whole(weight_set, token_set):
        return lax.map(lambda row_item: row_step(weight_set, row_item[0], row_item[1]), (token_set, id_rows))
    result, pullback = jax.vjp(whole, weights, tok_rows)
    grad_w, grad_tok = pullback(out_grad.astype(jnp.float32).reshape(rows_total, LEN, D))
    return (result.reshape(-1, D).astype(jnp.bfloat16), grad_tok.reshape(-1, D), grad_w[0], grad_w[1], grad_w[2], grad_w[3], grad_w[4], grad_w[5], grad_w[6], grad_w[7], grad_w[8], grad_w[9], grad_w[10], grad_w[11], grad_w[12], grad_w[13], grad_w[14])
```

```python
import functools

import jax
import jax.numpy as jnp
from jax import lax
from jax.experimental import pallas as pl
from jax.experimental.pallas import tpu as pltpu
from jax.sharding import PartitionSpec as P

HD = 72
LEN = 2048
BLOCK = 256
NORM_EPS = 1e-06
NEG_FILL = -1e30
BF16 = jnp.bfloat16
F32 = jnp.float32
MESH = pl.DeviceIdType.MESH
VMEM = pltpu.VMEM
DMA = pltpu.SemaphoreType.DMA
VSPEC = pl.BlockSpec(memory_space=pltpu.VMEM)
SSPEC = pl.BlockSpec(memory_space=pltpu.SMEM)


def nn(left, right):
    return lax.dot_general(left, right, (((1,), (0,)), ((), ())), preferred_element_type=F32)


def nt(left, right):
    return lax.dot_general(left, right, (((1,), (1,)), ((), ())), preferred_element_type=F32)


def tn(left, right):
    return lax.dot_general(left, right, (((0,), (0,)), ((), ())), preferred_element_type=F32)


def remote(src, dst, send_sem, recv_sem, **where):
    return pltpu.make_async_remote_copy(
        src_ref=src, dst_ref=dst, send_sem=send_sem, recv_sem=recv_sem,
        device_id=where, device_id_type=MESH,
    )


def place():
    me = lax.axis_index("tensor")
    core = lax.rem(me, 2)
    return me, core, lax.div(me, 2)


def greet_peers(axes):
    barrier = pltpu.get_barrier_semaphore()
    for axis, size in axes:
        me = lax.axis_index(axis)

        def greet(step, carry):
            pl.semaphore_signal(
                barrier, inc=1, device_id={axis: lax.rem(me + step, size)}, device_id_type=MESH
            )
            return carry

        lax.fori_loop(1, size, greet, 0)
    pl.semaphore_wait(barrier, sum(size - 1 for _, size in axes))


def greet_line(stages):
    me, core, stage = place()
    barrier = pltpu.get_barrier_semaphore()
    has_left, has_right = stage > 0, stage < stages - 1

    def greet(other):
        pl.semaphore_signal(barrier, inc=1, device_id={"tensor": other}, device_id_type=MESH)

    greet(me + 1 - 2 * core)
    pl.when(has_left)(lambda: greet(me - 2))
    pl.when(has_right)(lambda: greet(me + 2))
    pl.semaphore_wait(barrier, 1 + has_left.astype(jnp.int32) + has_right.astype(jnp.int32))


def normalize(values):
    average = jnp.mean(values, axis=-1, keepdims=True)
    centred = values - average
    variance = jnp.mean(centred * centred, axis=-1, keepdims=True)
    scale = lax.rsqrt(variance + NORM_EPS)
    return centred * scale, scale


class LineGather:
    def __init__(self, stages, buffer, send_sem, recv_sem):
        self.stages, self.buffer, self.send_sem, self.recv_sem = stages, buffer, send_sem, recv_sem
        self.me, self.core, self.stage = place()
        self.partner = self.me + 1 - 2 * self.core

    def copy(self, block, way, target):
        return remote(
            self.buffer.at[block], self.buffer.at[block],
            self.send_sem.at[block, way], self.recv_sem.at[block], tensor=target,
        )

    def each_copy(self, block, right, left, act):
        pl.when(right)(lambda: act(self.copy(block, 0, self.me + 2)))
        pl.when(left)(lambda: act(self.copy(block, 1, self.me - 2)))
        act(self.copy(block, 2, self.partner))

    def start(self):
        self.each_copy(
            self.me, self.stage < self.stages - 1, self.stage > 0, lambda copy: copy.start()
        )

    def steps(self):
        return 2 + 4 * (self.stages - 1)

    def locate(self, step):
        index = jnp.maximum(step - 2, 0)
        reach = lax.div(index, 4) + 1
        slot = lax.rem(index, 4)
        side, other = lax.rem(slot, 2), lax.div(slot, 2)
        far = jnp.where(side == 0, self.stage - reach, self.stage + reach)
        valid = (step < 2) | ((far >= 0) & (far < self.stages))
        far = jnp.where(step < 2, self.stage, far)
        crossed = jnp.where(step < 2, step, other)
        block = 2 * far + jnp.where(crossed == 0, self.core, 1 - self.core)
        relay = (step >= 2) & (other == 0)
        right = relay & (side == 0) & (self.stage < self.stages - 1)
        left = relay & (side == 1) & (self.stage > 0)
        return valid, block, relay, right, left

    def run(self, compute):
        def body(step, carry):
            valid, block, relay, right, left = self.locate(step)

            @pl.when(valid)
            def _():
                @pl.when(step > 0)
                def _():
                    self.copy(block, 2, self.partner).wait_recv()

                @pl.when(relay)
                def _():
                    self.each_copy(block, right, left, lambda copy: copy.start())

                compute(block)

            return carry

        lax.fori_loop(0, self.steps(), body, 0)

    def finish(self):
        self.each_copy(
            self.me, self.stage < self.stages - 1, self.stage > 0, lambda copy: copy.wait_send()
        )

        def body(step, carry):
            valid, block, relay, right, left = self.locate(step)

            @pl.when(valid & relay)
            def _():
                self.each_copy(block, right, left, lambda copy: copy.wait_send())

            return carry

        lax.fori_loop(2, self.steps(), body, 0)


class LineScatter:
    def __init__(self, stages, partial, cross, lane, sems):
        self.stages, self.partial, self.cross, self.lane = stages, partial, cross, lane
        self.cross_send, self.cross_recv, self.lane_send, self.lane_recv = sems
        self.me, self.core, self.stage = place()
        self.partner = self.me + 1 - 2 * self.core

    def cross_copy(self, far):
        return remote(
            self.partial.at[2 * far + 1 - self.core], self.cross.at[far],
            self.cross_send.at[far], self.cross_recv.at[far], tensor=self.partner,
        )

    def lane_copy(self, way, far):
        target = self.me + 2 if way == 0 else self.me - 2
        return remote(
            self.partial.at[2 * far + self.core], self.lane.at[way, far],
            self.lane_send.at[far], self.lane_recv.at[way, far], tensor=target,
        )

    def farthest(self, index):
        reach = self.stages - 1 - lax.div(index, 2)
        far = jnp.where(lax.rem(index, 2) == 0, self.stage + reach, self.stage - reach)
        valid = (far >= 0) & (far < self.stages) & ((reach > 0) | (lax.rem(index, 2) == 0))
        return valid, far

    def produce(self, compute):
        def body(index, carry):
            valid, far = self.farthest(index)

            @pl.when(valid)
            def _():
                self.partial[2 * far + 1 - self.core] = compute(2 * far + 1 - self.core).astype(BF16)
                self.cross_copy(far).start()
                self.partial[2 * far + self.core] = compute(2 * far + self.core).astype(BF16)

            return carry

        lax.fori_loop(0, 2 * self.stages, body, 0)

    def chip_sum(self, far):
        self.cross_copy(far).wait_recv()
        return self.partial[2 * far + self.core].astype(F32) + self.cross[far].astype(F32)

    def send_sum(self, way, far, incoming):
        total = self.chip_sum(far)
        if incoming:
            self.lane_copy(way, far).wait_recv()
            total = total + self.lane[way, far].astype(F32)
        self.partial[2 * far + self.core] = total.astype(BF16)
        self.lane_copy(way, far).start()

    def each_target(self, way, act):
        def body(index, carry):
            far = self.stages - 1 - index if way == 0 else index
            valid = far > self.stage if way == 0 else far < self.stage
            pl.when(valid)(lambda: act(far))
            return carry

        lax.fori_loop(0, self.stages - 1, body, 0)

    def send_first(self):
        @pl.when(self.stage == 0)
        def _():
            self.each_target(0, lambda far: self.send_sum(0, far, False))

        @pl.when(self.stage == self.stages - 1)
        def _():
            self.each_target(1, lambda far: self.send_sum(1, far, False))

    def send_rest(self):
        def body(index, carry):
            valid, far = self.farthest(index)

            @pl.when(valid & (far > self.stage) & (self.stage > 0))
            def _():
                self.send_sum(0, far, True)

            @pl.when(valid & (far < self.stage) & (self.stage < self.stages - 1))
            def _():
                self.send_sum(1, far, True)

            return carry

        lax.fori_loop(0, 2 * self.stages - 2, body, 0)

    def own(self, total_ref):
        total_ref[...] = self.chip_sum(self.stage)

        @pl.when(self.stage > 0)
        def _():
            self.lane_copy(0, self.stage).wait_recv()
            total_ref[...] += self.lane[0, self.stage].astype(F32)

        @pl.when(self.stage < self.stages - 1)
        def _():
            self.lane_copy(1, self.stage).wait_recv()
            total_ref[...] += self.lane[1, self.stage].astype(F32)

    def finish(self):
        def body(far, carry):
            self.cross_copy(far).wait_send()
            pl.when(far > self.stage)(lambda: self.lane_copy(0, far).wait_send())
            pl.when(far < self.stage)(lambda: self.lane_copy(1, far).wait_send())
            return carry

        lax.fori_loop(0, self.stages, body, 0)


def exchange(axis, size, slots, send_sem, recv_sem):
    me = lax.axis_index(axis)

    def copy_to(other, slot):
        return remote(
            slots.at[slot], slots.at[slot], send_sem.at[other], recv_sem.at[slot], **{axis: other}
        )

    def start(step, carry):
        copy_to(lax.rem(me + step, size), me).start()
        return carry

    def wait(step, carry):
        other = lax.rem(me + step, size)
        copy_to(other, other).wait_recv()
        copy_to(other, me).wait_send()
        return carry

    lax.fori_loop(1, size, start, 0)
    return lambda: lax.fori_loop(1, size, wait, 0)


def project_kernel(
    stages, tok_ref, gain_ref, bias_ref, wq_ref, wk_ref, wv_ref, bq_ref, bv_ref,
    norm_ref, q_ref, k_ref, v_ref, w_ref, send_sem, recv_sem,
):
    me, _, _ = place()
    width = wq_ref.shape[1]
    greet_line(stages)
    normed, _ = normalize(tok_ref[...].astype(F32))
    norm_ref[me] = (normed * gain_ref[...].astype(F32) + bias_ref[...].astype(F32)).astype(BF16)
    gather = LineGather(stages, norm_ref, send_sem, recv_sem)
    gather.start()
    w_ref[...] = jnp.concatenate([wq_ref[...], wk_ref[...], wv_ref[...]], axis=1)

    def compute(block):
        out = nn(norm_ref[block], w_ref[...])
        q_ref[block] = (out[:, :width] + bq_ref[...].astype(F32)).astype(BF16)
        k_ref[block] = out[:, width : 2 * width].astype(BF16)
        v_ref[block] = (out[:, 2 * width :] + bv_ref[...].astype(F32)).astype(BF16)

    gather.run(compute)
    gather.finish()


def project(tokens, gain, bias, wq, wk, wv, bq, bv, devices):
    rows, depth = tokens.shape
    width = wq.shape[1]
    head = jax.ShapeDtypeStruct((devices, rows, width), BF16)
    return pl.pallas_call(
        functools.partial(project_kernel, devices // 2),
        name="project",
        out_shape=(
            jax.ShapeDtypeStruct((devices, rows, depth), BF16), head, head, head,
            jax.ShapeDtypeStruct((depth, 3 * width), BF16),
        ),
        in_specs=[VSPEC] * 8,
        out_specs=(VSPEC,) * 5,
        scratch_shapes=[DMA((devices, 3)), DMA((devices,))],
        compiler_params=pltpu.CompilerParams(
            collective_id=0, has_side_effects=True, vmem_limit_bytes=40 << 20
        ),
    )(tokens, gain[None], bias[None], wq, wk, wv, bq[None], bv[None])


def block_ranges(ids):
    first, last = ids[::BLOCK], ids[BLOCK - 1 :: BLOCK]
    begin = jnp.sum((ids[None, :] > jnp.maximum(first, 0)[:, None]).astype(jnp.int32), axis=1)
    end = jnp.sum((ids[None, :] >= jnp.maximum(last, 1)[:, None]).astype(jnp.int32), axis=1)
    return jnp.stack([begin // BLOCK, (end + BLOCK - 1) // BLOCK])


def lanes_of(head, width):
    lane = lax.broadcasted_iota(jnp.int32, (1, width), 1)
    return (lane >= head * HD) & (lane < (head + 1) * HD)


def attend_kernel(heads, span_ref, q_ref, k_ref, v_ref, idc_ref, idr_ref, o_ref, log_ref, acc_ref):
    length, width = q_ref.shape
    scale = HD ** (-0.5)
    mean_value = jnp.sum(v_ref[...].astype(F32), axis=0, keepdims=True) * (1.0 / length)

    def per_block(block, carry):
        at = pl.ds(pl.multiple_of(block * BLOCK, BLOCK), BLOCK)
        query = q_ref[at, :]
        id_row = idr_ref[:, at]
        masked = [jnp.where(lanes_of(h, width), query, jnp.zeros_like(query)) for h in range(heads)]
        acc_ref[...] = jnp.zeros_like(acc_ref)
        blank = jnp.full((1, BLOCK), NEG_FILL, F32), jnp.zeros((1, BLOCK), F32)

        def per_key(other, state):
            keys_at = pl.ds(pl.multiple_of(other * BLOCK, BLOCK), BLOCK)
            key, value, id_col = k_ref[keys_at, :], v_ref[keys_at, :], idc_ref[keys_at, :]
            allowed = (id_col == id_row) & (id_col > 0)
            fresh = []
            for h in range(heads):
                top, total = state[h]
                scores = jnp.where(allowed, nt(key, masked[h]) * scale, NEG_FILL)
                new_top = jnp.maximum(top, jnp.max(scores, axis=0, keepdims=True))
                weight = jnp.exp(scores - new_top)
                shrink = jnp.exp(top - new_top)
                total = total * shrink + jnp.sum(weight, axis=0, keepdims=True)
                acc_ref[h] = acc_ref[h] * shrink + tn(value, weight.astype(BF16))
                fresh.append((new_top, total))
            return tuple(fresh)

        state = lax.fori_loop(
            span_ref[0, block], span_ref[1, block], per_key, (blank,) * heads
        )
        row = lax.broadcasted_iota(jnp.int32, (width, 1), 0)
        result = jnp.zeros((width, BLOCK), F32)
        for h in range(heads):
            top, total = state[h]
            result = jnp.where(row >= h * HD, acc_ref[h] / total, result)
            log_ref[h : h + 1, at] = jnp.where(id_row == 0, 0.0, top + jnp.log(total))
        o_ref[at, :] = jnp.where(idc_ref[at, :] == 0, mean_value, result.T).astype(BF16)
        return carry

    lax.fori_loop(0, length // BLOCK, per_block, 0)


def attend(q, k, v, span, id_col, id_row):
    length, width = q.shape
    heads = width // HD
    return pl.pallas_call(
        functools.partial(attend_kernel, heads),
        name="attend",
        out_shape=(
            jax.ShapeDtypeStruct((length, width), BF16),
            jax.ShapeDtypeStruct((heads, length), F32),
        ),
        in_specs=[SSPEC] + [VSPEC] * 5,
        out_specs=(VSPEC,) * 2,
        scratch_shapes=[VMEM((heads, width, BLOCK), F32)],
        compiler_params=pltpu.CompilerParams(vmem_limit_bytes=24 << 20),
    )(span, q, k, v, id_col, id_row)


def attend_back_kernel(
    heads, span_ref, q_ref, k_ref, v_ref, idc_ref, idr_ref, o_ref, log_ref, g_ref,
    out_ref, dq_ref, dk_ref, dv_ref, qh_ref, gh_ref, row_ref,
):
    length, width = q_ref.shape
    scale = HD ** (-0.5)
    ones = jnp.ones((8, width), F32)
    dq_ref[...] = jnp.zeros_like(dq_ref)

    def prepare(block, pad):
        at = pl.ds(pl.multiple_of(block * BLOCK, BLOCK), BLOCK)
        query, grad = q_ref[at, :], g_ref[at, :]
        product = grad.astype(F32) * o_ref[at, :].astype(F32)
        for h in range(heads):
            lanes = lanes_of(h, width)
            qh_ref[h, at, :] = jnp.where(lanes, query, jnp.zeros_like(query))
            gh_ref[h, at, :] = jnp.where(lanes, grad, jnp.zeros_like(grad))
            row = lax.dot_general(
                ones, jnp.where(lanes, product, 0.0), (((1,), (1,)), ((), ())),
                precision=lax.Precision.HIGHEST, preferred_element_type=F32,
            )
            row_ref[h : h + 1, at] = row[:1]
        return pad + jnp.sum(
            jnp.where(idc_ref[at, :] == 0, grad.astype(F32), 0.0), axis=0, keepdims=True
        )

    pad = lax.fori_loop(0, length // BLOCK, prepare, jnp.zeros((1, width), F32)) * (1.0 / length)

    def per_key(block, carry):
        at = pl.ds(pl.multiple_of(block * BLOCK, BLOCK), BLOCK)
        key, value, id_col = k_ref[at, :], v_ref[at, :], idc_ref[at, :]
        dk_ref[...] = jnp.zeros_like(dk_ref)
        dv_ref[...] = jnp.zeros_like(dv_ref)

        def per_query(other, inner):
            query_at = pl.ds(pl.multiple_of(other * BLOCK, BLOCK), BLOCK)
            allowed = (id_col == idr_ref[:, query_at]) & (id_col > 0)
            for h in range(heads):
                query, grad = qh_ref[h, query_at, :], gh_ref[h, query_at, :]
                scores = nt(key, query) * scale - log_ref[h : h + 1, query_at]
                prob = jnp.where(allowed, jnp.exp(jnp.where(allowed, scores, 0.0)), 0.0)
                dv_ref[...] += nn(prob.astype(BF16), grad)
                back = prob * (nt(value, grad) - row_ref[h : h + 1, query_at])
                back = back.astype(BF16)
                dk_ref[...] += nn(back, query)
                here = jnp.where(lanes_of(h, width), key, jnp.zeros_like(key))
                dq_ref[query_at, :] += tn(back, here)
            return inner

        lax.fori_loop(span_ref[0, block], span_ref[1, block], per_query, 0)
        out_ref[at, width : 2 * width] = (dk_ref[...] * scale).astype(BF16)
        out_ref[at, 2 * width :] = (dv_ref[...] + pad).astype(BF16)
        return carry

    lax.fori_loop(0, length // BLOCK, per_key, 0)
    out_ref[:, :width] = (dq_ref[...] * scale).astype(BF16)


def attend_back(q, k, v, span, id_col, id_row, o, log_total, grad):
    length, width = q.shape
    heads = width // HD
    return pl.pallas_call(
        functools.partial(attend_back_kernel, heads),
        name="attend_back",
        out_shape=jax.ShapeDtypeStruct((length, 3 * width), BF16),
        in_specs=[SSPEC] + [VSPEC] * 8,
        out_specs=VSPEC,
        scratch_shapes=[
            VMEM((length, width), F32), VMEM((BLOCK, width), F32), VMEM((BLOCK, width), F32),
            VMEM((heads, length, width), BF16), VMEM((heads, length, width), BF16),
            VMEM((heads, length), F32),
        ],
        compiler_params=pltpu.CompilerParams(vmem_limit_bytes=32 << 20),
    )(span, q, k, v, id_col, id_row, o, log_total, grad)


def close_kernel(
    stages, parts, dx_ref, w_ref, norm_ref, tok_ref, gain_ref, resid_ref, small_ref,
    gtok_ref, gw_ref, gsmall_ref,
    partial, cross, lane, total, acc, piece, arrive, back, slots_t, slots_d,
    cross_send, cross_recv, lane_send, lane_recv, piece_send, piece_recv, back_send, back_recv,
    st_send, st_recv, sd_send, sd_recv,
):
    me, _, _ = place()
    row = lax.axis_index("dp")
    devices = 2 * stages
    greet_peers((("tensor", devices), ("dp", parts)))
    scatter = LineScatter(
        stages, partial, cross, lane, (cross_send, cross_recv, lane_send, lane_recv)
    )
    scatter.produce(lambda block: nt(dx_ref[block], w_ref[...]))
    scatter.send_first()

    acc[...] = jnp.zeros_like(acc)

    def gather_weight(block, bias):
        grad = dx_ref[block]
        acc[...] += tn(norm_ref[block], grad)
        return bias + jnp.sum(grad.astype(F32), axis=0, keepdims=True)

    wide = dx_ref.shape[2]
    bias = lax.fori_loop(0, devices, gather_weight, jnp.zeros((1, wide), F32))
    high = acc.shape[0] // parts
    for part in range(parts):
        piece[part] = acc[part * high : (part + 1) * high, :].astype(BF16)

    def piece_copy(other, source):
        return remote(
            piece.at[other], arrive.at[source], piece_send.at[other], piece_recv.at[source], dp=other
        )

    def send_piece(step, carry):
        piece_copy(lax.rem(row + step, parts), row).start()
        return carry

    lax.fori_loop(1, parts, send_piece, 0)
    scatter.send_rest()

    own = piece[row].astype(F32)

    def add_piece(step, own):
        other = lax.rem(row + step, parts)
        piece_copy(other, other).wait_recv()
        return own + arrive[other].astype(F32)

    own = lax.fori_loop(1, parts, add_piece, own)

    def wait_piece(step, carry):
        piece_copy(lax.rem(row + step, parts), row).wait_send()
        return carry

    lax.fori_loop(1, parts, wait_piece, 0)
    back[row] = own.astype(BF16)
    wait_sums = exchange("dp", parts, back, back_send, back_recv)

    scatter.own(total)
    grad = total[...]
    normed, scale = normalize(tok_ref[...].astype(F32))
    slots_t[me] = small_ref[...]
    slots_t[me, 0:1, :] = jnp.sum(grad * normed, axis=0, keepdims=True)
    slots_t[me, 1:2, :] = jnp.sum(grad, axis=0, keepdims=True)
    slots_t[me, 6:7, 0:wide] = bias
    wait_small = exchange("tensor", devices, slots_t, st_send, st_recv)
    inner = grad * gain_ref[...].astype(F32)
    inner_mean = jnp.mean(inner, axis=-1, keepdims=True)
    inner_proj = jnp.mean(inner * normed, axis=-1, keepdims=True)
    gtok_ref[...] = resid_ref[...] + scale * (inner - inner_mean - normed * inner_proj)
    wait_small()
    sums = lax.fori_loop(
        1, devices, lambda slot, so_far: so_far + slots_t[slot], slots_t[0]
    )
    line = lax.broadcasted_iota(jnp.int32, sums.shape, 0)
    slots_d[row] = jnp.where(line < 6, sums, slots_t[me])
    wait_last = exchange("dp", parts, slots_d, sd_send, sd_recv)
    wait_sums()
    for part in range(parts):
        gw_ref[part * high : (part + 1) * high, :] = back[part].astype(F32)
    wait_last()
    gsmall_ref[...] = lax.fori_loop(
        1, parts, lambda slot, so_far: so_far + slots_d[slot], slots_d[0]
    )
    scatter.finish()


def close(dx, w, norm, tokens, gain, resid, small, parts):
    devices, rows, wide = dx.shape
    depth = tokens.shape[1]
    stages = devices // 2
    high = depth // parts
    return pl.pallas_call(
        functools.partial(close_kernel, stages, parts),
        name="close",
        out_shape=(
            jax.ShapeDtypeStruct((rows, depth), F32),
            jax.ShapeDtypeStruct((depth, wide), F32),
            jax.ShapeDtypeStruct(small.shape, F32),
        ),
        in_specs=[VSPEC] * 7,
        out_specs=(VSPEC,) * 3,
        scratch_shapes=[
            VMEM((devices, rows, depth), BF16), VMEM((stages, rows, depth), BF16),
            VMEM((2, stages, rows, depth), BF16), VMEM((rows, depth), F32),
            VMEM((depth, wide), F32), VMEM((parts, high, wide), BF16), VMEM((parts, high, wide), BF16),
            VMEM((parts, high, wide), BF16),
            VMEM((devices,) + small.shape, F32), VMEM((parts,) + small.shape, F32),
            DMA((stages,)), DMA((stages,)), DMA((stages,)), DMA((2, stages)),
            DMA((parts,)), DMA((parts,)), DMA((parts,)), DMA((parts,)),
            DMA((devices,)), DMA((devices,)), DMA((parts,)), DMA((parts,)),
        ],
        compiler_params=pltpu.CompilerParams(
            collective_id=1, has_side_effects=True, vmem_limit_bytes=56 << 20
        ),
    )(dx, w, norm, tokens, gain[None], resid, small)


def layer_norm(values, norm_gain, norm_bias):
    average = jnp.mean(values, axis=-1, keepdims=True)
    centred = values - average
    variance = jnp.mean(centred * centred, axis=-1, keepdims=True)
    return centred * lax.rsqrt(variance + NORM_EPS) * norm_gain + norm_bias


def gelu_tanh(values):
    return jax.nn.gelu(values, approximate=True)


def on_device(
    devices, parts, tokens, picture_ids, ln1_gain, ln1_bias, q_weight, q_bias, k_weight, v_weight, v_bias,
    o_weight, o_bias, ln2_gain, ln2_bias, fc1_weight, fc1_bias, fc2_weight, fc2_bias, out_grad,
):
    own_count, depth = tokens.shape
    tensor_rank = lax.axis_index("tensor")
    hidden_local = fc1_weight.shape[1]
    width = q_weight.shape[1]
    own_ids = lax.dynamic_slice_in_dim(picture_ids, tensor_rank * own_count, own_count)
    valid_mask = (own_ids > 0).astype(F32)[:, None]
    tok_own = tokens.astype(F32)

    norm1_all, q, k, v, w_all = project(
        tokens, ln1_gain, ln1_bias, q_weight, k_weight, v_weight, q_bias, v_bias, devices
    )
    span = block_ranges(picture_ids)
    id_col, id_row = picture_ids[:, None], picture_ids[None, :]
    q, k, v = (item.reshape(LEN, width) for item in (q, k, v))
    attended, log_total = attend(q, k, v, span, id_col, id_row)

    attn_sum = lax.psum_scatter(
        jnp.dot(attended, o_weight, preferred_element_type=F32).astype(BF16),
        "tensor", scatter_dimension=0, tiled=True,
    ).astype(F32)
    residual = tok_own + attn_sum + o_bias.astype(F32)
    normed2, norm2_pull = jax.vjp(
        layer_norm, residual, ln2_gain.astype(F32), ln2_bias.astype(F32)
    )
    ffn_input = lax.all_gather(normed2.astype(BF16), "tensor", axis=0, tiled=True)
    pre_act = jnp.dot(ffn_input, fc1_weight, preferred_element_type=F32) + fc1_bias.astype(F32)
    hidden_f, gelu_pull = jax.vjp(gelu_tanh, pre_act)
    hidden = hidden_f.astype(BF16)
    branch = lax.psum_scatter(
        jnp.dot(hidden, fc2_weight, preferred_element_type=F32).astype(BF16),
        "tensor", scatter_dimension=0, tiled=True,
    ).astype(F32)
    output = (valid_mask * (residual + branch + fc2_bias.astype(F32))).astype(BF16)
    grad_top = valid_mask * out_grad.astype(F32)
    grad_branch = grad_top.astype(BF16)
    grad_fc2b = jnp.sum(grad_top, axis=0)
    grad_branch_all = lax.all_gather(grad_branch, "tensor", axis=0, tiled=True)
    grad_hidden = jnp.einsum("rd,fd->rf", grad_branch_all, fc2_weight, preferred_element_type=F32)
    grad_fc2 = jnp.einsum("rf,rd->fd", hidden, grad_branch_all, preferred_element_type=F32)
    grad_pre_low = gelu_pull(grad_hidden)[0].astype(BF16)
    grad_fc1 = jnp.einsum("rd,rf->df", ffn_input, grad_pre_low, preferred_element_type=F32)
    grad_fc1b = jnp.sum(grad_pre_low.astype(F32), axis=0)
    grad_norm2 = lax.psum_scatter(
        jnp.einsum("rf,df->rd", grad_pre_low, fc1_weight, preferred_element_type=F32).astype(BF16),
        "tensor", scatter_dimension=0, tiled=True,
    ).astype(F32)
    grad_resid2, grad_ln2_gain, grad_ln2_bias = norm2_pull(grad_norm2)
    grad_residual = grad_top + grad_resid2
    grad_obias = jnp.sum(grad_residual, axis=0)
    grad_attn_all = lax.all_gather(grad_residual.astype(BF16), "tensor", axis=0, tiled=True)
    grad_ow = jnp.einsum("rc,rd->cd", attended, grad_attn_all, preferred_element_type=F32)
    grad_attended = jnp.einsum(
        "rd,cd->rc", grad_attn_all, o_weight, preferred_element_type=F32
    ).astype(BF16)

    dqkv = attend_back(q, k, v, span, id_col, id_row, attended, log_total, grad_attended)
    zero = jnp.zeros((1, depth), F32)
    small = jnp.concatenate(
        [
            zero, zero, grad_ln2_gain[None], grad_ln2_bias[None], grad_obias[None], grad_fc2b[None],
            zero, jnp.pad(grad_fc1b[None], ((0, 0), (0, depth - hidden_local))),
        ]
    )
    grad_tokens, grad_w, sums = close(
        dqkv.reshape(devices, own_count, 3 * width), w_all, norm1_all, tokens, ln1_gain,
        grad_residual, small, parts,
    )
    grad_ow, grad_fc1, grad_fc2 = (
        lax.psum(item.astype(BF16), "dp").astype(F32) for item in (grad_ow, grad_fc1, grad_fc2)
    )
    return (
        output, grad_tokens, sums[0], sums[1],
        grad_w[:, :width], sums[6, :width], grad_w[:, width : 2 * width], grad_w[:, 2 * width :],
        sums[6, 2 * width : 3 * width], grad_ow, sums[4], sums[2], sums[3],
        grad_fc1, sums[7, :hidden_local], grad_fc2, sums[5],
    )


def solution(mesh):
    rows, whole = P(("dp", "tensor"), None), P()
    columns, down, along = P(None, "tensor"), P("tensor", None), P("tensor")
    return jax.shard_map(
        functools.partial(on_device, mesh.shape["tensor"], mesh.shape["dp"]),
        mesh=mesh,
        in_specs=(
            rows, P("dp"), whole, whole, columns, along, columns, columns, along, down, whole,
            whole, whole, columns, along, down, whole, rows,
        ),
        out_specs=(
            rows, rows, whole, whole, columns, along, columns, columns, along, down, whole,
            whole, whole, columns, along, down, whole,
        ),
        check_vma=False,
    )
```

```python
import functools

import jax
import jax.numpy as jnp
from jax import lax
from jax.experimental import pallas as pl
from jax.experimental.pallas import tpu as pltpu
from jax.sharding import PartitionSpec as P

HD = 72
LEN = 2048
BLOCK = 256
NORM_EPS = 1e-06
NEG_FILL = -1e30
BF16 = jnp.bfloat16
F32 = jnp.float32
MESH = pl.DeviceIdType.MESH
VMEM = pltpu.VMEM
DMA = pltpu.SemaphoreType.DMA
VSPEC = pl.BlockSpec(memory_space=pltpu.VMEM)
SSPEC = pl.BlockSpec(memory_space=pltpu.SMEM)


def nn(left, right):
    return lax.dot_general(left, right, (((1,), (0,)), ((), ())), preferred_element_type=F32)


def nt(left, right):
    return lax.dot_general(left, right, (((1,), (1,)), ((), ())), preferred_element_type=F32)


def tn(left, right):
    return lax.dot_general(left, right, (((0,), (0,)), ((), ())), preferred_element_type=F32)


def remote(src, dst, send_sem, recv_sem, **where):
    return pltpu.make_async_remote_copy(
        src_ref=src, dst_ref=dst, send_sem=send_sem, recv_sem=recv_sem,
        device_id=where, device_id_type=MESH,
    )


def place():
    me = lax.axis_index("tensor")
    core = lax.rem(me, 2)
    return me, core, lax.div(me, 2)


def greet_peers(axes):
    barrier = pltpu.get_barrier_semaphore()
    for axis, size in axes:
        me = lax.axis_index(axis)

        def greet(step, carry):
            pl.semaphore_signal(
                barrier, inc=1, device_id={axis: lax.rem(me + step, size)}, device_id_type=MESH
            )
            return carry

        lax.fori_loop(1, size, greet, 0)
    pl.semaphore_wait(barrier, sum(size - 1 for _, size in axes))


def greet_line(stages):
    me, core, stage = place()
    barrier = pltpu.get_barrier_semaphore()
    has_left, has_right = stage > 0, stage < stages - 1

    def greet(other):
        pl.semaphore_signal(barrier, inc=1, device_id={"tensor": other}, device_id_type=MESH)

    greet(me + 1 - 2 * core)
    pl.when(has_left)(lambda: greet(me - 2))
    pl.when(has_right)(lambda: greet(me + 2))
    pl.semaphore_wait(barrier, 1 + has_left.astype(jnp.int32) + has_right.astype(jnp.int32))


def normalize(values):
    average = jnp.mean(values, axis=-1, keepdims=True)
    centred = values - average
    variance = jnp.mean(centred * centred, axis=-1, keepdims=True)
    scale = lax.rsqrt(variance + NORM_EPS)
    return centred * scale, scale


class LineGather:
    def __init__(self, stages, buffer, send_sem, recv_sem):
        self.stages, self.buffer, self.send_sem, self.recv_sem = stages, buffer, send_sem, recv_sem
        self.me, self.core, self.stage = place()
        self.partner = self.me + 1 - 2 * self.core

    def copy(self, block, way, target):
        return remote(
            self.buffer.at[block], self.buffer.at[block],
            self.send_sem.at[block, way], self.recv_sem.at[block], tensor=target,
        )

    def each_copy(self, block, right, left, act):
        pl.when(right)(lambda: act(self.copy(block, 0, self.me + 2)))
        pl.when(left)(lambda: act(self.copy(block, 1, self.me - 2)))
        act(self.copy(block, 2, self.partner))

    def start(self):
        self.each_copy(
            self.me, self.stage < self.stages - 1, self.stage > 0, lambda copy: copy.start()
        )

    def steps(self):
        return 2 + 4 * (self.stages - 1)

    def locate(self, step):
        index = jnp.maximum(step - 2, 0)
        reach = lax.div(index, 4) + 1
        slot = lax.rem(index, 4)
        side, other = lax.rem(slot, 2), lax.div(slot, 2)
        far = jnp.where(side == 0, self.stage - reach, self.stage + reach)
        valid = (step < 2) | ((far >= 0) & (far < self.stages))
        far = jnp.where(step < 2, self.stage, far)
        crossed = jnp.where(step < 2, step, other)
        block = 2 * far + jnp.where(crossed == 0, self.core, 1 - self.core)
        relay = (step >= 2) & (other == 0)
        right = relay & (side == 0) & (self.stage < self.stages - 1)
        left = relay & (side == 1) & (self.stage > 0)
        return valid, block, relay, right, left

    def run(self, compute, low=0, high=None):
        def body(step, carry):
            valid, block, relay, right, left = self.locate(step)

            @pl.when(valid)
            def _():
                @pl.when(step > 0)
                def _():
                    self.copy(block, 2, self.partner).wait_recv()

                @pl.when(relay)
                def _():
                    self.each_copy(block, right, left, lambda copy: copy.start())

                compute(block)

            return carry

        lax.fori_loop(low, self.steps() if high is None else high, body, 0)

    def run_reach(self, reach, compute):
        self.run(compute, jnp.maximum(4 * reach - 2, 0), 4 * reach + 2)

    def finish(self):
        self.each_copy(
            self.me, self.stage < self.stages - 1, self.stage > 0, lambda copy: copy.wait_send()
        )

        def body(step, carry):
            valid, block, relay, right, left = self.locate(step)

            @pl.when(valid & relay)
            def _():
                self.each_copy(block, right, left, lambda copy: copy.wait_send())

            return carry

        lax.fori_loop(2, self.steps(), body, 0)


class LineScatter:
    def __init__(self, stages, partial, cross, lane, sems):
        self.stages, self.partial, self.cross, self.lane = stages, partial, cross, lane
        self.cross_send, self.cross_recv, self.lane_send, self.lane_recv = sems
        self.me, self.core, self.stage = place()
        self.partner = self.me + 1 - 2 * self.core

    def cross_copy(self, far):
        return remote(
            self.partial.at[2 * far + 1 - self.core], self.cross.at[far],
            self.cross_send.at[far], self.cross_recv.at[far], tensor=self.partner,
        )

    def slot(self, way, far, holder):
        return far if way == 0 else jnp.where(far == holder, self.stages, far)

    def lane_copy(self, way, far, holder):
        target = self.me + 2 if way == 0 else self.me - 2
        slot = self.slot(way, far, holder)
        return remote(
            self.partial.at[2 * far + self.core], self.lane.at[slot],
            self.lane_send.at[far], self.lane_recv.at[slot], tensor=target,
        )

    def sent(self, way, far):
        return self.lane_copy(way, far, self.stage + (1 if way == 0 else -1))

    def received(self, way, far):
        self.lane_copy(way, far, self.stage).wait_recv()
        return self.lane[self.slot(way, far, self.stage)].astype(F32)

    def put(self, block, value):
        self.partial[block] = value.astype(BF16)

        @pl.when(lax.rem(block, 2) != self.core)
        def _():
            self.cross_copy(lax.div(block, 2)).start()

    def produce(self, compute):
        def body(index, carry):
            reach = self.stages - 1 - lax.div(index, 4)
            side, other = lax.rem(lax.div(index, 2), 2), lax.rem(index, 2)
            far = jnp.where(side == 0, self.stage + reach, self.stage - reach)

            @pl.when((far >= 0) & (far < self.stages) & ((reach > 0) | (side == 0)))
            def _():
                block = 2 * far + jnp.where(other == 0, 1 - self.core, self.core)
                self.put(block, compute(block))

            return carry

        lax.fori_loop(0, 4 * self.stages, body, 0)

    def chip_sum(self, far):
        return self.partial[2 * far + self.core].astype(F32) + self.cross[far].astype(F32)

    def send_sum(self, way, far, incoming):
        self.cross_copy(far).wait_recv()
        block = 2 * far + self.core

        @pl.when(incoming)
        def _():
            self.partial[block] = (self.chip_sum(far) + self.received(way, far)).astype(BF16)

        @pl.when(jnp.logical_not(incoming))
        def _():
            self.partial[block] = self.chip_sum(far).astype(BF16)

        self.sent(way, far).start()

    def step(self, reach):
        right, left = self.stage + reach, self.stage - reach
        pl.when(right < self.stages)(lambda: self.send_sum(0, right, self.stage > 0))
        pl.when(left >= 0)(lambda: self.send_sum(1, left, self.stage < self.stages - 1))

    def steps(self, first, last):
        lax.fori_loop(first, last, lambda index, carry: (self.step(self.stages - 1 - index), carry)[1], 0)

    def own(self, total_ref):
        self.cross_copy(self.stage).wait_recv()
        total_ref[...] = self.chip_sum(self.stage)

        @pl.when(self.stage > 0)
        def _():
            total_ref[...] += self.received(0, self.stage)

        @pl.when(self.stage < self.stages - 1)
        def _():
            total_ref[...] += self.received(1, self.stage)

    def finish(self):
        def body(far, carry):
            self.cross_copy(far).wait_send()
            pl.when(far > self.stage)(lambda: self.sent(0, far).wait_send())
            pl.when(far < self.stage)(lambda: self.sent(1, far).wait_send())
            return carry

        lax.fori_loop(0, self.stages, body, 0)


def scatter_shapes(stages, rows, depth):
    return [
        VMEM((2 * stages, rows, depth), BF16), VMEM((stages, rows, depth), BF16),
        VMEM((stages + 1, rows, depth), BF16),
        DMA((stages,)), DMA((stages,)), DMA((stages,)), DMA((stages + 1,)),
    ]


def exchange(axis, size, slots, send_sem, recv_sem):
    me = lax.axis_index(axis)

    def copy_to(other, slot):
        return remote(
            slots.at[slot], slots.at[slot], send_sem.at[other], recv_sem.at[slot], **{axis: other}
        )

    def start(step, carry):
        copy_to(lax.rem(me + step, size), me).start()
        return carry

    def wait(step, carry):
        other = lax.rem(me + step, size)
        copy_to(other, other).wait_recv()
        copy_to(other, me).wait_send()
        return carry

    lax.fori_loop(1, size, start, 0)
    return lambda: lax.fori_loop(1, size, wait, 0)


def project_kernel(
    stages, tok_ref, gain_ref, bias_ref, wq_ref, wk_ref, wv_ref, bq_ref, bv_ref,
    norm_ref, q_ref, k_ref, v_ref, w_ref, send_sem, recv_sem,
):
    me, _, _ = place()
    width = wq_ref.shape[1]
    greet_line(stages)
    normed, _ = normalize(tok_ref[...].astype(F32))
    norm_ref[me] = (normed * gain_ref[...].astype(F32) + bias_ref[...].astype(F32)).astype(BF16)
    gather = LineGather(stages, norm_ref, send_sem, recv_sem)
    gather.start()
    w_ref[...] = jnp.concatenate([wq_ref[...], wk_ref[...], wv_ref[...]], axis=1)

    def compute(block):
        out = nn(norm_ref[block], w_ref[...])
        q_ref[block] = (out[:, :width] + bq_ref[...].astype(F32)).astype(BF16)
        k_ref[block] = out[:, width : 2 * width].astype(BF16)
        v_ref[block] = (out[:, 2 * width :] + bv_ref[...].astype(F32)).astype(BF16)

    gather.run(compute)
    gather.finish()


def project(tokens, gain, bias, wq, wk, wv, bq, bv, devices):
    rows, depth = tokens.shape
    width = wq.shape[1]
    head = jax.ShapeDtypeStruct((devices, rows, width), BF16)
    return pl.pallas_call(
        functools.partial(project_kernel, devices // 2),
        name="project",
        out_shape=(
            jax.ShapeDtypeStruct((devices, rows, depth), BF16), head, head, head,
            jax.ShapeDtypeStruct((depth, 3 * width), BF16),
        ),
        in_specs=[VSPEC] * 8,
        out_specs=(VSPEC,) * 5,
        scratch_shapes=[DMA((devices, 3)), DMA((devices,))],
        compiler_params=pltpu.CompilerParams(
            collective_id=0, has_side_effects=True, vmem_limit_bytes=40 << 20
        ),
    )(tokens, gain[None], bias[None], wq, wk, wv, bq[None], bv[None])


def block_ranges(ids):
    first, last = ids[::BLOCK], ids[BLOCK - 1 :: BLOCK]
    begin = jnp.sum((ids[None, :] > jnp.maximum(first, 0)[:, None]).astype(jnp.int32), axis=1)
    end = jnp.sum((ids[None, :] >= jnp.maximum(last, 1)[:, None]).astype(jnp.int32), axis=1)
    return jnp.stack([begin // BLOCK, (end + BLOCK - 1) // BLOCK])


def lanes_of(head, width):
    lane = lax.broadcasted_iota(jnp.int32, (1, width), 1)
    return (lane >= head * HD) & (lane < (head + 1) * HD)


def attend_kernel(heads, span_ref, q_ref, k_ref, v_ref, idc_ref, idr_ref, o_ref, log_ref, acc_ref):
    length, width = q_ref.shape
    scale = HD ** (-0.5)
    mean_value = jnp.sum(v_ref[...].astype(F32), axis=0, keepdims=True) * (1.0 / length)

    def per_block(block, carry):
        at = pl.ds(pl.multiple_of(block * BLOCK, BLOCK), BLOCK)
        query = q_ref[at, :]
        id_row = idr_ref[:, at]
        masked = [jnp.where(lanes_of(h, width), query, jnp.zeros_like(query)) for h in range(heads)]
        acc_ref[...] = jnp.zeros_like(acc_ref)
        blank = jnp.full((1, BLOCK), NEG_FILL, F32), jnp.zeros((1, BLOCK), F32)

        def per_key(other, state):
            keys_at = pl.ds(pl.multiple_of(other * BLOCK, BLOCK), BLOCK)
            key, value, id_col = k_ref[keys_at, :], v_ref[keys_at, :], idc_ref[keys_at, :]
            allowed = (id_col == id_row) & (id_col > 0)
            fresh = []
            for h in range(heads):
                top, total = state[h]
                scores = jnp.where(allowed, nt(key, masked[h]) * scale, NEG_FILL)
                new_top = jnp.maximum(top, jnp.max(scores, axis=0, keepdims=True))
                weight = jnp.exp(scores - new_top)
                shrink = jnp.exp(top - new_top)
                total = total * shrink + jnp.sum(weight, axis=0, keepdims=True)
                acc_ref[h] = acc_ref[h] * shrink + tn(value, weight.astype(BF16))
                fresh.append((new_top, total))
            return tuple(fresh)

        state = lax.fori_loop(
            span_ref[0, block], span_ref[1, block], per_key, (blank,) * heads
        )
        row = lax.broadcasted_iota(jnp.int32, (width, 1), 0)
        result = jnp.zeros((width, BLOCK), F32)
        for h in range(heads):
            top, total = state[h]
            result = jnp.where(row >= h * HD, acc_ref[h] / total, result)
            log_ref[h : h + 1, at] = jnp.where(id_row == 0, 0.0, top + jnp.log(total))
        o_ref[at, :] = jnp.where(idc_ref[at, :] == 0, mean_value, result.T).astype(BF16)
        return carry

    lax.fori_loop(0, length // BLOCK, per_block, 0)


def attend(q, k, v, span, id_col, id_row):
    length, width = q.shape
    heads = width // HD
    return pl.pallas_call(
        functools.partial(attend_kernel, heads),
        name="attend",
        out_shape=(
            jax.ShapeDtypeStruct((length, width), BF16),
            jax.ShapeDtypeStruct((heads, length), F32),
        ),
        in_specs=[SSPEC] + [VSPEC] * 5,
        out_specs=(VSPEC,) * 2,
        scratch_shapes=[VMEM((heads, width, BLOCK), F32)],
        compiler_params=pltpu.CompilerParams(vmem_limit_bytes=24 << 20),
    )(span, q, k, v, id_col, id_row)


def attend_back_kernel(
    heads, span_ref, q_ref, k_ref, v_ref, idc_ref, idr_ref, o_ref, log_ref, g_ref,
    out_ref, dq_ref, dk_ref, dv_ref, qh_ref, gh_ref, row_ref,
):
    length, width = q_ref.shape
    scale = HD ** (-0.5)
    ones = jnp.ones((8, width), F32)
    dq_ref[...] = jnp.zeros_like(dq_ref)

    def prepare(block, pad):
        at = pl.ds(pl.multiple_of(block * BLOCK, BLOCK), BLOCK)
        query, grad = q_ref[at, :], g_ref[at, :]
        product = grad.astype(F32) * o_ref[at, :].astype(F32)
        for h in range(heads):
            lanes = lanes_of(h, width)
            qh_ref[h, at, :] = jnp.where(lanes, query, jnp.zeros_like(query))
            gh_ref[h, at, :] = jnp.where(lanes, grad, jnp.zeros_like(grad))
            row = lax.dot_general(
                ones, jnp.where(lanes, product, 0.0), (((1,), (1,)), ((), ())),
                precision=lax.Precision.HIGHEST, preferred_element_type=F32,
            )
            row_ref[h : h + 1, at] = row[:1]
        return pad + jnp.sum(
            jnp.where(idc_ref[at, :] == 0, grad.astype(F32), 0.0), axis=0, keepdims=True
        )

    pad = lax.fori_loop(0, length // BLOCK, prepare, jnp.zeros((1, width), F32)) * (1.0 / length)

    def per_key(block, carry):
        at = pl.ds(pl.multiple_of(block * BLOCK, BLOCK), BLOCK)
        key, value, id_col = k_ref[at, :], v_ref[at, :], idc_ref[at, :]
        dk_ref[...] = jnp.zeros_like(dk_ref)
        dv_ref[...] = jnp.zeros_like(dv_ref)

        def per_query(other, inner):
            query_at = pl.ds(pl.multiple_of(other * BLOCK, BLOCK), BLOCK)
            allowed = (id_col == idr_ref[:, query_at]) & (id_col > 0)
            for h in range(heads):
                query, grad = qh_ref[h, query_at, :], gh_ref[h, query_at, :]
                scores = nt(key, query) * scale - log_ref[h : h + 1, query_at]
                prob = jnp.where(allowed, jnp.exp(jnp.where(allowed, scores, 0.0)), 0.0)
                dv_ref[...] += nn(prob.astype(BF16), grad)
                back = prob * (nt(value, grad) - row_ref[h : h + 1, query_at])
                back = back.astype(BF16)
                dk_ref[...] += nn(back, query)
                here = jnp.where(lanes_of(h, width), key, jnp.zeros_like(key))
                dq_ref[query_at, :] += tn(back, here)
            return inner

        lax.fori_loop(span_ref[0, block], span_ref[1, block], per_query, 0)
        out_ref[at, width : 2 * width] = (dk_ref[...] * scale).astype(BF16)
        out_ref[at, 2 * width :] = (dv_ref[...] + pad).astype(BF16)
        return carry

    lax.fori_loop(0, length // BLOCK, per_key, 0)
    out_ref[:, :width] = (dq_ref[...] * scale).astype(BF16)


def attend_back(q, k, v, span, id_col, id_row, o, log_total, grad):
    length, width = q.shape
    heads = width // HD
    return pl.pallas_call(
        functools.partial(attend_back_kernel, heads),
        name="attend_back",
        out_shape=jax.ShapeDtypeStruct((length, 3 * width), BF16),
        in_specs=[SSPEC] + [VSPEC] * 8,
        out_specs=VSPEC,
        scratch_shapes=[
            VMEM((length, width), F32), VMEM((BLOCK, width), F32), VMEM((BLOCK, width), F32),
            VMEM((heads, length, width), BF16), VMEM((heads, length, width), BF16),
            VMEM((heads, length), F32),
        ],
        compiler_params=pltpu.CompilerParams(vmem_limit_bytes=32 << 20),
    )(span, q, k, v, id_col, id_row, o, log_total, grad)


def gelu_pair(u):
    slope = (2.0 / jnp.pi) ** 0.5
    bent = jnp.tanh(slope * (u + 0.044715 * u * u * u))
    half = 0.5 * (1.0 + bent)
    return u * half, half + 0.5 * u * (1.0 - bent * bent) * slope * (1.0 + 3 * 0.044715 * u * u)


def middle_kernel(
    stages, att_hbm, wo_hbm, fc1_hbm, fc2_hbm, tok_hbm, top_hbm, ids_ref,
    ob_ref, gain_ref, bias_ref, fb1_ref, fb2_ref,
    out_ref, gres_ref, gatt_ref, dwo_hbm, dfc1_hbm, dfc2_hbm, small_ref,
    wo, fc1, fc2, tok, top, load_sem,
    held, held_send, held_recv, norm_all, norm_send, norm_recv, top_all, top_send, top_recv,
    hidden, slope, grad_pre,
    br_part, br_cross, br_lane, br_s0, br_s1, br_s2, br_s3,
    gn_part, gn_cross, gn_lane, gn_s0, gn_s1, gn_s2, gn_s3,
    resid, total, acc1, acc2, low1, low2, out_sem, back, back_send, back_recv,
):
    me, _, _ = place()
    devices = 2 * stages
    rows, depth = tok_hbm.shape
    units = fc1_hbm.shape[1]
    loads = [
        pltpu.make_async_copy(src, dst, load_sem.at[index])
        for index, (src, dst) in enumerate(
            ((tok_hbm, tok), (top_hbm, top), (wo_hbm, wo), (fc1_hbm, fc1), (fc2_hbm, fc2),
             (att_hbm.at[me], held.at[me]))
        )
    ]
    for load in loads:
        load.start()
    greet_peers((("tensor", devices),))

    def held_copy(other, source):
        return remote(
            att_hbm.at[other], held.at[source], held_send.at[other], held_recv.at[source], tensor=other
        )

    def send_held(step, carry):
        held_copy(lax.rem(me + step, devices), me).start()
        return carry

    lax.fori_loop(1, devices, send_held, 0)
    gather2 = LineGather(stages, norm_all, norm_send, norm_recv)
    gather3 = LineGather(stages, top_all, top_send, top_recv)
    branch = LineScatter(stages, br_part, br_cross, br_lane, (br_s0, br_s1, br_s2, br_s3))
    gnorm = LineScatter(stages, gn_part, gn_cross, gn_lane, (gn_s0, gn_s1, gn_s2, gn_s3))

    mask = jnp.where(ids_ref[...] > 0, 1.0, 0.0)
    small_ref[...] = jnp.zeros_like(small_ref)
    loads[0].wait()
    loads[1].wait()
    top_own = top[...].astype(F32) * mask
    top_all[me] = top_own.astype(BF16)
    small_ref[5:6, :] = jnp.sum(top_own, axis=0, keepdims=True)
    resid[...] = tok[...].astype(F32) + ob_ref[...].astype(F32)
    loads[2].wait()
    loads[5].wait()
    resid[...] += nn(held[me], wo[me])

    def add_held(step, carry):
        other = lax.rem(me + devices - step, devices)
        held_copy(other, other).wait_recv()
        resid[...] += nn(held[other], wo[other])
        return carry

    lax.fori_loop(1, devices, add_held, 0)
    normed, _ = normalize(resid[...])
    norm_all[me] = (normed * gain_ref[...].astype(F32) + bias_ref[...].astype(F32)).astype(BF16)
    gather2.start()
    loads[3].wait()
    loads[4].wait()

    def forward(block):
        pre_act = nn(norm_all[block], fc1[...]) + fb1_ref[...].astype(F32)
        value, slope_now = gelu_pair(pre_act)
        hidden[block] = value.astype(BF16)
        slope[block] = slope_now
        branch.put(block, nn(hidden[block], fc2[...]))

    gather2.run(forward)
    gather3.start()

    def backward(block):
        grad = nt(top_all[block], fc2[...]) * slope[block]
        low = grad.astype(BF16)
        grad_pre[block] = low
        small_ref[7:8, 0:units] += jnp.sum(low.astype(F32), axis=0, keepdims=True)
        gnorm.put(block, nt(grad_pre[block], fc1[...]))

    def both(index, carry):
        gather3.run_reach(index, backward)
        pl.when(index < stages - 1)(lambda: branch.step(stages - 1 - index))
        return carry

    lax.fori_loop(0, stages, both, 0)
    gnorm.step(stages - 1)

    branch.own(total)
    out_ref[...] = (mask * (resid[...] + total[...] + fb2_ref[...].astype(F32))).astype(BF16)

    acc2[...] = jnp.zeros_like(acc2)

    def weight2(block, carry):
        acc2[...] += tn(hidden[block], top_all[block])
        return carry

    lax.fori_loop(0, devices, weight2, 0)
    low2[...] = acc2[...].astype(BF16)
    out2 = pltpu.make_async_copy(low2, dfc2_hbm, out_sem.at[0])
    out2.start()
    gnorm.steps(1, min(2, stages - 1))
    acc1[...] = jnp.zeros_like(acc1)

    def weight1(block, carry):
        acc1[...] += tn(norm_all[block], grad_pre[block])
        return carry

    lax.fori_loop(0, devices, weight1, 0)
    low1[...] = acc1[...].astype(BF16)
    out1 = pltpu.make_async_copy(low1, dfc1_hbm, out_sem.at[1])
    out1.start()
    gnorm.steps(2, stages - 1)

    gnorm.own(total)
    grad = total[...]
    normed, scale = normalize(resid[...])
    small_ref[2:3, :] = jnp.sum(grad * normed, axis=0, keepdims=True)
    small_ref[3:4, :] = jnp.sum(grad, axis=0, keepdims=True)
    inner = grad * gain_ref[...].astype(F32)
    inner_mean = jnp.mean(inner, axis=-1, keepdims=True)
    inner_proj = jnp.mean(inner * normed, axis=-1, keepdims=True)
    grad_resid = top[...].astype(F32) * mask + scale * (inner - inner_mean - normed * inner_proj)
    gres_ref[...] = grad_resid
    tok[...] = grad_resid.astype(BF16)
    small_ref[4:5, :] = jnp.sum(grad_resid, axis=0, keepdims=True)

    def back_copy(other, source):
        return remote(
            back.at[other], gatt_ref.at[source], back_send.at[other], back_recv.at[source], tensor=other
        )

    def send_back(step, carry):
        other = lax.rem(me + step, devices)
        back[other] = nt(tok[...], wo[other]).astype(BF16)
        back_copy(other, me).start()
        return carry

    lax.fori_loop(1, devices, send_back, 0)
    gatt_ref[me] = nt(tok[...], wo[me]).astype(BF16)

    def weight_o(block, carry):
        wo[block] = tn(held[block], tok[...]).astype(BF16)
        return carry

    lax.fori_loop(0, devices, weight_o, 0)
    out3 = pltpu.make_async_copy(wo, dwo_hbm, out_sem.at[2])
    out3.start()

    def settle(step, carry):
        other = lax.rem(me + devices - step, devices)
        back_copy(other, other).wait_recv()
        back_copy(other, me).wait_send()
        held_copy(other, me).wait_send()
        return carry

    lax.fori_loop(1, devices, settle, 0)
    gather2.finish()
    gather3.finish()
    branch.finish()
    gnorm.finish()
    out1.wait()
    out2.wait()
    out3.wait()


def middle(att, wo, fc1, fc2, tokens, out_grad, id_col, o_bias, gain, bias, fc1_bias, fc2_bias):
    devices, rows, width = att.shape
    depth, units = fc1.shape
    stages = devices // 2
    anywhere = pl.BlockSpec(memory_space=pl.ANY)
    return pl.pallas_call(
        functools.partial(middle_kernel, stages),
        name="middle",
        out_shape=(
            jax.ShapeDtypeStruct((rows, depth), BF16),
            jax.ShapeDtypeStruct((rows, depth), F32),
            jax.ShapeDtypeStruct((devices, rows, width), BF16),
            jax.ShapeDtypeStruct((devices, width, depth), BF16),
            jax.ShapeDtypeStruct((depth, units), BF16),
            jax.ShapeDtypeStruct((units, depth), BF16),
            jax.ShapeDtypeStruct((8, depth), F32),
        ),
        in_specs=[anywhere] * 6 + [VSPEC] * 6,
        out_specs=(VSPEC, VSPEC, VSPEC, anywhere, anywhere, anywhere, VSPEC),
        scratch_shapes=[
            VMEM((devices, width, depth), BF16), VMEM((depth, units), BF16), VMEM((units, depth), BF16),
            VMEM((rows, depth), BF16), VMEM((rows, depth), BF16), DMA((6,)),
            VMEM((devices, rows, width), BF16), DMA((devices,)), DMA((devices,)),
            VMEM((devices, rows, depth), BF16), DMA((devices, 3)), DMA((devices,)),
            VMEM((devices, rows, depth), BF16), DMA((devices, 3)), DMA((devices,)),
            VMEM((devices, rows, units), BF16), VMEM((devices, rows, units), F32),
            VMEM((devices, rows, units), BF16),
            *scatter_shapes(stages, rows, depth), *scatter_shapes(stages, rows, depth),
            VMEM((rows, depth), F32), VMEM((rows, depth), F32),
            VMEM((depth, units), F32), VMEM((units, depth), F32),
            VMEM((depth, units), BF16), VMEM((units, depth), BF16),
            DMA((3,)),
            VMEM((devices, rows, width), BF16), DMA((devices,)), DMA((devices,)),
        ],
        compiler_params=pltpu.CompilerParams(
            collective_id=2, has_side_effects=True, vmem_limit_bytes=67043328
        ),
    )(
        att, wo, fc1, fc2, tokens, out_grad, id_col, o_bias[None], gain[None], bias[None],
        fc1_bias[None], fc2_bias[None],
    )


def close_kernel(
    stages, parts, dx_ref, w_ref, norm_ref, tok_ref, gain_ref, resid_ref, small_ref,
    gtok_ref, gw_ref, gsmall_ref,
    partial, cross, lane, cross_send, cross_recv, lane_send, lane_recv,
    total, acc, piece, arrive, back, slots_t, slots_d, piece_send, piece_recv, back_send, back_recv,
    st_send, st_recv, sd_send, sd_recv,
):
    me, _, _ = place()
    row = lax.axis_index("dp")
    devices = 2 * stages
    greet_peers((("tensor", devices), ("dp", parts)))
    scatter = LineScatter(
        stages, partial, cross, lane, (cross_send, cross_recv, lane_send, lane_recv)
    )
    scatter.produce(lambda block: nt(dx_ref[block], w_ref[...]))
    scatter.step(stages - 1)

    acc[...] = jnp.zeros_like(acc)

    def gather_weight(block, bias):
        grad = dx_ref[block]
        acc[...] += tn(norm_ref[block], grad)
        return bias + jnp.sum(grad.astype(F32), axis=0, keepdims=True)

    wide = dx_ref.shape[2]
    bias = lax.fori_loop(0, devices, gather_weight, jnp.zeros((1, wide), F32))
    high = acc.shape[0] // parts
    for part in range(parts):
        piece[part] = acc[part * high : (part + 1) * high, :].astype(BF16)

    def piece_copy(other, source):
        return remote(
            piece.at[other], arrive.at[source], piece_send.at[other], piece_recv.at[source], dp=other
        )

    def send_piece(step, carry):
        piece_copy(lax.rem(row + step, parts), row).start()
        return carry

    lax.fori_loop(1, parts, send_piece, 0)
    scatter.steps(1, stages - 1)

    own = piece[row].astype(F32)

    def add_piece(step, own):
        other = lax.rem(row + step, parts)
        piece_copy(other, other).wait_recv()
        return own + arrive[other].astype(F32)

    own = lax.fori_loop(1, parts, add_piece, own)

    def wait_piece(step, carry):
        piece_copy(lax.rem(row + step, parts), row).wait_send()
        return carry

    lax.fori_loop(1, parts, wait_piece, 0)
    back[row] = own.astype(BF16)
    wait_sums = exchange("dp", parts, back, back_send, back_recv)

    scatter.own(total)
    grad = total[...]
    normed, scale = normalize(tok_ref[...].astype(F32))
    slots_t[me] = small_ref[...]
    slots_t[me, 0:1, :] = jnp.sum(grad * normed, axis=0, keepdims=True)
    slots_t[me, 1:2, :] = jnp.sum(grad, axis=0, keepdims=True)
    slots_t[me, 6:7, 0:wide] = bias
    wait_small = exchange("tensor", devices, slots_t, st_send, st_recv)
    inner = grad * gain_ref[...].astype(F32)
    inner_mean = jnp.mean(inner, axis=-1, keepdims=True)
    inner_proj = jnp.mean(inner * normed, axis=-1, keepdims=True)
    gtok_ref[...] = resid_ref[...] + scale * (inner - inner_mean - normed * inner_proj)
    wait_small()
    sums = lax.fori_loop(
        1, devices, lambda slot, so_far: so_far + slots_t[slot], slots_t[0]
    )
    line = lax.broadcasted_iota(jnp.int32, sums.shape, 0)
    slots_d[row] = jnp.where(line < 6, sums, slots_t[me])
    wait_last = exchange("dp", parts, slots_d, sd_send, sd_recv)
    wait_sums()
    for part in range(parts):
        gw_ref[part * high : (part + 1) * high, :] = back[part].astype(F32)
    wait_last()
    gsmall_ref[...] = lax.fori_loop(
        1, parts, lambda slot, so_far: so_far + slots_d[slot], slots_d[0]
    )
    scatter.finish()


def close(dx, w, norm, tokens, gain, resid, small, parts):
    devices, rows, wide = dx.shape
    depth = tokens.shape[1]
    stages = devices // 2
    high = depth // parts
    return pl.pallas_call(
        functools.partial(close_kernel, stages, parts),
        name="close",
        out_shape=(
            jax.ShapeDtypeStruct((rows, depth), F32),
            jax.ShapeDtypeStruct((depth, wide), F32),
            jax.ShapeDtypeStruct(small.shape, F32),
        ),
        in_specs=[VSPEC] * 7,
        out_specs=(VSPEC,) * 3,
        scratch_shapes=[
            *scatter_shapes(stages, rows, depth),
            VMEM((rows, depth), F32), VMEM((depth, wide), F32), VMEM((parts, high, wide), BF16), VMEM((parts, high, wide), BF16),
            VMEM((parts, high, wide), BF16),
            VMEM((devices,) + small.shape, F32), VMEM((parts,) + small.shape, F32),
            DMA((parts,)), DMA((parts,)), DMA((parts,)), DMA((parts,)),
            DMA((devices,)), DMA((devices,)), DMA((parts,)), DMA((parts,)),
        ],
        compiler_params=pltpu.CompilerParams(
            collective_id=1, has_side_effects=True, vmem_limit_bytes=56 << 20
        ),
    )(dx, w, norm, tokens, gain[None], resid, small)


def on_device(
    devices, parts, tokens, picture_ids, ln1_gain, ln1_bias, q_weight, q_bias, k_weight, v_weight, v_bias,
    o_weight, o_bias, ln2_gain, ln2_bias, fc1_weight, fc1_bias, fc2_weight, fc2_bias, out_grad,
):
    own_count, depth = tokens.shape
    hidden_local = fc1_weight.shape[1]
    own_ids = lax.dynamic_slice_in_dim(picture_ids, lax.axis_index("tensor") * own_count, own_count)
    width = q_weight.shape[1]
    norm1_all, q, k, v, w_all = project(
        tokens, ln1_gain, ln1_bias, q_weight, k_weight, v_weight, q_bias, v_bias, devices
    )
    span = block_ranges(picture_ids)
    id_col, id_row = picture_ids[:, None], picture_ids[None, :]
    o_weight, q = lax.optimization_barrier((o_weight, q))
    o_all = lax.all_gather(o_weight, "tensor", axis=0)
    q, k, v = (item.reshape(LEN, width) for item in (q, k, v))
    attended, log_total = attend(q, k, v, span, id_col, id_row)
    output, grad_residual, grad_attended, grad_ow, grad_fc1, grad_fc2, small = middle(
        attended.reshape(devices, own_count, width), o_all, fc1_weight, fc2_weight, tokens, out_grad,
        own_ids[:, None], o_bias, ln2_gain, ln2_bias, fc1_bias, fc2_bias,
    )
    grad_ow = lax.psum_scatter(grad_ow.reshape(-1, depth), "tensor", scatter_dimension=0, tiled=True)
    dqkv = attend_back(
        q, k, v, span, id_col, id_row, attended, log_total, grad_attended.reshape(LEN, width)
    )
    grad_tokens, grad_w, sums = close(
        dqkv.reshape(devices, own_count, 3 * width), w_all, norm1_all, tokens, ln1_gain,
        grad_residual, small, parts,
    )
    grad_ow, grad_fc1, grad_fc2 = (
        lax.psum(item, "dp").astype(F32) for item in (grad_ow, grad_fc1, grad_fc2)
    )
    return (
        output, grad_tokens, sums[0], sums[1],
        grad_w[:, :width], sums[6, :width], grad_w[:, width : 2 * width], grad_w[:, 2 * width :],
        sums[6, 2 * width : 3 * width], grad_ow, sums[4], sums[2], sums[3],
        grad_fc1, sums[7, :hidden_local], grad_fc2, sums[5],
    )


def solution(mesh):
    rows, whole = P(("dp", "tensor"), None), P()
    columns, down, along = P(None, "tensor"), P("tensor", None), P("tensor")
    return jax.shard_map(
        functools.partial(on_device, mesh.shape["tensor"], mesh.shape["dp"]),
        mesh=mesh,
        in_specs=(
            rows, P("dp"), whole, whole, columns, along, columns, columns, along, down, whole,
            whole, whole, columns, along, down, whole, rows,
        ),
        out_specs=(
            rows, rows, whole, whole, columns, along, columns, columns, along, down, whole,
            whole, whole, columns, along, down, whole,
        ),
        check_vma=False,
    )
```

```python
import functools

import jax
import jax.numpy as jnp
from jax import lax
from jax.experimental import pallas as pl
from jax.experimental.pallas import tpu as pltpu
from jax.sharding import PartitionSpec as P

HD = 72
LEN = 2048
BLOCK = 256
NORM_EPS = 1e-06
NEG_FILL = -1e30
BF16 = jnp.bfloat16
F32 = jnp.float32
MESH = pl.DeviceIdType.MESH
VMEM = pltpu.VMEM
DMA = pltpu.SemaphoreType.DMA
VSPEC = pl.BlockSpec(memory_space=pltpu.VMEM)
SSPEC = pl.BlockSpec(memory_space=pltpu.SMEM)
HBM = pl.BlockSpec(memory_space=pltpu.HBM)


def nn(left, right):
    return lax.dot_general(left, right, (((1,), (0,)), ((), ())), preferred_element_type=F32)


def nt(left, right):
    return lax.dot_general(left, right, (((1,), (1,)), ((), ())), preferred_element_type=F32)


def tn(left, right):
    return lax.dot_general(left, right, (((0,), (0,)), ((), ())), preferred_element_type=F32)


def remote(src, dst, send_sem, recv_sem, **where):
    return pltpu.make_async_remote_copy(
        src_ref=src, dst_ref=dst, send_sem=send_sem, recv_sem=recv_sem,
        device_id=where, device_id_type=MESH,
    )


def place():
    me = lax.axis_index("tensor")
    core = lax.rem(me, 2)
    return me, core, lax.div(me, 2)


def greet_peers(axes):
    barrier = pltpu.get_barrier_semaphore()
    for axis, size in axes:
        me = lax.axis_index(axis)

        def greet(step, carry):
            pl.semaphore_signal(
                barrier, inc=1, device_id={axis: lax.rem(me + step, size)}, device_id_type=MESH
            )
            return carry

        lax.fori_loop(1, size, greet, 0)
    pl.semaphore_wait(barrier, sum(size - 1 for _, size in axes))


def greet_line(stages):
    me, core, stage = place()
    barrier = pltpu.get_barrier_semaphore()
    has_left, has_right = stage > 0, stage < stages - 1

    def greet(other):
        pl.semaphore_signal(barrier, inc=1, device_id={"tensor": other}, device_id_type=MESH)

    greet(me + 1 - 2 * core)
    pl.when(has_left)(lambda: greet(me - 2))
    pl.when(has_right)(lambda: greet(me + 2))
    pl.semaphore_wait(barrier, 1 + has_left.astype(jnp.int32) + has_right.astype(jnp.int32))


def normalize(values):
    average = jnp.mean(values, axis=-1, keepdims=True)
    centred = values - average
    variance = jnp.mean(centred * centred, axis=-1, keepdims=True)
    scale = lax.rsqrt(variance + NORM_EPS)
    return centred * scale, scale


class LineGather:
    def __init__(self, stages, buffer, send_sem, recv_sem):
        self.stages, self.buffer, self.send_sem, self.recv_sem = stages, buffer, send_sem, recv_sem
        self.me, self.core, self.stage = place()
        self.partner = self.me + 1 - 2 * self.core

    def copy(self, block, way, target):
        return remote(
            self.buffer.at[block], self.buffer.at[block],
            self.send_sem.at[block, way], self.recv_sem.at[block], tensor=target,
        )

    def each_copy(self, block, right, left, act):
        pl.when(right)(lambda: act(self.copy(block, 0, self.me + 2)))
        pl.when(left)(lambda: act(self.copy(block, 1, self.me - 2)))
        act(self.copy(block, 2, self.partner))

    def start(self):
        self.each_copy(
            self.me, self.stage < self.stages - 1, self.stage > 0, lambda copy: copy.start()
        )

    def incoming(self, reach, side, core):
        far = jnp.where(side == 0, self.stage - reach, self.stage + reach)
        return (far >= 0) & (far < self.stages), 2 * far + core

    def arrive(self, block):
        self.copy(block, 2, self.partner).wait_recv()

    def ways(self, side):
        return (side == 0) & (self.stage < self.stages - 1), (side == 1) & (self.stage > 0)

    def relay(self, reach):
        for side in range(2):
            valid, block = self.incoming(reach, side, self.core)

            @pl.when(valid)
            def _():
                self.arrive(block)
                self.each_copy(block, *self.ways(jnp.int32(side)), lambda copy: copy.start())

    def use_own(self, compute):
        compute(self.me)
        self.arrive(self.partner)
        compute(self.partner)

    def use(self, reach, compute):
        def body(index, carry):
            side, other = lax.rem(index, 2), lax.div(index, 2)
            valid, block = self.incoming(
                reach, side, jnp.where(other == 0, self.core, 1 - self.core)
            )

            @pl.when(valid)
            def _():
                pl.when(other == 1)(lambda: self.arrive(block))
                compute(block)

            return carry

        lax.fori_loop(0, 4, body, 0)

    def run(self, compute):
        def body(reach, carry):
            self.relay(reach)
            self.use(reach, compute)
            return carry

        self.use_own(compute)
        lax.fori_loop(1, self.stages, body, 0)

    def finish(self):
        self.each_copy(
            self.me, self.stage < self.stages - 1, self.stage > 0, lambda copy: copy.wait_send()
        )

        def body(index, carry):
            reach, side = lax.div(index, 2) + 1, lax.rem(index, 2)
            valid, block = self.incoming(reach, side, self.core)

            @pl.when(valid)
            def _():
                self.each_copy(block, *self.ways(side), lambda copy: copy.wait_send())

            return carry

        lax.fori_loop(0, 2 * (self.stages - 1), body, 0)


class LineScatter:
    def __init__(self, stages, partial, cross, lane, sems):
        self.stages, self.partial, self.cross, self.lane = stages, partial, cross, lane
        self.cross_send, self.cross_recv, self.lane_send, self.lane_recv = sems
        self.me, self.core, self.stage = place()
        self.partner = self.me + 1 - 2 * self.core

    def cross_copy(self, far):
        return remote(
            self.partial.at[2 * far + 1 - self.core], self.cross.at[far],
            self.cross_send.at[far], self.cross_recv.at[far], tensor=self.partner,
        )

    def slot(self, way, far, holder):
        return far if way == 0 else jnp.where(far == holder, self.stages, far)

    def lane_copy(self, way, far, holder):
        target = self.me + 2 if way == 0 else self.me - 2
        slot = self.slot(way, far, holder)
        return remote(
            self.partial.at[2 * far + self.core], self.lane.at[slot],
            self.lane_send.at[far], self.lane_recv.at[slot], tensor=target,
        )

    def sent(self, way, far):
        return self.lane_copy(way, far, self.stage + (1 if way == 0 else -1))

    def received(self, way, far):
        self.lane_copy(way, far, self.stage).wait_recv()
        return self.lane[self.slot(way, far, self.stage)].astype(F32)

    def put(self, block, value):
        self.partial[block] = value.astype(BF16)

        @pl.when(lax.rem(block, 2) != self.core)
        def _():
            self.cross_copy(lax.div(block, 2)).start()

    def produce(self, compute):
        def body(index, carry):
            reach = self.stages - 1 - lax.div(index, 4)
            side, other = lax.rem(lax.div(index, 2), 2), lax.rem(index, 2)
            far = jnp.where(side == 0, self.stage + reach, self.stage - reach)

            @pl.when((far >= 0) & (far < self.stages) & ((reach > 0) | (side == 0)))
            def _():
                block = 2 * far + jnp.where(other == 0, 1 - self.core, self.core)
                self.put(block, compute(block))

            return carry

        lax.fori_loop(0, 4 * self.stages, body, 0)

    def chip_sum(self, far):
        return self.partial[2 * far + self.core].astype(F32) + self.cross[far].astype(F32)

    def send_sum(self, way, far, incoming):
        self.cross_copy(far).wait_recv()
        block = 2 * far + self.core

        @pl.when(incoming)
        def _():
            self.partial[block] = (self.chip_sum(far) + self.received(way, far)).astype(BF16)

        @pl.when(jnp.logical_not(incoming))
        def _():
            self.partial[block] = self.chip_sum(far).astype(BF16)

        self.sent(way, far).start()

    def step(self, reach):
        right, left = self.stage + reach, self.stage - reach
        pl.when(right < self.stages)(lambda: self.send_sum(0, right, self.stage > 0))
        pl.when(left >= 0)(lambda: self.send_sum(1, left, self.stage < self.stages - 1))

    def steps(self, first, last):
        lax.fori_loop(first, last, lambda index, carry: (self.step(self.stages - 1 - index), carry)[1], 0)

    def own(self, total_ref):
        self.cross_copy(self.stage).wait_recv()
        total_ref[...] = self.chip_sum(self.stage)

        @pl.when(self.stage > 0)
        def _():
            total_ref[...] += self.received(0, self.stage)

        @pl.when(self.stage < self.stages - 1)
        def _():
            total_ref[...] += self.received(1, self.stage)

    def finish(self):
        def body(far, carry):
            self.cross_copy(far).wait_send()
            pl.when(far > self.stage)(lambda: self.sent(0, far).wait_send())
            pl.when(far < self.stage)(lambda: self.sent(1, far).wait_send())
            return carry

        lax.fori_loop(0, self.stages, body, 0)


def scatter_shapes(stages, rows, depth):
    return [
        VMEM((2 * stages, rows, depth), BF16), VMEM((stages, rows, depth), BF16),
        VMEM((stages + 1, rows, depth), BF16),
        DMA((stages,)), DMA((stages,)), DMA((stages,)), DMA((stages + 1,)),
    ]


def exchange(axis, size, slots, send_sem, recv_sem):
    me = lax.axis_index(axis)

    def copy_to(other, slot):
        return remote(
            slots.at[slot], slots.at[slot], send_sem.at[other], recv_sem.at[slot], **{axis: other}
        )

    def start(step, carry):
        copy_to(lax.rem(me + step, size), me).start()
        return carry

    def wait(step, carry):
        other = lax.rem(me + step, size)
        copy_to(other, other).wait_recv()
        copy_to(other, me).wait_send()
        return carry

    lax.fori_loop(1, size, start, 0)
    return lambda: lax.fori_loop(1, size, wait, 0)


def piece_height(height, parts):
    return -(-height // (16 * parts)) * 16


class RowSum:
    def __init__(self, parts, piece, arrive, send_sem, recv_sem):
        self.parts, self.piece, self.arrive = parts, piece, arrive
        self.send_sem, self.recv_sem = send_sem, recv_sem
        self.row = lax.axis_index("dp")

    def copy(self, other, source):
        return remote(
            self.piece.at[other], self.arrive.at[source],
            self.send_sem.at[other], self.recv_sem.at[source], dp=other,
        )

    def others(self, act, start):
        return lax.fori_loop(
            1, self.parts, lambda step, carry: act(lax.rem(self.row + step, self.parts), carry), start
        )

    def start(self, total):
        high = self.piece.shape[1]
        for part in range(self.parts):
            self.piece[part] = total[part * high : (part + 1) * high, :].astype(BF16)

        def send(other, carry):
            self.copy(other, self.row).start()
            return carry

        self.others(send, 0)

    def reduce(self):
        def add(other, so_far):
            self.copy(other, other).wait_recv()
            self.copy(other, self.row).wait_send()
            return so_far + self.arrive[other].astype(F32)

        return self.others(add, self.piece[self.row].astype(F32)).astype(BF16)


def rowsum_shapes(parts, high, depth):
    return [
        VMEM((parts, high, depth), BF16), VMEM((parts, high, depth), BF16), DMA((parts,)), DMA((parts,)),
    ]


def column(row):
    return jnp.broadcast_to(row, (128, row.shape[1])).T[:, :1]


def project_kernel(
    stages, tok_ref, gain_ref, bias_ref, wq_ref, wk_ref, wv_ref, bq_ref, bv_ref,
    norm_hbm, q_ref, k_ref, v_ref, norm, weight, send_sem, recv_sem, out_sem,
):
    me, _, _ = place()
    width = wq_ref.shape[0]
    greet_line(stages)
    normed, _ = normalize(tok_ref[...].astype(F32))
    norm[me] = (normed * gain_ref[...].astype(F32) + bias_ref[...].astype(F32)).astype(BF16)
    gather = LineGather(stages, norm, send_sem, recv_sem)
    gather.start()
    weight[...] = jnp.concatenate([wq_ref[...], wk_ref[...], wv_ref[...]], axis=0)

    def keep(block):
        return pltpu.make_async_copy(norm.at[block], norm_hbm.at[block], out_sem.at[block])

    def compute(block):
        keep(block).start()
        out = nt(norm[block], weight[...])
        q_ref[block] = (out[:, :width] + bq_ref[...].astype(F32)).astype(BF16)
        k_ref[block] = out[:, width : 2 * width].astype(BF16)
        v_ref[block] = (out[:, 2 * width :] + bv_ref[...].astype(F32)).astype(BF16)

    gather.run(compute)
    gather.finish()
    lax.fori_loop(0, 2 * stages, lambda block, carry: (keep(block).wait(), carry)[1], 0)


def project(tokens, gain, bias, wq, wk, wv, bq, bv, devices):
    rows, depth = tokens.shape
    width = wq.shape[1]
    head = jax.ShapeDtypeStruct((devices, rows, width), BF16)
    return pl.pallas_call(
        functools.partial(project_kernel, devices // 2),
        name="project",
        out_shape=(jax.ShapeDtypeStruct((devices, rows, depth), BF16), head, head, head),
        in_specs=[VSPEC] * 8,
        out_specs=(HBM,) + (VSPEC,) * 3,
        scratch_shapes=[
            VMEM((devices, rows, depth), BF16), VMEM((3 * width, depth), BF16),
            DMA((devices, 3)), DMA((devices,)), DMA((devices,)),
        ],
        compiler_params=pltpu.CompilerParams(
            collective_id=0, has_side_effects=True, vmem_limit_bytes=24 << 20
        ),
    )(tokens, gain[None], bias[None], wq.T, wk.T, wv.T, bq[None], bv[None])


def block_ranges(ids):
    first, last = ids[::BLOCK], ids[BLOCK - 1 :: BLOCK]
    begin = jnp.sum((ids[None, :] > jnp.maximum(first, 0)[:, None]).astype(jnp.int32), axis=1)
    end = jnp.sum((ids[None, :] >= jnp.maximum(last, 1)[:, None]).astype(jnp.int32), axis=1)
    return jnp.stack([begin // BLOCK, (end + BLOCK - 1) // BLOCK])


def lanes_of(head, width):
    lane = lax.broadcasted_iota(jnp.int32, (1, width), 1)
    return (lane >= head * HD) & (lane < (head + 1) * HD)


def fill_columns(row_ref, column_ref):
    for block in range(row_ref.shape[1] // BLOCK):
        at = pl.ds(block * BLOCK, BLOCK)
        column_ref[at, :] = column(row_ref[:, at])


def attend_kernel(heads, span_ref, q_ref, k_ref, v_ref, idr_ref, o_ref, log_ref, idc_ref, acc_ref):
    length, width = q_ref.shape
    scale = HD ** (-0.5)
    mean_value = jnp.sum(v_ref[...].astype(F32), axis=0, keepdims=True) * (1.0 / length)

    fill_columns(idr_ref, idc_ref)

    def per_block(block, carry):
        at = pl.ds(pl.multiple_of(block * BLOCK, BLOCK), BLOCK)
        query = q_ref[at, :]
        id_row = idr_ref[:, at]
        masked = [jnp.where(lanes_of(h, width), query, jnp.zeros_like(query)) for h in range(heads)]
        acc_ref[...] = jnp.zeros_like(acc_ref)
        blank = jnp.full((1, BLOCK), NEG_FILL, F32), jnp.zeros((1, BLOCK), F32)

        def per_key(other, state):
            keys_at = pl.ds(pl.multiple_of(other * BLOCK, BLOCK), BLOCK)
            key, value, id_col = k_ref[keys_at, :], v_ref[keys_at, :], idc_ref[keys_at, :]
            allowed = (id_col == id_row) & (id_col > 0)
            fresh = []
            for h in range(heads):
                top, total = state[h]
                scores = jnp.where(allowed, nt(key, masked[h]) * scale, NEG_FILL)
                new_top = jnp.maximum(top, jnp.max(scores, axis=0, keepdims=True))
                weight = jnp.exp(scores - new_top)
                shrink = jnp.exp(top - new_top)
                total = total * shrink + jnp.sum(weight, axis=0, keepdims=True)
                acc_ref[h] = acc_ref[h] * shrink + tn(value, weight.astype(BF16))
                fresh.append((new_top, total))
            return tuple(fresh)

        state = lax.fori_loop(
            span_ref[0, block], span_ref[1, block], per_key, (blank,) * heads
        )
        row = lax.broadcasted_iota(jnp.int32, (width, 1), 0)
        result = jnp.zeros((width, BLOCK), F32)
        for h in range(heads):
            top, total = state[h]
            result = jnp.where(row >= h * HD, acc_ref[h] / total, result)
            log_ref[h : h + 1, at] = jnp.where(id_row == 0, 0.0, top + jnp.log(total))
        o_ref[at, :] = jnp.where(idc_ref[at, :] == 0, mean_value, result.T).astype(BF16)
        return carry

    lax.fori_loop(0, length // BLOCK, per_block, 0)


def attend(q, k, v, span, id_row):
    length, width = q.shape
    heads = width // HD
    return pl.pallas_call(
        functools.partial(attend_kernel, heads),
        name="attend",
        out_shape=(
            jax.ShapeDtypeStruct((length, width), BF16),
            jax.ShapeDtypeStruct((heads, length), F32),
        ),
        in_specs=[SSPEC] + [VSPEC] * 4,
        out_specs=(VSPEC,) * 2,
        scratch_shapes=[VMEM((length, 1), F32), VMEM((heads, width, BLOCK), F32)],
        compiler_params=pltpu.CompilerParams(vmem_limit_bytes=24 << 20),
    )(span, q, k, v, id_row)


def attend_back_kernel(
    heads, span_ref, q_ref, k_ref, v_ref, idr_ref, o_ref, log_ref, g_ref,
    out_ref, idc_ref, dq_ref, dk_ref, dv_ref, qh_ref, gh_ref, row_ref,
):
    length, width = q_ref.shape
    scale = HD ** (-0.5)
    ones = jnp.ones((8, width), F32)
    dq_ref[...] = jnp.zeros_like(dq_ref)
    fill_columns(idr_ref, idc_ref)

    def prepare(block, pad):
        at = pl.ds(pl.multiple_of(block * BLOCK, BLOCK), BLOCK)
        query, grad = q_ref[at, :], g_ref[at, :]
        product = grad.astype(F32) * o_ref[at, :].astype(F32)
        for h in range(heads):
            lanes = lanes_of(h, width)
            qh_ref[h, at, :] = jnp.where(lanes, query, jnp.zeros_like(query))
            gh_ref[h, at, :] = jnp.where(lanes, grad, jnp.zeros_like(grad))
            row = lax.dot_general(
                ones, jnp.where(lanes, product, 0.0), (((1,), (1,)), ((), ())),
                precision=lax.Precision.HIGHEST, preferred_element_type=F32,
            )
            row_ref[h : h + 1, at] = row[:1]
        return pad + jnp.sum(
            jnp.where(idc_ref[at, :] == 0, grad.astype(F32), 0.0), axis=0, keepdims=True
        )

    pad = lax.fori_loop(0, length // BLOCK, prepare, jnp.zeros((1, width), F32)) * (1.0 / length)

    def per_key(block, carry):
        at = pl.ds(pl.multiple_of(block * BLOCK, BLOCK), BLOCK)
        key, value, id_col = k_ref[at, :], v_ref[at, :], idc_ref[at, :]
        dk_ref[...] = jnp.zeros_like(dk_ref)
        dv_ref[...] = jnp.zeros_like(dv_ref)

        def per_query(other, inner):
            query_at = pl.ds(pl.multiple_of(other * BLOCK, BLOCK), BLOCK)
            allowed = (id_col == idr_ref[:, query_at]) & (id_col > 0)
            for h in range(heads):
                query, grad = qh_ref[h, query_at, :], gh_ref[h, query_at, :]
                scores = nt(key, query) * scale - log_ref[h : h + 1, query_at]
                prob = jnp.where(allowed, jnp.exp(jnp.where(allowed, scores, 0.0)), 0.0)
                dv_ref[...] += nn(prob.astype(BF16), grad)
                back = prob * (nt(value, grad) - row_ref[h : h + 1, query_at])
                back = back.astype(BF16)
                dk_ref[...] += nn(back, query)
                here = jnp.where(lanes_of(h, width), key, jnp.zeros_like(key))
                dq_ref[query_at, :] += tn(back, here)
            return inner

        lax.fori_loop(span_ref[0, block], span_ref[1, block], per_query, 0)
        out_ref[at, width : 2 * width] = (dk_ref[...] * scale).astype(BF16)
        out_ref[at, 2 * width :] = (dv_ref[...] + pad).astype(BF16)
        return carry

    lax.fori_loop(0, length // BLOCK, per_key, 0)
    out_ref[:, :width] = (dq_ref[...] * scale).astype(BF16)


def attend_back(q, k, v, span, id_row, o, log_total, grad):
    length, width = q.shape
    heads = width // HD
    return pl.pallas_call(
        functools.partial(attend_back_kernel, heads),
        name="attend_back",
        out_shape=jax.ShapeDtypeStruct((length, 3 * width), BF16),
        in_specs=[SSPEC] + [VSPEC] * 7,
        out_specs=VSPEC,
        scratch_shapes=[
            VMEM((length, 1), F32), VMEM((length, width), F32), VMEM((BLOCK, width), F32),
            VMEM((BLOCK, width), F32),
            VMEM((heads, length, width), BF16), VMEM((heads, length, width), BF16),
            VMEM((heads, length), F32),
        ],
        compiler_params=pltpu.CompilerParams(vmem_limit_bytes=32 << 20),
    )(span, q, k, v, id_row, o, log_total, grad)


def gelu_pair(u):
    slope = (2.0 / jnp.pi) ** 0.5
    bent = jnp.tanh(slope * (u + 0.044715 * u * u * u))
    half = 0.5 * (1.0 + bent)
    return u * half, half + 0.5 * u * (1.0 - bent * bent) * slope * (1.0 + 3 * 0.044715 * u * u)


def middle_kernel(
    stages, parts, att_hbm, wo_hbm, fc1_hbm, fc2_hbm, tok_hbm, top_hbm, ids_ref,
    ob_ref, gain_ref, bias_ref, fb1_ref, fb2_ref,
    out_ref, gres_ref, gatt_ref, fc_ref, small_ref,
    wo, fc1, fc2, tok, top, load_sem,
    held, held_send, held_recv, norm_all, norm_send, norm_recv, top_all, top_send, top_recv,
    hidden, slope, grad_pre,
    br_part, br_cross, br_lane, br_s0, br_s1, br_s2, br_s3,
    gn_part, gn_cross, gn_lane, gn_s0, gn_s1, gn_s2, gn_s3,
    resid, total, acc, piece, arrive, piece_send, piece_recv, back, back_send, back_recv,
):
    me, _, _ = place()
    devices = 2 * stages
    rows, depth = tok_hbm.shape
    units = fc1_hbm.shape[0]
    second = -(-units // 16) * 16
    loads = [
        pltpu.make_async_copy(src, dst, load_sem.at[index])
        for index, (src, dst) in enumerate(
            ((tok_hbm, tok), (top_hbm, top), (wo_hbm, wo), (fc1_hbm, fc1), (fc2_hbm, fc2),
             (att_hbm.at[me], held.at[me]))
        )
    ]
    for load in loads:
        load.start()
    greet_peers((("tensor", devices), ("dp", parts)))

    def held_copy(other, source):
        return remote(
            att_hbm.at[other], held.at[source], held_send.at[other], held_recv.at[source], tensor=other
        )

    def send_held(step, carry):
        held_copy(lax.rem(me + step, devices), me).start()
        return carry

    lax.fori_loop(1, devices, send_held, 0)
    gather2 = LineGather(stages, norm_all, norm_send, norm_recv)
    gather3 = LineGather(stages, top_all, top_send, top_recv)
    branch = LineScatter(stages, br_part, br_cross, br_lane, (br_s0, br_s1, br_s2, br_s3))
    gnorm = LineScatter(stages, gn_part, gn_cross, gn_lane, (gn_s0, gn_s1, gn_s2, gn_s3))

    mask = column(jnp.where(ids_ref[...] > 0, 1.0, 0.0))
    acc[...] = jnp.zeros_like(acc)
    small_ref[...] = jnp.zeros_like(small_ref)
    loads[0].wait()
    loads[1].wait()
    top_own = top[...].astype(F32) * mask
    top_all[me] = top_own.astype(BF16)
    small_ref[5:6, :] = jnp.sum(top_own, axis=0, keepdims=True)
    resid[...] = tok[...].astype(F32) + ob_ref[...].astype(F32)
    loads[2].wait()
    loads[5].wait()
    resid[...] += nn(held[me], wo[me])

    def add_held(step, carry):
        other = lax.rem(me + devices - step, devices)
        held_copy(other, other).wait_recv()
        resid[...] += nn(held[other], wo[other])
        return carry

    lax.fori_loop(1, devices, add_held, 0)
    normed, _ = normalize(resid[...])
    norm_all[me] = (normed * gain_ref[...].astype(F32) + bias_ref[...].astype(F32)).astype(BF16)
    gather2.start()
    loads[3].wait()
    loads[4].wait()

    def forward(block):
        pre_act = nt(norm_all[block], fc1[...]) + fb1_ref[...].astype(F32)
        value, slope_now = gelu_pair(pre_act)
        hidden[block] = value.astype(BF16)
        slope[block] = slope_now.astype(BF16)
        branch.put(block, nn(hidden[block], fc2[...]))

    gather2.run(forward)
    gather3.start()

    def backward(block):
        grad = nt(top_all[block], fc2[...]) * slope[block].astype(F32)
        low = grad.astype(BF16)
        grad_pre[block] = low
        small_ref[7:8, 0:units] += jnp.sum(low.astype(F32), axis=0, keepdims=True)
        gnorm.put(block, nn(grad_pre[block], fc1[...]))
        acc[0:units, :] += tn(grad_pre[block], norm_all[block])
        acc[second : second + units, :] += tn(hidden[block], top_all[block])

    def both(reach, carry):
        gather3.relay(reach)
        pl.when(reach < stages - 1)(lambda: branch.step(stages - 1 - reach))
        gather3.use(reach, backward)
        return carry

    branch.step(stages - 1)
    gather3.use_own(backward)
    lax.fori_loop(1, stages, both, 0)
    gnorm.step(stages - 1)
    sums = RowSum(parts, piece, arrive, piece_send, piece_recv)
    sums.start(acc)
    branch.own(total)
    out_ref[...] = (mask * (resid[...] + total[...] + fb2_ref[...].astype(F32))).astype(BF16)
    gnorm.steps(1, stages - 1)

    gnorm.own(total)
    grad = total[...]
    normed, scale = normalize(resid[...])
    small_ref[2:3, :] = jnp.sum(grad * normed, axis=0, keepdims=True)
    small_ref[3:4, :] = jnp.sum(grad, axis=0, keepdims=True)
    inner = grad * gain_ref[...].astype(F32)
    inner_mean = jnp.mean(inner, axis=-1, keepdims=True)
    inner_proj = jnp.mean(inner * normed, axis=-1, keepdims=True)
    grad_resid = top[...].astype(F32) * mask + scale * (inner - inner_mean - normed * inner_proj)
    gres_ref[...] = grad_resid
    tok[...] = grad_resid.astype(BF16)
    small_ref[4:5, :] = jnp.sum(grad_resid, axis=0, keepdims=True)

    def back_copy(other, source):
        return remote(
            back.at[other], gatt_ref.at[source], back_send.at[other], back_recv.at[source], tensor=other
        )

    def send_back(step, carry):
        other = lax.rem(me + step, devices)
        back[other] = nt(tok[...], wo[other]).astype(BF16)
        back_copy(other, me).start()
        return carry

    lax.fori_loop(1, devices, send_back, 0)
    gatt_ref[me] = nt(tok[...], wo[me]).astype(BF16)

    fc_ref[...] = sums.reduce()

    def settle(step, carry):
        other = lax.rem(me + devices - step, devices)
        back_copy(other, other).wait_recv()
        back_copy(other, me).wait_send()
        held_copy(other, me).wait_send()
        return carry

    lax.fori_loop(1, devices, settle, 0)
    gather2.finish()
    gather3.finish()
    branch.finish()
    gnorm.finish()


def middle(att, wo, fc1, fc2, tokens, out_grad, ids, o_bias, gain, bias, fc1_bias, fc2_bias, parts):
    devices, rows, width = att.shape
    depth, units = fc1.shape
    stages = devices // 2
    high = piece_height(2 * (-(-units // 16) * 16), parts)
    return pl.pallas_call(
        functools.partial(middle_kernel, stages, parts),
        name="middle",
        out_shape=(
            jax.ShapeDtypeStruct((rows, depth), BF16),
            jax.ShapeDtypeStruct((rows, depth), F32),
            jax.ShapeDtypeStruct((devices, rows, width), BF16),
            jax.ShapeDtypeStruct((high, depth), BF16),
            jax.ShapeDtypeStruct((8, depth), F32),
        ),
        in_specs=[HBM] * 6 + [VSPEC] * 6,
        out_specs=(VSPEC,) * 5,
        scratch_shapes=[
            VMEM((devices, width, depth), BF16), VMEM((units, depth), BF16), VMEM((units, depth), BF16),
            VMEM((rows, depth), BF16), VMEM((rows, depth), BF16), DMA((6,)),
            VMEM((devices, rows, width), BF16), DMA((devices,)), DMA((devices,)),
            VMEM((devices, rows, depth), BF16), DMA((devices, 3)), DMA((devices,)),
            VMEM((devices, rows, depth), BF16), DMA((devices, 3)), DMA((devices,)),
            VMEM((devices, rows, units), BF16), VMEM((devices, rows, units), BF16),
            VMEM((devices, rows, units), BF16),
            *scatter_shapes(stages, rows, depth), *scatter_shapes(stages, rows, depth),
            VMEM((rows, depth), F32), VMEM((rows, depth), F32),
            VMEM((parts * high, depth), F32), *rowsum_shapes(parts, high, depth),
            VMEM((devices, rows, width), BF16), DMA((devices,)), DMA((devices,)),
        ],
        compiler_params=pltpu.CompilerParams(
            collective_id=2, has_side_effects=True, vmem_limit_bytes=67043328
        ),
    )(
        att, wo, fc1.T, fc2, tokens, out_grad, ids, o_bias[None], gain[None], bias[None],
        fc1_bias[None], fc2_bias[None],
    )


def close_kernel(
    stages, parts, dx_ref, wq_ref, wk_ref, wv_ref, norm_hbm, att_ref, tok_ref, gain_ref, resid_ref,
    small_ref, fc_ref,
    gtok_ref, gw_hbm, go_hbm, gfc_hbm, gsmall_ref,
    weight, norm, norm_sem, gatt_all, gatt_send, gatt_recv,
    partial, cross, lane, cross_send, cross_recv, lane_send, lane_recv,
    total, acc, acc_o, w_piece, w_arrive, w_send, w_recv, o_piece, o_arrive, o_send, o_recv,
    w_all, o_all, fc_all, wa_send, wa_recv, oa_send, oa_recv, fa_send, fa_recv, out_sem,
    slots_t, slots_d, st_send, st_recv, sd_send, sd_recv,
):
    me, _, _ = place()
    row = lax.axis_index("dp")
    devices = 2 * stages
    wide, width = dx_ref.shape[2], att_ref.shape[2]
    load = pltpu.make_async_copy(norm_hbm, norm, norm_sem)
    load.start()
    greet_peers((("tensor", devices), ("dp", parts)))
    gatt_all[me] = resid_ref[...].astype(BF16)
    gather = LineGather(stages, gatt_all, gatt_send, gatt_recv)
    gather.start()
    fc_all[row] = fc_ref[...]
    wait_fc = exchange("dp", parts, fc_all, fa_send, fa_recv)
    weight[...] = jnp.concatenate([wq_ref[...], wk_ref[...], wv_ref[...]], axis=0)
    scatter = LineScatter(
        stages, partial, cross, lane, (cross_send, cross_recv, lane_send, lane_recv)
    )
    scatter.produce(lambda block: nn(dx_ref[block], weight[...]))
    scatter.step(stages - 1)

    acc[...] = jnp.zeros_like(acc)
    acc_o[...] = jnp.zeros_like(acc_o)
    load.wait()

    def weight_block(block, bias):
        grad = dx_ref[block]
        acc[0:wide, :] += tn(grad, norm[block])
        return bias + jnp.sum(grad.astype(F32), axis=0, keepdims=True)

    bias = lax.fori_loop(0, devices, weight_block, jnp.zeros((1, wide), F32))
    w_sum = RowSum(parts, w_piece, w_arrive, w_send, w_recv)
    w_sum.start(acc)

    def weight_o(block):
        acc_o[0:width, :] += tn(att_ref[block], gatt_all[block])

    gather.use_own(weight_o)

    def both(reach, carry):
        gather.relay(reach)
        pl.when(reach < stages - 1)(lambda: scatter.step(stages - 1 - reach))
        gather.use(reach, weight_o)
        return carry

    lax.fori_loop(1, stages - 1, both, 0)
    w_all[row] = w_sum.reduce()
    wait_w = exchange("dp", parts, w_all, wa_send, wa_recv)
    lax.fori_loop(stages - 1, stages, both, 0)
    o_sum = RowSum(parts, o_piece, o_arrive, o_send, o_recv)
    o_sum.start(acc_o)

    scatter.own(total)
    grad = total[...]
    normed, scale = normalize(tok_ref[...].astype(F32))
    slots_t[me] = small_ref[...]
    slots_t[me, 0:1, :] = jnp.sum(grad * normed, axis=0, keepdims=True)
    slots_t[me, 1:2, :] = jnp.sum(grad, axis=0, keepdims=True)
    slots_t[me, 6:7, 0:wide] = bias
    wait_small = exchange("tensor", devices, slots_t, st_send, st_recv)
    inner = grad * gain_ref[...].astype(F32)
    inner_mean = jnp.mean(inner, axis=-1, keepdims=True)
    inner_proj = jnp.mean(inner * normed, axis=-1, keepdims=True)
    gtok_ref[...] = resid_ref[...] + scale * (inner - inner_mean - normed * inner_proj)
    o_all[row] = o_sum.reduce()
    wait_o = exchange("dp", parts, o_all, oa_send, oa_recv)
    wait_small()
    sums = lax.fori_loop(
        1, devices, lambda slot, so_far: so_far + slots_t[slot], slots_t[0]
    )
    line = lax.broadcasted_iota(jnp.int32, sums.shape, 0)
    slots_d[row] = jnp.where(line < 6, sums, slots_t[me])
    wait_last = exchange("dp", parts, slots_d, sd_send, sd_recv)
    outs = []
    for index, (wait, src, dst) in enumerate(
        ((wait_fc, fc_all, gfc_hbm), (wait_w, w_all, gw_hbm), (wait_o, o_all, go_hbm))
    ):
        wait()
        out = pltpu.make_async_copy(src, dst, out_sem.at[index])
        out.start()
        outs.append(out)
    wait_last()
    gsmall_ref[...] = lax.fori_loop(
        1, parts, lambda slot, so_far: so_far + slots_d[slot], slots_d[0]
    )
    gather.finish()
    scatter.finish()
    for out in outs:
        out.wait()


def close(dx, wq, wk, wv, norm, att, tokens, gain, resid, small, fc, parts):
    devices, rows, wide = dx.shape
    depth = tokens.shape[1]
    stages = devices // 2
    width = wide // 3
    w_high, o_high, fc_high = piece_height(wide, parts), piece_height(width, parts), fc.shape[0]
    pieces = [(parts, high, depth) for high in (w_high, o_high, fc_high)]
    return pl.pallas_call(
        functools.partial(close_kernel, stages, parts),
        name="close",
        out_shape=(
            jax.ShapeDtypeStruct((rows, depth), F32),
            *(jax.ShapeDtypeStruct(shape, BF16) for shape in pieces),
            jax.ShapeDtypeStruct(small.shape, F32),
        ),
        in_specs=[VSPEC] * 4 + [HBM] + [VSPEC] * 6,
        out_specs=(VSPEC, HBM, HBM, HBM, VSPEC),
        scratch_shapes=[
            VMEM((wide, depth), BF16), VMEM((devices, rows, depth), BF16), DMA,
            VMEM((devices, rows, depth), BF16), DMA((devices, 3)), DMA((devices,)),
            *scatter_shapes(stages, rows, depth),
            VMEM((rows, depth), F32), VMEM((parts * w_high, depth), F32),
            VMEM((parts * o_high, depth), F32),
            *rowsum_shapes(parts, w_high, depth), *rowsum_shapes(parts, o_high, depth),
            *(VMEM(shape, BF16) for shape in pieces), *[DMA((parts,))] * 6, DMA((3,)),
            VMEM((devices,) + small.shape, F32), VMEM((parts,) + small.shape, F32),
            DMA((devices,)), DMA((devices,)), DMA((parts,)), DMA((parts,)),
        ],
        compiler_params=pltpu.CompilerParams(
            collective_id=1, has_side_effects=True, vmem_limit_bytes=50 << 20
        ),
    )(dx, wq.T, wk.T, wv.T, norm, att, tokens, gain[None], resid, small, fc)


def on_device(
    devices, parts, tokens, picture_ids, ln1_gain, ln1_bias, q_weight, q_bias, k_weight, v_weight, v_bias,
    o_weight, o_bias, ln2_gain, ln2_bias, fc1_weight, fc1_bias, fc2_weight, fc2_bias, out_grad,
):
    own_count, depth = tokens.shape
    hidden_local = fc1_weight.shape[1]
    own_ids = lax.dynamic_slice_in_dim(picture_ids, lax.axis_index("tensor") * own_count, own_count)
    width = q_weight.shape[1]
    norm1_all, q, k, v = project(
        tokens, ln1_gain, ln1_bias, q_weight, k_weight, v_weight, q_bias, v_bias, devices
    )
    span = block_ranges(picture_ids)
    id_row = picture_ids.astype(F32)[None, :]
    o_weight, q = lax.optimization_barrier((o_weight, q))
    o_all = lax.all_gather(o_weight, "tensor", axis=0)
    q, k, v = (item.reshape(LEN, width) for item in (q, k, v))
    attended, log_total = attend(q, k, v, span, id_row)
    heads_first = attended.reshape(devices, own_count, width)
    output, grad_residual, grad_attended, fc_piece, small = middle(
        heads_first, o_all, fc1_weight, fc2_weight, tokens, out_grad,
        own_ids.astype(F32)[None, :], o_bias, ln2_gain, ln2_bias, fc1_bias, fc2_bias, parts,
    )
    dqkv = attend_back(
        q, k, v, span, id_row, attended, log_total, grad_attended.reshape(LEN, width)
    )
    grad_tokens, grad_w, grad_o, grad_fc, sums = close(
        dqkv.reshape(devices, own_count, 3 * width), q_weight, k_weight, v_weight, norm1_all,
        heads_first, tokens, ln1_gain, grad_residual, small, fc_piece, parts,
    )
    grad_w, grad_o, grad_fc = (item.reshape(-1, depth) for item in (grad_w, grad_o, grad_fc))
    second = -(-hidden_local // 16) * 16
    return (
        output, grad_tokens, sums[0], sums[1],
        grad_w[:width].astype(F32).T, sums[6, :width], grad_w[width : 2 * width].astype(F32).T,
        grad_w[2 * width : 3 * width].astype(F32).T, sums[6, 2 * width : 3 * width],
        grad_o[:width].astype(F32), sums[4], sums[2], sums[3],
        grad_fc[:hidden_local].astype(F32).T, sums[7, :hidden_local],
        grad_fc[second : second + hidden_local].astype(F32), sums[5],
    )


def solution(mesh):
    rows, whole = P(("dp", "tensor"), None), P()
    columns, down, along = P(None, "tensor"), P("tensor", None), P("tensor")
    return jax.shard_map(
        functools.partial(on_device, mesh.shape["tensor"], mesh.shape["dp"]),
        mesh=mesh,
        in_specs=(
            rows, P("dp"), whole, whole, columns, along, columns, columns, along, down, whole,
            whole, whole, columns, along, down, whole, rows,
        ),
        out_specs=(
            rows, rows, whole, whole, columns, along, columns, columns, along, down, whole,
            whole, whole, columns, along, down, whole,
        ),
        check_vma=False,
    )
```

```python
import functools

import jax
import jax.numpy as jnp
from jax import lax
from jax.experimental import pallas as pl
from jax.experimental.pallas import tpu as pltpu
from jax.sharding import PartitionSpec as P

HD = 72
LEN = 2048
BLOCK = 256
NORM_EPS = 1e-06
NEG_FILL = -1e30
LOG2E = 1.4426950408889634
VMEM_ALL = 67043328
BF16 = jnp.bfloat16
F32 = jnp.float32
MESH = pl.DeviceIdType.MESH
VMEM = pltpu.VMEM
DMA = pltpu.SemaphoreType.DMA
VSPEC = pl.BlockSpec(memory_space=pltpu.VMEM)
SSPEC = pl.BlockSpec(memory_space=pltpu.SMEM)
HBM = pl.BlockSpec(memory_space=pltpu.HBM)


def nn(left, right):
    return lax.dot_general(left, right, (((1,), (0,)), ((), ())), preferred_element_type=F32)


def nt(left, right):
    return lax.dot_general(left, right, (((1,), (1,)), ((), ())), preferred_element_type=F32)


def tn(left, right):
    return lax.dot_general(left, right, (((0,), (0,)), ((), ())), preferred_element_type=F32)


def remote(src, dst, send_sem, recv_sem, **where):
    return pltpu.make_async_remote_copy(
        src_ref=src, dst_ref=dst, send_sem=send_sem, recv_sem=recv_sem,
        device_id=where, device_id_type=MESH,
    )


def loading(sems, pairs):
    copies = [
        pltpu.make_async_copy(src, dst, sems.at[index]) for index, (src, dst) in enumerate(pairs)
    ]
    for copy in copies:
        copy.start()
    return copies


def place():
    me = lax.axis_index("tensor")
    core = lax.rem(me, 2)
    return me, core, lax.div(me, 2)


def greet_peers(axes):
    barrier = pltpu.get_barrier_semaphore()
    for axis, size in axes:
        me = lax.axis_index(axis)

        def greet(step, carry):
            pl.semaphore_signal(
                barrier, inc=1, device_id={axis: lax.rem(me + step, size)}, device_id_type=MESH
            )
            return carry

        lax.fori_loop(1, size, greet, 0)
    pl.semaphore_wait(barrier, sum(size - 1 for _, size in axes))


def greet_line(stages):
    me, core, stage = place()
    barrier = pltpu.get_barrier_semaphore()
    has_left, has_right = stage > 0, stage < stages - 1

    def greet(other):
        pl.semaphore_signal(barrier, inc=1, device_id={"tensor": other}, device_id_type=MESH)

    greet(me + 1 - 2 * core)
    pl.when(has_left)(lambda: greet(me - 2))
    pl.when(has_right)(lambda: greet(me + 2))
    pl.semaphore_wait(barrier, 1 + has_left.astype(jnp.int32) + has_right.astype(jnp.int32))


def normalize(values):
    average = jnp.mean(values, axis=-1, keepdims=True)
    centred = values - average
    variance = jnp.mean(centred * centred, axis=-1, keepdims=True)
    scale = lax.rsqrt(variance + NORM_EPS)
    return centred * scale, scale


class LineGather:
    def __init__(self, stages, buffer, send_sem, recv_sem):
        self.stages, self.buffer, self.send_sem, self.recv_sem = stages, buffer, send_sem, recv_sem
        self.me, self.core, self.stage = place()
        self.partner = self.me + 1 - 2 * self.core

    def copy(self, block, way, target):
        return remote(
            self.buffer.at[block], self.buffer.at[block],
            self.send_sem.at[block, way], self.recv_sem.at[block], tensor=target,
        )

    def each_copy(self, block, right, left, act):
        pl.when(right)(lambda: act(self.copy(block, 0, self.me + 2)))
        pl.when(left)(lambda: act(self.copy(block, 1, self.me - 2)))
        act(self.copy(block, 2, self.partner))

    def start(self):
        self.each_copy(
            self.me, self.stage < self.stages - 1, self.stage > 0, lambda copy: copy.start()
        )

    def start_inward(self):
        low = self.stage < self.stages // 2
        self.each_copy(self.me, low, jnp.logical_not(low), lambda copy: copy.start())

    def start_outward(self):
        low = self.stage < self.stages // 2
        pl.when(jnp.logical_not(low) & (self.stage < self.stages - 1))(
            lambda: self.copy(self.me, 0, self.me + 2).start()
        )
        pl.when(low & (self.stage > 0))(lambda: self.copy(self.me, 1, self.me - 2).start())

    def incoming(self, reach, side, core):
        far = jnp.where(side == 0, self.stage - reach, self.stage + reach)
        return (far >= 0) & (far < self.stages), 2 * far + core

    def arrive(self, block):
        self.copy(block, 2, self.partner).wait_recv()

    def ways(self, side):
        return (side == 0) & (self.stage < self.stages - 1), (side == 1) & (self.stage > 0)

    def relay(self, reach):
        for side in range(2):
            valid, block = self.incoming(reach, side, self.core)

            @pl.when(valid)
            def _():
                self.arrive(block)
                self.each_copy(block, *self.ways(jnp.int32(side)), lambda copy: copy.start())

    def use_own(self, compute):
        compute(self.me)
        self.arrive(self.partner)
        compute(self.partner)

    def use(self, reach, compute):
        def body(index, carry):
            side, other = lax.rem(index, 2), lax.div(index, 2)
            valid, block = self.incoming(
                reach, side, jnp.where(other == 0, self.core, 1 - self.core)
            )

            @pl.when(valid)
            def _():
                pl.when(other == 1)(lambda: self.arrive(block))
                compute(block)

            return carry

        lax.fori_loop(0, 4, body, 0)

    def run(self, compute):
        def body(reach, carry):
            self.relay(reach)
            self.use(reach, compute)
            return carry

        self.use_own(compute)
        lax.fori_loop(1, self.stages, body, 0)

    def finish(self):
        self.each_copy(
            self.me, self.stage < self.stages - 1, self.stage > 0, lambda copy: copy.wait_send()
        )

        def body(index, carry):
            reach, side = lax.div(index, 2) + 1, lax.rem(index, 2)
            valid, block = self.incoming(reach, side, self.core)

            @pl.when(valid)
            def _():
                self.each_copy(block, *self.ways(side), lambda copy: copy.wait_send())

            return carry

        lax.fori_loop(0, 2 * (self.stages - 1), body, 0)


class LineScatter:
    def __init__(self, stages, partial, cross, lane, sems):
        self.stages, self.partial, self.cross, self.lane = stages, partial, cross, lane
        self.cross_send, self.cross_recv, self.lane_send, self.lane_recv = sems
        self.me, self.core, self.stage = place()
        self.partner = self.me + 1 - 2 * self.core

    def cross_copy(self, far):
        return remote(
            self.partial.at[2 * far + 1 - self.core], self.cross.at[far],
            self.cross_send.at[far], self.cross_recv.at[far], tensor=self.partner,
        )

    def slot(self, way, far, holder):
        return far if way == 0 else jnp.where(far == holder, self.stages, far)

    def lane_copy(self, way, far, holder):
        target = self.me + 2 if way == 0 else self.me - 2
        slot = self.slot(way, far, holder)
        return remote(
            self.partial.at[2 * far + self.core], self.lane.at[slot],
            self.lane_send.at[far], self.lane_recv.at[slot], tensor=target,
        )

    def sent(self, way, far):
        return self.lane_copy(way, far, self.stage + (1 if way == 0 else -1))

    def received(self, way, far):
        self.lane_copy(way, far, self.stage).wait_recv()
        return self.lane[self.slot(way, far, self.stage)].astype(F32)

    def put(self, block, value):
        self.partial[block] = value.astype(BF16)

        @pl.when(lax.rem(block, 2) != self.core)
        def _():
            self.cross_copy(lax.div(block, 2)).start()

    def produce(self, compute):
        def body(index, carry):
            reach = self.stages - 1 - lax.div(index, 4)
            side, other = lax.rem(lax.div(index, 2), 2), lax.rem(index, 2)
            far = jnp.where(side == 0, self.stage + reach, self.stage - reach)

            @pl.when((far >= 0) & (far < self.stages) & ((reach > 0) | (side == 0)))
            def _():
                block = 2 * far + jnp.where(other == 0, 1 - self.core, self.core)
                self.put(block, compute(block))

            return carry

        lax.fori_loop(0, 4 * self.stages, body, 0)

    def chip_sum(self, far):
        return self.partial[2 * far + self.core].astype(F32) + self.cross[far].astype(F32)

    def send_sum(self, way, far, incoming):
        self.cross_copy(far).wait_recv()
        block = 2 * far + self.core

        @pl.when(incoming)
        def _():
            self.partial[block] = (self.chip_sum(far) + self.received(way, far)).astype(BF16)

        @pl.when(jnp.logical_not(incoming))
        def _():
            self.partial[block] = self.chip_sum(far).astype(BF16)

        self.sent(way, far).start()

    def step(self, reach):
        right, left = self.stage + reach, self.stage - reach
        pl.when(right < self.stages)(lambda: self.send_sum(0, right, self.stage > 0))
        pl.when(left >= 0)(lambda: self.send_sum(1, left, self.stage < self.stages - 1))

    def steps(self, first, last):
        lax.fori_loop(first, last, lambda index, carry: (self.step(self.stages - 1 - index), carry)[1], 0)

    def own(self, total_ref):
        self.cross_copy(self.stage).wait_recv()
        total_ref[...] = self.chip_sum(self.stage)

        @pl.when(self.stage > 0)
        def _():
            total_ref[...] += self.received(0, self.stage)

        @pl.when(self.stage < self.stages - 1)
        def _():
            total_ref[...] += self.received(1, self.stage)

    def finish(self):
        def body(far, carry):
            self.cross_copy(far).wait_send()
            pl.when(far > self.stage)(lambda: self.sent(0, far).wait_send())
            pl.when(far < self.stage)(lambda: self.sent(1, far).wait_send())
            return carry

        lax.fori_loop(0, self.stages, body, 0)


def scatter_shapes(stages, rows, depth):
    return [
        VMEM((2 * stages, rows, depth), BF16), VMEM((stages, rows, depth), BF16),
        VMEM((stages + 1, rows, depth), BF16),
        DMA((stages,)), DMA((stages,)), DMA((stages,)), DMA((stages + 1,)),
    ]


def exchange(axis, size, slots, send_sem, recv_sem):
    me = lax.axis_index(axis)

    def copy_to(other, slot):
        return remote(
            slots.at[slot], slots.at[slot], send_sem.at[other], recv_sem.at[slot], **{axis: other}
        )

    def start(step, carry):
        copy_to(lax.rem(me + step, size), me).start()
        return carry

    def wait(step, carry):
        other = lax.rem(me + step, size)
        copy_to(other, other).wait_recv()
        copy_to(other, me).wait_send()
        return carry

    lax.fori_loop(1, size, start, 0)
    return lambda: lax.fori_loop(1, size, wait, 0)


def piece_height(height, parts):
    return -(-height // (16 * parts)) * 16


class RowSum:
    def __init__(self, parts, piece, arrive, send_sem, recv_sem):
        self.parts, self.piece, self.arrive = parts, piece, arrive
        self.send_sem, self.recv_sem = send_sem, recv_sem
        self.row = lax.axis_index("dp")

    def copy(self, other, source):
        return remote(
            self.piece.at[other], self.arrive.at[source],
            self.send_sem.at[other], self.recv_sem.at[source], dp=other,
        )

    def others(self, act, start):
        return lax.fori_loop(
            1, self.parts, lambda step, carry: act(lax.rem(self.row + step, self.parts), carry), start
        )

    def start(self, total):
        high = self.piece.shape[1]
        for part in range(self.parts):
            self.piece[part] = total[part * high : (part + 1) * high, :].astype(BF16)

        def send(other, carry):
            self.copy(other, self.row).start()
            return carry

        self.others(send, 0)

    def reduce(self):
        def add(other, so_far):
            self.copy(other, other).wait_recv()
            self.copy(other, self.row).wait_send()
            return so_far + self.arrive[other].astype(F32)

        return self.others(add, self.piece[self.row].astype(F32)).astype(BF16)


def rowsum_shapes(parts, high, depth):
    return [
        VMEM((parts, high, depth), BF16), VMEM((parts, high, depth), BF16), DMA((parts,)), DMA((parts,)),
    ]


def column(row):
    return jnp.broadcast_to(row, (128, row.shape[1])).T[:, :1]


def project_kernel(
    stages, tok_hbm, vec_ref, wq_hbm, wk_hbm, wv_hbm, ids_ref,
    norm_hbm, q_hbm, k_hbm, v_hbm, span_ref, idr_ref, ido_ref,
    tok, norm, q_ref, k_ref, v_ref, weight, send_sem, recv_sem, out_sem, load_sem,
):
    me, _, _ = place()
    width, rows = wq_hbm.shape[0], tok.shape[0]
    loads = loading(
        load_sem,
        ((tok_hbm, tok), (wq_hbm, weight.at[0]), (wk_hbm, weight.at[1]), (wv_hbm, weight.at[2])),
    )
    greet_line(stages)
    loads[0].wait()
    normed, _ = normalize(tok[...].astype(F32))
    norm[me] = (normed * vec_ref[0:1, :] + vec_ref[1:2, :]).astype(BF16)
    gather = LineGather(stages, norm, send_sem, recv_sem)
    gather.start()
    ids = ids_ref[...].astype(F32)
    idr_ref[...] = ids
    ido_ref[...] = idr_ref[:, pl.ds(pl.multiple_of(me * rows, rows), rows)]
    for block in range(ids.shape[1] // BLOCK):
        first = ids[:, block * BLOCK : block * BLOCK + 1]
        last = ids[:, (block + 1) * BLOCK - 1 : (block + 1) * BLOCK]
        begin = jnp.sum(jnp.where(ids > first, 1.0, 0.0))
        end = jnp.sum(jnp.where(ids >= jnp.maximum(last, 1.0), 1.0, 0.0))
        span_ref[0, block] = lax.div(begin.astype(jnp.int32), BLOCK)
        span_ref[1, block] = lax.div(end.astype(jnp.int32) + (BLOCK - 1), BLOCK)
    for load in loads[1:]:
        load.wait()

    def keep(block):
        return [
            pltpu.make_async_copy(src.at[block], dst.at[block], out_sem.at[index, block])
            for index, (src, dst) in enumerate(
                ((norm, norm_hbm), (q_ref, q_hbm), (k_ref, k_hbm), (v_ref, v_hbm))
            )
        ]

    def compute(block):
        q_ref[block] = (nt(norm[block], weight[0]) + vec_ref[7:8, :width]).astype(BF16)
        k_ref[block] = nt(norm[block], weight[1]).astype(BF16)
        v_ref[block] = (nt(norm[block], weight[2]) + vec_ref[8:9, :width]).astype(BF16)
        for copy in keep(block):
            copy.start()

    gather.run(compute)
    gather.finish()

    def kept(block, carry):
        for copy in keep(block):
            copy.wait()
        return carry

    lax.fori_loop(0, 2 * stages, kept, 0)


def project(tokens, vectors, wq, wk, wv, ids, devices):
    rows, depth = tokens.shape
    width, length = wq.shape[1], ids.shape[1]
    head = jax.ShapeDtypeStruct((devices, rows, width), BF16)
    return pl.pallas_call(
        functools.partial(project_kernel, devices // 2),
        name="project",
        out_shape=(
            jax.ShapeDtypeStruct((devices, rows, depth), BF16), head, head, head,
            jax.ShapeDtypeStruct((2, length // BLOCK), jnp.int32),
            jax.ShapeDtypeStruct((1, length), F32), jax.ShapeDtypeStruct((1, rows), F32),
        ),
        in_specs=[HBM, VSPEC, HBM, HBM, HBM, VSPEC],
        out_specs=(HBM, HBM, HBM, HBM, SSPEC, VSPEC, VSPEC),
        scratch_shapes=[
            VMEM((rows, depth), BF16), VMEM((devices, rows, depth), BF16),
            *[VMEM((devices, rows, width), BF16)] * 3, VMEM((3, width, depth), BF16),
            DMA((devices, 3)), DMA((devices,)), DMA((4, devices)), DMA((4,)),
        ],
        compiler_params=pltpu.CompilerParams(
            collective_id=0, has_side_effects=True, vmem_limit_bytes=VMEM_ALL
        ),
    )(tokens, vectors, wq.T, wk.T, wv.T, ids)


def lanes_of(head, width):
    lane = lax.broadcasted_iota(jnp.int32, (1, width), 1)
    return (lane >= head * HD) & (lane < (head + 1) * HD)


def fill_columns(row_ref, column_ref):
    for block in range(row_ref.shape[1] // BLOCK):
        at = pl.ds(block * BLOCK, BLOCK)
        column_ref[at, :] = column(row_ref[:, at])


def head_rows(head, width):
    row = lax.broadcasted_iota(jnp.int32, (width, 1), 0)
    return (row >= head * HD) & (row < (head + 1) * HD)


def side_by_side(block_t, heads):
    width = block_t.shape[0]
    zero = jnp.zeros_like(block_t)
    return jnp.concatenate([jnp.where(head_rows(h, width), block_t, zero) for h in range(heads)], axis=1)


def stacked(block, heads):
    width = block.shape[1]
    zero = jnp.zeros_like(block)
    return jnp.concatenate([jnp.where(lanes_of(h, width), block, zero) for h in range(heads)], axis=0)


def repeat_lanes(row, heads):
    return jnp.concatenate([row] * heads, axis=1)


def attend_kernel(
    heads, span_ref, q_hbm, k_hbm, v_hbm, idr_ref, o_ref, log_ref,
    q_ref, k_ref, v_ref, load_sem, idc_ref, vt_ref, acc_ref,
):
    length, width = q_ref.shape
    scale = HD ** (-0.5) * LOG2E
    loads = loading(load_sem, ((v_hbm, v_ref), (q_hbm, q_ref), (k_hbm, k_ref)))
    fill_columns(idr_ref, idc_ref)
    for load in loads:
        load.wait()

    def turn(block, total):
        at = pl.ds(pl.multiple_of(block * BLOCK, BLOCK), BLOCK)
        value = v_ref[at, :].astype(F32)
        vt_ref[block] = value.T.astype(BF16)
        return total + jnp.sum(value, axis=0, keepdims=True)

    mean_value = lax.fori_loop(0, length // BLOCK, turn, jnp.zeros((1, width), F32)) * (1.0 / length)

    def per_block(block, carry):
        at = pl.ds(pl.multiple_of(block * BLOCK, BLOCK), BLOCK)
        query = side_by_side(q_ref[at, :].astype(F32).T.astype(BF16), heads)
        id_row = idr_ref[:, at]
        id_rows = repeat_lanes(id_row, heads)
        acc_ref[...] = jnp.zeros_like(acc_ref)

        def per_key(other, state):
            top, total = state
            keys_at = pl.ds(pl.multiple_of(other * BLOCK, BLOCK), BLOCK)
            id_col = idc_ref[keys_at, :]
            allowed = (id_col == id_rows) & (id_col > 0)
            scores = jnp.where(allowed, nn(k_ref[keys_at, :], query) * scale, NEG_FILL)
            new_top = jnp.maximum(top, jnp.max(scores, axis=0, keepdims=True))
            weight = jnp.exp2(scores - new_top)
            shrink = jnp.exp2(top - new_top)
            total = total * shrink + jnp.sum(weight, axis=0, keepdims=True)
            acc_ref[...] = acc_ref[...] * shrink + nn(vt_ref[other], weight.astype(BF16))
            return new_top, total

        top, total = lax.fori_loop(
            span_ref[0, block], span_ref[1, block], per_key,
            (jnp.full((1, heads * BLOCK), NEG_FILL, F32), jnp.zeros((1, heads * BLOCK), F32)),
        )
        scaled = acc_ref[...] / total
        logs = jnp.where(id_rows == 0, 0.0, top + jnp.log2(total))
        result = jnp.zeros((width, BLOCK), F32)
        for h in range(heads):
            here = slice(h * BLOCK, (h + 1) * BLOCK)
            result = jnp.where(head_rows(h, width), scaled[:, here], result)
            log_ref[h : h + 1, at] = logs[:, here]
        o_ref[at, :] = jnp.where(idc_ref[at, :] == 0, mean_value, result.T).astype(BF16)
        return carry

    lax.fori_loop(0, length // BLOCK, per_block, 0)


def attend(q, k, v, span, id_row):
    length, width = q.shape
    heads = width // HD
    return pl.pallas_call(
        functools.partial(attend_kernel, heads),
        name="attend",
        out_shape=(
            jax.ShapeDtypeStruct((length, width), BF16),
            jax.ShapeDtypeStruct((heads, length), F32),
        ),
        in_specs=[SSPEC, HBM, HBM, HBM, VSPEC],
        out_specs=(VSPEC,) * 2,
        scratch_shapes=[
            *[VMEM((length, width), BF16)] * 3, DMA((3,)),
            VMEM((length, 1), F32), VMEM((length // BLOCK, width, BLOCK), BF16),
            VMEM((width, heads * BLOCK), F32),
        ],
        compiler_params=pltpu.CompilerParams(vmem_limit_bytes=VMEM_ALL),
    )(span, q, k, v, id_row)


def attend_back_kernel(
    heads, span_ref, q_hbm, k_hbm, v_hbm, idr_ref, o_hbm, log_ref, g_hbm,
    out_ref, q_ref, k_ref, v_ref, o_ref, g_ref, load_sem,
    idc_ref, dq_ref, dk_ref, dv_ref, q_side, q_stack, g_side, g_stack, row_ref, log_side,
):
    length, width = q_ref.shape
    score_scale = HD ** (-0.5)
    loads = loading(
        load_sem, ((q_hbm, q_ref), (g_hbm, g_ref), (o_hbm, o_ref), (k_hbm, k_ref), (v_hbm, v_ref))
    )
    dq_ref[...] = jnp.zeros_like(dq_ref)
    fill_columns(idr_ref, idc_ref)
    for load in loads:
        load.wait()

    def prepare(block, pad):
        at = pl.ds(pl.multiple_of(block * BLOCK, BLOCK), BLOCK)
        query, grad = q_ref[at, :], g_ref[at, :]
        wide = grad.astype(F32)
        grad_t = wide.T
        product = (wide * o_ref[at, :].astype(F32)).T
        q_side[block] = side_by_side(query.astype(F32).T.astype(BF16), heads)
        g_side[block] = side_by_side(grad_t.astype(BF16), heads)
        q_stack[block] = stacked(query, heads)
        g_stack[block] = stacked(grad, heads)
        for h in range(heads):
            here = slice(h * BLOCK, (h + 1) * BLOCK)
            row_ref[block, :, here] = jnp.sum(
                jnp.where(head_rows(h, width), product, 0.0), axis=0, keepdims=True
            )
            log_side[block, :, here] = log_ref[h : h + 1, at]
        return pad + jnp.sum(jnp.where(idc_ref[at, :] == 0, wide, 0.0), axis=0, keepdims=True)

    pad = lax.fori_loop(0, length // BLOCK, prepare, jnp.zeros((1, width), F32)) * (1.0 / length)

    def per_key(block, carry):
        at = pl.ds(pl.multiple_of(block * BLOCK, BLOCK), BLOCK)
        key, value, id_col = k_ref[at, :], v_ref[at, :], idc_ref[at, :]
        key_side = side_by_side(key.astype(F32).T.astype(BF16), heads)
        real = id_col > 0
        dk_ref[...] = jnp.zeros_like(dk_ref)
        dv_ref[...] = jnp.zeros_like(dv_ref)

        def per_query(other, inner):
            query_at = pl.ds(pl.multiple_of(other * BLOCK, BLOCK), BLOCK)
            allowed = (id_col == repeat_lanes(idr_ref[:, query_at], heads)) & real
            scores = nn(key, q_side[other]) * (score_scale * LOG2E) - log_side[other]
            prob = jnp.exp2(jnp.where(allowed, scores, NEG_FILL))
            dv_ref[...] += nn(prob.astype(BF16), g_stack[other])
            back = (prob * (nn(value, g_side[other]) - row_ref[other])).astype(BF16)
            dk_ref[...] += nn(back, q_stack[other])
            back_rows = jnp.concatenate(
                [back[:, h * BLOCK : (h + 1) * BLOCK] for h in range(heads)], axis=0
            )
            dq_ref[other] += nn(key_side, back_rows)
            return inner

        lax.fori_loop(span_ref[0, block], span_ref[1, block], per_query, 0)
        out_ref[at, width : 2 * width] = (dk_ref[...] * score_scale).astype(BF16)
        out_ref[at, 2 * width :] = (dv_ref[...] + pad).astype(BF16)
        return carry

    lax.fori_loop(0, length // BLOCK, per_key, 0)

    def settle(block, carry):
        at = pl.ds(pl.multiple_of(block * BLOCK, BLOCK), BLOCK)
        out_ref[at, :width] = (dq_ref[block].T * score_scale).astype(BF16)
        return carry

    lax.fori_loop(0, length // BLOCK, settle, 0)


def attend_back(q, k, v, span, id_row, o, log_total, grad):
    length, width = q.shape
    heads = width // HD
    blocks = length // BLOCK
    whole = VMEM((length, width), BF16)
    side, stack = VMEM((blocks, width, heads * BLOCK), BF16), VMEM((blocks, heads * BLOCK, width), BF16)
    line = VMEM((blocks, 1, heads * BLOCK), F32)
    return pl.pallas_call(
        functools.partial(attend_back_kernel, heads),
        name="attend_back",
        out_shape=jax.ShapeDtypeStruct((length, 3 * width), BF16),
        in_specs=[SSPEC, HBM, HBM, HBM, VSPEC, HBM, VSPEC, HBM],
        out_specs=VSPEC,
        scratch_shapes=[
            whole, whole, whole, whole, whole, DMA((5,)),
            VMEM((length, 1), F32), VMEM((blocks, width, BLOCK), F32), VMEM((BLOCK, width), F32),
            VMEM((BLOCK, width), F32), side, stack, side, stack, line, line,
        ],
        compiler_params=pltpu.CompilerParams(vmem_limit_bytes=VMEM_ALL),
    )(span, q, k, v, id_row, o, log_total, grad)


def gelu_pair(u):
    slope = (2.0 / jnp.pi) ** 0.5
    bent = jnp.tanh(slope * (u + 0.044715 * u * u * u))
    half = 0.5 * (1.0 + bent)
    return u * half, half + 0.5 * u * (1.0 - bent * bent) * slope * (1.0 + 3 * 0.044715 * u * u)


def middle_kernel(
    stages, parts, att_hbm, wo_hbm, fc1_hbm, fc2_hbm, tok_hbm, top_hbm, ids_ref, vec_ref,
    out_ref, gres_ref, gatt_ref, fc_ref, small_ref,
    wo, fc1, fc2, tok, top, load_sem,
    held, held_send, held_recv, norm_all, norm_send, norm_recv, top_all, top_send, top_recv,
    hidden, slope, grad_pre,
    br_part, br_cross, br_lane, br_s0, br_s1, br_s2, br_s3,
    gn_part, gn_cross, gn_lane, gn_s0, gn_s1, gn_s2, gn_s3,
    resid, total, acc, piece, arrive, piece_send, piece_recv, back, back_send, back_recv,
):
    me, _, _ = place()
    devices = 2 * stages
    rows, depth = tok_hbm.shape
    units = fc1_hbm.shape[0]
    second = -(-units // 16) * 16
    loads = loading(
        load_sem,
        ((tok_hbm, tok), (top_hbm, top), (wo_hbm, wo), (fc1_hbm, fc1), (fc2_hbm, fc2),
         (att_hbm.at[me], held.at[me])),
    )
    greet_peers((("tensor", devices), ("dp", parts)))

    def held_copy(other, source):
        return remote(
            att_hbm.at[other], held.at[source], held_send.at[other], held_recv.at[source], tensor=other
        )

    def send_held(step, carry):
        held_copy(lax.rem(me + step, devices), me).start()
        return carry

    lax.fori_loop(1, devices, send_held, 0)
    gather2 = LineGather(stages, norm_all, norm_send, norm_recv)
    gather3 = LineGather(stages, top_all, top_send, top_recv)
    branch = LineScatter(stages, br_part, br_cross, br_lane, (br_s0, br_s1, br_s2, br_s3))
    gnorm = LineScatter(stages, gn_part, gn_cross, gn_lane, (gn_s0, gn_s1, gn_s2, gn_s3))

    mask = column(jnp.where(ids_ref[...] > 0, 1.0, 0.0))
    acc[...] = jnp.zeros_like(acc)
    small_ref[...] = jnp.zeros_like(small_ref)
    loads[0].wait()
    loads[1].wait()
    top_own = top[...].astype(F32) * mask
    top_all[me] = top_own.astype(BF16)
    small_ref[5:6, :] = jnp.sum(top_own, axis=0, keepdims=True)
    resid[...] = tok[...].astype(F32) + vec_ref[2:3, :]
    loads[2].wait()
    loads[5].wait()
    resid[...] += nn(held[me], wo[me])

    def add_held(step, carry):
        other = lax.rem(me + devices - step, devices)
        held_copy(other, other).wait_recv()
        resid[...] += nn(held[other], wo[other])
        return carry

    lax.fori_loop(1, devices, add_held, 0)
    normed, _ = normalize(resid[...])
    norm_all[me] = (normed * vec_ref[3:4, :] + vec_ref[4:5, :]).astype(BF16)
    gather2.start()
    gather3.start_inward()
    loads[3].wait()
    loads[4].wait()

    def forward(block):
        pre_act = nt(norm_all[block], fc1[...]) + vec_ref[6:7, 0:units]
        value, slope_now = gelu_pair(pre_act)
        hidden[block] = value.astype(BF16)
        slope[block] = slope_now.astype(BF16)
        branch.put(block, nn(hidden[block], fc2[...]))

    gather2.run(forward)
    gather3.start_outward()

    def backward(block):
        grad = nt(top_all[block], fc2[...]) * slope[block].astype(F32)
        low = grad.astype(BF16)
        grad_pre[block] = low
        small_ref[7:8, 0:units] += jnp.sum(low.astype(F32), axis=0, keepdims=True)
        gnorm.put(block, nn(grad_pre[block], fc1[...]))
        acc[0:units, :] += tn(grad_pre[block], norm_all[block])
        acc[second : second + units, :] += tn(hidden[block], top_all[block])

    def both(reach, carry):
        gather3.relay(reach)
        pl.when(reach < stages - 1)(lambda: branch.step(stages - 1 - reach))
        gather3.use(reach, backward)
        return carry

    branch.step(stages - 1)
    gather3.use_own(backward)
    lax.fori_loop(1, stages, both, 0)
    gnorm.step(stages - 1)
    sums = RowSum(parts, piece, arrive, piece_send, piece_recv)
    sums.start(acc)
    branch.own(total)
    out_ref[...] = (mask * (resid[...] + total[...] + vec_ref[5:6, :])).astype(BF16)
    gnorm.steps(1, stages - 1)

    gnorm.own(total)
    grad = total[...]
    normed, scale = normalize(resid[...])
    small_ref[2:3, :] = jnp.sum(grad * normed, axis=0, keepdims=True)
    small_ref[3:4, :] = jnp.sum(grad, axis=0, keepdims=True)
    inner = grad * vec_ref[3:4, :]
    inner_mean = jnp.mean(inner, axis=-1, keepdims=True)
    inner_proj = jnp.mean(inner * normed, axis=-1, keepdims=True)
    grad_resid = top[...].astype(F32) * mask + scale * (inner - inner_mean - normed * inner_proj)
    gres_ref[...] = grad_resid
    tok[...] = grad_resid.astype(BF16)
    small_ref[4:5, :] = jnp.sum(grad_resid, axis=0, keepdims=True)

    def back_copy(other, source):
        return remote(
            back.at[other], gatt_ref.at[source], back_send.at[other], back_recv.at[source], tensor=other
        )

    def send_back(step, carry):
        other = lax.rem(me + step, devices)
        back[other] = nt(tok[...], wo[other]).astype(BF16)
        back_copy(other, me).start()
        return carry

    lax.fori_loop(1, devices, send_back, 0)
    gatt_ref[me] = nt(tok[...], wo[me]).astype(BF16)

    fc_ref[...] = sums.reduce()

    def settle(step, carry):
        other = lax.rem(me + devices - step, devices)
        back_copy(other, other).wait_recv()
        back_copy(other, me).wait_send()
        held_copy(other, me).wait_send()
        return carry

    lax.fori_loop(1, devices, settle, 0)
    gather2.finish()
    gather3.finish()
    branch.finish()
    gnorm.finish()


def middle(att, wo, fc1, fc2, tokens, out_grad, ids, vectors, parts):
    devices, rows, width = att.shape
    depth, units = fc1.shape
    stages = devices // 2
    high = piece_height(2 * (-(-units // 16) * 16), parts)
    return pl.pallas_call(
        functools.partial(middle_kernel, stages, parts),
        name="middle",
        out_shape=(
            jax.ShapeDtypeStruct((rows, depth), BF16),
            jax.ShapeDtypeStruct((rows, depth), F32),
            jax.ShapeDtypeStruct((devices, rows, width), BF16),
            jax.ShapeDtypeStruct((high, depth), BF16),
            jax.ShapeDtypeStruct((8, depth), F32),
        ),
        in_specs=[HBM] * 6 + [VSPEC] * 2,
        out_specs=(VSPEC,) * 5,
        scratch_shapes=[
            VMEM((devices, width, depth), BF16), VMEM((units, depth), BF16), VMEM((units, depth), BF16),
            VMEM((rows, depth), BF16), VMEM((rows, depth), BF16), DMA((6,)),
            VMEM((devices, rows, width), BF16), DMA((devices,)), DMA((devices,)),
            VMEM((devices, rows, depth), BF16), DMA((devices, 3)), DMA((devices,)),
            VMEM((devices, rows, depth), BF16), DMA((devices, 3)), DMA((devices,)),
            VMEM((devices, rows, units), BF16), VMEM((devices, rows, units), BF16),
            VMEM((devices, rows, units), BF16),
            *scatter_shapes(stages, rows, depth), *scatter_shapes(stages, rows, depth),
            VMEM((rows, depth), F32), VMEM((rows, depth), F32),
            VMEM((parts * high, depth), F32), *rowsum_shapes(parts, high, depth),
            VMEM((devices, rows, width), BF16), DMA((devices,)), DMA((devices,)),
        ],
        compiler_params=pltpu.CompilerParams(
            collective_id=2, has_side_effects=True, vmem_limit_bytes=VMEM_ALL
        ),
    )(
        att, wo, fc1.T, fc2, tokens, out_grad, ids, vectors,
    )


def close_kernel(
    stages, parts, dx_hbm, wq_hbm, wk_hbm, wv_hbm, norm_hbm, att_hbm, tok_hbm, vec_ref, resid_hbm,
    small_ref, fc_hbm,
    gtok_ref, gw_hbm, go_hbm, gfc_hbm, gsmall_ref,
    dx_ref, weight, norm, att_ref, tok_ref, resid_ref, load_sem, gatt_all, gatt_send, gatt_recv,
    partial, cross, lane, cross_send, cross_recv, lane_send, lane_recv,
    total, acc, acc_o, w_piece, w_arrive, w_send, w_recv, o_piece, o_arrive, o_send, o_recv,
    w_all, o_all, fc_all, wa_send, wa_recv, oa_send, oa_recv, fa_send, fa_recv, out_sem,
    slots_t, slots_d, st_send, st_recv, sd_send, sd_recv,
):
    me, _, _ = place()
    row = lax.axis_index("dp")
    devices = 2 * stages
    wide, width = dx_ref.shape[2], att_ref.shape[2]
    loads = loading(
        load_sem,
        ((resid_hbm, resid_ref), (fc_hbm, fc_all.at[row]), (dx_hbm, dx_ref),
         *((src, weight.at[pl.ds(index * width, width)]) for index, src in enumerate((wq_hbm, wk_hbm, wv_hbm))),
         (norm_hbm, norm), (att_hbm, att_ref), (tok_hbm, tok_ref)),
    )
    greet_peers((("tensor", devices), ("dp", parts)))
    loads[0].wait()
    gatt_all[me] = resid_ref[...].astype(BF16)
    gather = LineGather(stages, gatt_all, gatt_send, gatt_recv)
    gather.start()
    loads[1].wait()
    wait_fc = exchange("dp", parts, fc_all, fa_send, fa_recv)
    for load in loads[2:6]:
        load.wait()
    scatter = LineScatter(
        stages, partial, cross, lane, (cross_send, cross_recv, lane_send, lane_recv)
    )
    scatter.produce(lambda block: nn(dx_ref[block], weight[...]))
    scatter.step(stages - 1)

    acc[...] = jnp.zeros_like(acc)
    acc_o[...] = jnp.zeros_like(acc_o)
    for load in loads[6:]:
        load.wait()

    def weight_block(block, bias):
        grad = dx_ref[block]
        acc[0:wide, :] += tn(grad, norm[block])
        return bias + jnp.sum(grad.astype(F32), axis=0, keepdims=True)

    bias = lax.fori_loop(0, devices, weight_block, jnp.zeros((1, wide), F32))
    w_sum = RowSum(parts, w_piece, w_arrive, w_send, w_recv)
    w_sum.start(acc)

    def weight_o(block):
        acc_o[0:width, :] += tn(att_ref[block], gatt_all[block])

    gather.use_own(weight_o)

    def both(reach, carry):
        gather.relay(reach)
        pl.when(reach < stages - 1)(lambda: scatter.step(stages - 1 - reach))
        gather.use(reach, weight_o)
        return carry

    lax.fori_loop(1, stages - 1, both, 0)
    w_all[row] = w_sum.reduce()
    wait_w = exchange("dp", parts, w_all, wa_send, wa_recv)
    lax.fori_loop(stages - 1, stages, both, 0)
    o_sum = RowSum(parts, o_piece, o_arrive, o_send, o_recv)
    o_sum.start(acc_o)

    scatter.own(total)
    grad = total[...]
    normed, scale = normalize(tok_ref[...].astype(F32))
    slots_t[me] = small_ref[...]
    slots_t[me, 0:1, :] = jnp.sum(grad * normed, axis=0, keepdims=True)
    slots_t[me, 1:2, :] = jnp.sum(grad, axis=0, keepdims=True)
    slots_t[me, 6:7, 0:wide] = bias
    wait_small = exchange("tensor", devices, slots_t, st_send, st_recv)
    inner = grad * vec_ref[0:1, :]
    inner_mean = jnp.mean(inner, axis=-1, keepdims=True)
    inner_proj = jnp.mean(inner * normed, axis=-1, keepdims=True)
    gtok_ref[...] = resid_ref[...] + scale * (inner - inner_mean - normed * inner_proj)
    o_all[row] = o_sum.reduce()
    wait_o = exchange("dp", parts, o_all, oa_send, oa_recv)
    wait_small()
    sums = lax.fori_loop(
        1, devices, lambda slot, so_far: so_far + slots_t[slot], slots_t[0]
    )
    line = lax.broadcasted_iota(jnp.int32, sums.shape, 0)
    slots_d[row] = jnp.where(line < 6, sums, slots_t[me])
    wait_last = exchange("dp", parts, slots_d, sd_send, sd_recv)
    outs = []
    for index, (wait, src, dst) in enumerate(
        ((wait_fc, fc_all, gfc_hbm), (wait_w, w_all, gw_hbm), (wait_o, o_all, go_hbm))
    ):
        wait()
        out = pltpu.make_async_copy(src, dst, out_sem.at[index])
        out.start()
        outs.append(out)
    wait_last()
    gsmall_ref[...] = lax.fori_loop(
        1, parts, lambda slot, so_far: so_far + slots_d[slot], slots_d[0]
    )
    gather.finish()
    scatter.finish()
    for out in outs:
        out.wait()


def close(dx, wq, wk, wv, norm, att, tokens, vectors, resid, small, fc, parts):
    devices, rows, wide = dx.shape
    depth = tokens.shape[1]
    stages = devices // 2
    width = wide // 3
    w_high, o_high, fc_high = piece_height(wide, parts), piece_height(width, parts), fc.shape[0]
    pieces = [(parts, high, depth) for high in (w_high, o_high, fc_high)]
    return pl.pallas_call(
        functools.partial(close_kernel, stages, parts),
        name="close",
        out_shape=(
            jax.ShapeDtypeStruct((rows, depth), F32),
            *(jax.ShapeDtypeStruct(shape, BF16) for shape in pieces),
            jax.ShapeDtypeStruct(small.shape, F32),
        ),
        in_specs=[HBM] * 7 + [VSPEC, HBM, VSPEC, HBM],
        out_specs=(VSPEC, HBM, HBM, HBM, VSPEC),
        scratch_shapes=[
            VMEM((devices, rows, wide), BF16), VMEM((wide, depth), BF16),
            VMEM((devices, rows, depth), BF16), VMEM((devices, rows, width), BF16),
            VMEM((rows, depth), BF16), VMEM((rows, depth), F32), DMA((9,)),
            VMEM((devices, rows, depth), BF16), DMA((devices, 3)), DMA((devices,)),
            *scatter_shapes(stages, rows, depth),
            VMEM((rows, depth), F32), VMEM((parts * w_high, depth), F32),
            VMEM((parts * o_high, depth), F32),
            *rowsum_shapes(parts, w_high, depth), *rowsum_shapes(parts, o_high, depth),
            *(VMEM(shape, BF16) for shape in pieces), *[DMA((parts,))] * 6, DMA((3,)),
            VMEM((devices,) + small.shape, F32), VMEM((parts,) + small.shape, F32),
            DMA((devices,)), DMA((devices,)), DMA((parts,)), DMA((parts,)),
        ],
        compiler_params=pltpu.CompilerParams(
            collective_id=1, has_side_effects=True, vmem_limit_bytes=VMEM_ALL
        ),
    )(dx, wq.T, wk.T, wv.T, norm, att, tokens, vectors, resid, small, fc)


def on_device(
    devices, parts, tokens, picture_ids, ln1_gain, ln1_bias, q_weight, q_bias, k_weight, v_weight, v_bias,
    o_weight, o_bias, ln2_gain, ln2_bias, fc1_weight, fc1_bias, fc2_weight, fc2_bias, out_grad,
):
    own_count, depth = tokens.shape
    hidden_local = fc1_weight.shape[1]
    width = q_weight.shape[1]
    vectors = jnp.stack(
        [
            jnp.pad(item.astype(F32), (0, depth - item.shape[0]))
            for item in (
                ln1_gain, ln1_bias, o_bias, ln2_gain, ln2_bias, fc2_bias, fc1_bias, q_bias, v_bias
            )
        ]
    )
    norm1_all, q, k, v, span, id_row, own_ids = project(
        tokens, vectors, q_weight, k_weight, v_weight, picture_ids[None, :], devices
    )
    o_weight, q = lax.optimization_barrier((o_weight, q))
    o_all = lax.all_gather(o_weight, "tensor", axis=0)
    q, k, v = (item.reshape(LEN, width) for item in (q, k, v))
    attended, log_total = attend(q, k, v, span, id_row)
    heads_first = attended.reshape(devices, own_count, width)
    output, grad_residual, grad_attended, fc_piece, small = middle(
        heads_first, o_all, fc1_weight, fc2_weight, tokens, out_grad,
        own_ids, vectors, parts,
    )
    dqkv = attend_back(
        q, k, v, span, id_row, attended, log_total, grad_attended.reshape(LEN, width)
    )
    grad_tokens, grad_w, grad_o, grad_fc, sums = close(
        dqkv.reshape(devices, own_count, 3 * width), q_weight, k_weight, v_weight, norm1_all,
        heads_first, tokens, vectors, grad_residual, small, fc_piece, parts,
    )
    grad_w, grad_o, grad_fc = (item.reshape(-1, depth) for item in (grad_w, grad_o, grad_fc))
    second = -(-hidden_local // 16) * 16
    return (
        output, grad_tokens, sums[0], sums[1],
        grad_w[:width].astype(F32).T, sums[6, :width], grad_w[width : 2 * width].astype(F32).T,
        grad_w[2 * width : 3 * width].astype(F32).T, sums[6, 2 * width : 3 * width],
        grad_o[:width].astype(F32), sums[4], sums[2], sums[3],
        grad_fc[:hidden_local].astype(F32).T, sums[7, :hidden_local],
        grad_fc[second : second + hidden_local].astype(F32), sums[5],
    )


def solution(mesh):
    rows, whole = P(("dp", "tensor"), None), P()
    columns, down, along = P(None, "tensor"), P("tensor", None), P("tensor")
    return jax.shard_map(
        functools.partial(on_device, mesh.shape["tensor"], mesh.shape["dp"]),
        mesh=mesh,
        in_specs=(
            rows, P("dp"), whole, whole, columns, along, columns, columns, along, down, whole,
            whole, whole, columns, along, down, whole, rows,
        ),
        out_specs=(
            rows, rows, whole, whole, columns, along, columns, columns, along, down, whole,
            whole, whole, columns, along, down, whole,
        ),
        check_vma=False,
    )
```

```python
import functools

import jax
import jax.numpy as jnp
from jax import lax
from jax.experimental import pallas as pl
from jax.experimental.pallas import tpu as pltpu
from jax.sharding import PartitionSpec as P

HD = 72
LEN = 2048
BLOCK = 256
NORM_EPS = 1e-06
NEG_FILL = -1e30
LOG2E = 1.4426950408889634
VMEM_ALL = 67043328
BF16 = jnp.bfloat16
F32 = jnp.float32
MESH = pl.DeviceIdType.MESH
VMEM = pltpu.VMEM
DMA = pltpu.SemaphoreType.DMA
VSPEC = pl.BlockSpec(memory_space=pltpu.VMEM)
SSPEC = pl.BlockSpec(memory_space=pltpu.SMEM)
HBM = pl.BlockSpec(memory_space=pltpu.HBM)


def nn(left, right):
    return lax.dot_general(left, right, (((1,), (0,)), ((), ())), preferred_element_type=F32)


def nt(left, right):
    return lax.dot_general(left, right, (((1,), (1,)), ((), ())), preferred_element_type=F32)


def tn(left, right):
    return lax.dot_general(left, right, (((0,), (0,)), ((), ())), preferred_element_type=F32)


def remote(src, dst, send_sem, recv_sem, **where):
    return pltpu.make_async_remote_copy(
        src_ref=src, dst_ref=dst, send_sem=send_sem, recv_sem=recv_sem,
        device_id=where, device_id_type=MESH,
    )


def loading(sems, pairs):
    copies = [
        pltpu.make_async_copy(src, dst, sems.at[index]) for index, (src, dst) in enumerate(pairs)
    ]
    for copy in copies:
        copy.start()
    return copies


def place():
    me = lax.axis_index("tensor")
    core = lax.rem(me, 2)
    return me, core, lax.div(me, 2)


def greet_peers(axes):
    barrier = pltpu.get_barrier_semaphore()
    for axis, size in axes:
        me = lax.axis_index(axis)

        def greet(step, carry):
            pl.semaphore_signal(
                barrier, inc=1, device_id={axis: lax.rem(me + step, size)}, device_id_type=MESH
            )
            return carry

        lax.fori_loop(1, size, greet, 0)
    pl.semaphore_wait(barrier, sum(size - 1 for _, size in axes))


def greet_line(stages, parts):
    me, core, stage = place()
    row = lax.axis_index("dp")
    barrier = pltpu.get_barrier_semaphore()

    def greet_row(step, carry):
        other = lax.rem(row + step, parts)
        pl.semaphore_signal(barrier, inc=1, device_id={"dp": other}, device_id_type=MESH)
        return carry

    lax.fori_loop(1, parts, greet_row, 0)
    has_left, has_right = stage > 0, stage < stages - 1

    def greet(other):
        pl.semaphore_signal(barrier, inc=1, device_id={"tensor": other}, device_id_type=MESH)

    greet(me + 1 - 2 * core)
    pl.when(has_left)(lambda: greet(me - 2))
    pl.when(has_right)(lambda: greet(me + 2))
    pl.semaphore_wait(barrier, parts + has_left.astype(jnp.int32) + has_right.astype(jnp.int32))


def normalize(values):
    average = jnp.mean(values, axis=-1, keepdims=True)
    centred = values - average
    variance = jnp.mean(centred * centred, axis=-1, keepdims=True)
    scale = lax.rsqrt(variance + NORM_EPS)
    return centred * scale, scale


class LineGather:
    def __init__(self, stages, buffer, send_sem, recv_sem):
        self.stages, self.buffer, self.send_sem, self.recv_sem = stages, buffer, send_sem, recv_sem
        self.me, self.core, self.stage = place()
        self.partner = self.me + 1 - 2 * self.core

    def copy(self, block, way, target):
        return remote(
            self.buffer.at[block], self.buffer.at[block],
            self.send_sem.at[block, way], self.recv_sem.at[block], tensor=target,
        )

    def each_copy(self, block, right, left, act):
        pl.when(right)(lambda: act(self.copy(block, 0, self.me + 2)))
        pl.when(left)(lambda: act(self.copy(block, 1, self.me - 2)))
        act(self.copy(block, 2, self.partner))

    def start(self):
        self.each_copy(
            self.me, self.stage < self.stages - 1, self.stage > 0, lambda copy: copy.start()
        )

    def start_inward(self):
        low = self.stage < self.stages // 2
        self.each_copy(self.me, low, jnp.logical_not(low), lambda copy: copy.start())

    def start_outward(self):
        low = self.stage < self.stages // 2
        pl.when(jnp.logical_not(low) & (self.stage < self.stages - 1))(
            lambda: self.copy(self.me, 0, self.me + 2).start()
        )
        pl.when(low & (self.stage > 0))(lambda: self.copy(self.me, 1, self.me - 2).start())

    def incoming(self, reach, side, core):
        far = jnp.where(side == 0, self.stage - reach, self.stage + reach)
        return (far >= 0) & (far < self.stages), 2 * far + core

    def arrive(self, block):
        self.copy(block, 2, self.partner).wait_recv()

    def ways(self, side):
        return (side == 0) & (self.stage < self.stages - 1), (side == 1) & (self.stage > 0)

    def relay(self, reach):
        for side in range(2):
            valid, block = self.incoming(reach, side, self.core)

            @pl.when(valid)
            def _():
                self.arrive(block)
                self.each_copy(block, *self.ways(jnp.int32(side)), lambda copy: copy.start())

    def use_own(self, compute):
        compute(self.me)
        self.arrive(self.partner)
        compute(self.partner)

    def use(self, reach, compute):
        def body(index, carry):
            side, other = lax.rem(index, 2), lax.div(index, 2)
            valid, block = self.incoming(
                reach, side, jnp.where(other == 0, self.core, 1 - self.core)
            )

            @pl.when(valid)
            def _():
                pl.when(other == 1)(lambda: self.arrive(block))
                compute(block)

            return carry

        lax.fori_loop(0, 4, body, 0)

    def run(self, compute, after_first=lambda: None):
        def body(reach, carry):
            self.relay(reach)
            pl.when(reach == 1)(after_first)
            self.use(reach, compute)
            return carry

        self.use_own(compute)
        lax.fori_loop(1, self.stages, body, 0)

    def at_end(self):
        return (self.stage == 0) | (self.stage == self.stages - 1)

    def finish(self):
        self.each_copy(
            self.me, self.stage < self.stages - 1, self.stage > 0, lambda copy: copy.wait_send()
        )

        def body(index, carry):
            reach, side = lax.div(index, 2) + 1, lax.rem(index, 2)
            valid, block = self.incoming(reach, side, self.core)

            @pl.when(valid)
            def _():
                self.each_copy(block, *self.ways(side), lambda copy: copy.wait_send())

            return carry

        lax.fori_loop(0, 2 * (self.stages - 1), body, 0)


class LineScatter:
    def __init__(self, stages, partial, cross, lane, sems):
        self.stages, self.partial, self.cross, self.lane = stages, partial, cross, lane
        self.cross_send, self.cross_recv, self.lane_send, self.lane_recv = sems
        self.me, self.core, self.stage = place()
        self.partner = self.me + 1 - 2 * self.core

    def cross_copy(self, far):
        return remote(
            self.partial.at[2 * far + 1 - self.core], self.cross.at[far],
            self.cross_send.at[far], self.cross_recv.at[far], tensor=self.partner,
        )

    def slot(self, way, far, holder):
        return far if way == 0 else jnp.where(far == holder, self.stages, far)

    def lane_copy(self, way, far, holder):
        target = self.me + 2 if way == 0 else self.me - 2
        slot = self.slot(way, far, holder)
        return remote(
            self.partial.at[2 * far + self.core], self.lane.at[slot],
            self.lane_send.at[far], self.lane_recv.at[slot], tensor=target,
        )

    def sent(self, way, far):
        return self.lane_copy(way, far, self.stage + (1 if way == 0 else -1))

    def received(self, way, far):
        self.lane_copy(way, far, self.stage).wait_recv()
        return self.lane[self.slot(way, far, self.stage)].astype(F32)

    def put(self, block, value):
        self.partial[block] = value.astype(BF16)

        @pl.when(lax.rem(block, 2) != self.core)
        def _():
            self.cross_copy(lax.div(block, 2)).start()

    def produce(self, compute):
        def body(index, carry):
            reach = self.stages - 1 - lax.div(index, 4)
            side, other = lax.rem(lax.div(index, 2), 2), lax.rem(index, 2)
            far = jnp.where(side == 0, self.stage + reach, self.stage - reach)

            @pl.when((far >= 0) & (far < self.stages) & ((reach > 0) | (side == 0)))
            def _():
                block = 2 * far + jnp.where(other == 0, 1 - self.core, self.core)
                self.put(block, compute(block))

            return carry

        lax.fori_loop(0, 4 * self.stages, body, 0)

    def chip_sum(self, far):
        return self.partial[2 * far + self.core].astype(F32) + self.cross[far].astype(F32)

    def send_sum(self, way, far, incoming):
        self.cross_copy(far).wait_recv()
        block = 2 * far + self.core

        @pl.when(incoming)
        def _():
            self.partial[block] = (self.chip_sum(far) + self.received(way, far)).astype(BF16)

        @pl.when(jnp.logical_not(incoming))
        def _():
            self.partial[block] = self.chip_sum(far).astype(BF16)

        self.sent(way, far).start()

    def step(self, reach):
        right, left = self.stage + reach, self.stage - reach
        pl.when(right < self.stages)(lambda: self.send_sum(0, right, self.stage > 0))
        pl.when(left >= 0)(lambda: self.send_sum(1, left, self.stage < self.stages - 1))

    def steps(self, first, last):
        lax.fori_loop(first, last, lambda index, carry: (self.step(self.stages - 1 - index), carry)[1], 0)

    def own(self, total_ref):
        self.cross_copy(self.stage).wait_recv()
        total_ref[...] = self.chip_sum(self.stage)

        @pl.when(self.stage > 0)
        def _():
            total_ref[...] += self.received(0, self.stage)

        @pl.when(self.stage < self.stages - 1)
        def _():
            total_ref[...] += self.received(1, self.stage)

    def finish(self):
        def body(far, carry):
            self.cross_copy(far).wait_send()
            pl.when(far > self.stage)(lambda: self.sent(0, far).wait_send())
            pl.when(far < self.stage)(lambda: self.sent(1, far).wait_send())
            return carry

        lax.fori_loop(0, self.stages, body, 0)


def scatter_shapes(stages, rows, depth):
    return [
        VMEM((2 * stages, rows, depth), BF16), VMEM((stages, rows, depth), BF16),
        VMEM((stages + 1, rows, depth), BF16),
        DMA((stages,)), DMA((stages,)), DMA((stages,)), DMA((stages + 1,)),
    ]


def exchange(axis, size, slots, send_sem, recv_sem):
    me = lax.axis_index(axis)

    def copy_to(other, slot):
        return remote(
            slots.at[slot], slots.at[slot], send_sem.at[other], recv_sem.at[slot], **{axis: other}
        )

    def start(step, carry):
        copy_to(lax.rem(me + step, size), me).start()
        return carry

    def wait(step, carry):
        other = lax.rem(me + step, size)
        copy_to(other, other).wait_recv()
        copy_to(other, me).wait_send()
        return carry

    lax.fori_loop(1, size, start, 0)
    return lambda: lax.fori_loop(1, size, wait, 0)


def piece_height(height, parts):
    return -(-height // (16 * parts)) * 16


class RowSum:
    def __init__(self, parts, piece, arrive, send_sem, recv_sem):
        self.parts, self.piece, self.arrive = parts, piece, arrive
        self.send_sem, self.recv_sem = send_sem, recv_sem
        self.row = lax.axis_index("dp")

    def copy(self, other, source):
        return remote(
            self.piece.at[other], self.arrive.at[source],
            self.send_sem.at[other], self.recv_sem.at[source], dp=other,
        )

    def others(self, act, start):
        return lax.fori_loop(
            1, self.parts, lambda step, carry: act(lax.rem(self.row + step, self.parts), carry), start
        )

    def start(self, total):
        high = self.piece.shape[1]
        for part in range(self.parts):
            self.piece[part] = total[part * high : (part + 1) * high, :].astype(BF16)

        def send(other, carry):
            self.copy(other, self.row).start()
            return carry

        self.others(send, 0)

    def reduce(self):
        def add(other, so_far):
            self.copy(other, other).wait_recv()
            self.copy(other, self.row).wait_send()
            return so_far + self.arrive[other].astype(F32)

        return self.others(add, self.piece[self.row].astype(F32)).astype(BF16)


def rowsum_shapes(parts, high, depth):
    return [
        VMEM((parts, high, depth), BF16), VMEM((parts, high, depth), BF16), DMA((parts,)), DMA((parts,)),
    ]


def column(row):
    return jnp.broadcast_to(row, (128, row.shape[1])).T[:, :1]


def piece_rows(width, parts):
    return min(rows for rows in range(8, width + 1, 8) if width % rows == 0 and width // rows <= parts)


class WeightSpread:
    def __init__(self, stages, parts, buffer, sems):
        self.stages, self.parts, self.buffer = stages, parts, buffer
        self.line_send, self.line_recv, self.row_send, self.row_recv, self.core_send, self.core_recv = sems
        self.count = buffer.shape[0]
        self.me, self.core, self.stage = place()
        self.partner = self.me + 1 - 2 * self.core
        self.row = lax.axis_index("dp")
        self.here = self.row < self.count
        self.slot = jnp.minimum(self.row, self.count - 1)
        self.gather = LineGather(stages, buffer.at[self.slot], self.line_send, self.line_recv)

    def row_copy(self, other, source, far):
        block = 2 * far + self.core
        return remote(
            self.buffer.at[source, block], self.buffer.at[source, block],
            self.row_send.at[other, far], self.row_recv.at[source, far], dp=other,
        )

    def core_copy(self, source, far, core):
        block = 2 * far + core
        return remote(
            self.buffer.at[source, block], self.buffer.at[source, block],
            self.core_send.at[source, far], self.core_recv.at[source, far], tensor=self.partner,
        )

    def rows_and_stages(self, act):
        def body(index, carry):
            act(lax.div(index, self.stages) + 1, lax.rem(index, self.stages))
            return carry

        lax.fori_loop(0, (self.parts - 1) * self.stages, body, 0)

    def to_other(self, step, far):
        self.row_copy(lax.rem(self.row + step, self.parts), self.slot, far).start()

    def run(self):
        @pl.when(self.here)
        def _():
            self.gather.run(lambda block: None)
            self.rows_and_stages(self.to_other)

    def pieces(self, act):
        def body(index, carry):
            source, far = lax.div(index, self.stages), lax.rem(index, self.stages)
            pl.when(source != self.row)(lambda: act(source, far))
            return carry

        lax.fori_loop(0, self.count * self.stages, body, 0)

    def pass_on(self):
        def act(source, far):
            self.row_copy(self.row, source, far).wait_recv()
            self.core_copy(source, far, self.core).start()

        self.pieces(act)

    def finish(self):
        @pl.when(self.here)
        def _():
            self.gather.finish()
            self.rows_and_stages(
                lambda step, far: self.row_copy(
                    lax.rem(self.row + step, self.parts), self.slot, far
                ).wait_send()
            )

        def act(source, far):
            self.core_copy(source, far, 1 - self.core).wait_recv()
            self.core_copy(source, far, self.core).wait_send()

        self.pieces(act)


def project_kernel(
    stages, parts, tok_hbm, g1_ref, b1_ref, bo_ref, g2_ref, b2_ref, bf2_ref, bf1_ref, bq_ref, bv_ref, wo_hbm, wq_hbm, wk_hbm, wv_hbm, ids_ref,
    norm_hbm, q_hbm, k_hbm, v_hbm, wo_out, vec_ref, span_ref, idr_ref, ido_ref,
    wo_all, line_send, line_recv, row_send, row_recv, core_send, core_recv, tok, norm, q_ref, k_ref, v_ref, weight, send_sem, recv_sem, out_sem, load_sem,
):
    me, _, _ = place()
    width, rows = wq_hbm.shape[0], tok.shape[0]
    loads = loading(
        load_sem,
        ((tok_hbm, tok), (wq_hbm, weight.at[0]), (wk_hbm, weight.at[1]), (wv_hbm, weight.at[2])),
    )
    spread = WeightSpread(
        stages, parts, wo_all, (line_send, line_recv, row_send, row_recv, core_send, core_recv)
    )
    high = wo_all.shape[2]
    own_piece = pltpu.make_async_copy(
        wo_hbm.at[pl.ds(pl.multiple_of(spread.slot * high, high), high)],
        wo_all.at[spread.slot, me], load_sem.at[4],
    )
    pl.when(spread.here)(own_piece.start)
    vec_ref[...] = jnp.zeros_like(vec_ref)
    for index, ref in enumerate(
        (g1_ref, b1_ref, bo_ref, g2_ref, b2_ref, bf2_ref, bf1_ref, bq_ref, bv_ref)
    ):
        vec_ref[index : index + 1, 0 : ref.shape[0]] = ref[...].astype(F32)[None, :]
    greet_line(stages, parts)
    loads[0].wait()
    normed, _ = normalize(tok[...].astype(F32))
    norm[me] = (normed * vec_ref[0:1, :] + vec_ref[1:2, :]).astype(BF16)
    gather = LineGather(stages, norm, send_sem, recv_sem)
    gather.start()

    @pl.when(spread.here)
    def _():
        own_piece.wait()
        spread.gather.start()

    ids = ids_ref[...].astype(F32)
    idr_ref[...] = ids
    ido_ref[...] = idr_ref[:, pl.ds(pl.multiple_of(me * rows, rows), rows)]
    for block in range(ids.shape[1] // BLOCK):
        first = ids[:, block * BLOCK : block * BLOCK + 1]
        last = ids[:, (block + 1) * BLOCK - 1 : (block + 1) * BLOCK]
        begin = jnp.sum(jnp.where(ids > first, 1.0, 0.0))
        end = jnp.sum(jnp.where(ids >= jnp.maximum(last, 1.0), 1.0, 0.0))
        span_ref[0, block] = lax.div(begin.astype(jnp.int32), BLOCK)
        span_ref[1, block] = lax.div(end.astype(jnp.int32) + (BLOCK - 1), BLOCK)
    for load in loads[1:]:
        load.wait()

    def keep(block):
        return [
            pltpu.make_async_copy(src.at[block], dst.at[block], out_sem.at[index, block])
            for index, (src, dst) in enumerate(
                ((norm, norm_hbm), (q_ref, q_hbm), (k_ref, k_hbm), (v_ref, v_hbm))
            )
        ]

    def compute(block):
        q_ref[block] = (nt(norm[block], weight[0]) + vec_ref[7:8, :width]).astype(BF16)
        k_ref[block] = nt(norm[block], weight[1]).astype(BF16)
        v_ref[block] = (nt(norm[block], weight[2]) + vec_ref[8:9, :width]).astype(BF16)
        for copy in keep(block):
            copy.start()

    spread.run()
    gather.run(compute)
    spread.pass_on()
    gather.finish()
    spread.finish()
    out_copy = pltpu.make_async_copy(wo_all, wo_out, load_sem.at[5])
    out_copy.start()

    def kept(block, carry):
        for copy in keep(block):
            copy.wait()
        return carry

    lax.fori_loop(0, 2 * stages, kept, 0)
    out_copy.wait()


def project(tokens, vectors, wo, wq, wk, wv, ids, devices, parts):
    rows, depth = tokens.shape
    width, length = wq.shape[1], ids.shape[1]
    stages = devices // 2
    high = piece_rows(width, parts)
    head = jax.ShapeDtypeStruct((devices, rows, width), BF16)
    pieces = (width // high, devices, high, depth)
    return pl.pallas_call(
        functools.partial(project_kernel, stages, parts),
        name="project",
        out_shape=(
            jax.ShapeDtypeStruct((devices, rows, depth), BF16), head, head, head,
            jax.ShapeDtypeStruct(pieces, BF16), jax.ShapeDtypeStruct((16, depth), F32),
            jax.ShapeDtypeStruct((2, length // BLOCK), jnp.int32),
            jax.ShapeDtypeStruct((1, length), F32), jax.ShapeDtypeStruct((1, rows), F32),
        ),
        in_specs=[HBM] + [VSPEC] * 9 + [HBM, HBM, HBM, HBM, VSPEC],
        out_specs=(HBM, HBM, HBM, HBM, HBM, VSPEC, SSPEC, VSPEC, VSPEC),
        scratch_shapes=[
            VMEM(pieces, BF16), DMA((devices, 3)), DMA((devices,)),
            *[DMA((parts, stages))] * 4,
            VMEM((rows, depth), BF16), VMEM((devices, rows, depth), BF16),
            *[VMEM((devices, rows, width), BF16)] * 3, VMEM((3, width, depth), BF16),
            DMA((devices, 3)), DMA((devices,)), DMA((4, devices)), DMA((6,)),
        ],
        compiler_params=pltpu.CompilerParams(
            collective_id=0, has_side_effects=True, vmem_limit_bytes=VMEM_ALL
        ),
    )(tokens, *vectors, wo, wq.T, wk.T, wv.T, ids)


def lanes_of(head, width):
    lane = lax.broadcasted_iota(jnp.int32, (1, width), 1)
    return (lane >= head * HD) & (lane < (head + 1) * HD)


def fill_columns(row_ref, column_ref):
    for block in range(row_ref.shape[1] // BLOCK):
        at = pl.ds(block * BLOCK, BLOCK)
        column_ref[at, :] = column(row_ref[:, at])


def head_rows(head, width):
    row = lax.broadcasted_iota(jnp.int32, (width, 1), 0)
    return (row >= head * HD) & (row < (head + 1) * HD)


def side_by_side(block_t, heads):
    width = block_t.shape[0]
    zero = jnp.zeros_like(block_t)
    return jnp.concatenate([jnp.where(head_rows(h, width), block_t, zero) for h in range(heads)], axis=1)


def stacked(block, heads):
    width = block.shape[1]
    zero = jnp.zeros_like(block)
    return jnp.concatenate([jnp.where(lanes_of(h, width), block, zero) for h in range(heads)], axis=0)


def repeat_lanes(row, heads):
    return jnp.concatenate([row] * heads, axis=1)


def attend_kernel(
    heads, span_ref, q_hbm, k_hbm, v_hbm, idr_ref, o_ref, log_ref,
    q_ref, k_ref, v_ref, load_sem, idc_ref, vt_ref, acc_ref,
):
    length, width = q_ref.shape
    scale = HD ** (-0.5) * LOG2E
    loads = loading(load_sem, ((v_hbm, v_ref), (q_hbm, q_ref), (k_hbm, k_ref)))
    fill_columns(idr_ref, idc_ref)
    for load in loads:
        load.wait()

    def turn(block, total):
        at = pl.ds(pl.multiple_of(block * BLOCK, BLOCK), BLOCK)
        value = v_ref[at, :].astype(F32)
        vt_ref[block] = value.T.astype(BF16)
        return total + jnp.sum(value, axis=0, keepdims=True)

    mean_value = lax.fori_loop(0, length // BLOCK, turn, jnp.zeros((1, width), F32)) * (1.0 / length)

    def per_block(block, carry):
        at = pl.ds(pl.multiple_of(block * BLOCK, BLOCK), BLOCK)
        query = side_by_side(q_ref[at, :].astype(F32).T.astype(BF16), heads)
        id_row = idr_ref[:, at]
        id_rows = repeat_lanes(id_row, heads)
        acc_ref[...] = jnp.zeros_like(acc_ref)

        def per_key(other, state):
            top, total = state
            keys_at = pl.ds(pl.multiple_of(other * BLOCK, BLOCK), BLOCK)
            id_col = idc_ref[keys_at, :]
            allowed = (id_col == id_rows) & (id_col > 0)
            scores = jnp.where(allowed, nn(k_ref[keys_at, :], query) * scale, NEG_FILL)
            new_top = jnp.maximum(top, jnp.max(scores, axis=0, keepdims=True))
            weight = jnp.exp2(scores - new_top)
            shrink = jnp.exp2(top - new_top)
            total = total * shrink + jnp.sum(weight, axis=0, keepdims=True)
            acc_ref[...] = acc_ref[...] * shrink + nn(vt_ref[other], weight.astype(BF16))
            return new_top, total

        top, total = lax.fori_loop(
            span_ref[0, block], span_ref[1, block], per_key,
            (jnp.full((1, heads * BLOCK), NEG_FILL, F32), jnp.zeros((1, heads * BLOCK), F32)),
        )
        scaled = acc_ref[...] / total
        logs = jnp.where(id_rows == 0, 0.0, top + jnp.log2(total))
        result = jnp.zeros((width, BLOCK), F32)
        for h in range(heads):
            here = slice(h * BLOCK, (h + 1) * BLOCK)
            result = jnp.where(head_rows(h, width), scaled[:, here], result)
            log_ref[h : h + 1, at] = logs[:, here]
        o_ref[at, :] = jnp.where(idc_ref[at, :] == 0, mean_value, result.T).astype(BF16)
        return carry

    lax.fori_loop(0, length // BLOCK, per_block, 0)


def attend(q, k, v, span, id_row):
    length, width = q.shape
    heads = width // HD
    return pl.pallas_call(
        functools.partial(attend_kernel, heads),
        name="attend",
        out_shape=(
            jax.ShapeDtypeStruct((length, width), BF16),
            jax.ShapeDtypeStruct((heads, length), F32),
        ),
        in_specs=[SSPEC, HBM, HBM, HBM, VSPEC],
        out_specs=(VSPEC,) * 2,
        scratch_shapes=[
            *[VMEM((length, width), BF16)] * 3, DMA((3,)),
            VMEM((length, 1), F32), VMEM((length // BLOCK, width, BLOCK), BF16),
            VMEM((width, heads * BLOCK), F32),
        ],
        compiler_params=pltpu.CompilerParams(vmem_limit_bytes=VMEM_ALL),
    )(span, q, k, v, id_row)


def attend_back_kernel(
    heads, span_ref, q_hbm, k_hbm, v_hbm, idr_ref, o_hbm, log_ref, g_hbm,
    out_ref, q_ref, k_ref, v_ref, o_ref, g_ref, load_sem,
    idc_ref, dq_ref, dk_ref, dv_ref, q_side, q_stack, g_side, g_stack, row_ref, log_side,
):
    length, width = q_ref.shape
    score_scale = HD ** (-0.5)
    loads = loading(
        load_sem, ((q_hbm, q_ref), (g_hbm, g_ref), (o_hbm, o_ref), (k_hbm, k_ref), (v_hbm, v_ref))
    )
    dq_ref[...] = jnp.zeros_like(dq_ref)
    fill_columns(idr_ref, idc_ref)
    for load in loads:
        load.wait()

    def prepare(block, pad):
        at = pl.ds(pl.multiple_of(block * BLOCK, BLOCK), BLOCK)
        query, grad = q_ref[at, :], g_ref[at, :]
        wide = grad.astype(F32)
        grad_t = wide.T
        product = (wide * o_ref[at, :].astype(F32)).T
        q_side[block] = side_by_side(query.astype(F32).T.astype(BF16), heads)
        g_side[block] = side_by_side(grad_t.astype(BF16), heads)
        q_stack[block] = stacked(query, heads)
        g_stack[block] = stacked(grad, heads)
        for h in range(heads):
            here = slice(h * BLOCK, (h + 1) * BLOCK)
            row_ref[block, :, here] = jnp.sum(
                jnp.where(head_rows(h, width), product, 0.0), axis=0, keepdims=True
            )
            log_side[block, :, here] = log_ref[h : h + 1, at]
        return pad + jnp.sum(jnp.where(idc_ref[at, :] == 0, wide, 0.0), axis=0, keepdims=True)

    pad = lax.fori_loop(0, length // BLOCK, prepare, jnp.zeros((1, width), F32)) * (1.0 / length)

    def per_key(block, carry):
        at = pl.ds(pl.multiple_of(block * BLOCK, BLOCK), BLOCK)
        key, value, id_col = k_ref[at, :], v_ref[at, :], idc_ref[at, :]
        key_side = side_by_side(key.astype(F32).T.astype(BF16), heads)
        real = id_col > 0
        dk_ref[...] = jnp.zeros_like(dk_ref)
        dv_ref[...] = jnp.zeros_like(dv_ref)

        def per_query(other, inner):
            query_at = pl.ds(pl.multiple_of(other * BLOCK, BLOCK), BLOCK)
            allowed = (id_col == repeat_lanes(idr_ref[:, query_at], heads)) & real
            scores = nn(key, q_side[other]) * (score_scale * LOG2E) - log_side[other]
            prob = jnp.exp2(jnp.where(allowed, scores, NEG_FILL))
            dv_ref[...] += nn(prob.astype(BF16), g_stack[other])
            back = (prob * (nn(value, g_side[other]) - row_ref[other])).astype(BF16)
            dk_ref[...] += nn(back, q_stack[other])
            back_rows = jnp.concatenate(
                [back[:, h * BLOCK : (h + 1) * BLOCK] for h in range(heads)], axis=0
            )
            dq_ref[other] += nn(key_side, back_rows)
            return inner

        lax.fori_loop(span_ref[0, block], span_ref[1, block], per_query, 0)
        out_ref[at, width : 2 * width] = (dk_ref[...] * score_scale).astype(BF16)
        out_ref[at, 2 * width :] = (dv_ref[...] + pad).astype(BF16)
        return carry

    lax.fori_loop(0, length // BLOCK, per_key, 0)

    def settle(block, carry):
        at = pl.ds(pl.multiple_of(block * BLOCK, BLOCK), BLOCK)
        out_ref[at, :width] = (dq_ref[block].T * score_scale).astype(BF16)
        return carry

    lax.fori_loop(0, length // BLOCK, settle, 0)


def attend_back(q, k, v, span, id_row, o, log_total, grad):
    length, width = q.shape
    heads = width // HD
    blocks = length // BLOCK
    whole = VMEM((length, width), BF16)
    side, stack = VMEM((blocks, width, heads * BLOCK), BF16), VMEM((blocks, heads * BLOCK, width), BF16)
    line = VMEM((blocks, 1, heads * BLOCK), F32)
    return pl.pallas_call(
        functools.partial(attend_back_kernel, heads),
        name="attend_back",
        out_shape=jax.ShapeDtypeStruct((length, 3 * width), BF16),
        in_specs=[SSPEC, HBM, HBM, HBM, VSPEC, HBM, VSPEC, HBM],
        out_specs=VSPEC,
        scratch_shapes=[
            whole, whole, whole, whole, whole, DMA((5,)),
            VMEM((length, 1), F32), VMEM((blocks, width, BLOCK), F32), VMEM((BLOCK, width), F32),
            VMEM((BLOCK, width), F32), side, stack, side, stack, line, line,
        ],
        compiler_params=pltpu.CompilerParams(vmem_limit_bytes=VMEM_ALL),
    )(span, q, k, v, id_row, o, log_total, grad)


def gelu_pair(u):
    slope = (2.0 / jnp.pi) ** 0.5
    bent = jnp.tanh(slope * (u + 0.044715 * u * u * u))
    half = 0.5 * (1.0 + bent)
    return u * half, half + 0.5 * u * (1.0 - bent * bent) * slope * (1.0 + 3 * 0.044715 * u * u)


def middle_kernel(
    stages, parts, att_hbm, wo_hbm, fc1_hbm, fc2_hbm, tok_hbm, top_hbm, ids_ref, vec_ref,
    out_ref, gres_ref, gatt_ref, fc_ref, small_ref,
    wo, fc1, fc2, tok, top, load_sem,
    held, held_send, held_recv, norm_all, norm_send, norm_recv, top_all, top_send, top_recv,
    hidden, slope, grad_pre,
    br_part, br_cross, br_lane, br_s0, br_s1, br_s2, br_s3,
    gn_part, gn_cross, gn_lane, gn_s0, gn_s1, gn_s2, gn_s3,
    resid, total, acc, piece, arrive, piece_send, piece_recv, back, back_send, back_recv,
):
    me, _, _ = place()
    devices = 2 * stages
    rows, depth = tok_hbm.shape
    high = wo_hbm.shape[2]
    units = fc1_hbm.shape[0]
    second = -(-units // 16) * 16
    loads = loading(
        load_sem,
        ((tok_hbm, tok), (top_hbm, top), (fc1_hbm, fc1), (fc2_hbm, fc2), (att_hbm.at[me], held.at[me]),
         *((wo_hbm.at[index], wo.at[:, pl.ds(index * high, high)]) for index in range(wo_hbm.shape[0]))),
    )
    greet_peers((("tensor", devices), ("dp", parts)))

    def held_copy(other, source):
        return remote(
            att_hbm.at[other], held.at[source], held_send.at[other], held_recv.at[source], tensor=other
        )

    def send_held(step, carry):
        held_copy(lax.rem(me + step, devices), me).start()
        return carry

    lax.fori_loop(1, devices, send_held, 0)
    gather2 = LineGather(stages, norm_all, norm_send, norm_recv)
    gather3 = LineGather(stages, top_all, top_send, top_recv)
    branch = LineScatter(stages, br_part, br_cross, br_lane, (br_s0, br_s1, br_s2, br_s3))
    gnorm = LineScatter(stages, gn_part, gn_cross, gn_lane, (gn_s0, gn_s1, gn_s2, gn_s3))

    mask = column(jnp.where(ids_ref[...] > 0, 1.0, 0.0))
    acc[...] = jnp.zeros_like(acc)
    small_ref[...] = jnp.zeros_like(small_ref)
    loads[0].wait()
    loads[1].wait()
    top_own = top[...].astype(F32) * mask
    top_all[me] = top_own.astype(BF16)
    small_ref[5:6, :] = jnp.sum(top_own, axis=0, keepdims=True)
    resid[...] = tok[...].astype(F32) + vec_ref[2:3, :]
    for load in loads[4:]:
        load.wait()
    resid[...] += nn(held[me], wo[me])

    def add_held(step, carry):
        other = lax.rem(me + devices - step, devices)
        held_copy(other, other).wait_recv()
        resid[...] += nn(held[other], wo[other])
        return carry

    lax.fori_loop(1, devices, add_held, 0)
    normed, _ = normalize(resid[...])
    norm_all[me] = (normed * vec_ref[3:4, :] + vec_ref[4:5, :]).astype(BF16)
    gather2.start()
    loads[2].wait()
    loads[3].wait()

    def forward(block):
        pre_act = nt(norm_all[block], fc1[...]) + vec_ref[6:7, 0:units]
        value, slope_now = gelu_pair(pre_act)
        hidden[block] = value.astype(BF16)
        slope[block] = slope_now.astype(BF16)
        branch.put(block, nn(hidden[block], fc2[...]))

    at_end = gather2.at_end()
    gather2.run(forward, lambda: pl.when(at_end)(gather3.start_inward))
    pl.when(jnp.logical_not(at_end))(gather3.start_inward)
    gather3.start_outward()
    pl.when(at_end)(lambda: branch.steps(0, stages - 1))

    def backward(block):
        grad = nt(top_all[block], fc2[...]) * slope[block].astype(F32)
        low = grad.astype(BF16)
        grad_pre[block] = low
        small_ref[7:8, 0:units] += jnp.sum(low.astype(F32), axis=0, keepdims=True)
        gnorm.put(block, nn(grad_pre[block], fc1[...]))
        acc[0:units, :] += tn(grad_pre[block], norm_all[block])
        acc[second : second + units, :] += tn(hidden[block], top_all[block])

    gather3.run(backward)
    gnorm.step(stages - 1)
    sums = RowSum(parts, piece, arrive, piece_send, piece_recv)
    sums.start(acc)

    def both(index, carry):
        reach = stages - 1 - index
        pl.when(jnp.logical_not(at_end))(lambda: branch.step(reach))
        gnorm.step(reach)
        return carry

    lax.fori_loop(1, stages - 1, both, 0)
    branch.own(total)
    out_ref[...] = (mask * (resid[...] + total[...] + vec_ref[5:6, :])).astype(BF16)

    gnorm.own(total)
    grad = total[...]
    normed, scale = normalize(resid[...])
    small_ref[2:3, :] = jnp.sum(grad * normed, axis=0, keepdims=True)
    small_ref[3:4, :] = jnp.sum(grad, axis=0, keepdims=True)
    inner = grad * vec_ref[3:4, :]
    inner_mean = jnp.mean(inner, axis=-1, keepdims=True)
    inner_proj = jnp.mean(inner * normed, axis=-1, keepdims=True)
    grad_resid = top[...].astype(F32) * mask + scale * (inner - inner_mean - normed * inner_proj)
    gres_ref[...] = grad_resid
    tok[...] = grad_resid.astype(BF16)
    small_ref[4:5, :] = jnp.sum(grad_resid, axis=0, keepdims=True)

    def back_copy(other, source):
        return remote(
            back.at[other], gatt_ref.at[source], back_send.at[other], back_recv.at[source], tensor=other
        )

    def send_back(step, carry):
        other = lax.rem(me + step, devices)
        back[other] = nt(tok[...], wo[other]).astype(BF16)
        back_copy(other, me).start()
        return carry

    lax.fori_loop(1, devices, send_back, 0)
    gatt_ref[me] = nt(tok[...], wo[me]).astype(BF16)

    fc_ref[...] = sums.reduce()

    def settle(step, carry):
        other = lax.rem(me + devices - step, devices)
        back_copy(other, other).wait_recv()
        back_copy(other, me).wait_send()
        held_copy(other, me).wait_send()
        return carry

    lax.fori_loop(1, devices, settle, 0)
    gather2.finish()
    gather3.finish()
    branch.finish()
    gnorm.finish()


def middle(att, wo, fc1, fc2, tokens, out_grad, ids, vectors, parts):
    devices, rows, width = att.shape
    depth, units = fc1.shape
    stages = devices // 2
    high = piece_height(2 * (-(-units // 16) * 16), parts)
    return pl.pallas_call(
        functools.partial(middle_kernel, stages, parts),
        name="middle",
        out_shape=(
            jax.ShapeDtypeStruct((rows, depth), BF16),
            jax.ShapeDtypeStruct((rows, depth), F32),
            jax.ShapeDtypeStruct((devices, rows, width), BF16),
            jax.ShapeDtypeStruct((high, depth), BF16),
            jax.ShapeDtypeStruct((8, depth), F32),
        ),
        in_specs=[HBM] * 6 + [VSPEC] * 2,
        out_specs=(VSPEC,) * 5,
        scratch_shapes=[
            VMEM((devices, width, depth), BF16), VMEM((units, depth), BF16), VMEM((units, depth), BF16),
            VMEM((rows, depth), BF16), VMEM((rows, depth), BF16), DMA((5 + wo.shape[0],)),
            VMEM((devices, rows, width), BF16), DMA((devices,)), DMA((devices,)),
            VMEM((devices, rows, depth), BF16), DMA((devices, 3)), DMA((devices,)),
            VMEM((devices, rows, depth), BF16), DMA((devices, 3)), DMA((devices,)),
            VMEM((devices, rows, units), BF16), VMEM((devices, rows, units), BF16),
            VMEM((devices, rows, units), BF16),
            *scatter_shapes(stages, rows, depth), *scatter_shapes(stages, rows, depth),
            VMEM((rows, depth), F32), VMEM((rows, depth), F32),
            VMEM((parts * high, depth), F32), *rowsum_shapes(parts, high, depth),
            VMEM((devices, rows, width), BF16), DMA((devices,)), DMA((devices,)),
        ],
        compiler_params=pltpu.CompilerParams(
            collective_id=2, has_side_effects=True, vmem_limit_bytes=VMEM_ALL
        ),
    )(
        att, wo, fc1.T, fc2, tokens, out_grad, ids, vectors,
    )


def close_kernel(
    stages, parts, dx_hbm, wq_hbm, wk_hbm, wv_hbm, norm_hbm, att_hbm, tok_hbm, vec_ref, resid_hbm,
    small_ref, fc_hbm,
    gtok_ref, gw_hbm, go_hbm, gfc_hbm, gsmall_ref,
    dx_ref, weight, norm, att_ref, tok_ref, resid_ref, load_sem, gatt_all, gatt_send, gatt_recv,
    partial, cross, lane, cross_send, cross_recv, lane_send, lane_recv,
    total, acc, acc_o, w_piece, w_arrive, w_send, w_recv, o_piece, o_arrive, o_send, o_recv,
    w_all, o_all, fc_all, wa_send, wa_recv, oa_send, oa_recv, fa_send, fa_recv, out_sem,
    slots_t, slots_d, st_send, st_recv, sd_send, sd_recv,
):
    me, _, _ = place()
    row = lax.axis_index("dp")
    devices = 2 * stages
    wide, width = dx_ref.shape[2], att_ref.shape[2]
    loads = loading(
        load_sem,
        ((resid_hbm, resid_ref), (fc_hbm, fc_all.at[row]), (dx_hbm, dx_ref),
         *((src, weight.at[pl.ds(index * width, width)]) for index, src in enumerate((wq_hbm, wk_hbm, wv_hbm))),
         (norm_hbm, norm), (att_hbm, att_ref), (tok_hbm, tok_ref)),
    )
    greet_peers((("tensor", devices), ("dp", parts)))
    loads[0].wait()
    gatt_all[me] = resid_ref[...].astype(BF16)
    gather = LineGather(stages, gatt_all, gatt_send, gatt_recv)
    gather.start()
    loads[1].wait()
    wait_fc = exchange("dp", parts, fc_all, fa_send, fa_recv)
    for load in loads[2:6]:
        load.wait()
    scatter = LineScatter(
        stages, partial, cross, lane, (cross_send, cross_recv, lane_send, lane_recv)
    )
    scatter.produce(lambda block: nn(dx_ref[block], weight[...]))
    scatter.step(stages - 1)

    acc[...] = jnp.zeros_like(acc)
    acc_o[...] = jnp.zeros_like(acc_o)
    for load in loads[6:]:
        load.wait()

    def weight_block(block, bias):
        grad = dx_ref[block]
        acc[0:wide, :] += tn(grad, norm[block])
        return bias + jnp.sum(grad.astype(F32), axis=0, keepdims=True)

    bias = lax.fori_loop(0, devices, weight_block, jnp.zeros((1, wide), F32))
    w_sum = RowSum(parts, w_piece, w_arrive, w_send, w_recv)
    w_sum.start(acc)

    def weight_o(block):
        acc_o[0:width, :] += tn(att_ref[block], gatt_all[block])

    gather.use_own(weight_o)

    def both(reach, carry):
        gather.relay(reach)
        pl.when(reach < stages - 1)(lambda: scatter.step(stages - 1 - reach))
        gather.use(reach, weight_o)
        return carry

    lax.fori_loop(1, stages - 1, both, 0)
    w_all[row] = w_sum.reduce()
    wait_w = exchange("dp", parts, w_all, wa_send, wa_recv)
    lax.fori_loop(stages - 1, stages, both, 0)
    o_sum = RowSum(parts, o_piece, o_arrive, o_send, o_recv)
    o_sum.start(acc_o)
    o_all[row] = o_sum.reduce()
    wait_o = exchange("dp", parts, o_all, oa_send, oa_recv)

    scatter.own(total)
    grad = total[...]
    normed, scale = normalize(tok_ref[...].astype(F32))
    slots_t[me] = small_ref[...]
    slots_t[me, 0:1, :] = jnp.sum(grad * normed, axis=0, keepdims=True)
    slots_t[me, 1:2, :] = jnp.sum(grad, axis=0, keepdims=True)
    slots_t[me, 6:7, 0:wide] = bias
    wait_small = exchange("tensor", devices, slots_t, st_send, st_recv)
    inner = grad * vec_ref[0:1, :]
    inner_mean = jnp.mean(inner, axis=-1, keepdims=True)
    inner_proj = jnp.mean(inner * normed, axis=-1, keepdims=True)
    gtok_ref[...] = resid_ref[...] + scale * (inner - inner_mean - normed * inner_proj)
    wait_small()
    sums = lax.fori_loop(
        1, devices, lambda slot, so_far: so_far + slots_t[slot], slots_t[0]
    )
    line = lax.broadcasted_iota(jnp.int32, sums.shape, 0)
    slots_d[row] = jnp.where(line < 6, sums, slots_t[me])
    wait_last = exchange("dp", parts, slots_d, sd_send, sd_recv)
    outs = []
    for index, (wait, src, dst) in enumerate(
        ((wait_fc, fc_all, gfc_hbm), (wait_w, w_all, gw_hbm), (wait_o, o_all, go_hbm))
    ):
        wait()
        out = pltpu.make_async_copy(src, dst, out_sem.at[index])
        out.start()
        outs.append(out)
    wait_last()
    gsmall_ref[...] = lax.fori_loop(
        1, parts, lambda slot, so_far: so_far + slots_d[slot], slots_d[0]
    )
    gather.finish()
    scatter.finish()
    for out in outs:
        out.wait()


def close(dx, wq, wk, wv, norm, att, tokens, vectors, resid, small, fc, parts):
    devices, rows, wide = dx.shape
    depth = tokens.shape[1]
    stages = devices // 2
    width = wide // 3
    w_high, o_high, fc_high = piece_height(wide, parts), piece_height(width, parts), fc.shape[0]
    pieces = [(parts, high, depth) for high in (w_high, o_high, fc_high)]
    return pl.pallas_call(
        functools.partial(close_kernel, stages, parts),
        name="close",
        out_shape=(
            jax.ShapeDtypeStruct((rows, depth), F32),
            *(jax.ShapeDtypeStruct(shape, BF16) for shape in pieces),
            jax.ShapeDtypeStruct(small.shape, F32),
        ),
        in_specs=[HBM] * 7 + [VSPEC, HBM, VSPEC, HBM],
        out_specs=(VSPEC, HBM, HBM, HBM, VSPEC),
        scratch_shapes=[
            VMEM((devices, rows, wide), BF16), VMEM((wide, depth), BF16),
            VMEM((devices, rows, depth), BF16), VMEM((devices, rows, width), BF16),
            VMEM((rows, depth), BF16), VMEM((rows, depth), F32), DMA((9,)),
            VMEM((devices, rows, depth), BF16), DMA((devices, 3)), DMA((devices,)),
            *scatter_shapes(stages, rows, depth),
            VMEM((rows, depth), F32), VMEM((parts * w_high, depth), F32),
            VMEM((parts * o_high, depth), F32),
            *rowsum_shapes(parts, w_high, depth), *rowsum_shapes(parts, o_high, depth),
            *(VMEM(shape, BF16) for shape in pieces), *[DMA((parts,))] * 6, DMA((3,)),
            VMEM((devices,) + small.shape, F32), VMEM((parts,) + small.shape, F32),
            DMA((devices,)), DMA((devices,)), DMA((parts,)), DMA((parts,)),
        ],
        compiler_params=pltpu.CompilerParams(
            collective_id=1, has_side_effects=True, vmem_limit_bytes=VMEM_ALL
        ),
    )(dx, wq.T, wk.T, wv.T, norm, att, tokens, vectors, resid, small, fc)


def on_device(
    devices, parts, tokens, picture_ids, ln1_gain, ln1_bias, q_weight, q_bias, k_weight, v_weight, v_bias,
    o_weight, o_bias, ln2_gain, ln2_bias, fc1_weight, fc1_bias, fc2_weight, fc2_bias, out_grad,
):
    own_count, depth = tokens.shape
    hidden_local = fc1_weight.shape[1]
    width = q_weight.shape[1]
    norm1_all, q, k, v, o_all, vectors, span, id_row, own_ids = project(
        tokens,
        (ln1_gain, ln1_bias, o_bias, ln2_gain, ln2_bias, fc2_bias, fc1_bias, q_bias, v_bias),
        o_weight, q_weight, k_weight, v_weight, picture_ids[None, :], devices, parts,
    )
    q, k, v = (item.reshape(LEN, width) for item in (q, k, v))
    attended, log_total = attend(q, k, v, span, id_row)
    heads_first = attended.reshape(devices, own_count, width)
    output, grad_residual, grad_attended, fc_piece, small = middle(
        heads_first, o_all, fc1_weight, fc2_weight, tokens, out_grad,
        own_ids, vectors, parts,
    )
    dqkv = attend_back(
        q, k, v, span, id_row, attended, log_total, grad_attended.reshape(LEN, width)
    )
    grad_tokens, grad_w, grad_o, grad_fc, sums = close(
        dqkv.reshape(devices, own_count, 3 * width), q_weight, k_weight, v_weight, norm1_all,
        heads_first, tokens, vectors, grad_residual, small, fc_piece, parts,
    )
    grad_w, grad_o, grad_fc = (item.reshape(-1, depth) for item in (grad_w, grad_o, grad_fc))
    second = -(-hidden_local // 16) * 16
    return (
        output, grad_tokens, sums[0], sums[1],
        grad_w[:width].astype(F32).T, sums[6, :width], grad_w[width : 2 * width].astype(F32).T,
        grad_w[2 * width : 3 * width].astype(F32).T, sums[6, 2 * width : 3 * width],
        grad_o[:width].astype(F32), sums[4], sums[2], sums[3],
        grad_fc[:hidden_local].astype(F32).T, sums[7, :hidden_local],
        grad_fc[second : second + hidden_local].astype(F32), sums[5],
    )


def solution(mesh):
    rows, whole = P(("dp", "tensor"), None), P()
    columns, down, along = P(None, "tensor"), P("tensor", None), P("tensor")
    return jax.shard_map(
        functools.partial(on_device, mesh.shape["tensor"], mesh.shape["dp"]),
        mesh=mesh,
        in_specs=(
            rows, P("dp"), whole, whole, columns, along, columns, columns, along, down, whole,
            whole, whole, columns, along, down, whole, rows,
        ),
        out_specs=(
            rows, rows, whole, whole, columns, along, columns, columns, along, down, whole,
            whole, whole, columns, along, down, whole,
        ),
        check_vma=False,
    )
```

```python
import functools

import jax
import jax.numpy as jnp
from jax import lax
from jax.experimental import pallas as pl
from jax.experimental.pallas import tpu as pltpu
from jax.sharding import PartitionSpec as P

HD = 72
LEN = 2048
BLOCK = 256
NORM_EPS = 1e-06
NEG_FILL = -1e30
LOG2E = 1.4426950408889634
VMEM_ALL = 67043328
BF16 = jnp.bfloat16
F32 = jnp.float32
MESH = pl.DeviceIdType.MESH
VMEM = pltpu.VMEM
DMA = pltpu.SemaphoreType.DMA
VSPEC = pl.BlockSpec(memory_space=pltpu.VMEM)
SSPEC = pl.BlockSpec(memory_space=pltpu.SMEM)
HBM = pl.BlockSpec(memory_space=pltpu.HBM)


def nn(left, right):
    return lax.dot_general(left, right, (((1,), (0,)), ((), ())), preferred_element_type=F32)


def nt(left, right):
    return lax.dot_general(left, right, (((1,), (1,)), ((), ())), preferred_element_type=F32)


def tn(left, right):
    return lax.dot_general(left, right, (((0,), (0,)), ((), ())), preferred_element_type=F32)


def remote(src, dst, send_sem, recv_sem, **where):
    return pltpu.make_async_remote_copy(
        src_ref=src, dst_ref=dst, send_sem=send_sem, recv_sem=recv_sem,
        device_id=where, device_id_type=MESH,
    )


def loading(sems, pairs):
    copies = [
        pltpu.make_async_copy(src, dst, sems.at[index]) for index, (src, dst) in enumerate(pairs)
    ]
    for copy in copies:
        copy.start()
    return copies


def place():
    me = lax.axis_index("tensor")
    core = lax.rem(me, 2)
    return me, core, lax.div(me, 2)


def greet_peers(axes):
    barrier = pltpu.get_barrier_semaphore()
    for axis, size in axes:
        me = lax.axis_index(axis)

        def greet(step, carry):
            pl.semaphore_signal(
                barrier, inc=1, device_id={axis: lax.rem(me + step, size)}, device_id_type=MESH
            )
            return carry

        lax.fori_loop(1, size, greet, 0)
    pl.semaphore_wait(barrier, sum(size - 1 for _, size in axes))


def greet_line(stages, parts):
    me, core, stage = place()
    row = lax.axis_index("dp")
    barrier = pltpu.get_barrier_semaphore()

    def greet_row(step, carry):
        other = lax.rem(row + step, parts)
        pl.semaphore_signal(barrier, inc=1, device_id={"dp": other}, device_id_type=MESH)
        return carry

    lax.fori_loop(1, parts, greet_row, 0)
    has_left, has_right = stage > 0, stage < stages - 1

    def greet(other):
        pl.semaphore_signal(barrier, inc=1, device_id={"tensor": other}, device_id_type=MESH)

    greet(me + 1 - 2 * core)
    pl.when(has_left)(lambda: greet(me - 2))
    pl.when(has_right)(lambda: greet(me + 2))
    pl.semaphore_wait(barrier, parts + has_left.astype(jnp.int32) + has_right.astype(jnp.int32))


def normalize(values):
    average = jnp.mean(values, axis=-1, keepdims=True)
    centred = values - average
    variance = jnp.mean(centred * centred, axis=-1, keepdims=True)
    scale = lax.rsqrt(variance + NORM_EPS)
    return centred * scale, scale


class LineGather:
    def __init__(self, stages, buffer, send_sem, recv_sem):
        self.stages, self.buffer, self.send_sem, self.recv_sem = stages, buffer, send_sem, recv_sem
        self.me, self.core, self.stage = place()
        self.partner = self.me + 1 - 2 * self.core

    def copy(self, block, way, target):
        return remote(
            self.buffer.at[block], self.buffer.at[block],
            self.send_sem.at[block, way], self.recv_sem.at[block], tensor=target,
        )

    def each_copy(self, block, right, left, act):
        pl.when(right)(lambda: act(self.copy(block, 0, self.me + 2)))
        pl.when(left)(lambda: act(self.copy(block, 1, self.me - 2)))
        act(self.copy(block, 2, self.partner))

    def start(self):
        self.each_copy(
            self.me, self.stage < self.stages - 1, self.stage > 0, lambda copy: copy.start()
        )

    def start_inward(self):
        low = self.stage < self.stages // 2
        self.each_copy(self.me, low, jnp.logical_not(low), lambda copy: copy.start())

    def start_outward(self):
        low = self.stage < self.stages // 2
        pl.when(jnp.logical_not(low) & (self.stage < self.stages - 1))(
            lambda: self.copy(self.me, 0, self.me + 2).start()
        )
        pl.when(low & (self.stage > 0))(lambda: self.copy(self.me, 1, self.me - 2).start())

    def incoming(self, reach, side, core):
        far = jnp.where(side == 0, self.stage - reach, self.stage + reach)
        return (far >= 0) & (far < self.stages), 2 * far + core

    def arrive(self, block):
        self.copy(block, 2, self.partner).wait_recv()

    def ways(self, side):
        return (side == 0) & (self.stage < self.stages - 1), (side == 1) & (self.stage > 0)

    def relay(self, reach):
        for side in range(2):
            valid, block = self.incoming(reach, side, self.core)

            @pl.when(valid)
            def _():
                self.arrive(block)
                self.each_copy(block, *self.ways(jnp.int32(side)), lambda copy: copy.start())

    def use_own(self, compute):
        compute(self.me)
        self.arrive(self.partner)
        compute(self.partner)

    def use(self, reach, compute):
        def body(index, carry):
            side, other = lax.rem(index, 2), lax.div(index, 2)
            valid, block = self.incoming(
                reach, side, jnp.where(other == 0, self.core, 1 - self.core)
            )

            @pl.when(valid)
            def _():
                pl.when(other == 1)(lambda: self.arrive(block))
                compute(block)

            return carry

        lax.fori_loop(0, 4, body, 0)

    def run(self, compute, after_first=lambda: None):
        def body(reach, carry):
            self.relay(reach)
            pl.when(reach == 1)(after_first)
            self.use(reach, compute)
            return carry

        self.use_own(compute)
        lax.fori_loop(1, self.stages, body, 0)

    def at_end(self):
        return (self.stage == 0) | (self.stage == self.stages - 1)

    def finish(self):
        self.each_copy(
            self.me, self.stage < self.stages - 1, self.stage > 0, lambda copy: copy.wait_send()
        )

        def body(index, carry):
            reach, side = lax.div(index, 2) + 1, lax.rem(index, 2)
            valid, block = self.incoming(reach, side, self.core)

            @pl.when(valid)
            def _():
                self.each_copy(block, *self.ways(side), lambda copy: copy.wait_send())

            return carry

        lax.fori_loop(0, 2 * (self.stages - 1), body, 0)


class LineScatter:
    def __init__(self, stages, partial, cross, lane, sems):
        self.stages, self.partial, self.cross, self.lane = stages, partial, cross, lane
        self.cross_send, self.cross_recv, self.lane_send, self.lane_recv = sems
        self.me, self.core, self.stage = place()
        self.partner = self.me + 1 - 2 * self.core

    def cross_copy(self, far):
        return remote(
            self.partial.at[2 * far + 1 - self.core], self.cross.at[far],
            self.cross_send.at[far], self.cross_recv.at[far], tensor=self.partner,
        )

    def slot(self, way, far, holder):
        return far if way == 0 else jnp.where(far == holder, self.stages, far)

    def lane_copy(self, way, far, holder):
        target = self.me + 2 if way == 0 else self.me - 2
        slot = self.slot(way, far, holder)
        return remote(
            self.partial.at[2 * far + self.core], self.lane.at[slot],
            self.lane_send.at[far], self.lane_recv.at[slot], tensor=target,
        )

    def sent(self, way, far):
        return self.lane_copy(way, far, self.stage + (1 if way == 0 else -1))

    def received(self, way, far):
        self.lane_copy(way, far, self.stage).wait_recv()
        return self.lane[self.slot(way, far, self.stage)].astype(F32)

    def put(self, block, value):
        self.partial[block] = value.astype(BF16)

        @pl.when(lax.rem(block, 2) != self.core)
        def _():
            self.cross_copy(lax.div(block, 2)).start()

    def produce(self, compute):
        def body(index, carry):
            reach = self.stages - 1 - lax.div(index, 4)
            side, other = lax.rem(lax.div(index, 2), 2), lax.rem(index, 2)
            far = jnp.where(side == 0, self.stage + reach, self.stage - reach)

            @pl.when((far >= 0) & (far < self.stages) & ((reach > 0) | (side == 0)))
            def _():
                block = 2 * far + jnp.where(other == 0, 1 - self.core, self.core)
                self.put(block, compute(block))

            return carry

        lax.fori_loop(0, 4 * self.stages, body, 0)

    def chip_sum(self, far):
        return self.partial[2 * far + self.core].astype(F32) + self.cross[far].astype(F32)

    def send_sum(self, way, far, incoming):
        self.cross_copy(far).wait_recv()
        block = 2 * far + self.core

        @pl.when(incoming)
        def _():
            self.partial[block] = (self.chip_sum(far) + self.received(way, far)).astype(BF16)

        @pl.when(jnp.logical_not(incoming))
        def _():
            self.partial[block] = self.chip_sum(far).astype(BF16)

        self.sent(way, far).start()

    def step(self, reach):
        right, left = self.stage + reach, self.stage - reach
        pl.when(right < self.stages)(lambda: self.send_sum(0, right, self.stage > 0))
        pl.when(left >= 0)(lambda: self.send_sum(1, left, self.stage < self.stages - 1))

    def steps(self, first, last):
        lax.fori_loop(first, last, lambda index, carry: (self.step(self.stages - 1 - index), carry)[1], 0)

    def own(self, total_ref):
        self.cross_copy(self.stage).wait_recv()
        total_ref[...] = self.chip_sum(self.stage)

        @pl.when(self.stage > 0)
        def _():
            total_ref[...] += self.received(0, self.stage)

        @pl.when(self.stage < self.stages - 1)
        def _():
            total_ref[...] += self.received(1, self.stage)

    def finish(self):
        def body(far, carry):
            self.cross_copy(far).wait_send()
            pl.when(far > self.stage)(lambda: self.sent(0, far).wait_send())
            pl.when(far < self.stage)(lambda: self.sent(1, far).wait_send())
            return carry

        lax.fori_loop(0, self.stages, body, 0)


def scatter_shapes(stages, rows, depth):
    return [
        VMEM((2 * stages, rows, depth), BF16), VMEM((stages, rows, depth), BF16),
        VMEM((stages + 1, rows, depth), BF16),
        DMA((stages,)), DMA((stages,)), DMA((stages,)), DMA((stages + 1,)),
    ]


def exchange(axis, size, slots, send_sem, recv_sem):
    me = lax.axis_index(axis)

    def copy_to(other, slot):
        return remote(
            slots.at[slot], slots.at[slot], send_sem.at[other], recv_sem.at[slot], **{axis: other}
        )

    def start(step, carry):
        copy_to(lax.rem(me + step, size), me).start()
        return carry

    def wait(step, carry):
        other = lax.rem(me + step, size)
        copy_to(other, other).wait_recv()
        copy_to(other, me).wait_send()
        return carry

    lax.fori_loop(1, size, start, 0)
    return lambda: lax.fori_loop(1, size, wait, 0)


def piece_height(height, parts):
    return -(-height // (16 * parts)) * 16


class RowSum:
    def __init__(self, parts, piece, arrive, send_sem, recv_sem):
        self.parts, self.piece, self.arrive = parts, piece, arrive
        self.send_sem, self.recv_sem = send_sem, recv_sem
        self.row = lax.axis_index("dp")

    def copy(self, other, source):
        return remote(
            self.piece.at[other], self.arrive.at[source],
            self.send_sem.at[other], self.recv_sem.at[source], dp=other,
        )

    def others(self, act, start):
        return lax.fori_loop(
            1, self.parts, lambda step, carry: act(lax.rem(self.row + step, self.parts), carry), start
        )

    def start(self, total):
        high = self.piece.shape[1]
        for part in range(self.parts):
            self.piece[part] = total[part * high : (part + 1) * high, :].astype(BF16)

        def send(other, carry):
            self.copy(other, self.row).start()
            return carry

        self.others(send, 0)

    def reduce(self):
        def add(other, so_far):
            self.copy(other, other).wait_recv()
            self.copy(other, self.row).wait_send()
            return so_far + self.arrive[other].astype(F32)

        return self.others(add, self.piece[self.row].astype(F32)).astype(BF16)


def rowsum_shapes(parts, high, depth):
    return [
        VMEM((parts, high, depth), BF16), VMEM((parts, high, depth), BF16), DMA((parts,)), DMA((parts,)),
    ]


def column(row):
    return jnp.broadcast_to(row, (128, row.shape[1])).T[:, :1]


def piece_rows(width, parts):
    return min(rows for rows in range(8, width + 1, 8) if width % rows == 0 and width // rows <= parts)


class WeightSpread:
    def __init__(self, stages, parts, buffer, sems):
        self.stages, self.parts, self.buffer = stages, parts, buffer
        self.line_send, self.line_recv, self.row_send, self.row_recv, self.core_send, self.core_recv = sems
        self.count = buffer.shape[0]
        self.me, self.core, self.stage = place()
        self.partner = self.me + 1 - 2 * self.core
        self.row = lax.axis_index("dp")
        self.here = self.row < self.count
        self.slot = jnp.minimum(self.row, self.count - 1)
        self.gather = LineGather(stages, buffer.at[self.slot], self.line_send, self.line_recv)

    def row_copy(self, other, source, far):
        block = 2 * far + self.core
        return remote(
            self.buffer.at[source, block], self.buffer.at[source, block],
            self.row_send.at[other, far], self.row_recv.at[source, far], dp=other,
        )

    def core_copy(self, source, far, core):
        block = 2 * far + core
        return remote(
            self.buffer.at[source, block], self.buffer.at[source, block],
            self.core_send.at[source, far], self.core_recv.at[source, far], tensor=self.partner,
        )

    def rows_and_stages(self, act):
        def body(index, carry):
            act(lax.div(index, self.stages) + 1, lax.rem(index, self.stages))
            return carry

        lax.fori_loop(0, (self.parts - 1) * self.stages, body, 0)

    def to_other(self, step, far):
        self.row_copy(lax.rem(self.row + step, self.parts), self.slot, far).start()

    def run(self):
        @pl.when(self.here)
        def _():
            self.gather.run(lambda block: None)
            self.rows_and_stages(self.to_other)

    def pieces(self, act):
        def body(index, carry):
            source, far = lax.div(index, self.stages), lax.rem(index, self.stages)
            pl.when(source != self.row)(lambda: act(source, far))
            return carry

        lax.fori_loop(0, self.count * self.stages, body, 0)

    def pass_on(self):
        def act(source, far):
            self.row_copy(self.row, source, far).wait_recv()
            self.core_copy(source, far, self.core).start()

        self.pieces(act)

    def finish(self):
        @pl.when(self.here)
        def _():
            self.gather.finish()
            self.rows_and_stages(
                lambda step, far: self.row_copy(
                    lax.rem(self.row + step, self.parts), self.slot, far
                ).wait_send()
            )

        def act(source, far):
            self.core_copy(source, far, 1 - self.core).wait_recv()
            self.core_copy(source, far, self.core).wait_send()

        self.pieces(act)


def project_kernel(
    stages, parts, tok_hbm, g1_ref, b1_ref, bo_ref, g2_ref, b2_ref, bf2_ref, bf1_ref, bq_ref, bv_ref, wo_hbm, wq_hbm, wk_hbm, wv_hbm, ids_ref,
    norm_hbm, q_hbm, k_hbm, v_hbm, wo_out, vec_ref, span_ref, idr_ref, ido_ref,
    wo_all, line_send, line_recv, row_send, row_recv, core_send, core_recv, tok, norm, q_ref, k_ref, v_ref, weight, send_sem, recv_sem, out_sem, load_sem,
):
    me, _, _ = place()
    width, rows = wq_hbm.shape[0], tok.shape[0]
    loads = loading(
        load_sem,
        ((tok_hbm, tok), (wq_hbm, weight.at[0]), (wk_hbm, weight.at[1]), (wv_hbm, weight.at[2])),
    )
    spread = WeightSpread(
        stages, parts, wo_all, (line_send, line_recv, row_send, row_recv, core_send, core_recv)
    )
    high = wo_all.shape[2]
    own_piece = pltpu.make_async_copy(
        wo_hbm.at[pl.ds(pl.multiple_of(spread.slot * high, high), high)],
        wo_all.at[spread.slot, me], load_sem.at[4],
    )
    pl.when(spread.here)(own_piece.start)
    vec_ref[...] = jnp.zeros_like(vec_ref)
    for index, ref in enumerate(
        (g1_ref, b1_ref, bo_ref, g2_ref, b2_ref, bf2_ref, bf1_ref, bq_ref, bv_ref)
    ):
        vec_ref[index : index + 1, 0 : ref.shape[0]] = ref[...].astype(F32)[None, :]
    greet_line(stages, parts)
    loads[0].wait()
    normed, _ = normalize(tok[...].astype(F32))
    norm[me] = (normed * vec_ref[0:1, :] + vec_ref[1:2, :]).astype(BF16)
    gather = LineGather(stages, norm, send_sem, recv_sem)
    gather.start()

    @pl.when(spread.here)
    def _():
        own_piece.wait()
        spread.gather.start()

    ids = ids_ref[...].astype(F32)
    idr_ref[...] = ids
    ido_ref[...] = idr_ref[:, pl.ds(pl.multiple_of(me * rows, rows), rows)]
    for block in range(ids.shape[1] // BLOCK):
        first = ids[:, block * BLOCK : block * BLOCK + 1]
        last = ids[:, (block + 1) * BLOCK - 1 : (block + 1) * BLOCK]
        begin = jnp.sum(jnp.where(ids > first, 1.0, 0.0))
        end = jnp.sum(jnp.where(ids >= jnp.maximum(last, 1.0), 1.0, 0.0))
        span_ref[0, block] = lax.div(begin.astype(jnp.int32), BLOCK)
        span_ref[1, block] = lax.div(end.astype(jnp.int32) + (BLOCK - 1), BLOCK)
    for load in loads[1:]:
        load.wait()

    def keep(block):
        return [
            pltpu.make_async_copy(src.at[block], dst.at[block], out_sem.at[index, block])
            for index, (src, dst) in enumerate(
                ((norm, norm_hbm), (q_ref, q_hbm), (k_ref, k_hbm), (v_ref, v_hbm))
            )
        ]

    def compute(block):
        q_ref[block] = (nt(norm[block], weight[0]) + vec_ref[7:8, :width]).astype(BF16)
        k_ref[block] = nt(norm[block], weight[1]).astype(BF16)
        v_ref[block] = (nt(norm[block], weight[2]) + vec_ref[8:9, :width]).astype(BF16)
        for copy in keep(block):
            copy.start()

    spread.run()
    gather.run(compute)
    spread.pass_on()
    gather.finish()
    spread.finish()
    out_copy = pltpu.make_async_copy(wo_all, wo_out, load_sem.at[5])
    out_copy.start()

    def kept(block, carry):
        for copy in keep(block):
            copy.wait()
        return carry

    lax.fori_loop(0, 2 * stages, kept, 0)
    out_copy.wait()


def project(tokens, vectors, wo, wq, wk, wv, ids, devices, parts):
    rows, depth = tokens.shape
    width, length = wq.shape[1], ids.shape[1]
    stages = devices // 2
    high = piece_rows(width, parts)
    head = jax.ShapeDtypeStruct((devices, rows, width), BF16)
    pieces = (width // high, devices, high, depth)
    return pl.pallas_call(
        functools.partial(project_kernel, stages, parts),
        name="project",
        out_shape=(
            jax.ShapeDtypeStruct((devices, rows, depth), BF16), head, head, head,
            jax.ShapeDtypeStruct(pieces, BF16), jax.ShapeDtypeStruct((16, depth), F32),
            jax.ShapeDtypeStruct((2, length // BLOCK), jnp.int32),
            jax.ShapeDtypeStruct((1, length), F32), jax.ShapeDtypeStruct((1, rows), F32),
        ),
        in_specs=[HBM] + [VSPEC] * 9 + [HBM, HBM, HBM, HBM, VSPEC],
        out_specs=(HBM, HBM, HBM, HBM, HBM, VSPEC, SSPEC, VSPEC, VSPEC),
        scratch_shapes=[
            VMEM(pieces, BF16), DMA((devices, 3)), DMA((devices,)),
            *[DMA((parts, stages))] * 4,
            VMEM((rows, depth), BF16), VMEM((devices, rows, depth), BF16),
            *[VMEM((devices, rows, width), BF16)] * 3, VMEM((3, width, depth), BF16),
            DMA((devices, 3)), DMA((devices,)), DMA((4, devices)), DMA((6,)),
        ],
        compiler_params=pltpu.CompilerParams(
            collective_id=0, has_side_effects=True, vmem_limit_bytes=VMEM_ALL
        ),
    )(tokens, *vectors, wo, wq.T, wk.T, wv.T, ids)


def lanes_of(head, width):
    lane = lax.broadcasted_iota(jnp.int32, (1, width), 1)
    return (lane >= head * HD) & (lane < (head + 1) * HD)


def fill_columns(row_ref, column_ref):
    for block in range(row_ref.shape[1] // BLOCK):
        at = pl.ds(block * BLOCK, BLOCK)
        column_ref[at, :] = column(row_ref[:, at])


def head_rows(head, width):
    row = lax.broadcasted_iota(jnp.int32, (width, 1), 0)
    return (row >= head * HD) & (row < (head + 1) * HD)


def side_by_side(block_t, heads):
    width = block_t.shape[0]
    zero = jnp.zeros_like(block_t)
    return jnp.concatenate([jnp.where(head_rows(h, width), block_t, zero) for h in range(heads)], axis=1)


def stacked(block, heads):
    width = block.shape[1]
    zero = jnp.zeros_like(block)
    return jnp.concatenate([jnp.where(lanes_of(h, width), block, zero) for h in range(heads)], axis=0)


def repeat_lanes(row, heads):
    return jnp.concatenate([row] * heads, axis=1)


def attend_kernel(
    heads, span_ref, q_hbm, k_hbm, v_hbm, idr_ref, o_ref, log_ref,
    q_ref, k_ref, v_ref, load_sem, idc_ref, vt_ref, acc_ref,
):
    length, width = q_ref.shape
    scale = HD ** (-0.5) * LOG2E
    loads = loading(load_sem, ((v_hbm, v_ref), (q_hbm, q_ref), (k_hbm, k_ref)))
    fill_columns(idr_ref, idc_ref)
    for load in loads:
        load.wait()

    def turn(block, total):
        at = pl.ds(pl.multiple_of(block * BLOCK, BLOCK), BLOCK)
        value = v_ref[at, :].astype(F32)
        vt_ref[block] = value.T.astype(BF16)
        return total + jnp.sum(value, axis=0, keepdims=True)

    mean_value = lax.fori_loop(0, length // BLOCK, turn, jnp.zeros((1, width), F32)) * (1.0 / length)

    def per_block(block, carry):
        at = pl.ds(pl.multiple_of(block * BLOCK, BLOCK), BLOCK)
        query = side_by_side(q_ref[at, :].astype(F32).T.astype(BF16), heads)
        id_row = idr_ref[:, at]
        id_rows = repeat_lanes(id_row, heads)
        acc_ref[...] = jnp.zeros_like(acc_ref)

        def per_key(other, state):
            top, total = state
            keys_at = pl.ds(pl.multiple_of(other * BLOCK, BLOCK), BLOCK)
            id_col = idc_ref[keys_at, :]
            allowed = (id_col == id_rows) & (id_col > 0)
            scores = jnp.where(allowed, nn(k_ref[keys_at, :], query) * scale, NEG_FILL)
            new_top = jnp.maximum(top, jnp.max(scores, axis=0, keepdims=True))
            weight = jnp.exp2(scores - new_top)
            shrink = jnp.exp2(top - new_top)
            total = total * shrink + jnp.sum(weight, axis=0, keepdims=True)
            acc_ref[...] = acc_ref[...] * shrink + nn(vt_ref[other], weight.astype(BF16))
            return new_top, total

        top, total = lax.fori_loop(
            span_ref[0, block], span_ref[1, block], per_key,
            (jnp.full((1, heads * BLOCK), NEG_FILL, F32), jnp.zeros((1, heads * BLOCK), F32)),
        )
        scaled = acc_ref[...] / total
        logs = jnp.where(id_rows == 0, 0.0, top + jnp.log2(total))
        result = jnp.zeros((width, BLOCK), F32)
        for h in range(heads):
            here = slice(h * BLOCK, (h + 1) * BLOCK)
            result = jnp.where(head_rows(h, width), scaled[:, here], result)
            log_ref[h : h + 1, at] = logs[:, here]
        o_ref[at, :] = jnp.where(idc_ref[at, :] == 0, mean_value, result.T).astype(BF16)
        return carry

    lax.fori_loop(0, length // BLOCK, per_block, 0)


def attend(q, k, v, span, id_row):
    length, width = q.shape
    heads = width // HD
    return pl.pallas_call(
        functools.partial(attend_kernel, heads),
        name="attend",
        out_shape=(
            jax.ShapeDtypeStruct((length, width), BF16),
            jax.ShapeDtypeStruct((heads, length), F32),
        ),
        in_specs=[SSPEC, HBM, HBM, HBM, VSPEC],
        out_specs=(VSPEC,) * 2,
        scratch_shapes=[
            *[VMEM((length, width), BF16)] * 3, DMA((3,)),
            VMEM((length, 1), F32), VMEM((length // BLOCK, width, BLOCK), BF16),
            VMEM((width, heads * BLOCK), F32),
        ],
        compiler_params=pltpu.CompilerParams(vmem_limit_bytes=VMEM_ALL),
    )(span, q, k, v, id_row)


def attend_back_kernel(
    heads, span_ref, q_hbm, k_hbm, v_hbm, idr_ref, o_hbm, log_ref, g_hbm, fc_hbm, layer_hbm,
    out_ref, fc1_hbm, fc2_hbm, layer_out, fc, fc1, fc2, layer, side_sem, q_ref, k_ref, v_ref, o_ref, g_ref, load_sem,
    idc_ref, dq_ref, dk_ref, dv_ref, q_side, q_stack, g_side, g_stack, row_ref, log_side,
):
    length, width = q_ref.shape
    score_scale = HD ** (-0.5)
    loads = loading(
        load_sem, ((q_hbm, q_ref), (g_hbm, g_ref), (o_hbm, o_ref), (k_hbm, k_ref), (v_hbm, v_ref))
    )
    layer_in = pltpu.make_async_copy(layer_hbm, layer, side_sem.at[0])
    fc_in = pltpu.make_async_copy(fc_hbm, fc, side_sem.at[1])
    layer_in.start()
    fc_in.start()
    dq_ref[...] = jnp.zeros_like(dq_ref)
    fill_columns(idr_ref, idc_ref)
    for load in loads:
        load.wait()

    def prepare(block, pad):
        at = pl.ds(pl.multiple_of(block * BLOCK, BLOCK), BLOCK)
        query, grad = q_ref[at, :], g_ref[at, :]
        wide = grad.astype(F32)
        grad_t = wide.T
        product = (wide * o_ref[at, :].astype(F32)).T
        q_side[block] = side_by_side(query.astype(F32).T.astype(BF16), heads)
        g_side[block] = side_by_side(grad_t.astype(BF16), heads)
        q_stack[block] = stacked(query, heads)
        g_stack[block] = stacked(grad, heads)
        for h in range(heads):
            here = slice(h * BLOCK, (h + 1) * BLOCK)
            row_ref[block, :, here] = jnp.sum(
                jnp.where(head_rows(h, width), product, 0.0), axis=0, keepdims=True
            )
            log_side[block, :, here] = log_ref[h : h + 1, at]
        return pad + jnp.sum(jnp.where(idc_ref[at, :] == 0, wide, 0.0), axis=0, keepdims=True)

    pad = lax.fori_loop(0, length // BLOCK, prepare, jnp.zeros((1, width), F32)) * (1.0 / length)
    units = fc1.shape[0]
    second = -(-units // 16) * 16
    layer_in.wait()
    fc_in.wait()
    fc1[...] = fc[0:units, :].astype(F32)
    fc2[...] = fc[second : second + units, :].astype(F32)
    outs = [
        pltpu.make_async_copy(src, dst, side_sem.at[2 + index])
        for index, (src, dst) in enumerate(((layer, layer_out), (fc1, fc1_hbm), (fc2, fc2_hbm)))
    ]
    for out in outs:
        out.start()

    def per_key(block, carry):
        at = pl.ds(pl.multiple_of(block * BLOCK, BLOCK), BLOCK)
        key, value, id_col = k_ref[at, :], v_ref[at, :], idc_ref[at, :]
        key_side = side_by_side(key.astype(F32).T.astype(BF16), heads)
        real = id_col > 0
        dk_ref[...] = jnp.zeros_like(dk_ref)
        dv_ref[...] = jnp.zeros_like(dv_ref)

        def per_query(other, inner):
            query_at = pl.ds(pl.multiple_of(other * BLOCK, BLOCK), BLOCK)
            allowed = (id_col == repeat_lanes(idr_ref[:, query_at], heads)) & real
            scores = nn(key, q_side[other]) * (score_scale * LOG2E) - log_side[other]
            prob = jnp.exp2(jnp.where(allowed, scores, NEG_FILL))
            dv_ref[...] += nn(prob.astype(BF16), g_stack[other])
            back = (prob * (nn(value, g_side[other]) - row_ref[other])).astype(BF16)
            dk_ref[...] += nn(back, q_stack[other])
            back_rows = jnp.concatenate(
                [back[:, h * BLOCK : (h + 1) * BLOCK] for h in range(heads)], axis=0
            )
            dq_ref[other] += nn(key_side, back_rows)
            return inner

        lax.fori_loop(span_ref[0, block], span_ref[1, block], per_query, 0)
        out_ref[at, width : 2 * width] = (dk_ref[...] * score_scale).astype(BF16)
        out_ref[at, 2 * width :] = (dv_ref[...] + pad).astype(BF16)
        return carry

    lax.fori_loop(0, length // BLOCK, per_key, 0)

    def settle(block, carry):
        at = pl.ds(pl.multiple_of(block * BLOCK, BLOCK), BLOCK)
        out_ref[at, :width] = (dq_ref[block].T * score_scale).astype(BF16)
        return carry

    lax.fori_loop(0, length // BLOCK, settle, 0)
    for out in outs:
        out.wait()


def attend_back(q, k, v, span, id_row, o, log_total, grad, fc, layer, units):
    length, width = q.shape
    heads = width // HD
    blocks, depth = length // BLOCK, layer.shape[1]
    whole = VMEM((length, width), BF16)
    side, stack = VMEM((blocks, width, heads * BLOCK), BF16), VMEM((blocks, heads * BLOCK, width), BF16)
    line = VMEM((blocks, 1, heads * BLOCK), F32)
    return pl.pallas_call(
        functools.partial(attend_back_kernel, heads),
        name="attend_back",
        out_shape=(
            jax.ShapeDtypeStruct((length, 3 * width), BF16), jax.ShapeDtypeStruct((units, depth), F32),
            jax.ShapeDtypeStruct((units, depth), F32), jax.ShapeDtypeStruct(layer.shape, BF16),
        ),
        in_specs=[SSPEC, HBM, HBM, HBM, VSPEC, HBM, VSPEC, HBM, HBM, HBM],
        out_specs=(VSPEC, HBM, HBM, HBM),
        scratch_shapes=[
            VMEM(fc.shape, BF16), VMEM((units, depth), F32), VMEM((units, depth), F32),
            VMEM(layer.shape, BF16), DMA((5,)),
            whole, whole, whole, whole, whole, DMA((5,)),
            VMEM((length, 1), F32), VMEM((blocks, width, BLOCK), F32), VMEM((BLOCK, width), F32),
            VMEM((BLOCK, width), F32), side, stack, side, stack, line, line,
        ],
        compiler_params=pltpu.CompilerParams(vmem_limit_bytes=VMEM_ALL),
    )(span, q, k, v, id_row, o, log_total, grad, fc, layer)


def gelu_pair(u):
    slope = (2.0 / jnp.pi) ** 0.5
    bent = jnp.tanh(slope * (u + 0.044715 * u * u * u))
    half = 0.5 * (1.0 + bent)
    return u * half, half + 0.5 * u * (1.0 - bent * bent) * slope * (1.0 + 3 * 0.044715 * u * u)


def middle_kernel(
    stages, parts, att_hbm, wo_hbm, fc1_hbm, fc2_hbm, tok_hbm, top_hbm, ids_ref, vec_ref,
    out_ref, gres_ref, gatt_ref, fc_hbm, small_ref,
    wo, fc1, fc2, tok, top, load_sem,
    held, held_send, held_recv, norm_all, norm_send, norm_recv, top_all, top_send, top_recv,
    hidden, slope, grad_pre,
    br_part, br_cross, br_lane, br_s0, br_s1, br_s2, br_s3,
    gn_part, gn_cross, gn_lane, gn_s0, gn_s1, gn_s2, gn_s3,
    resid, total, acc, piece, arrive, piece_send, piece_recv, fa_send, fa_recv, free_sem, out_sem,
    back, back_send, back_recv,
):
    me, _, _ = place()
    devices = 2 * stages
    rows, depth = tok_hbm.shape
    high = wo_hbm.shape[2]
    units = fc1_hbm.shape[0]
    second = -(-units // 16) * 16
    loads = loading(
        load_sem,
        ((tok_hbm, tok), (top_hbm, top), (fc1_hbm, fc1), (fc2_hbm, fc2), (att_hbm.at[me], held.at[me]),
         *((wo_hbm.at[index], wo.at[:, pl.ds(index * high, high)]) for index in range(wo_hbm.shape[0]))),
    )
    greet_peers((("tensor", devices), ("dp", parts)))

    def held_copy(other, source):
        return remote(
            att_hbm.at[other], held.at[source], held_send.at[other], held_recv.at[source], tensor=other
        )

    def send_held(step, carry):
        held_copy(lax.rem(me + step, devices), me).start()
        return carry

    lax.fori_loop(1, devices, send_held, 0)
    gather2 = LineGather(stages, norm_all, norm_send, norm_recv)
    gather3 = LineGather(stages, top_all, top_send, top_recv)
    branch = LineScatter(stages, br_part, br_cross, br_lane, (br_s0, br_s1, br_s2, br_s3))
    gnorm = LineScatter(stages, gn_part, gn_cross, gn_lane, (gn_s0, gn_s1, gn_s2, gn_s3))

    mask = column(jnp.where(ids_ref[...] > 0, 1.0, 0.0))
    acc[...] = jnp.zeros_like(acc)
    small_ref[...] = jnp.zeros_like(small_ref)
    loads[0].wait()
    loads[1].wait()
    top_own = top[...].astype(F32) * mask
    top_all[me] = top_own.astype(BF16)
    small_ref[5:6, :] = jnp.sum(top_own, axis=0, keepdims=True)
    resid[...] = tok[...].astype(F32) + vec_ref[2:3, :]
    for load in loads[4:]:
        load.wait()
    resid[...] += nn(held[me], wo[me])

    def add_held(step, carry):
        other = lax.rem(me + devices - step, devices)
        held_copy(other, other).wait_recv()
        resid[...] += nn(held[other], wo[other])
        return carry

    lax.fori_loop(1, devices, add_held, 0)
    normed, _ = normalize(resid[...])
    norm_all[me] = (normed * vec_ref[3:4, :] + vec_ref[4:5, :]).astype(BF16)
    gather2.start()
    loads[2].wait()
    loads[3].wait()

    def forward(block):
        pre_act = nt(norm_all[block], fc1[...]) + vec_ref[6:7, 0:units]
        value, slope_now = gelu_pair(pre_act)
        hidden[block] = value.astype(BF16)
        slope[block] = slope_now.astype(BF16)
        branch.put(block, nn(hidden[block], fc2[...]))

    at_end = gather2.at_end()
    gather2.run(forward, lambda: pl.when(at_end)(gather3.start_inward))
    pl.when(jnp.logical_not(at_end))(gather3.start_inward)
    gather3.start_outward()
    pl.when(at_end)(lambda: branch.steps(0, stages - 1))

    def backward(block):
        grad = nt(top_all[block], fc2[...]) * slope[block].astype(F32)
        low = grad.astype(BF16)
        grad_pre[block] = low
        small_ref[7:8, 0:units] += jnp.sum(low.astype(F32), axis=0, keepdims=True)
        gnorm.put(block, nn(grad_pre[block], fc1[...]))
        acc[0:units, :] += tn(grad_pre[block], norm_all[block])
        acc[second : second + units, :] += tn(hidden[block], top_all[block])

    gather3.run(backward)
    gnorm.step(stages - 1)
    sums = RowSum(parts, piece, arrive, piece_send, piece_recv)
    sums.start(acc)

    pl.when(jnp.logical_not(at_end))(lambda: branch.steps(1, stages - 1))
    gnorm.steps(1, stages - 1)
    fc_sum = sums.reduce()

    def to_rows(act):
        lax.fori_loop(
            1, parts, lambda step, carry: (act(lax.rem(sums.row + step, parts)), carry)[1], 0
        )

    to_rows(
        lambda other: pl.semaphore_signal(
            free_sem, inc=1, device_id={"dp": other}, device_id_type=MESH
        )
    )
    pl.semaphore_wait(free_sem, parts - 1)
    arrive[sums.row] = fc_sum
    wait_fc = exchange("dp", parts, arrive, fa_send, fa_recv)
    branch.own(total)
    out_ref[...] = (mask * (resid[...] + total[...] + vec_ref[5:6, :])).astype(BF16)

    gnorm.own(total)
    grad = total[...]
    normed, scale = normalize(resid[...])
    small_ref[2:3, :] = jnp.sum(grad * normed, axis=0, keepdims=True)
    small_ref[3:4, :] = jnp.sum(grad, axis=0, keepdims=True)
    inner = grad * vec_ref[3:4, :]
    inner_mean = jnp.mean(inner, axis=-1, keepdims=True)
    inner_proj = jnp.mean(inner * normed, axis=-1, keepdims=True)
    grad_resid = top[...].astype(F32) * mask + scale * (inner - inner_mean - normed * inner_proj)
    gres_ref[...] = grad_resid
    tok[...] = grad_resid.astype(BF16)
    small_ref[4:5, :] = jnp.sum(grad_resid, axis=0, keepdims=True)

    def back_copy(other, source):
        return remote(
            back.at[other], gatt_ref.at[source], back_send.at[other], back_recv.at[source], tensor=other
        )

    def send_back(step, carry):
        other = lax.rem(me + step, devices)
        back[other] = nt(tok[...], wo[other]).astype(BF16)
        back_copy(other, me).start()
        return carry

    lax.fori_loop(1, devices, send_back, 0)
    gatt_ref[me] = nt(tok[...], wo[me]).astype(BF16)

    wait_fc()
    out_fc = pltpu.make_async_copy(arrive, fc_hbm, out_sem)
    out_fc.start()

    def settle(step, carry):
        other = lax.rem(me + devices - step, devices)
        back_copy(other, other).wait_recv()
        back_copy(other, me).wait_send()
        held_copy(other, me).wait_send()
        return carry

    lax.fori_loop(1, devices, settle, 0)
    gather2.finish()
    gather3.finish()
    branch.finish()
    gnorm.finish()
    out_fc.wait()


def middle(att, wo, fc1, fc2, tokens, out_grad, ids, vectors, parts):
    devices, rows, width = att.shape
    depth, units = fc1.shape
    stages = devices // 2
    high = piece_height(2 * (-(-units // 16) * 16), parts)
    return pl.pallas_call(
        functools.partial(middle_kernel, stages, parts),
        name="middle",
        out_shape=(
            jax.ShapeDtypeStruct((rows, depth), BF16),
            jax.ShapeDtypeStruct((rows, depth), F32),
            jax.ShapeDtypeStruct((devices, rows, width), BF16),
            jax.ShapeDtypeStruct((parts, high, depth), BF16),
            jax.ShapeDtypeStruct((8, depth), F32),
        ),
        in_specs=[HBM] * 6 + [VSPEC] * 2,
        out_specs=(VSPEC, VSPEC, VSPEC, HBM, VSPEC),
        scratch_shapes=[
            VMEM((devices, width, depth), BF16), VMEM((units, depth), BF16), VMEM((units, depth), BF16),
            VMEM((rows, depth), BF16), VMEM((rows, depth), BF16), DMA((5 + wo.shape[0],)),
            VMEM((devices, rows, width), BF16), DMA((devices,)), DMA((devices,)),
            VMEM((devices, rows, depth), BF16), DMA((devices, 3)), DMA((devices,)),
            VMEM((devices, rows, depth), BF16), DMA((devices, 3)), DMA((devices,)),
            VMEM((devices, rows, units), BF16), VMEM((devices, rows, units), BF16),
            VMEM((devices, rows, units), BF16),
            *scatter_shapes(stages, rows, depth), *scatter_shapes(stages, rows, depth),
            VMEM((rows, depth), F32), VMEM((rows, depth), F32),
            VMEM((parts * high, depth), F32), *rowsum_shapes(parts, high, depth),
            DMA((parts,)), DMA((parts,)), pltpu.SemaphoreType.REGULAR, DMA,
            VMEM((devices, rows, width), BF16), DMA((devices,)), DMA((devices,)),
        ],
        compiler_params=pltpu.CompilerParams(
            collective_id=2, has_side_effects=True, vmem_limit_bytes=VMEM_ALL
        ),
    )(
        att, wo, fc1.T, fc2, tokens, out_grad, ids, vectors,
    )


def close_kernel(
    stages, parts, dx_hbm, wq_hbm, wk_hbm, wv_hbm, norm_hbm, att_hbm, tok_hbm, vec_ref, resid_hbm,
    small_ref,
    gtok_ref, gw_hbm, go_hbm, gsmall_ref,
    dx_ref, weight, norm, att_ref, tok_ref, resid_ref, load_sem, gatt_all, gatt_send, gatt_recv,
    partial, cross, lane, cross_send, cross_recv, lane_send, lane_recv,
    total, acc, acc_o, w_piece, w_arrive, w_send, w_recv, o_piece, o_arrive, o_send, o_recv,
    w_all, o_all, wa_send, wa_recv, oa_send, oa_recv, out_sem,
    slots_t, slots_d, st_send, st_recv, sd_send, sd_recv,
):
    me, _, _ = place()
    row = lax.axis_index("dp")
    devices = 2 * stages
    wide, width = dx_ref.shape[2], att_ref.shape[2]
    loads = loading(
        load_sem,
        ((resid_hbm, resid_ref), (dx_hbm, dx_ref),
         *((src, weight.at[pl.ds(index * width, width)]) for index, src in enumerate((wq_hbm, wk_hbm, wv_hbm))),
         (norm_hbm, norm), (att_hbm, att_ref), (tok_hbm, tok_ref)),
    )
    greet_peers((("tensor", devices), ("dp", parts)))
    loads[0].wait()
    gatt_all[me] = resid_ref[...].astype(BF16)
    gather = LineGather(stages, gatt_all, gatt_send, gatt_recv)
    gather.start()
    for load in loads[1:5]:
        load.wait()
    scatter = LineScatter(
        stages, partial, cross, lane, (cross_send, cross_recv, lane_send, lane_recv)
    )
    scatter.produce(lambda block: nn(dx_ref[block], weight[...]))
    scatter.step(stages - 1)

    acc[...] = jnp.zeros_like(acc)
    acc_o[...] = jnp.zeros_like(acc_o)
    for load in loads[5:]:
        load.wait()

    def weight_block(block, bias):
        grad = dx_ref[block]
        acc[0:wide, :] += tn(grad, norm[block])
        return bias + jnp.sum(grad.astype(F32), axis=0, keepdims=True)

    bias = lax.fori_loop(0, devices, weight_block, jnp.zeros((1, wide), F32))
    w_sum = RowSum(parts, w_piece, w_arrive, w_send, w_recv)
    w_sum.start(acc)

    def weight_o(block):
        acc_o[0:width, :] += tn(att_ref[block], gatt_all[block])

    gather.use_own(weight_o)

    def both(reach, carry):
        gather.relay(reach)
        pl.when(reach < stages - 1)(lambda: scatter.step(stages - 1 - reach))
        gather.use(reach, weight_o)
        return carry

    lax.fori_loop(1, stages - 1, both, 0)
    w_all[row] = w_sum.reduce()
    wait_w = exchange("dp", parts, w_all, wa_send, wa_recv)
    lax.fori_loop(stages - 1, stages, both, 0)
    o_sum = RowSum(parts, o_piece, o_arrive, o_send, o_recv)
    o_sum.start(acc_o)
    o_all[row] = o_sum.reduce()
    wait_o = exchange("dp", parts, o_all, oa_send, oa_recv)

    scatter.own(total)
    grad = total[...]
    normed, scale = normalize(tok_ref[...].astype(F32))
    slots_t[me] = small_ref[...]
    slots_t[me, 0:1, :] = jnp.sum(grad * normed, axis=0, keepdims=True)
    slots_t[me, 1:2, :] = jnp.sum(grad, axis=0, keepdims=True)
    slots_t[me, 6:7, 0:wide] = bias
    wait_small = exchange("tensor", devices, slots_t, st_send, st_recv)
    inner = grad * vec_ref[0:1, :]
    inner_mean = jnp.mean(inner, axis=-1, keepdims=True)
    inner_proj = jnp.mean(inner * normed, axis=-1, keepdims=True)
    gtok_ref[...] = resid_ref[...] + scale * (inner - inner_mean - normed * inner_proj)
    wait_small()
    sums = lax.fori_loop(
        1, devices, lambda slot, so_far: so_far + slots_t[slot], slots_t[0]
    )
    line = lax.broadcasted_iota(jnp.int32, sums.shape, 0)
    slots_d[row] = jnp.where(line < 6, sums, slots_t[me])
    wait_last = exchange("dp", parts, slots_d, sd_send, sd_recv)
    outs = []
    for index, (wait, src, dst) in enumerate(
        ((wait_w, w_all, gw_hbm), (wait_o, o_all, go_hbm))
    ):
        wait()
        out = pltpu.make_async_copy(src, dst, out_sem.at[index])
        out.start()
        outs.append(out)
    wait_last()
    gsmall_ref[...] = lax.fori_loop(
        1, parts, lambda slot, so_far: so_far + slots_d[slot], slots_d[0]
    )
    gather.finish()
    scatter.finish()
    for out in outs:
        out.wait()


def close(dx, wq, wk, wv, norm, att, tokens, vectors, resid, small, parts):
    devices, rows, wide = dx.shape
    depth = tokens.shape[1]
    stages = devices // 2
    width = wide // 3
    w_high, o_high = piece_height(wide, parts), piece_height(width, parts)
    pieces = [(parts, high, depth) for high in (w_high, o_high)]
    return pl.pallas_call(
        functools.partial(close_kernel, stages, parts),
        name="close",
        out_shape=(
            jax.ShapeDtypeStruct((rows, depth), F32),
            *(jax.ShapeDtypeStruct(shape, BF16) for shape in pieces),
            jax.ShapeDtypeStruct(small.shape, F32),
        ),
        in_specs=[HBM] * 7 + [VSPEC, HBM, VSPEC],
        out_specs=(VSPEC, HBM, HBM, VSPEC),
        scratch_shapes=[
            VMEM((devices, rows, wide), BF16), VMEM((wide, depth), BF16),
            VMEM((devices, rows, depth), BF16), VMEM((devices, rows, width), BF16),
            VMEM((rows, depth), BF16), VMEM((rows, depth), F32), DMA((8,)),
            VMEM((devices, rows, depth), BF16), DMA((devices, 3)), DMA((devices,)),
            *scatter_shapes(stages, rows, depth),
            VMEM((rows, depth), F32), VMEM((parts * w_high, depth), F32),
            VMEM((parts * o_high, depth), F32),
            *rowsum_shapes(parts, w_high, depth), *rowsum_shapes(parts, o_high, depth),
            *(VMEM(shape, BF16) for shape in pieces), *[DMA((parts,))] * 4, DMA((2,)),
            VMEM((devices,) + small.shape, F32), VMEM((parts,) + small.shape, F32),
            DMA((devices,)), DMA((devices,)), DMA((parts,)), DMA((parts,)),
        ],
        compiler_params=pltpu.CompilerParams(
            collective_id=1, has_side_effects=True, vmem_limit_bytes=VMEM_ALL
        ),
    )(dx, wq.T, wk.T, wv.T, norm, att, tokens, vectors, resid, small)


def settle_kernel(
    gtok_hbm, gw_hbm, go_hbm, sums_ref,
    gtok_out, wq_ref, wk_ref, wv_ref, wo_ref,
    g1_ref, b1_ref, g2_ref, b2_ref, bo_ref, bf2_ref, bq_ref, bv_ref, bf1_ref,
    gtok, gw, go, sems,
):
    width, units = wq_ref.shape[0], bf1_ref.shape[0]
    loads = loading(sems, ((gtok_hbm, gtok), (gw_hbm, gw), (go_hbm, go)))
    for row, ref in enumerate((g1_ref, b1_ref, g2_ref, b2_ref, bo_ref, bf2_ref)):
        ref[...] = sums_ref[row, :]
    bq_ref[...] = sums_ref[6:7, 0:width].reshape(width)
    bv_ref[...] = sums_ref[6:7, 2 * width : 3 * width].reshape(width)
    bf1_ref[...] = sums_ref[7:8, 0:units].reshape(units)
    loads[0].wait()
    out = pltpu.make_async_copy(gtok, gtok_out, sems.at[3])
    out.start()
    loads[1].wait()
    loads[2].wait()
    wq_ref[...] = gw[0:width, :].astype(F32)
    wk_ref[...] = gw[width : 2 * width, :].astype(F32)
    wv_ref[...] = gw[2 * width : 3 * width, :].astype(F32)
    wo_ref[...] = go[0:width, :].astype(F32)
    out.wait()


def settle(gtok, gw, go, sums, width, units):
    depth = gtok.shape[1]
    weight = jax.ShapeDtypeStruct((width, depth), F32)
    return pl.pallas_call(
        settle_kernel,
        name="settle",
        out_shape=(
            jax.ShapeDtypeStruct(gtok.shape, F32), weight, weight, weight, weight,
            *(jax.ShapeDtypeStruct((size,), F32) for size in (depth,) * 6 + (width, width, units)),
        ),
        in_specs=[HBM, HBM, HBM, VSPEC],
        out_specs=(HBM,) + (VSPEC,) * 13,
        scratch_shapes=[
            VMEM(gtok.shape, F32), VMEM(gw.shape, BF16), VMEM(go.shape, BF16), DMA((4,)),
        ],
        compiler_params=pltpu.CompilerParams(vmem_limit_bytes=VMEM_ALL),
    )(gtok, gw, go, sums)


def on_device(
    devices, parts, tokens, picture_ids, ln1_gain, ln1_bias, q_weight, q_bias, k_weight, v_weight, v_bias,
    o_weight, o_bias, ln2_gain, ln2_bias, fc1_weight, fc1_bias, fc2_weight, fc2_bias, out_grad,
):
    own_count, depth = tokens.shape
    hidden_local = fc1_weight.shape[1]
    width = q_weight.shape[1]
    norm1_all, q, k, v, o_all, vectors, span, id_row, own_ids = project(
        tokens,
        (ln1_gain, ln1_bias, o_bias, ln2_gain, ln2_bias, fc2_bias, fc1_bias, q_bias, v_bias),
        o_weight, q_weight, k_weight, v_weight, picture_ids[None, :], devices, parts,
    )
    q, k, v = (item.reshape(LEN, width) for item in (q, k, v))
    attended, log_total = attend(q, k, v, span, id_row)
    heads_first = attended.reshape(devices, own_count, width)
    output, grad_residual, grad_attended, fc_sum, small = middle(
        heads_first, o_all, fc1_weight, fc2_weight, tokens, out_grad,
        own_ids, vectors, parts,
    )
    dqkv, grad_fc1, grad_fc2, output = attend_back(
        q, k, v, span, id_row, attended, log_total, grad_attended.reshape(LEN, width),
        fc_sum.reshape(-1, depth), output, hidden_local,
    )
    grad_tokens, grad_w, grad_o, sums = close(
        dqkv.reshape(devices, own_count, 3 * width), q_weight, k_weight, v_weight, norm1_all,
        heads_first, tokens, vectors, grad_residual, small, parts,
    )
    (
        grad_tokens, grad_q, grad_k, grad_v, grad_o, grad_g1, grad_b1, grad_g2, grad_b2, grad_bo,
        grad_bf2, grad_bq, grad_bv, grad_bf1,
    ) = settle(
        grad_tokens, grad_w.reshape(-1, depth), grad_o.reshape(-1, depth), sums, width, hidden_local
    )
    return (
        output, grad_tokens, grad_g1, grad_b1, grad_q.T, grad_bq, grad_k.T, grad_v.T, grad_bv,
        grad_o, grad_bo, grad_g2, grad_b2, grad_fc1.T, grad_bf1, grad_fc2, grad_bf2,
    )


def solution(mesh):
    rows, whole = P(("dp", "tensor"), None), P()
    columns, down, along = P(None, "tensor"), P("tensor", None), P("tensor")
    return jax.shard_map(
        functools.partial(on_device, mesh.shape["tensor"], mesh.shape["dp"]),
        mesh=mesh,
        in_specs=(
            rows, P("dp"), whole, whole, columns, along, columns, columns, along, down, whole,
            whole, whole, columns, along, down, whole, rows,
        ),
        out_specs=(
            rows, rows, whole, whole, columns, along, columns, columns, along, down, whole,
            whole, whole, columns, along, down, whole,
        ),
        check_vma=False,
    )
```

```python
import functools

import jax
import jax.numpy as jnp
from jax import lax
from jax.experimental import pallas as pl
from jax.experimental.pallas import tpu as pltpu
from jax.sharding import PartitionSpec as P

HD = 72
LEN = 2048
BLOCK = 256
NORM_EPS = 1e-06
NEG_FILL = -1e30
LOG2E = 1.4426950408889634
VMEM_ALL = 67043328
BF16 = jnp.bfloat16
F32 = jnp.float32
MESH = pl.DeviceIdType.MESH
VMEM = pltpu.VMEM
DMA = pltpu.SemaphoreType.DMA
VSPEC = pl.BlockSpec(memory_space=pltpu.VMEM)
SSPEC = pl.BlockSpec(memory_space=pltpu.SMEM)
HBM = pl.BlockSpec(memory_space=pltpu.HBM)


def nn(left, right):
    return lax.dot_general(left, right, (((1,), (0,)), ((), ())), preferred_element_type=F32)


def nt(left, right):
    return lax.dot_general(left, right, (((1,), (1,)), ((), ())), preferred_element_type=F32)


def tn(left, right):
    return lax.dot_general(left, right, (((0,), (0,)), ((), ())), preferred_element_type=F32)


def remote(src, dst, send_sem, recv_sem, **where):
    return pltpu.make_async_remote_copy(
        src_ref=src, dst_ref=dst, send_sem=send_sem, recv_sem=recv_sem,
        device_id=where, device_id_type=MESH,
    )


def loading(sems, pairs):
    copies = [
        pltpu.make_async_copy(src, dst, sems.at[index]) for index, (src, dst) in enumerate(pairs)
    ]
    for copy in copies:
        copy.start()
    return copies


def place():
    me = lax.axis_index("tensor")
    core = lax.rem(me, 2)
    return me, core, lax.div(me, 2)


def greet_peers(axes):
    barrier = pltpu.get_barrier_semaphore()
    for axis, size in axes:
        me = lax.axis_index(axis)

        def greet(step, carry):
            pl.semaphore_signal(
                barrier, inc=1, device_id={axis: lax.rem(me + step, size)}, device_id_type=MESH
            )
            return carry

        lax.fori_loop(1, size, greet, 0)
    pl.semaphore_wait(barrier, sum(size - 1 for _, size in axes))


def normalize(values):
    average = jnp.mean(values, axis=-1, keepdims=True)
    centred = values - average
    variance = jnp.mean(centred * centred, axis=-1, keepdims=True)
    scale = lax.rsqrt(variance + NORM_EPS)
    return centred * scale, scale


class LineGather:
    def __init__(self, stages, buffer, send_sem, recv_sem):
        self.stages, self.buffer, self.send_sem, self.recv_sem = stages, buffer, send_sem, recv_sem
        self.me, self.core, self.stage = place()
        self.partner = self.me + 1 - 2 * self.core

    def copy(self, block, way, target):
        return remote(
            self.buffer.at[block], self.buffer.at[block],
            self.send_sem.at[block, way], self.recv_sem.at[block], tensor=target,
        )

    def each_copy(self, block, right, left, act):
        pl.when(right)(lambda: act(self.copy(block, 0, self.me + 2)))
        pl.when(left)(lambda: act(self.copy(block, 1, self.me - 2)))
        act(self.copy(block, 2, self.partner))

    def start(self):
        self.each_copy(
            self.me, self.stage < self.stages - 1, self.stage > 0, lambda copy: copy.start()
        )

    def start_inward(self):
        low = self.stage < self.stages // 2
        self.each_copy(self.me, low, jnp.logical_not(low), lambda copy: copy.start())

    def start_outward(self):
        low = self.stage < self.stages // 2
        pl.when(jnp.logical_not(low) & (self.stage < self.stages - 1))(
            lambda: self.copy(self.me, 0, self.me + 2).start()
        )
        pl.when(low & (self.stage > 0))(lambda: self.copy(self.me, 1, self.me - 2).start())

    def incoming(self, reach, side, core):
        far = jnp.where(side == 0, self.stage - reach, self.stage + reach)
        return (far >= 0) & (far < self.stages), 2 * far + core

    def arrive(self, block):
        self.copy(block, 2, self.partner).wait_recv()

    def ways(self, side):
        return (side == 0) & (self.stage < self.stages - 1), (side == 1) & (self.stage > 0)

    def relay(self, reach):
        for side in range(2):
            valid, block = self.incoming(reach, side, self.core)

            @pl.when(valid)
            def _():
                self.arrive(block)
                self.each_copy(block, *self.ways(jnp.int32(side)), lambda copy: copy.start())

    def use_own(self, compute):
        compute(self.me)
        self.arrive(self.partner)
        compute(self.partner)

    def use(self, reach, compute):
        def body(index, carry):
            side, other = lax.rem(index, 2), lax.div(index, 2)
            valid, block = self.incoming(
                reach, side, jnp.where(other == 0, self.core, 1 - self.core)
            )

            @pl.when(valid)
            def _():
                pl.when(other == 1)(lambda: self.arrive(block))
                compute(block)

            return carry

        lax.fori_loop(0, 4, body, 0)

    def run(self, compute, after_first=lambda: None):
        def body(reach, carry):
            self.relay(reach)
            pl.when(reach == 1)(after_first)
            self.use(reach, compute)
            return carry

        self.use_own(compute)
        lax.fori_loop(1, self.stages, body, 0)

    def at_end(self):
        return (self.stage == 0) | (self.stage == self.stages - 1)

    def finish(self):
        self.each_copy(
            self.me, self.stage < self.stages - 1, self.stage > 0, lambda copy: copy.wait_send()
        )

        def body(index, carry):
            reach, side = lax.div(index, 2) + 1, lax.rem(index, 2)
            valid, block = self.incoming(reach, side, self.core)

            @pl.when(valid)
            def _():
                self.each_copy(block, *self.ways(side), lambda copy: copy.wait_send())

            return carry

        lax.fori_loop(0, 2 * (self.stages - 1), body, 0)


class LineScatter:
    def __init__(self, stages, partial, cross, lane, sems):
        self.stages, self.partial, self.cross, self.lane = stages, partial, cross, lane
        self.cross_send, self.cross_recv, self.lane_send, self.lane_recv = sems
        self.me, self.core, self.stage = place()
        self.partner = self.me + 1 - 2 * self.core

    def cross_copy(self, far):
        return remote(
            self.partial.at[2 * far + 1 - self.core], self.cross.at[far],
            self.cross_send.at[far], self.cross_recv.at[far], tensor=self.partner,
        )

    def slot(self, way, far, holder):
        return far if way == 0 else jnp.where(far == holder, self.stages, far)

    def lane_copy(self, way, far, holder):
        target = self.me + 2 if way == 0 else self.me - 2
        slot = self.slot(way, far, holder)
        return remote(
            self.partial.at[2 * far + self.core], self.lane.at[slot],
            self.lane_send.at[far], self.lane_recv.at[slot], tensor=target,
        )

    def sent(self, way, far):
        return self.lane_copy(way, far, self.stage + (1 if way == 0 else -1))

    def received(self, way, far):
        self.lane_copy(way, far, self.stage).wait_recv()
        return self.lane[self.slot(way, far, self.stage)].astype(F32)

    def put(self, block, value):
        self.partial[block] = value.astype(BF16)

        @pl.when(lax.rem(block, 2) != self.core)
        def _():
            self.cross_copy(lax.div(block, 2)).start()

    def produce(self, compute):
        def body(index, carry):
            reach = self.stages - 1 - lax.div(index, 4)
            side, other = lax.rem(lax.div(index, 2), 2), lax.rem(index, 2)
            far = jnp.where(side == 0, self.stage + reach, self.stage - reach)

            @pl.when((far >= 0) & (far < self.stages) & ((reach > 0) | (side == 0)))
            def _():
                block = 2 * far + jnp.where(other == 0, 1 - self.core, self.core)
                self.put(block, compute(block))

            return carry

        lax.fori_loop(0, 4 * self.stages, body, 0)

    def chip_sum(self, far):
        return self.partial[2 * far + self.core].astype(F32) + self.cross[far].astype(F32)

    def send_sum(self, way, far, incoming):
        self.cross_copy(far).wait_recv()
        block = 2 * far + self.core

        @pl.when(incoming)
        def _():
            self.partial[block] = (self.chip_sum(far) + self.received(way, far)).astype(BF16)

        @pl.when(jnp.logical_not(incoming))
        def _():
            self.partial[block] = self.chip_sum(far).astype(BF16)

        self.sent(way, far).start()

    def step(self, reach):
        right, left = self.stage + reach, self.stage - reach
        pl.when(right < self.stages)(lambda: self.send_sum(0, right, self.stage > 0))
        pl.when(left >= 0)(lambda: self.send_sum(1, left, self.stage < self.stages - 1))

    def steps(self, first, last):
        lax.fori_loop(first, last, lambda index, carry: (self.step(self.stages - 1 - index), carry)[1], 0)

    def own(self, total_ref):
        self.cross_copy(self.stage).wait_recv()
        total_ref[...] = self.chip_sum(self.stage)

        @pl.when(self.stage > 0)
        def _():
            total_ref[...] += self.received(0, self.stage)

        @pl.when(self.stage < self.stages - 1)
        def _():
            total_ref[...] += self.received(1, self.stage)

    def finish(self):
        def body(far, carry):
            self.cross_copy(far).wait_send()
            pl.when(far > self.stage)(lambda: self.sent(0, far).wait_send())
            pl.when(far < self.stage)(lambda: self.sent(1, far).wait_send())
            return carry

        lax.fori_loop(0, self.stages, body, 0)


def scatter_shapes(stages, rows, depth):
    return [
        VMEM((2 * stages, rows, depth), BF16), VMEM((stages, rows, depth), BF16),
        VMEM((stages + 1, rows, depth), BF16),
        DMA((stages,)), DMA((stages,)), DMA((stages,)), DMA((stages + 1,)),
    ]


def exchange(axis, size, slots, send_sem, recv_sem):
    me = lax.axis_index(axis)

    def copy_to(other, slot):
        return remote(
            slots.at[slot], slots.at[slot], send_sem.at[other], recv_sem.at[slot], **{axis: other}
        )

    def start(step, carry):
        copy_to(lax.rem(me + step, size), me).start()
        return carry

    def wait(step, carry):
        other = lax.rem(me + step, size)
        copy_to(other, other).wait_recv()
        copy_to(other, me).wait_send()
        return carry

    lax.fori_loop(1, size, start, 0)
    return lambda: lax.fori_loop(1, size, wait, 0)


def piece_height(height, parts):
    return -(-height // (16 * parts)) * 16


class RowSum:
    def __init__(self, parts, piece, arrive, send_sem, recv_sem):
        self.parts, self.piece, self.arrive = parts, piece, arrive
        self.send_sem, self.recv_sem = send_sem, recv_sem
        self.row = lax.axis_index("dp")

    def copy(self, other, source):
        return remote(
            self.piece.at[other], self.arrive.at[source],
            self.send_sem.at[other], self.recv_sem.at[source], dp=other,
        )

    def others(self, act, start):
        return lax.fori_loop(
            1, self.parts, lambda step, carry: act(lax.rem(self.row + step, self.parts), carry), start
        )

    def start(self, total):
        high = self.piece.shape[1]
        for part in range(self.parts):
            self.piece[part] = total[part * high : (part + 1) * high, :].astype(BF16)

        def send(other, carry):
            self.copy(other, self.row).start()
            return carry

        self.others(send, 0)

    def reduce(self):
        def add(other, so_far):
            self.copy(other, other).wait_recv()
            self.copy(other, self.row).wait_send()
            return so_far + self.arrive[other].astype(F32)

        return self.others(add, self.piece[self.row].astype(F32)).astype(BF16)


def rowsum_shapes(parts, high, depth):
    return [
        VMEM((parts, high, depth), BF16), VMEM((parts, high, depth), BF16), DMA((parts,)), DMA((parts,)),
    ]


def column(row):
    return jnp.broadcast_to(row, (128, row.shape[1])).T[:, :1]


def piece_rows(width, parts):
    return min(rows for rows in range(8, width + 1, 8) if width % rows == 0 and width // rows <= parts)


class WeightSpread:
    def __init__(self, stages, parts, buffer, sems):
        self.stages, self.parts, self.buffer = stages, parts, buffer
        self.line_send, self.line_recv, self.row_send, self.row_recv, self.core_send, self.core_recv = sems
        self.count = buffer.shape[0]
        self.me, self.core, self.stage = place()
        self.partner = self.me + 1 - 2 * self.core
        self.row = lax.axis_index("dp")
        self.here = self.row < self.count
        self.slot = jnp.minimum(self.row, self.count - 1)

    def copy(self, source, block, send_sem, recv_sem, **where):
        ref = self.buffer.at[source, block]
        return remote(ref, ref, send_sem, recv_sem, **where)

    def line_copy(self, other, far):
        return self.copy(
            self.slot, 2 * far + self.core, self.line_send.at[other], self.line_recv.at[far],
            tensor=2 * other + self.core,
        )

    def row_copy(self, other, source, far):
        return self.copy(
            source, 2 * far + self.core, self.row_send.at[other, far], self.row_recv.at[source, far],
            dp=other,
        )

    def core_copy(self, source, far, core):
        return self.copy(
            source, 2 * far + core, self.core_send.at[source, far], self.core_recv.at[source, far],
            tensor=self.partner,
        )

    def other_stages(self, act):
        def body(step, carry):
            act(lax.rem(self.stage + step, self.stages))
            return carry

        lax.fori_loop(1, self.stages, body, 0)

    def other_rows(self, act):
        def body(index, carry):
            step = lax.div(index, self.stages) + 1
            act(lax.rem(self.row + step, self.parts), lax.rem(index, self.stages))
            return carry

        lax.fori_loop(0, (self.parts - 1) * self.stages, body, 0)

    def pieces(self, act):
        def body(index, carry):
            act(lax.div(index, self.stages), lax.rem(index, self.stages))
            return carry

        lax.fori_loop(0, self.count * self.stages, body, 0)

    def start(self):
        self.other_stages(lambda other: self.line_copy(other, self.stage).start())

    def to_rows(self):
        self.other_stages(lambda other: self.line_copy(other, other).wait_recv())
        self.other_rows(lambda other, far: self.row_copy(other, self.slot, far).start())

    def pass_on(self):
        def act(source, far):
            pl.when(source != self.row)(lambda: self.row_copy(self.row, source, far).wait_recv())
            self.core_copy(source, far, self.core).start()

        self.pieces(act)

    def finish(self):
        @pl.when(self.here)
        def _():
            self.other_stages(lambda other: self.line_copy(other, self.stage).wait_send())
            self.other_rows(lambda other, far: self.row_copy(other, self.slot, far).wait_send())

        def act(source, far):
            self.core_copy(source, far, 1 - self.core).wait_recv()
            self.core_copy(source, far, self.core).wait_send()

        self.pieces(act)


def project_kernel(
    stages, parts, tok_hbm, g1_ref, b1_ref, bo_ref, g2_ref, b2_ref, bf2_ref, bf1_ref, bq_ref, bv_ref, wo_hbm, wq_hbm, wk_hbm, wv_hbm, ids_ref,
    norm_hbm, q_hbm, k_hbm, v_hbm, wo_out, vec_ref, span_ref, idr_ref, ido_ref,
    wo_all, line_send, line_recv, row_send, row_recv, core_send, core_recv, tok, norm, q_ref, k_ref, v_ref, weight, send_sem, recv_sem, out_sem, load_sem,
):
    me, _, _ = place()
    width, rows = wq_hbm.shape[0], tok.shape[0]
    loads = loading(
        load_sem,
        ((tok_hbm, tok), (wq_hbm, weight.at[0]), (wk_hbm, weight.at[1]), (wv_hbm, weight.at[2])),
    )
    spread = WeightSpread(
        stages, parts, wo_all, (line_send, line_recv, row_send, row_recv, core_send, core_recv)
    )
    high = wo_all.shape[2]
    own_piece = pltpu.make_async_copy(
        wo_hbm.at[pl.ds(pl.multiple_of(spread.slot * high, high), high)],
        wo_all.at[spread.slot, me], load_sem.at[4],
    )
    pl.when(spread.here)(own_piece.start)
    vec_ref[...] = jnp.zeros_like(vec_ref)
    for index, ref in enumerate(
        (g1_ref, b1_ref, bo_ref, g2_ref, b2_ref, bf2_ref, bf1_ref, bq_ref, bv_ref)
    ):
        vec_ref[index : index + 1, 0 : ref.shape[0]] = ref[...].astype(F32)[None, :]
    greet_peers((("tensor", 2 * stages), ("dp", parts)))
    loads[0].wait()
    normed, _ = normalize(tok[...].astype(F32))
    norm[me] = (normed * vec_ref[0:1, :] + vec_ref[1:2, :]).astype(BF16)
    gather = LineGather(stages, norm, send_sem, recv_sem)
    gather.start()

    @pl.when(spread.here)
    def _():
        own_piece.wait()
        spread.start()

    ids = ids_ref[...].astype(F32)
    idr_ref[...] = ids
    ido_ref[...] = idr_ref[:, pl.ds(pl.multiple_of(me * rows, rows), rows)]
    for block in range(ids.shape[1] // BLOCK):
        first = ids[:, block * BLOCK : block * BLOCK + 1]
        last = ids[:, (block + 1) * BLOCK - 1 : (block + 1) * BLOCK]
        begin = jnp.sum(jnp.where(ids > first, 1.0, 0.0))
        end = jnp.sum(jnp.where(ids >= jnp.maximum(last, 1.0), 1.0, 0.0))
        span_ref[0, block] = lax.div(begin.astype(jnp.int32), BLOCK)
        span_ref[1, block] = lax.div(end.astype(jnp.int32) + (BLOCK - 1), BLOCK)
    for load in loads[1:]:
        load.wait()

    def keep(block):
        return [
            pltpu.make_async_copy(src.at[block], dst.at[block], out_sem.at[index, block])
            for index, (src, dst) in enumerate(
                ((norm, norm_hbm), (q_ref, q_hbm), (k_ref, k_hbm), (v_ref, v_hbm))
            )
        ]

    def compute(block):
        q_ref[block] = (nt(norm[block], weight[0]) + vec_ref[7:8, :width]).astype(BF16)
        k_ref[block] = nt(norm[block], weight[1]).astype(BF16)
        v_ref[block] = (nt(norm[block], weight[2]) + vec_ref[8:9, :width]).astype(BF16)
        for copy in keep(block):
            copy.start()

    gather.run(compute, lambda: pl.when(spread.here)(spread.to_rows))
    spread.pass_on()
    gather.finish()
    spread.finish()
    out_copy = pltpu.make_async_copy(wo_all, wo_out, load_sem.at[5])
    out_copy.start()

    def kept(block, carry):
        for copy in keep(block):
            copy.wait()
        return carry

    lax.fori_loop(0, 2 * stages, kept, 0)
    out_copy.wait()


def project(tokens, vectors, wo, wq, wk, wv, ids, devices, parts):
    rows, depth = tokens.shape
    width, length = wq.shape[1], ids.shape[1]
    stages = devices // 2
    high = piece_rows(width, parts)
    head = jax.ShapeDtypeStruct((devices, rows, width), BF16)
    pieces = (width // high, devices, high, depth)
    return pl.pallas_call(
        functools.partial(project_kernel, stages, parts),
        name="project",
        out_shape=(
            jax.ShapeDtypeStruct((devices, rows, depth), BF16), head, head, head,
            jax.ShapeDtypeStruct(pieces, BF16), jax.ShapeDtypeStruct((16, depth), F32),
            jax.ShapeDtypeStruct((2, length // BLOCK), jnp.int32),
            jax.ShapeDtypeStruct((1, length), F32), jax.ShapeDtypeStruct((1, rows), F32),
        ),
        in_specs=[HBM] + [VSPEC] * 9 + [HBM, HBM, HBM, HBM, VSPEC],
        out_specs=(HBM, HBM, HBM, HBM, HBM, VSPEC, SSPEC, VSPEC, VSPEC),
        scratch_shapes=[
            VMEM(pieces, BF16), DMA((stages,)), DMA((stages,)),
            *[DMA((parts, stages))] * 4,
            VMEM((rows, depth), BF16), VMEM((devices, rows, depth), BF16),
            *[VMEM((devices, rows, width), BF16)] * 3, VMEM((3, width, depth), BF16),
            DMA((devices, 3)), DMA((devices,)), DMA((4, devices)), DMA((6,)),
        ],
        compiler_params=pltpu.CompilerParams(
            collective_id=0, has_side_effects=True, vmem_limit_bytes=VMEM_ALL
        ),
    )(tokens, *vectors, wo, wq.T, wk.T, wv.T, ids)


def lanes_of(head, width):
    lane = lax.broadcasted_iota(jnp.int32, (1, width), 1)
    return (lane >= head * HD) & (lane < (head + 1) * HD)


def fill_columns(row_ref, column_ref):
    for block in range(row_ref.shape[1] // BLOCK):
        at = pl.ds(block * BLOCK, BLOCK)
        column_ref[at, :] = column(row_ref[:, at])


def head_rows(head, width):
    row = lax.broadcasted_iota(jnp.int32, (width, 1), 0)
    return (row >= head * HD) & (row < (head + 1) * HD)


def side_by_side(block_t, heads):
    width = block_t.shape[0]
    zero = jnp.zeros_like(block_t)
    return jnp.concatenate([jnp.where(head_rows(h, width), block_t, zero) for h in range(heads)], axis=1)


def stacked(block, heads):
    width = block.shape[1]
    zero = jnp.zeros_like(block)
    return jnp.concatenate([jnp.where(lanes_of(h, width), block, zero) for h in range(heads)], axis=0)


def repeat_lanes(row, heads):
    return jnp.concatenate([row] * heads, axis=1)


def attend_kernel(
    heads, span_ref, q_hbm, k_hbm, v_hbm, idr_ref, o_ref, log_ref,
    q_ref, k_ref, v_ref, load_sem, idc_ref, vt_ref, acc_ref,
):
    length, width = q_ref.shape
    scale = HD ** (-0.5) * LOG2E
    loads = loading(load_sem, ((v_hbm, v_ref), (q_hbm, q_ref), (k_hbm, k_ref)))
    fill_columns(idr_ref, idc_ref)
    for load in loads:
        load.wait()

    def turn(block, total):
        at = pl.ds(pl.multiple_of(block * BLOCK, BLOCK), BLOCK)
        value = v_ref[at, :].astype(F32)
        vt_ref[block] = value.T.astype(BF16)
        return total + jnp.sum(value, axis=0, keepdims=True)

    mean_value = lax.fori_loop(0, length // BLOCK, turn, jnp.zeros((1, width), F32)) * (1.0 / length)

    def per_block(block, carry):
        at = pl.ds(pl.multiple_of(block * BLOCK, BLOCK), BLOCK)
        query = side_by_side(q_ref[at, :].astype(F32).T.astype(BF16), heads)
        id_row = idr_ref[:, at]
        id_rows = repeat_lanes(id_row, heads)
        acc_ref[...] = jnp.zeros_like(acc_ref)

        def per_key(other, state):
            top, total = state
            keys_at = pl.ds(pl.multiple_of(other * BLOCK, BLOCK), BLOCK)
            id_col = idc_ref[keys_at, :]
            allowed = (id_col == id_rows) & (id_col > 0)
            scores = jnp.where(allowed, nn(k_ref[keys_at, :], query) * scale, NEG_FILL)
            new_top = jnp.maximum(top, jnp.max(scores, axis=0, keepdims=True))
            weight = jnp.exp2(scores - new_top)
            shrink = jnp.exp2(top - new_top)
            total = total * shrink + jnp.sum(weight, axis=0, keepdims=True)
            acc_ref[...] = acc_ref[...] * shrink + nn(vt_ref[other], weight.astype(BF16))
            return new_top, total

        top, total = lax.fori_loop(
            span_ref[0, block], span_ref[1, block], per_key,
            (jnp.full((1, heads * BLOCK), NEG_FILL, F32), jnp.zeros((1, heads * BLOCK), F32)),
        )
        scaled = acc_ref[...] / total
        logs = jnp.where(id_rows == 0, 0.0, top + jnp.log2(total))
        result = jnp.zeros((width, BLOCK), F32)
        for h in range(heads):
            here = slice(h * BLOCK, (h + 1) * BLOCK)
            result = jnp.where(head_rows(h, width), scaled[:, here], result)
            log_ref[h : h + 1, at] = logs[:, here]
        o_ref[at, :] = jnp.where(idc_ref[at, :] == 0, mean_value, result.T).astype(BF16)
        return carry

    lax.fori_loop(0, length // BLOCK, per_block, 0)


def attend(q, k, v, span, id_row):
    length, width = q.shape
    heads = width // HD
    return pl.pallas_call(
        functools.partial(attend_kernel, heads),
        name="attend",
        out_shape=(
            jax.ShapeDtypeStruct((length, width), BF16),
            jax.ShapeDtypeStruct((heads, length), F32),
        ),
        in_specs=[SSPEC, HBM, HBM, HBM, VSPEC],
        out_specs=(VSPEC,) * 2,
        scratch_shapes=[
            *[VMEM((length, width), BF16)] * 3, DMA((3,)),
            VMEM((length, 1), F32), VMEM((length // BLOCK, width, BLOCK), BF16),
            VMEM((width, heads * BLOCK), F32),
        ],
        compiler_params=pltpu.CompilerParams(vmem_limit_bytes=VMEM_ALL),
    )(span, q, k, v, id_row)


def attend_back_kernel(
    heads, span_ref, q_hbm, k_hbm, v_hbm, idr_ref, o_hbm, log_ref, g_hbm, fc_hbm, layer_hbm,
    out_ref, fc1_hbm, fc2_hbm, layer_out, fc, fc1, fc2, layer, side_sem, q_ref, k_ref, v_ref, o_ref, g_ref, load_sem,
    idc_ref, dq_ref, dk_ref, dv_ref, q_side, q_stack, g_side, g_stack, row_ref, log_side,
):
    length, width = q_ref.shape
    score_scale = HD ** (-0.5)
    loads = loading(
        load_sem, ((q_hbm, q_ref), (g_hbm, g_ref), (o_hbm, o_ref), (k_hbm, k_ref), (v_hbm, v_ref))
    )
    layer_in = pltpu.make_async_copy(layer_hbm, layer, side_sem.at[0])
    fc_in = pltpu.make_async_copy(fc_hbm, fc, side_sem.at[1])
    layer_in.start()
    fc_in.start()
    dq_ref[...] = jnp.zeros_like(dq_ref)
    fill_columns(idr_ref, idc_ref)
    for load in loads:
        load.wait()

    def prepare(block, pad):
        at = pl.ds(pl.multiple_of(block * BLOCK, BLOCK), BLOCK)
        query, grad = q_ref[at, :], g_ref[at, :]
        wide = grad.astype(F32)
        grad_t = wide.T
        product = (wide * o_ref[at, :].astype(F32)).T
        q_side[block] = side_by_side(query.astype(F32).T.astype(BF16), heads)
        g_side[block] = side_by_side(grad_t.astype(BF16), heads)
        q_stack[block] = stacked(query, heads)
        g_stack[block] = stacked(grad, heads)
        for h in range(heads):
            here = slice(h * BLOCK, (h + 1) * BLOCK)
            row_ref[block, :, here] = jnp.sum(
                jnp.where(head_rows(h, width), product, 0.0), axis=0, keepdims=True
            )
            log_side[block, :, here] = log_ref[h : h + 1, at]
        return pad + jnp.sum(jnp.where(idc_ref[at, :] == 0, wide, 0.0), axis=0, keepdims=True)

    pad = lax.fori_loop(0, length // BLOCK, prepare, jnp.zeros((1, width), F32)) * (1.0 / length)
    units = fc1.shape[0]
    second = -(-units // 16) * 16
    layer_in.wait()
    fc_in.wait()
    fc1[...] = fc[0:units, :].astype(F32)
    fc2[...] = fc[second : second + units, :].astype(F32)
    outs = [
        pltpu.make_async_copy(src, dst, side_sem.at[2 + index])
        for index, (src, dst) in enumerate(((layer, layer_out), (fc1, fc1_hbm), (fc2, fc2_hbm)))
    ]
    for out in outs:
        out.start()

    def per_key(block, carry):
        at = pl.ds(pl.multiple_of(block * BLOCK, BLOCK), BLOCK)
        key, value, id_col = k_ref[at, :], v_ref[at, :], idc_ref[at, :]
        key_side = side_by_side(key.astype(F32).T.astype(BF16), heads)
        real = id_col > 0
        dk_ref[...] = jnp.zeros_like(dk_ref)
        dv_ref[...] = jnp.zeros_like(dv_ref)

        def per_query(other, inner):
            query_at = pl.ds(pl.multiple_of(other * BLOCK, BLOCK), BLOCK)
            allowed = (id_col == repeat_lanes(idr_ref[:, query_at], heads)) & real
            scores = nn(key, q_side[other]) * (score_scale * LOG2E) - log_side[other]
            prob = jnp.exp2(jnp.where(allowed, scores, NEG_FILL))
            dv_ref[...] += nn(prob.astype(BF16), g_stack[other])
            back = (prob * (nn(value, g_side[other]) - row_ref[other])).astype(BF16)
            dk_ref[...] += nn(back, q_stack[other])
            back_rows = jnp.concatenate(
                [back[:, h * BLOCK : (h + 1) * BLOCK] for h in range(heads)], axis=0
            )
            dq_ref[other] += nn(key_side, back_rows)
            return inner

        lax.fori_loop(span_ref[0, block], span_ref[1, block], per_query, 0)
        out_ref[at, width : 2 * width] = (dk_ref[...] * score_scale).astype(BF16)
        out_ref[at, 2 * width :] = (dv_ref[...] + pad).astype(BF16)
        return carry

    lax.fori_loop(0, length // BLOCK, per_key, 0)

    def settle(block, carry):
        at = pl.ds(pl.multiple_of(block * BLOCK, BLOCK), BLOCK)
        out_ref[at, :width] = (dq_ref[block].T * score_scale).astype(BF16)
        return carry

    lax.fori_loop(0, length // BLOCK, settle, 0)
    for out in outs:
        out.wait()


def attend_back(q, k, v, span, id_row, o, log_total, grad, fc, layer, units):
    length, width = q.shape
    heads = width // HD
    blocks, depth = length // BLOCK, layer.shape[1]
    whole = VMEM((length, width), BF16)
    side, stack = VMEM((blocks, width, heads * BLOCK), BF16), VMEM((blocks, heads * BLOCK, width), BF16)
    line = VMEM((blocks, 1, heads * BLOCK), F32)
    return pl.pallas_call(
        functools.partial(attend_back_kernel, heads),
        name="attend_back",
        out_shape=(
            jax.ShapeDtypeStruct((length, 3 * width), BF16), jax.ShapeDtypeStruct((units, depth), F32),
            jax.ShapeDtypeStruct((units, depth), F32), jax.ShapeDtypeStruct(layer.shape, BF16),
        ),
        in_specs=[SSPEC, HBM, HBM, HBM, VSPEC, HBM, VSPEC, HBM, HBM, HBM],
        out_specs=(VSPEC, HBM, HBM, HBM),
        scratch_shapes=[
            VMEM(fc.shape, BF16), VMEM((units, depth), F32), VMEM((units, depth), F32),
            VMEM(layer.shape, BF16), DMA((5,)),
            whole, whole, whole, whole, whole, DMA((5,)),
            VMEM((length, 1), F32), VMEM((blocks, width, BLOCK), F32), VMEM((BLOCK, width), F32),
            VMEM((BLOCK, width), F32), side, stack, side, stack, line, line,
        ],
        compiler_params=pltpu.CompilerParams(vmem_limit_bytes=VMEM_ALL),
    )(span, q, k, v, id_row, o, log_total, grad, fc, layer)


def gelu_pair(u):
    slope = (2.0 / jnp.pi) ** 0.5
    bent = jnp.tanh(slope * (u + 0.044715 * u * u * u))
    half = 0.5 * (1.0 + bent)
    return u * half, half + 0.5 * u * (1.0 - bent * bent) * slope * (1.0 + 3 * 0.044715 * u * u)


def middle_kernel(
    stages, parts, att_hbm, wo_hbm, fc1_hbm, fc2_hbm, tok_hbm, top_hbm, ids_ref, vec_ref,
    out_ref, gres_ref, gatt_ref, fc_hbm, small_ref,
    wo, fc1, fc2, tok, top, load_sem,
    held, held_send, held_recv, norm_all, norm_send, norm_recv, top_all, top_send, top_recv,
    hidden, slope, grad_pre,
    br_part, br_cross, br_lane, br_s0, br_s1, br_s2, br_s3,
    gn_part, gn_cross, gn_lane, gn_s0, gn_s1, gn_s2, gn_s3,
    resid, total, acc, piece, arrive, piece_send, piece_recv, fa_send, fa_recv, free_sem, out_sem,
    back, back_send, back_recv,
):
    me, _, _ = place()
    devices = 2 * stages
    rows, depth = tok_hbm.shape
    high = wo_hbm.shape[2]
    units = fc1_hbm.shape[0]
    second = -(-units // 16) * 16
    loads = loading(
        load_sem,
        ((tok_hbm, tok), (top_hbm, top), (fc1_hbm, fc1), (fc2_hbm, fc2), (att_hbm.at[me], held.at[me]),
         *((wo_hbm.at[index], wo.at[:, pl.ds(index * high, high)]) for index in range(wo_hbm.shape[0]))),
    )
    greet_peers((("tensor", devices), ("dp", parts)))

    def held_copy(other, source):
        return remote(
            att_hbm.at[other], held.at[source], held_send.at[other], held_recv.at[source], tensor=other
        )

    def send_held(step, carry):
        held_copy(lax.rem(me + step, devices), me).start()
        return carry

    lax.fori_loop(1, devices, send_held, 0)
    gather2 = LineGather(stages, norm_all, norm_send, norm_recv)
    gather3 = LineGather(stages, top_all, top_send, top_recv)
    branch = LineScatter(stages, br_part, br_cross, br_lane, (br_s0, br_s1, br_s2, br_s3))
    gnorm = LineScatter(stages, gn_part, gn_cross, gn_lane, (gn_s0, gn_s1, gn_s2, gn_s3))

    mask = column(jnp.where(ids_ref[...] > 0, 1.0, 0.0))
    acc[...] = jnp.zeros_like(acc)
    small_ref[...] = jnp.zeros_like(small_ref)
    loads[0].wait()
    loads[1].wait()
    top_own = top[...].astype(F32) * mask
    top_all[me] = top_own.astype(BF16)
    small_ref[5:6, :] = jnp.sum(top_own, axis=0, keepdims=True)
    resid[...] = tok[...].astype(F32) + vec_ref[2:3, :]
    for load in loads[4:]:
        load.wait()
    resid[...] += nn(held[me], wo[me])

    def add_held(step, carry):
        other = lax.rem(me + devices - step, devices)
        held_copy(other, other).wait_recv()
        resid[...] += nn(held[other], wo[other])
        return carry

    lax.fori_loop(1, devices, add_held, 0)
    normed, _ = normalize(resid[...])
    norm_all[me] = (normed * vec_ref[3:4, :] + vec_ref[4:5, :]).astype(BF16)
    gather2.start()
    loads[2].wait()
    loads[3].wait()

    def forward(block):
        pre_act = nt(norm_all[block], fc1[...]) + vec_ref[6:7, 0:units]
        value, slope_now = gelu_pair(pre_act)
        hidden[block] = value.astype(BF16)
        slope[block] = slope_now.astype(BF16)
        branch.put(block, nn(hidden[block], fc2[...]))

    at_end = gather2.at_end()
    gather2.run(forward, lambda: pl.when(at_end)(gather3.start_inward))
    pl.when(jnp.logical_not(at_end))(gather3.start_inward)
    gather3.start_outward()
    pl.when(at_end)(lambda: branch.steps(0, stages - 1))

    def backward(block):
        grad = nt(top_all[block], fc2[...]) * slope[block].astype(F32)
        low = grad.astype(BF16)
        grad_pre[block] = low
        small_ref[7:8, 0:units] += jnp.sum(low.astype(F32), axis=0, keepdims=True)
        gnorm.put(block, nn(grad_pre[block], fc1[...]))
        acc[0:units, :] += tn(grad_pre[block], norm_all[block])
        acc[second : second + units, :] += tn(hidden[block], top_all[block])

    gather3.run(backward)
    gnorm.step(stages - 1)
    sums = RowSum(parts, piece, arrive, piece_send, piece_recv)
    sums.start(acc)

    pl.when(jnp.logical_not(at_end))(lambda: branch.steps(1, stages - 1))
    gnorm.steps(1, stages - 1)
    fc_sum = sums.reduce()

    def to_rows(act):
        lax.fori_loop(
            1, parts, lambda step, carry: (act(lax.rem(sums.row + step, parts)), carry)[1], 0
        )

    to_rows(
        lambda other: pl.semaphore_signal(
            free_sem, inc=1, device_id={"dp": other}, device_id_type=MESH
        )
    )
    pl.semaphore_wait(free_sem, parts - 1)
    arrive[sums.row] = fc_sum
    wait_fc = exchange("dp", parts, arrive, fa_send, fa_recv)
    branch.own(total)
    out_ref[...] = (mask * (resid[...] + total[...] + vec_ref[5:6, :])).astype(BF16)

    gnorm.own(total)
    grad = total[...]
    normed, scale = normalize(resid[...])
    small_ref[2:3, :] = jnp.sum(grad * normed, axis=0, keepdims=True)
    small_ref[3:4, :] = jnp.sum(grad, axis=0, keepdims=True)
    inner = grad * vec_ref[3:4, :]
    inner_mean = jnp.mean(inner, axis=-1, keepdims=True)
    inner_proj = jnp.mean(inner * normed, axis=-1, keepdims=True)
    grad_resid = top[...].astype(F32) * mask + scale * (inner - inner_mean - normed * inner_proj)
    gres_ref[...] = grad_resid
    tok[...] = grad_resid.astype(BF16)
    small_ref[4:5, :] = jnp.sum(grad_resid, axis=0, keepdims=True)

    def back_copy(other, source):
        return remote(
            back.at[other], gatt_ref.at[source], back_send.at[other], back_recv.at[source], tensor=other
        )

    def send_back(step, carry):
        other = lax.rem(me + step, devices)
        back[other] = nt(tok[...], wo[other]).astype(BF16)
        back_copy(other, me).start()
        return carry

    lax.fori_loop(1, devices, send_back, 0)
    gatt_ref[me] = nt(tok[...], wo[me]).astype(BF16)

    wait_fc()
    out_fc = pltpu.make_async_copy(arrive, fc_hbm, out_sem)
    out_fc.start()

    def settle(step, carry):
        other = lax.rem(me + devices - step, devices)
        back_copy(other, other).wait_recv()
        back_copy(other, me).wait_send()
        held_copy(other, me).wait_send()
        return carry

    lax.fori_loop(1, devices, settle, 0)
    gather2.finish()
    gather3.finish()
    branch.finish()
    gnorm.finish()
    out_fc.wait()


def middle(att, wo, fc1, fc2, tokens, out_grad, ids, vectors, parts):
    devices, rows, width = att.shape
    depth, units = fc1.shape
    stages = devices // 2
    high = piece_height(2 * (-(-units // 16) * 16), parts)
    return pl.pallas_call(
        functools.partial(middle_kernel, stages, parts),
        name="middle",
        out_shape=(
            jax.ShapeDtypeStruct((rows, depth), BF16),
            jax.ShapeDtypeStruct((rows, depth), F32),
            jax.ShapeDtypeStruct((devices, rows, width), BF16),
            jax.ShapeDtypeStruct((parts, high, depth), BF16),
            jax.ShapeDtypeStruct((8, depth), F32),
        ),
        in_specs=[HBM] * 6 + [VSPEC] * 2,
        out_specs=(VSPEC, VSPEC, VSPEC, HBM, VSPEC),
        scratch_shapes=[
            VMEM((devices, width, depth), BF16), VMEM((units, depth), BF16), VMEM((units, depth), BF16),
            VMEM((rows, depth), BF16), VMEM((rows, depth), BF16), DMA((5 + wo.shape[0],)),
            VMEM((devices, rows, width), BF16), DMA((devices,)), DMA((devices,)),
            VMEM((devices, rows, depth), BF16), DMA((devices, 3)), DMA((devices,)),
            VMEM((devices, rows, depth), BF16), DMA((devices, 3)), DMA((devices,)),
            VMEM((devices, rows, units), BF16), VMEM((devices, rows, units), BF16),
            VMEM((devices, rows, units), BF16),
            *scatter_shapes(stages, rows, depth), *scatter_shapes(stages, rows, depth),
            VMEM((rows, depth), F32), VMEM((rows, depth), F32),
            VMEM((parts * high, depth), F32), *rowsum_shapes(parts, high, depth),
            DMA((parts,)), DMA((parts,)), pltpu.SemaphoreType.REGULAR, DMA,
            VMEM((devices, rows, width), BF16), DMA((devices,)), DMA((devices,)),
        ],
        compiler_params=pltpu.CompilerParams(
            collective_id=2, has_side_effects=True, vmem_limit_bytes=VMEM_ALL
        ),
    )(
        att, wo, fc1.T, fc2, tokens, out_grad, ids, vectors,
    )


def close_kernel(
    stages, parts, dx_hbm, wq_hbm, wk_hbm, wv_hbm, norm_hbm, att_hbm, tok_hbm, vec_ref, resid_hbm,
    small_ref,
    gtok_ref, gw_hbm, go_hbm, gsmall_ref,
    dx_ref, weight, norm, att_ref, tok_ref, resid_ref, load_sem, gatt_all, gatt_send, gatt_recv,
    partial, cross, lane, cross_send, cross_recv, lane_send, lane_recv,
    total, acc, acc_o, w_piece, w_arrive, w_send, w_recv, o_piece, o_arrive, o_send, o_recv,
    w_all, o_all, wa_send, wa_recv, oa_send, oa_recv, out_sem,
    slots_t, slots_d, st_send, st_recv, sd_send, sd_recv,
):
    me, _, _ = place()
    row = lax.axis_index("dp")
    devices = 2 * stages
    wide, width = dx_ref.shape[2], att_ref.shape[2]
    loads = loading(
        load_sem,
        ((resid_hbm, resid_ref), (dx_hbm, dx_ref),
         *((src, weight.at[pl.ds(index * width, width)]) for index, src in enumerate((wq_hbm, wk_hbm, wv_hbm))),
         (norm_hbm, norm), (att_hbm, att_ref), (tok_hbm, tok_ref)),
    )
    greet_peers((("tensor", devices), ("dp", parts)))
    loads[0].wait()
    gatt_all[me] = resid_ref[...].astype(BF16)
    gather = LineGather(stages, gatt_all, gatt_send, gatt_recv)
    gather.start()
    for load in loads[1:5]:
        load.wait()
    scatter = LineScatter(
        stages, partial, cross, lane, (cross_send, cross_recv, lane_send, lane_recv)
    )
    scatter.produce(lambda block: nn(dx_ref[block], weight[...]))
    scatter.step(stages - 1)

    acc[...] = jnp.zeros_like(acc)
    acc_o[...] = jnp.zeros_like(acc_o)
    for load in loads[5:]:
        load.wait()

    def weight_block(block, bias):
        grad = dx_ref[block]
        acc[0:wide, :] += tn(grad, norm[block])
        return bias + jnp.sum(grad.astype(F32), axis=0, keepdims=True)

    bias = lax.fori_loop(0, devices, weight_block, jnp.zeros((1, wide), F32))
    w_sum = RowSum(parts, w_piece, w_arrive, w_send, w_recv)
    w_sum.start(acc)

    def weight_o(block):
        acc_o[0:width, :] += tn(att_ref[block], gatt_all[block])

    gather.use_own(weight_o)

    def both(reach, carry):
        gather.relay(reach)
        pl.when(reach < stages - 1)(lambda: scatter.step(stages - 1 - reach))
        gather.use(reach, weight_o)
        return carry

    lax.fori_loop(1, min(2, stages), both, 0)
    w_all[row] = w_sum.reduce()
    wait_w = exchange("dp", parts, w_all, wa_send, wa_recv)
    lax.fori_loop(min(2, stages), stages, both, 0)
    o_sum = RowSum(parts, o_piece, o_arrive, o_send, o_recv)
    o_sum.start(acc_o)
    o_all[row] = o_sum.reduce()
    wait_o = exchange("dp", parts, o_all, oa_send, oa_recv)

    scatter.own(total)
    grad = total[...]
    normed, scale = normalize(tok_ref[...].astype(F32))
    slots_t[me] = small_ref[...]
    slots_t[me, 0:1, :] = jnp.sum(grad * normed, axis=0, keepdims=True)
    slots_t[me, 1:2, :] = jnp.sum(grad, axis=0, keepdims=True)
    slots_t[me, 6:7, 0:wide] = bias
    wait_small = exchange("tensor", devices, slots_t, st_send, st_recv)
    inner = grad * vec_ref[0:1, :]
    inner_mean = jnp.mean(inner, axis=-1, keepdims=True)
    inner_proj = jnp.mean(inner * normed, axis=-1, keepdims=True)
    gtok_ref[...] = resid_ref[...] + scale * (inner - inner_mean - normed * inner_proj)
    wait_small()
    sums = lax.fori_loop(
        1, devices, lambda slot, so_far: so_far + slots_t[slot], slots_t[0]
    )
    line = lax.broadcasted_iota(jnp.int32, sums.shape, 0)
    slots_d[row] = jnp.where(line < 6, sums, slots_t[me])
    wait_last = exchange("dp", parts, slots_d, sd_send, sd_recv)
    outs = []
    for index, (wait, src, dst) in enumerate(
        ((wait_w, w_all, gw_hbm), (wait_o, o_all, go_hbm))
    ):
        wait()
        out = pltpu.make_async_copy(src, dst, out_sem.at[index])
        out.start()
        outs.append(out)
    wait_last()
    gsmall_ref[...] = lax.fori_loop(
        1, parts, lambda slot, so_far: so_far + slots_d[slot], slots_d[0]
    )
    gather.finish()
    scatter.finish()
    for out in outs:
        out.wait()


def close(dx, wq, wk, wv, norm, att, tokens, vectors, resid, small, parts):
    devices, rows, wide = dx.shape
    depth = tokens.shape[1]
    stages = devices // 2
    width = wide // 3
    w_high, o_high = piece_height(wide, parts), piece_height(width, parts)
    pieces = [(parts, high, depth) for high in (w_high, o_high)]
    return pl.pallas_call(
        functools.partial(close_kernel, stages, parts),
        name="close",
        out_shape=(
            jax.ShapeDtypeStruct((rows, depth), F32),
            *(jax.ShapeDtypeStruct(shape, BF16) for shape in pieces),
            jax.ShapeDtypeStruct(small.shape, F32),
        ),
        in_specs=[HBM] * 7 + [VSPEC, HBM, VSPEC],
        out_specs=(VSPEC, HBM, HBM, VSPEC),
        scratch_shapes=[
            VMEM((devices, rows, wide), BF16), VMEM((wide, depth), BF16),
            VMEM((devices, rows, depth), BF16), VMEM((devices, rows, width), BF16),
            VMEM((rows, depth), BF16), VMEM((rows, depth), F32), DMA((8,)),
            VMEM((devices, rows, depth), BF16), DMA((devices, 3)), DMA((devices,)),
            *scatter_shapes(stages, rows, depth),
            VMEM((rows, depth), F32), VMEM((parts * w_high, depth), F32),
            VMEM((parts * o_high, depth), F32),
            *rowsum_shapes(parts, w_high, depth), *rowsum_shapes(parts, o_high, depth),
            *(VMEM(shape, BF16) for shape in pieces), *[DMA((parts,))] * 4, DMA((2,)),
            VMEM((devices,) + small.shape, F32), VMEM((parts,) + small.shape, F32),
            DMA((devices,)), DMA((devices,)), DMA((parts,)), DMA((parts,)),
        ],
        compiler_params=pltpu.CompilerParams(
            collective_id=1, has_side_effects=True, vmem_limit_bytes=VMEM_ALL
        ),
    )(dx, wq.T, wk.T, wv.T, norm, att, tokens, vectors, resid, small)


def settle_kernel(
    gtok_hbm, gw_hbm, go_hbm, sums_ref,
    gtok_out, wq_ref, wk_ref, wv_ref, wo_ref,
    g1_ref, b1_ref, g2_ref, b2_ref, bo_ref, bf2_ref, bq_ref, bv_ref, bf1_ref,
    gtok, gw, go, sems,
):
    width, units = wq_ref.shape[0], bf1_ref.shape[0]
    loads = loading(sems, ((gtok_hbm, gtok), (gw_hbm, gw), (go_hbm, go)))
    for row, ref in enumerate((g1_ref, b1_ref, g2_ref, b2_ref, bo_ref, bf2_ref)):
        ref[...] = sums_ref[row, :]
    bq_ref[...] = sums_ref[6:7, 0:width].reshape(width)
    bv_ref[...] = sums_ref[6:7, 2 * width : 3 * width].reshape(width)
    bf1_ref[...] = sums_ref[7:8, 0:units].reshape(units)
    loads[0].wait()
    out = pltpu.make_async_copy(gtok, gtok_out, sems.at[3])
    out.start()
    loads[1].wait()
    loads[2].wait()
    wq_ref[...] = gw[0:width, :].astype(F32)
    wk_ref[...] = gw[width : 2 * width, :].astype(F32)
    wv_ref[...] = gw[2 * width : 3 * width, :].astype(F32)
    wo_ref[...] = go[0:width, :].astype(F32)
    out.wait()


def settle(gtok, gw, go, sums, width, units):
    depth = gtok.shape[1]
    weight = jax.ShapeDtypeStruct((width, depth), F32)
    return pl.pallas_call(
        settle_kernel,
        name="settle",
        out_shape=(
            jax.ShapeDtypeStruct(gtok.shape, F32), weight, weight, weight, weight,
            *(jax.ShapeDtypeStruct((size,), F32) for size in (depth,) * 6 + (width, width, units)),
        ),
        in_specs=[HBM, HBM, HBM, VSPEC],
        out_specs=(HBM,) + (VSPEC,) * 13,
        scratch_shapes=[
            VMEM(gtok.shape, F32), VMEM(gw.shape, BF16), VMEM(go.shape, BF16), DMA((4,)),
        ],
        compiler_params=pltpu.CompilerParams(vmem_limit_bytes=VMEM_ALL),
    )(gtok, gw, go, sums)


def on_device(
    devices, parts, tokens, picture_ids, ln1_gain, ln1_bias, q_weight, q_bias, k_weight, v_weight, v_bias,
    o_weight, o_bias, ln2_gain, ln2_bias, fc1_weight, fc1_bias, fc2_weight, fc2_bias, out_grad,
):
    own_count, depth = tokens.shape
    hidden_local = fc1_weight.shape[1]
    width = q_weight.shape[1]
    norm1_all, q, k, v, o_all, vectors, span, id_row, own_ids = project(
        tokens,
        (ln1_gain, ln1_bias, o_bias, ln2_gain, ln2_bias, fc2_bias, fc1_bias, q_bias, v_bias),
        o_weight, q_weight, k_weight, v_weight, picture_ids[None, :], devices, parts,
    )
    q, k, v = (item.reshape(LEN, width) for item in (q, k, v))
    attended, log_total = attend(q, k, v, span, id_row)
    heads_first = attended.reshape(devices, own_count, width)
    output, grad_residual, grad_attended, fc_sum, small = middle(
        heads_first, o_all, fc1_weight, fc2_weight, tokens, out_grad,
        own_ids, vectors, parts,
    )
    dqkv, grad_fc1, grad_fc2, output = attend_back(
        q, k, v, span, id_row, attended, log_total, grad_attended.reshape(LEN, width),
        fc_sum.reshape(-1, depth), output, hidden_local,
    )
    grad_tokens, grad_w, grad_o, sums = close(
        dqkv.reshape(devices, own_count, 3 * width), q_weight, k_weight, v_weight, norm1_all,
        heads_first, tokens, vectors, grad_residual, small, parts,
    )
    (
        grad_tokens, grad_q, grad_k, grad_v, grad_o, grad_g1, grad_b1, grad_g2, grad_b2, grad_bo,
        grad_bf2, grad_bq, grad_bv, grad_bf1,
    ) = settle(
        grad_tokens, grad_w.reshape(-1, depth), grad_o.reshape(-1, depth), sums, width, hidden_local
    )
    return (
        output, grad_tokens, grad_g1, grad_b1, grad_q.T, grad_bq, grad_k.T, grad_v.T, grad_bv,
        grad_o, grad_bo, grad_g2, grad_b2, grad_fc1.T, grad_bf1, grad_fc2, grad_bf2,
    )


def solution(mesh):
    rows, whole = P(("dp", "tensor"), None), P()
    columns, down, along = P(None, "tensor"), P("tensor", None), P("tensor")
    return jax.shard_map(
        functools.partial(on_device, mesh.shape["tensor"], mesh.shape["dp"]),
        mesh=mesh,
        in_specs=(
            rows, P("dp"), whole, whole, columns, along, columns, columns, along, down, whole,
            whole, whole, columns, along, down, whole, rows,
        ),
        out_specs=(
            rows, rows, whole, whole, columns, along, columns, columns, along, down, whole,
            whole, whole, columns, along, down, whole,
        ),
        check_vma=False,
    )
```

```python
import functools

import jax
import jax.numpy as jnp
from jax import lax
from jax.experimental import pallas as pl
from jax.experimental.pallas import tpu as pltpu
from jax.sharding import PartitionSpec as P

HD = 72
LEN = 2048
BLOCK = 256
NORM_EPS = 1e-06
NEG_FILL = -1e30
LOG2E = 1.4426950408889634
VMEM_ALL = 67043328
BF16 = jnp.bfloat16
F32 = jnp.float32
MESH = pl.DeviceIdType.MESH
VMEM = pltpu.VMEM
DMA = pltpu.SemaphoreType.DMA
VSPEC = pl.BlockSpec(memory_space=pltpu.VMEM)
SSPEC = pl.BlockSpec(memory_space=pltpu.SMEM)
HBM = pl.BlockSpec(memory_space=pltpu.HBM)


def nn(left, right):
    return lax.dot_general(left, right, (((1,), (0,)), ((), ())), preferred_element_type=F32)


def nt(left, right):
    return lax.dot_general(left, right, (((1,), (1,)), ((), ())), preferred_element_type=F32)


def tn(left, right):
    return lax.dot_general(left, right, (((0,), (0,)), ((), ())), preferred_element_type=F32)


def remote(src, dst, send_sem, recv_sem, **where):
    return pltpu.make_async_remote_copy(
        src_ref=src, dst_ref=dst, send_sem=send_sem, recv_sem=recv_sem,
        device_id=where, device_id_type=MESH,
    )


def loading(sems, pairs):
    copies = [
        pltpu.make_async_copy(src, dst, sems.at[index]) for index, (src, dst) in enumerate(pairs)
    ]
    for copy in copies:
        copy.start()
    return copies


def place():
    me = lax.axis_index("tensor")
    core = lax.rem(me, 2)
    return me, core, lax.div(me, 2)


def greet_peers(axes):
    barrier = pltpu.get_barrier_semaphore()
    for axis, size in axes:
        me = lax.axis_index(axis)

        def greet(step, carry):
            pl.semaphore_signal(
                barrier, inc=1, device_id={axis: lax.rem(me + step, size)}, device_id_type=MESH
            )
            return carry

        lax.fori_loop(1, size, greet, 0)
    pl.semaphore_wait(barrier, sum(size - 1 for _, size in axes))


def normalize(values):
    average = jnp.mean(values, axis=-1, keepdims=True)
    centred = values - average
    variance = jnp.mean(centred * centred, axis=-1, keepdims=True)
    scale = lax.rsqrt(variance + NORM_EPS)
    return centred * scale, scale


class LineGather:
    def __init__(self, stages, buffer, send_sem, recv_sem):
        self.stages, self.buffer, self.send_sem, self.recv_sem = stages, buffer, send_sem, recv_sem
        self.me, self.core, self.stage = place()
        self.partner = self.me + 1 - 2 * self.core

    def copy(self, block, way, target):
        return remote(
            self.buffer.at[block], self.buffer.at[block],
            self.send_sem.at[block, way], self.recv_sem.at[block], tensor=target,
        )

    def each_copy(self, block, right, left, act):
        pl.when(right)(lambda: act(self.copy(block, 0, self.me + 2)))
        pl.when(left)(lambda: act(self.copy(block, 1, self.me - 2)))
        act(self.copy(block, 2, self.partner))

    def start(self):
        self.each_copy(
            self.me, self.stage < self.stages - 1, self.stage > 0, lambda copy: copy.start()
        )

    def start_inward(self):
        low = self.stage < self.stages // 2
        self.each_copy(self.me, low, jnp.logical_not(low), lambda copy: copy.start())

    def start_outward(self):
        low = self.stage < self.stages // 2
        pl.when(jnp.logical_not(low) & (self.stage < self.stages - 1))(
            lambda: self.copy(self.me, 0, self.me + 2).start()
        )
        pl.when(low & (self.stage > 0))(lambda: self.copy(self.me, 1, self.me - 2).start())

    def incoming(self, reach, side, core):
        far = jnp.where(side == 0, self.stage - reach, self.stage + reach)
        return (far >= 0) & (far < self.stages), 2 * far + core

    def arrive(self, block):
        self.copy(block, 2, self.partner).wait_recv()

    def ways(self, side):
        return (side == 0) & (self.stage < self.stages - 1), (side == 1) & (self.stage > 0)

    def relay(self, reach):
        for side in range(2):
            valid, block = self.incoming(reach, side, self.core)

            @pl.when(valid)
            def _():
                self.arrive(block)
                self.each_copy(block, *self.ways(jnp.int32(side)), lambda copy: copy.start())

    def use_own(self, compute):
        compute(self.me)
        self.arrive(self.partner)
        compute(self.partner)

    def use(self, reach, compute):
        def body(index, carry):
            side, other = lax.rem(index, 2), lax.div(index, 2)
            valid, block = self.incoming(
                reach, side, jnp.where(other == 0, self.core, 1 - self.core)
            )

            @pl.when(valid)
            def _():
                pl.when(other == 1)(lambda: self.arrive(block))
                compute(block)

            return carry

        lax.fori_loop(0, 4, body, 0)

    def run(self, compute, after_first=lambda: None, before_last=lambda: None):
        def body(reach, carry):
            pl.when(reach == self.stages - 1)(before_last)
            self.relay(reach)
            pl.when(reach == 1)(after_first)
            self.use(reach, compute)
            return carry

        self.use_own(compute)
        lax.fori_loop(1, self.stages, body, 0)

    def at_end(self):
        return (self.stage == 0) | (self.stage == self.stages - 1)

    def finish(self):
        self.each_copy(
            self.me, self.stage < self.stages - 1, self.stage > 0, lambda copy: copy.wait_send()
        )

        def body(index, carry):
            reach, side = lax.div(index, 2) + 1, lax.rem(index, 2)
            valid, block = self.incoming(reach, side, self.core)

            @pl.when(valid)
            def _():
                self.each_copy(block, *self.ways(side), lambda copy: copy.wait_send())

            return carry

        lax.fori_loop(0, 2 * (self.stages - 1), body, 0)


class LineScatter:
    def __init__(self, stages, partial, cross, lane, sems):
        self.stages, self.partial, self.cross, self.lane = stages, partial, cross, lane
        self.cross_send, self.cross_recv, self.lane_send, self.lane_recv = sems
        self.me, self.core, self.stage = place()
        self.partner = self.me + 1 - 2 * self.core

    def cross_copy(self, far):
        return remote(
            self.partial.at[2 * far + 1 - self.core], self.cross.at[far],
            self.cross_send.at[far], self.cross_recv.at[far], tensor=self.partner,
        )

    def slot(self, way, far, holder):
        return far if way == 0 else jnp.where(far == holder, self.stages, far)

    def lane_copy(self, way, far, holder):
        target = self.me + 2 if way == 0 else self.me - 2
        slot = self.slot(way, far, holder)
        return remote(
            self.partial.at[2 * far + self.core], self.lane.at[slot],
            self.lane_send.at[far], self.lane_recv.at[slot], tensor=target,
        )

    def sent(self, way, far):
        return self.lane_copy(way, far, self.stage + (1 if way == 0 else -1))

    def received(self, way, far):
        self.lane_copy(way, far, self.stage).wait_recv()
        return self.lane[self.slot(way, far, self.stage)].astype(F32)

    def put(self, block, value):
        self.partial[block] = value.astype(BF16)

        @pl.when(lax.rem(block, 2) != self.core)
        def _():
            self.cross_copy(lax.div(block, 2)).start()

    def produce(self, compute):
        def body(index, carry):
            reach = self.stages - 1 - lax.div(index, 4)
            side, other = lax.rem(lax.div(index, 2), 2), lax.rem(index, 2)
            far = jnp.where(side == 0, self.stage + reach, self.stage - reach)

            @pl.when((far >= 0) & (far < self.stages) & ((reach > 0) | (side == 0)))
            def _():
                block = 2 * far + jnp.where(other == 0, 1 - self.core, self.core)
                self.put(block, compute(block))

            return carry

        lax.fori_loop(0, 4 * self.stages, body, 0)

    def chip_sum(self, far):
        return self.partial[2 * far + self.core].astype(F32) + self.cross[far].astype(F32)

    def send_sum(self, way, far, incoming):
        self.cross_copy(far).wait_recv()
        block = 2 * far + self.core

        @pl.when(incoming)
        def _():
            self.partial[block] = (self.chip_sum(far) + self.received(way, far)).astype(BF16)

        @pl.when(jnp.logical_not(incoming))
        def _():
            self.partial[block] = self.chip_sum(far).astype(BF16)

        self.sent(way, far).start()

    def step(self, reach):
        right, left = self.stage + reach, self.stage - reach
        pl.when(right < self.stages)(lambda: self.send_sum(0, right, self.stage > 0))
        pl.when(left >= 0)(lambda: self.send_sum(1, left, self.stage < self.stages - 1))

    def steps(self, first, last):
        lax.fori_loop(first, last, lambda index, carry: (self.step(self.stages - 1 - index), carry)[1], 0)

    def own(self, total_ref):
        self.cross_copy(self.stage).wait_recv()
        total_ref[...] = self.chip_sum(self.stage)

        @pl.when(self.stage > 0)
        def _():
            total_ref[...] += self.received(0, self.stage)

        @pl.when(self.stage < self.stages - 1)
        def _():
            total_ref[...] += self.received(1, self.stage)

    def finish(self):
        def body(far, carry):
            self.cross_copy(far).wait_send()
            pl.when(far > self.stage)(lambda: self.sent(0, far).wait_send())
            pl.when(far < self.stage)(lambda: self.sent(1, far).wait_send())
            return carry

        lax.fori_loop(0, self.stages, body, 0)


def scatter_shapes(stages, rows, depth):
    return [
        VMEM((2 * stages, rows, depth), BF16), VMEM((stages, rows, depth), BF16),
        VMEM((stages + 1, rows, depth), BF16),
        DMA((stages,)), DMA((stages,)), DMA((stages,)), DMA((stages + 1,)),
    ]


def exchange(axis, size, slots, send_sem, recv_sem):
    me = lax.axis_index(axis)

    def copy_to(other, slot):
        return remote(
            slots.at[slot], slots.at[slot], send_sem.at[other], recv_sem.at[slot], **{axis: other}
        )

    def start(step, carry):
        copy_to(lax.rem(me + step, size), me).start()
        return carry

    def wait(step, carry):
        other = lax.rem(me + step, size)
        copy_to(other, other).wait_recv()
        copy_to(other, me).wait_send()
        return carry

    lax.fori_loop(1, size, start, 0)
    return lambda: lax.fori_loop(1, size, wait, 0)


def piece_height(height, parts):
    return -(-height // (16 * parts)) * 16


class RowSum:
    def __init__(self, parts, piece, arrive, send_sem, recv_sem):
        self.parts, self.piece, self.arrive = parts, piece, arrive
        self.send_sem, self.recv_sem = send_sem, recv_sem
        self.row = lax.axis_index("dp")

    def copy(self, other, source):
        return remote(
            self.piece.at[other], self.arrive.at[source],
            self.send_sem.at[other], self.recv_sem.at[source], dp=other,
        )

    def others(self, act, start):
        return lax.fori_loop(
            1, self.parts, lambda step, carry: act(lax.rem(self.row + step, self.parts), carry), start
        )

    def start(self, total):
        high = self.piece.shape[1]
        for part in range(self.parts):
            self.piece[part] = total[part * high : (part + 1) * high, :].astype(BF16)

        def send(other, carry):
            self.copy(other, self.row).start()
            return carry

        self.others(send, 0)

    def reduce(self):
        def add(other, so_far):
            self.copy(other, other).wait_recv()
            self.copy(other, self.row).wait_send()
            return so_far + self.arrive[other].astype(F32)

        return self.others(add, self.piece[self.row].astype(F32)).astype(BF16)


def rowsum_shapes(parts, high, depth):
    return [
        VMEM((parts, high, depth), BF16), VMEM((parts, high, depth), BF16), DMA((parts,)), DMA((parts,)),
    ]


def column(row):
    return jnp.broadcast_to(row, (128, row.shape[1])).T[:, :1]


def piece_rows(width, parts):
    return min(rows for rows in range(8, width + 1, 8) if width % rows == 0 and width // rows <= parts)


class WeightSpread:
    def __init__(self, stages, parts, buffer, sems):
        self.stages, self.parts, self.buffer = stages, parts, buffer
        self.line_send, self.line_recv, self.row_send, self.row_recv, self.core_send, self.core_recv = sems
        self.count = buffer.shape[0]
        self.me, self.core, self.stage = place()
        self.partner = self.me + 1 - 2 * self.core
        self.row = lax.axis_index("dp")
        self.here = self.row < self.count
        self.slot = jnp.minimum(self.row, self.count - 1)

    def copy(self, source, block, send_sem, recv_sem, **where):
        ref = self.buffer.at[source, block]
        return remote(ref, ref, send_sem, recv_sem, **where)

    def line_copy(self, other, far):
        return self.copy(
            self.slot, 2 * far + self.core, self.line_send.at[other], self.line_recv.at[far],
            tensor=2 * other + self.core,
        )

    def row_copy(self, other, source, far):
        return self.copy(
            source, 2 * far + self.core, self.row_send.at[other, far], self.row_recv.at[source, far],
            dp=other,
        )

    def core_copy(self, source, far, core):
        return self.copy(
            source, 2 * far + core, self.core_send.at[source, far], self.core_recv.at[source, far],
            tensor=self.partner,
        )

    def other_stages(self, act):
        def body(step, carry):
            act(lax.rem(self.stage + step, self.stages))
            return carry

        lax.fori_loop(1, self.stages, body, 0)

    def other_rows(self, act):
        def body(index, carry):
            step = lax.div(index, self.stages) + 1
            act(lax.rem(self.row + step, self.parts), lax.rem(index, self.stages))
            return carry

        lax.fori_loop(0, (self.parts - 1) * self.stages, body, 0)

    def pieces(self, act):
        def body(index, carry):
            act(lax.div(index, self.stages), lax.rem(index, self.stages))
            return carry

        lax.fori_loop(0, self.count * self.stages, body, 0)

    def start(self):
        self.other_stages(lambda other: self.line_copy(other, self.stage).start())

    def to_rows(self):
        self.other_stages(lambda other: self.line_copy(other, other).wait_recv())
        self.other_rows(lambda other, far: self.row_copy(other, self.slot, far).start())

    def pass_on(self):
        def act(source, far):
            pl.when(source != self.row)(lambda: self.row_copy(self.row, source, far).wait_recv())
            self.core_copy(source, far, self.core).start()

        self.pieces(act)

    def finish(self):
        @pl.when(self.here)
        def _():
            self.other_stages(lambda other: self.line_copy(other, self.stage).wait_send())
            self.other_rows(lambda other, far: self.row_copy(other, self.slot, far).wait_send())

        def act(source, far):
            self.core_copy(source, far, 1 - self.core).wait_recv()
            self.core_copy(source, far, self.core).wait_send()

        self.pieces(act)


def project_kernel(
    stages, parts, tok_hbm, g1_ref, b1_ref, bo_ref, g2_ref, b2_ref, bf2_ref, bf1_ref, bq_ref, bv_ref, wo_hbm, wq_hbm, wk_hbm, wv_hbm, ids_ref,
    norm_hbm, q_hbm, k_hbm, v_hbm, wo_out, vec_ref, span_ref, idr_ref, ido_ref,
    wo_all, line_send, line_recv, row_send, row_recv, core_send, core_recv, tok, norm, q_ref, k_ref, v_ref, weight, send_sem, recv_sem, out_sem, load_sem,
):
    me, _, _ = place()
    width, rows = wq_hbm.shape[0], tok.shape[0]
    loads = loading(
        load_sem,
        ((tok_hbm, tok), (wq_hbm, weight.at[0]), (wk_hbm, weight.at[1]), (wv_hbm, weight.at[2])),
    )
    spread = WeightSpread(
        stages, parts, wo_all, (line_send, line_recv, row_send, row_recv, core_send, core_recv)
    )
    high = wo_all.shape[2]
    own_piece = pltpu.make_async_copy(
        wo_hbm.at[pl.ds(pl.multiple_of(spread.slot * high, high), high)],
        wo_all.at[spread.slot, me], load_sem.at[4],
    )
    pl.when(spread.here)(own_piece.start)
    vec_ref[...] = jnp.zeros_like(vec_ref)
    for index, ref in enumerate(
        (g1_ref, b1_ref, bo_ref, g2_ref, b2_ref, bf2_ref, bf1_ref, bq_ref, bv_ref)
    ):
        vec_ref[index : index + 1, 0 : ref.shape[0]] = ref[...].astype(F32)[None, :]
    greet_peers((("tensor", 2 * stages), ("dp", parts)))

    @pl.when(spread.here)
    def _():
        own_piece.wait()
        spread.start()

    loads[0].wait()
    normed, _ = normalize(tok[...].astype(F32))
    norm[me] = (normed * vec_ref[0:1, :] + vec_ref[1:2, :]).astype(BF16)
    gather = LineGather(stages, norm, send_sem, recv_sem)
    gather.start()
    ids = ids_ref[...].astype(F32)
    idr_ref[...] = ids
    ido_ref[...] = idr_ref[:, pl.ds(pl.multiple_of(me * rows, rows), rows)]
    for block in range(ids.shape[1] // BLOCK):
        first = ids[:, block * BLOCK : block * BLOCK + 1]
        last = ids[:, (block + 1) * BLOCK - 1 : (block + 1) * BLOCK]
        begin = jnp.sum(jnp.where(ids > first, 1.0, 0.0))
        end = jnp.sum(jnp.where(ids >= jnp.maximum(last, 1.0), 1.0, 0.0))
        span_ref[0, block] = lax.div(begin.astype(jnp.int32), BLOCK)
        span_ref[1, block] = lax.div(end.astype(jnp.int32) + (BLOCK - 1), BLOCK)
    for load in loads[1:]:
        load.wait()

    def keep(block):
        return [
            pltpu.make_async_copy(src.at[block], dst.at[block], out_sem.at[index, block])
            for index, (src, dst) in enumerate(
                ((norm, norm_hbm), (q_ref, q_hbm), (k_ref, k_hbm), (v_ref, v_hbm))
            )
        ]

    def compute(block):
        q_ref[block] = (nt(norm[block], weight[0]) + vec_ref[7:8, :width]).astype(BF16)
        k_ref[block] = nt(norm[block], weight[1]).astype(BF16)
        v_ref[block] = (nt(norm[block], weight[2]) + vec_ref[8:9, :width]).astype(BF16)
        for copy in keep(block):
            copy.start()

    gather.run(compute, lambda: pl.when(spread.here)(spread.to_rows), spread.pass_on)
    spread.finish()
    out_copy = pltpu.make_async_copy(wo_all, wo_out, load_sem.at[5])
    out_copy.start()
    gather.finish()

    def kept(block, carry):
        for copy in keep(block):
            copy.wait()
        return carry

    lax.fori_loop(0, 2 * stages, kept, 0)
    out_copy.wait()


def project(tokens, vectors, wo, wq, wk, wv, ids, devices, parts):
    rows, depth = tokens.shape
    width, length = wq.shape[1], ids.shape[1]
    stages = devices // 2
    high = piece_rows(width, parts)
    head = jax.ShapeDtypeStruct((devices, rows, width), BF16)
    pieces = (width // high, devices, high, depth)
    return pl.pallas_call(
        functools.partial(project_kernel, stages, parts),
        name="project",
        out_shape=(
            jax.ShapeDtypeStruct((devices, rows, depth), BF16), head, head, head,
            jax.ShapeDtypeStruct(pieces, BF16), jax.ShapeDtypeStruct((16, depth), F32),
            jax.ShapeDtypeStruct((2, length // BLOCK), jnp.int32),
            jax.ShapeDtypeStruct((1, length), F32), jax.ShapeDtypeStruct((1, rows), F32),
        ),
        in_specs=[HBM] + [VSPEC] * 9 + [HBM, HBM, HBM, HBM, VSPEC],
        out_specs=(HBM, HBM, HBM, HBM, HBM, VSPEC, SSPEC, VSPEC, VSPEC),
        scratch_shapes=[
            VMEM(pieces, BF16), DMA((stages,)), DMA((stages,)),
            *[DMA((parts, stages))] * 4,
            VMEM((rows, depth), BF16), VMEM((devices, rows, depth), BF16),
            *[VMEM((devices, rows, width), BF16)] * 3, VMEM((3, width, depth), BF16),
            DMA((devices, 3)), DMA((devices,)), DMA((4, devices)), DMA((6,)),
        ],
        compiler_params=pltpu.CompilerParams(
            collective_id=0, has_side_effects=True, vmem_limit_bytes=VMEM_ALL
        ),
    )(tokens, *vectors, wo, wq.T, wk.T, wv.T, ids)


def lanes_of(head, width):
    lane = lax.broadcasted_iota(jnp.int32, (1, width), 1)
    return (lane >= head * HD) & (lane < (head + 1) * HD)


def fill_columns(row_ref, column_ref):
    for block in range(row_ref.shape[1] // BLOCK):
        at = pl.ds(block * BLOCK, BLOCK)
        column_ref[at, :] = column(row_ref[:, at])


def head_rows(head, width):
    row = lax.broadcasted_iota(jnp.int32, (width, 1), 0)
    return (row >= head * HD) & (row < (head + 1) * HD)


def side_by_side(block_t, heads):
    width = block_t.shape[0]
    zero = jnp.zeros_like(block_t)
    return jnp.concatenate([jnp.where(head_rows(h, width), block_t, zero) for h in range(heads)], axis=1)


def stacked(block, heads):
    width = block.shape[1]
    zero = jnp.zeros_like(block)
    return jnp.concatenate([jnp.where(lanes_of(h, width), block, zero) for h in range(heads)], axis=0)


def repeat_lanes(row, heads):
    return jnp.concatenate([row] * heads, axis=1)


def attend_kernel(
    heads, span_ref, q_hbm, k_hbm, v_hbm, idr_ref, o_ref, log_ref,
    q_ref, k_ref, v_ref, load_sem, idc_ref, vt_ref, acc_ref,
):
    length, width = q_ref.shape
    scale = HD ** (-0.5) * LOG2E
    loads = loading(load_sem, ((v_hbm, v_ref), (q_hbm, q_ref), (k_hbm, k_ref)))
    fill_columns(idr_ref, idc_ref)
    for load in loads:
        load.wait()

    def turn(block, total):
        at = pl.ds(pl.multiple_of(block * BLOCK, BLOCK), BLOCK)
        value = v_ref[at, :].astype(F32)
        vt_ref[block] = value.T.astype(BF16)
        return total + jnp.sum(value, axis=0, keepdims=True)

    mean_value = lax.fori_loop(0, length // BLOCK, turn, jnp.zeros((1, width), F32)) * (1.0 / length)

    def per_block(block, carry):
        at = pl.ds(pl.multiple_of(block * BLOCK, BLOCK), BLOCK)
        query = side_by_side(q_ref[at, :].astype(F32).T.astype(BF16), heads)
        id_row = idr_ref[:, at]
        id_rows = repeat_lanes(id_row, heads)
        acc_ref[...] = jnp.zeros_like(acc_ref)

        def per_key(other, state):
            top, total = state
            keys_at = pl.ds(pl.multiple_of(other * BLOCK, BLOCK), BLOCK)
            id_col = idc_ref[keys_at, :]
            allowed = (id_col == id_rows) & (id_col > 0)
            scores = jnp.where(allowed, nn(k_ref[keys_at, :], query) * scale, NEG_FILL)
            new_top = jnp.maximum(top, jnp.max(scores, axis=0, keepdims=True))
            weight = jnp.exp2(scores - new_top)
            shrink = jnp.exp2(top - new_top)
            total = total * shrink + jnp.sum(weight, axis=0, keepdims=True)
            acc_ref[...] = acc_ref[...] * shrink + nn(vt_ref[other], weight.astype(BF16))
            return new_top, total

        top, total = lax.fori_loop(
            span_ref[0, block], span_ref[1, block], per_key,
            (jnp.full((1, heads * BLOCK), NEG_FILL, F32), jnp.zeros((1, heads * BLOCK), F32)),
        )
        scaled = acc_ref[...] / total
        logs = jnp.where(id_rows == 0, 0.0, top + jnp.log2(total))
        result = jnp.zeros((width, BLOCK), F32)
        for h in range(heads):
            here = slice(h * BLOCK, (h + 1) * BLOCK)
            result = jnp.where(head_rows(h, width), scaled[:, here], result)
            log_ref[h : h + 1, at] = logs[:, here]
        o_ref[at, :] = jnp.where(idc_ref[at, :] == 0, mean_value, result.T).astype(BF16)
        return carry

    lax.fori_loop(0, length // BLOCK, per_block, 0)


def attend(q, k, v, span, id_row):
    length, width = q.shape
    heads = width // HD
    return pl.pallas_call(
        functools.partial(attend_kernel, heads),
        name="attend",
        out_shape=(
            jax.ShapeDtypeStruct((length, width), BF16),
            jax.ShapeDtypeStruct((heads, length), F32),
        ),
        in_specs=[SSPEC, HBM, HBM, HBM, VSPEC],
        out_specs=(VSPEC,) * 2,
        scratch_shapes=[
            *[VMEM((length, width), BF16)] * 3, DMA((3,)),
            VMEM((length, 1), F32), VMEM((length // BLOCK, width, BLOCK), BF16),
            VMEM((width, heads * BLOCK), F32),
        ],
        compiler_params=pltpu.CompilerParams(vmem_limit_bytes=VMEM_ALL),
    )(span, q, k, v, id_row)


def attend_back_kernel(
    heads, span_ref, q_hbm, k_hbm, v_hbm, idr_ref, o_hbm, log_ref, g_hbm, fc_hbm, layer_hbm,
    out_ref, fc1_hbm, fc2_hbm, layer_out, fc, fc1, fc2, layer, side_sem, q_ref, k_ref, v_ref, o_ref, g_ref, load_sem,
    idc_ref, dq_ref, dk_ref, dv_ref, q_side, q_stack, g_side, g_stack, row_ref, log_side,
):
    length, width = q_ref.shape
    score_scale = HD ** (-0.5)
    loads = loading(
        load_sem, ((q_hbm, q_ref), (g_hbm, g_ref), (o_hbm, o_ref), (k_hbm, k_ref), (v_hbm, v_ref))
    )
    layer_in = pltpu.make_async_copy(layer_hbm, layer, side_sem.at[0])
    fc_in = pltpu.make_async_copy(fc_hbm, fc, side_sem.at[1])
    layer_in.start()
    fc_in.start()
    dq_ref[...] = jnp.zeros_like(dq_ref)
    fill_columns(idr_ref, idc_ref)
    for load in loads:
        load.wait()

    def prepare(block, pad):
        at = pl.ds(pl.multiple_of(block * BLOCK, BLOCK), BLOCK)
        query, grad = q_ref[at, :], g_ref[at, :]
        wide = grad.astype(F32)
        grad_t = wide.T
        product = (wide * o_ref[at, :].astype(F32)).T
        q_side[block] = side_by_side(query.astype(F32).T.astype(BF16), heads)
        g_side[block] = side_by_side(grad_t.astype(BF16), heads)
        q_stack[block] = stacked(query, heads)
        g_stack[block] = stacked(grad, heads)
        for h in range(heads):
            here = slice(h * BLOCK, (h + 1) * BLOCK)
            row_ref[block, :, here] = jnp.sum(
                jnp.where(head_rows(h, width), product, 0.0), axis=0, keepdims=True
            )
            log_side[block, :, here] = log_ref[h : h + 1, at]
        return pad + jnp.sum(jnp.where(idc_ref[at, :] == 0, wide, 0.0), axis=0, keepdims=True)

    pad = lax.fori_loop(0, length // BLOCK, prepare, jnp.zeros((1, width), F32)) * (1.0 / length)
    units = fc1.shape[0]
    second = -(-units // 16) * 16
    layer_in.wait()
    fc_in.wait()
    fc1[...] = fc[0:units, :].astype(F32)
    fc2[...] = fc[second : second + units, :].astype(F32)
    outs = [
        pltpu.make_async_copy(src, dst, side_sem.at[2 + index])
        for index, (src, dst) in enumerate(((layer, layer_out), (fc1, fc1_hbm), (fc2, fc2_hbm)))
    ]
    for out in outs:
        out.start()

    def per_key(block, carry):
        at = pl.ds(pl.multiple_of(block * BLOCK, BLOCK), BLOCK)
        key, value, id_col = k_ref[at, :], v_ref[at, :], idc_ref[at, :]
        key_side = side_by_side(key.astype(F32).T.astype(BF16), heads)
        real = id_col > 0
        dk_ref[...] = jnp.zeros_like(dk_ref)
        dv_ref[...] = jnp.zeros_like(dv_ref)

        def per_query(other, inner):
            query_at = pl.ds(pl.multiple_of(other * BLOCK, BLOCK), BLOCK)
            allowed = (id_col == repeat_lanes(idr_ref[:, query_at], heads)) & real
            scores = nn(key, q_side[other]) * (score_scale * LOG2E) - log_side[other]
            prob = jnp.exp2(jnp.where(allowed, scores, NEG_FILL))
            dv_ref[...] += nn(prob.astype(BF16), g_stack[other])
            back = (prob * (nn(value, g_side[other]) - row_ref[other])).astype(BF16)
            dk_ref[...] += nn(back, q_stack[other])
            back_rows = jnp.concatenate(
                [back[:, h * BLOCK : (h + 1) * BLOCK] for h in range(heads)], axis=0
            )
            dq_ref[other] += nn(key_side, back_rows)
            return inner

        lax.fori_loop(span_ref[0, block], span_ref[1, block], per_query, 0)
        out_ref[at, width : 2 * width] = (dk_ref[...] * score_scale).astype(BF16)
        out_ref[at, 2 * width :] = (dv_ref[...] + pad).astype(BF16)
        return carry

    lax.fori_loop(0, length // BLOCK, per_key, 0)

    def settle(block, carry):
        at = pl.ds(pl.multiple_of(block * BLOCK, BLOCK), BLOCK)
        out_ref[at, :width] = (dq_ref[block].T * score_scale).astype(BF16)
        return carry

    lax.fori_loop(0, length // BLOCK, settle, 0)
    for out in outs:
        out.wait()


def attend_back(q, k, v, span, id_row, o, log_total, grad, fc, layer, units):
    length, width = q.shape
    heads = width // HD
    blocks, depth = length // BLOCK, layer.shape[1]
    whole = VMEM((length, width), BF16)
    side, stack = VMEM((blocks, width, heads * BLOCK), BF16), VMEM((blocks, heads * BLOCK, width), BF16)
    line = VMEM((blocks, 1, heads * BLOCK), F32)
    return pl.pallas_call(
        functools.partial(attend_back_kernel, heads),
        name="attend_back",
        out_shape=(
            jax.ShapeDtypeStruct((length, 3 * width), BF16), jax.ShapeDtypeStruct((units, depth), F32),
            jax.ShapeDtypeStruct((units, depth), F32), jax.ShapeDtypeStruct(layer.shape, BF16),
        ),
        in_specs=[SSPEC, HBM, HBM, HBM, VSPEC, HBM, VSPEC, HBM, HBM, HBM],
        out_specs=(VSPEC, HBM, HBM, HBM),
        scratch_shapes=[
            VMEM(fc.shape, BF16), VMEM((units, depth), F32), VMEM((units, depth), F32),
            VMEM(layer.shape, BF16), DMA((5,)),
            whole, whole, whole, whole, whole, DMA((5,)),
            VMEM((length, 1), F32), VMEM((blocks, width, BLOCK), F32), VMEM((BLOCK, width), F32),
            VMEM((BLOCK, width), F32), side, stack, side, stack, line, line,
        ],
        compiler_params=pltpu.CompilerParams(vmem_limit_bytes=VMEM_ALL),
    )(span, q, k, v, id_row, o, log_total, grad, fc, layer)


def gelu_pair(u):
    slope = (2.0 / jnp.pi) ** 0.5
    bent = jnp.tanh(slope * (u + 0.044715 * u * u * u))
    half = 0.5 * (1.0 + bent)
    return u * half, half + 0.5 * u * (1.0 - bent * bent) * slope * (1.0 + 3 * 0.044715 * u * u)


def middle_kernel(
    stages, parts, att_hbm, wo_hbm, fc1_hbm, fc2_hbm, tok_hbm, top_hbm, ids_ref, vec_ref,
    out_ref, gres_ref, gatt_ref, fc_hbm, small_ref,
    wo, fc1, fc2, tok, top, load_sem,
    held, held_send, held_recv, norm_all, norm_send, norm_recv, top_all, top_send, top_recv,
    hidden, slope, grad_pre,
    br_part, br_cross, br_lane, br_s0, br_s1, br_s2, br_s3,
    gn_part, gn_cross, gn_lane, gn_s0, gn_s1, gn_s2, gn_s3,
    resid, total, acc, piece, arrive, piece_send, piece_recv, fa_send, fa_recv, free_sem, out_sem,
    back, back_send, back_recv,
):
    me, _, _ = place()
    devices = 2 * stages
    rows, depth = tok_hbm.shape
    high = wo_hbm.shape[2]
    units = fc1_hbm.shape[0]
    second = -(-units // 16) * 16
    loads = loading(
        load_sem,
        ((tok_hbm, tok), (top_hbm, top), (fc1_hbm, fc1), (fc2_hbm, fc2), (att_hbm.at[me], held.at[me]),
         *((wo_hbm.at[index], wo.at[:, pl.ds(index * high, high)]) for index in range(wo_hbm.shape[0]))),
    )
    greet_peers((("tensor", devices), ("dp", parts)))

    def held_copy(other, source):
        return remote(
            att_hbm.at[other], held.at[source], held_send.at[other], held_recv.at[source], tensor=other
        )

    def send_held(step, carry):
        held_copy(lax.rem(me + step, devices), me).start()
        return carry

    lax.fori_loop(1, devices, send_held, 0)
    gather2 = LineGather(stages, norm_all, norm_send, norm_recv)
    gather3 = LineGather(stages, top_all, top_send, top_recv)
    branch = LineScatter(stages, br_part, br_cross, br_lane, (br_s0, br_s1, br_s2, br_s3))
    gnorm = LineScatter(stages, gn_part, gn_cross, gn_lane, (gn_s0, gn_s1, gn_s2, gn_s3))

    mask = column(jnp.where(ids_ref[...] > 0, 1.0, 0.0))
    acc[...] = jnp.zeros_like(acc)
    small_ref[...] = jnp.zeros_like(small_ref)
    loads[0].wait()
    loads[1].wait()
    top_own = top[...].astype(F32) * mask
    top_all[me] = top_own.astype(BF16)
    small_ref[5:6, :] = jnp.sum(top_own, axis=0, keepdims=True)
    resid[...] = tok[...].astype(F32) + vec_ref[2:3, :]
    for load in loads[4:]:
        load.wait()
    resid[...] += nn(held[me], wo[me])

    def add_held(step, carry):
        other = lax.rem(me + devices - step, devices)
        held_copy(other, other).wait_recv()
        resid[...] += nn(held[other], wo[other])
        return carry

    lax.fori_loop(1, devices, add_held, 0)
    normed, _ = normalize(resid[...])
    norm_all[me] = (normed * vec_ref[3:4, :] + vec_ref[4:5, :]).astype(BF16)
    gather2.start()
    loads[2].wait()
    loads[3].wait()

    def forward(block):
        pre_act = nt(norm_all[block], fc1[...]) + vec_ref[6:7, 0:units]
        value, slope_now = gelu_pair(pre_act)
        hidden[block] = value.astype(BF16)
        slope[block] = slope_now.astype(BF16)
        branch.put(block, nn(hidden[block], fc2[...]))

    at_end = gather2.at_end()
    gather2.run(forward, lambda: pl.when(at_end)(gather3.start_inward))
    pl.when(jnp.logical_not(at_end))(gather3.start_inward)
    gather3.start_outward()
    pl.when(at_end)(lambda: branch.steps(0, stages - 1))

    def backward(block):
        grad = nt(top_all[block], fc2[...]) * slope[block].astype(F32)
        low = grad.astype(BF16)
        grad_pre[block] = low
        small_ref[7:8, 0:units] += jnp.sum(low.astype(F32), axis=0, keepdims=True)
        gnorm.put(block, nn(grad_pre[block], fc1[...]))
        acc[0:units, :] += tn(grad_pre[block], norm_all[block])
        acc[second : second + units, :] += tn(hidden[block], top_all[block])

    gather3.run(backward)
    gnorm.step(stages - 1)
    sums = RowSum(parts, piece, arrive, piece_send, piece_recv)
    sums.start(acc)

    pl.when(jnp.logical_not(at_end))(lambda: branch.steps(1, stages - 1))
    gnorm.steps(1, stages - 1)
    fc_sum = sums.reduce()

    def to_rows(act):
        lax.fori_loop(
            1, parts, lambda step, carry: (act(lax.rem(sums.row + step, parts)), carry)[1], 0
        )

    to_rows(
        lambda other: pl.semaphore_signal(
            free_sem, inc=1, device_id={"dp": other}, device_id_type=MESH
        )
    )
    pl.semaphore_wait(free_sem, parts - 1)
    arrive[sums.row] = fc_sum
    wait_fc = exchange("dp", parts, arrive, fa_send, fa_recv)
    branch.own(total)
    out_ref[...] = (mask * (resid[...] + total[...] + vec_ref[5:6, :])).astype(BF16)

    gnorm.own(total)
    grad = total[...]
    normed, scale = normalize(resid[...])
    small_ref[2:3, :] = jnp.sum(grad * normed, axis=0, keepdims=True)
    small_ref[3:4, :] = jnp.sum(grad, axis=0, keepdims=True)
    inner = grad * vec_ref[3:4, :]
    inner_mean = jnp.mean(inner, axis=-1, keepdims=True)
    inner_proj = jnp.mean(inner * normed, axis=-1, keepdims=True)
    grad_resid = top[...].astype(F32) * mask + scale * (inner - inner_mean - normed * inner_proj)
    gres_ref[...] = grad_resid
    tok[...] = grad_resid.astype(BF16)
    small_ref[4:5, :] = jnp.sum(grad_resid, axis=0, keepdims=True)

    def back_copy(other, source):
        return remote(
            back.at[other], gatt_ref.at[source], back_send.at[other], back_recv.at[source], tensor=other
        )

    def send_back(step, carry):
        other = lax.rem(me + step, devices)
        back[other] = nt(tok[...], wo[other]).astype(BF16)
        back_copy(other, me).start()
        return carry

    lax.fori_loop(1, devices, send_back, 0)
    gatt_ref[me] = nt(tok[...], wo[me]).astype(BF16)

    wait_fc()
    out_fc = pltpu.make_async_copy(arrive, fc_hbm, out_sem)
    out_fc.start()

    def settle(step, carry):
        other = lax.rem(me + devices - step, devices)
        back_copy(other, other).wait_recv()
        back_copy(other, me).wait_send()
        held_copy(other, me).wait_send()
        return carry

    lax.fori_loop(1, devices, settle, 0)
    gather2.finish()
    gather3.finish()
    branch.finish()
    gnorm.finish()
    out_fc.wait()


def middle(att, wo, fc1, fc2, tokens, out_grad, ids, vectors, parts):
    devices, rows, width = att.shape
    depth, units = fc1.shape
    stages = devices // 2
    high = piece_height(2 * (-(-units // 16) * 16), parts)
    return pl.pallas_call(
        functools.partial(middle_kernel, stages, parts),
        name="middle",
        out_shape=(
            jax.ShapeDtypeStruct((rows, depth), BF16),
            jax.ShapeDtypeStruct((rows, depth), F32),
            jax.ShapeDtypeStruct((devices, rows, width), BF16),
            jax.ShapeDtypeStruct((parts, high, depth), BF16),
            jax.ShapeDtypeStruct((8, depth), F32),
        ),
        in_specs=[HBM] * 6 + [VSPEC] * 2,
        out_specs=(VSPEC, VSPEC, VSPEC, HBM, VSPEC),
        scratch_shapes=[
            VMEM((devices, width, depth), BF16), VMEM((units, depth), BF16), VMEM((units, depth), BF16),
            VMEM((rows, depth), BF16), VMEM((rows, depth), BF16), DMA((5 + wo.shape[0],)),
            VMEM((devices, rows, width), BF16), DMA((devices,)), DMA((devices,)),
            VMEM((devices, rows, depth), BF16), DMA((devices, 3)), DMA((devices,)),
            VMEM((devices, rows, depth), BF16), DMA((devices, 3)), DMA((devices,)),
            VMEM((devices, rows, units), BF16), VMEM((devices, rows, units), BF16),
            VMEM((devices, rows, units), BF16),
            *scatter_shapes(stages, rows, depth), *scatter_shapes(stages, rows, depth),
            VMEM((rows, depth), F32), VMEM((rows, depth), F32),
            VMEM((parts * high, depth), F32), *rowsum_shapes(parts, high, depth),
            DMA((parts,)), DMA((parts,)), pltpu.SemaphoreType.REGULAR, DMA,
            VMEM((devices, rows, width), BF16), DMA((devices,)), DMA((devices,)),
        ],
        compiler_params=pltpu.CompilerParams(
            collective_id=2, has_side_effects=True, vmem_limit_bytes=VMEM_ALL
        ),
    )(
        att, wo, fc1.T, fc2, tokens, out_grad, ids, vectors,
    )


def add_slots(slots):
    return lax.fori_loop(
        1, slots.shape[0], lambda slot, so_far: so_far + slots[slot], slots[0]
    )


def close_kernel(
    stages, parts, dx_hbm, wq_hbm, wk_hbm, wv_hbm, norm_hbm, att_hbm, tok_hbm, vec_ref, resid_hbm,
    small_ref,
    gtok_ref, gw_hbm, go_hbm, gsmall_ref,
    dx_ref, weight, norm, att_ref, tok_ref, resid_ref, load_sem, gatt_all, gatt_send, gatt_recv,
    partial, cross, lane, cross_send, cross_recv, lane_send, lane_recv,
    total, acc, acc_o, w_piece, w_arrive, w_send, w_recv, o_piece, o_arrive, o_send, o_recv,
    w_all, o_all, wa_send, wa_recv, oa_send, oa_recv, out_sem,
    slots_t, slots_d, st_send, st_recv, sd_send, sd_recv,
    late_t, late_d, lt_send, lt_recv, ld_send, ld_recv,
):
    me, _, _ = place()
    row = lax.axis_index("dp")
    devices = 2 * stages
    wide, width = dx_ref.shape[2], att_ref.shape[2]
    loads = loading(
        load_sem,
        ((resid_hbm, resid_ref), (dx_hbm, dx_ref),
         *((src, weight.at[pl.ds(index * width, width)]) for index, src in enumerate((wq_hbm, wk_hbm, wv_hbm))),
         (norm_hbm, norm), (att_hbm, att_ref), (tok_hbm, tok_ref)),
    )
    greet_peers((("tensor", devices), ("dp", parts)))
    slots_t[me] = small_ref[...]
    wait_small = exchange("tensor", devices, slots_t, st_send, st_recv)
    loads[0].wait()
    gatt_all[me] = resid_ref[...].astype(BF16)
    gather = LineGather(stages, gatt_all, gatt_send, gatt_recv)
    gather.start()
    for load in loads[1:5]:
        load.wait()
    scatter = LineScatter(
        stages, partial, cross, lane, (cross_send, cross_recv, lane_send, lane_recv)
    )
    scatter.produce(lambda block: nn(dx_ref[block], weight[...]))
    scatter.step(stages - 1)

    acc[...] = jnp.zeros_like(acc)
    acc_o[...] = jnp.zeros_like(acc_o)
    for load in loads[5:]:
        load.wait()

    def weight_block(block, bias):
        grad = dx_ref[block]
        acc[0:wide, :] += tn(grad, norm[block])
        return bias + jnp.sum(grad.astype(F32), axis=0, keepdims=True)

    bias = lax.fori_loop(0, devices, weight_block, jnp.zeros((1, wide), F32))
    w_sum = RowSum(parts, w_piece, w_arrive, w_send, w_recv)
    w_sum.start(acc)

    def weight_o(block):
        acc_o[0:width, :] += tn(att_ref[block], gatt_all[block])

    gather.use_own(weight_o)

    def both(reach, carry):
        gather.relay(reach)
        pl.when(reach < stages - 1)(lambda: scatter.step(stages - 1 - reach))
        gather.use(reach, weight_o)
        return carry

    lax.fori_loop(1, min(2, stages), both, 0)
    w_all[row] = w_sum.reduce()
    wait_w = exchange("dp", parts, w_all, wa_send, wa_recv)
    wait_small()
    line = lax.broadcasted_iota(jnp.int32, small_ref.shape, 0)
    sums = add_slots(slots_t)
    slots_d[row] = jnp.where(line < 6, sums, small_ref[...])
    slots_d[row, 6:7, 0:wide] = bias
    wait_rows = exchange("dp", parts, slots_d, sd_send, sd_recv)
    lax.fori_loop(min(2, stages), stages, both, 0)
    o_sum = RowSum(parts, o_piece, o_arrive, o_send, o_recv)
    o_sum.start(acc_o)
    o_all[row] = o_sum.reduce()
    wait_o = exchange("dp", parts, o_all, oa_send, oa_recv)

    scatter.own(total)
    grad = total[...]
    normed, scale = normalize(tok_ref[...].astype(F32))
    quarter = late_t.shape[2]
    for index, value in enumerate((grad * normed, grad)):
        line_sum = jnp.sum(value, axis=0, keepdims=True)
        for part in range(4):
            late_t[me, 4 * index + part : 4 * index + part + 1, :] = line_sum[
                :, part * quarter : (part + 1) * quarter
            ]
    wait_late = exchange("tensor", devices, late_t, lt_send, lt_recv)
    inner = grad * vec_ref[0:1, :]
    inner_mean = jnp.mean(inner, axis=-1, keepdims=True)
    inner_proj = jnp.mean(inner * normed, axis=-1, keepdims=True)
    gtok_ref[...] = resid_ref[...] + scale * (inner - inner_mean - normed * inner_proj)
    wait_late()
    late_d[row] = add_slots(late_t)
    wait_last = exchange("dp", parts, late_d, ld_send, ld_recv)
    outs = []
    for index, (wait, src, dst) in enumerate(
        ((wait_w, w_all, gw_hbm), (wait_o, o_all, go_hbm))
    ):
        wait()
        out = pltpu.make_async_copy(src, dst, out_sem.at[index])
        out.start()
        outs.append(out)
    wait_rows()
    gsmall_ref[...] = add_slots(slots_d)
    wait_last()
    late = add_slots(late_d)
    for index in range(2):
        for part in range(4):
            gsmall_ref[index : index + 1, part * quarter : (part + 1) * quarter] = late[
                4 * index + part : 4 * index + part + 1, :
            ]
    gather.finish()
    scatter.finish()
    for out in outs:
        out.wait()


def close(dx, wq, wk, wv, norm, att, tokens, vectors, resid, small, parts):
    devices, rows, wide = dx.shape
    depth = tokens.shape[1]
    stages = devices // 2
    width = wide // 3
    w_high, o_high = piece_height(wide, parts), piece_height(width, parts)
    pieces = [(parts, high, depth) for high in (w_high, o_high)]
    return pl.pallas_call(
        functools.partial(close_kernel, stages, parts),
        name="close",
        out_shape=(
            jax.ShapeDtypeStruct((rows, depth), F32),
            *(jax.ShapeDtypeStruct(shape, BF16) for shape in pieces),
            jax.ShapeDtypeStruct(small.shape, F32),
        ),
        in_specs=[HBM] * 7 + [VSPEC, HBM, VSPEC],
        out_specs=(VSPEC, HBM, HBM, VSPEC),
        scratch_shapes=[
            VMEM((devices, rows, wide), BF16), VMEM((wide, depth), BF16),
            VMEM((devices, rows, depth), BF16), VMEM((devices, rows, width), BF16),
            VMEM((rows, depth), BF16), VMEM((rows, depth), F32), DMA((8,)),
            VMEM((devices, rows, depth), BF16), DMA((devices, 3)), DMA((devices,)),
            *scatter_shapes(stages, rows, depth),
            VMEM((rows, depth), F32), VMEM((parts * w_high, depth), F32),
            VMEM((parts * o_high, depth), F32),
            *rowsum_shapes(parts, w_high, depth), *rowsum_shapes(parts, o_high, depth),
            *(VMEM(shape, BF16) for shape in pieces), *[DMA((parts,))] * 4, DMA((2,)),
            VMEM((devices,) + small.shape, F32), VMEM((parts,) + small.shape, F32),
            DMA((devices,)), DMA((devices,)), DMA((parts,)), DMA((parts,)),
            VMEM((devices, 8, depth // 4), F32), VMEM((parts, 8, depth // 4), F32),
            DMA((devices,)), DMA((devices,)), DMA((parts,)), DMA((parts,)),
        ],
        compiler_params=pltpu.CompilerParams(
            collective_id=1, has_side_effects=True, vmem_limit_bytes=VMEM_ALL
        ),
    )(dx, wq.T, wk.T, wv.T, norm, att, tokens, vectors, resid, small)


def settle_kernel(
    gtok_hbm, gw_hbm, go_hbm, sums_ref,
    gtok_out, wq_ref, wk_ref, wv_ref, wo_ref,
    g1_ref, b1_ref, g2_ref, b2_ref, bo_ref, bf2_ref, bq_ref, bv_ref, bf1_ref,
    gtok, gw, go, sems,
):
    width, units = wq_ref.shape[0], bf1_ref.shape[0]
    loads = loading(sems, ((gtok_hbm, gtok), (gw_hbm, gw), (go_hbm, go)))
    for row, ref in enumerate((g1_ref, b1_ref, g2_ref, b2_ref, bo_ref, bf2_ref)):
        ref[...] = sums_ref[row, :]
    bq_ref[...] = sums_ref[6:7, 0:width].reshape(width)
    bv_ref[...] = sums_ref[6:7, 2 * width : 3 * width].reshape(width)
    bf1_ref[...] = sums_ref[7:8, 0:units].reshape(units)
    loads[0].wait()
    out = pltpu.make_async_copy(gtok, gtok_out, sems.at[3])
    out.start()
    loads[1].wait()
    loads[2].wait()
    wq_ref[...] = gw[0:width, :].astype(F32)
    wk_ref[...] = gw[width : 2 * width, :].astype(F32)
    wv_ref[...] = gw[2 * width : 3 * width, :].astype(F32)
    wo_ref[...] = go[0:width, :].astype(F32)
    out.wait()


def settle(gtok, gw, go, sums, width, units):
    depth = gtok.shape[1]
    weight = jax.ShapeDtypeStruct((width, depth), F32)
    return pl.pallas_call(
        settle_kernel,
        name="settle",
        out_shape=(
            jax.ShapeDtypeStruct(gtok.shape, F32), weight, weight, weight, weight,
            *(jax.ShapeDtypeStruct((size,), F32) for size in (depth,) * 6 + (width, width, units)),
        ),
        in_specs=[HBM, HBM, HBM, VSPEC],
        out_specs=(HBM,) + (VSPEC,) * 13,
        scratch_shapes=[
            VMEM(gtok.shape, F32), VMEM(gw.shape, BF16), VMEM(go.shape, BF16), DMA((4,)),
        ],
        compiler_params=pltpu.CompilerParams(vmem_limit_bytes=VMEM_ALL),
    )(gtok, gw, go, sums)


def on_device(
    devices, parts, tokens, picture_ids, ln1_gain, ln1_bias, q_weight, q_bias, k_weight, v_weight, v_bias,
    o_weight, o_bias, ln2_gain, ln2_bias, fc1_weight, fc1_bias, fc2_weight, fc2_bias, out_grad,
):
    own_count, depth = tokens.shape
    hidden_local = fc1_weight.shape[1]
    width = q_weight.shape[1]
    norm1_all, q, k, v, o_all, vectors, span, id_row, own_ids = project(
        tokens,
        (ln1_gain, ln1_bias, o_bias, ln2_gain, ln2_bias, fc2_bias, fc1_bias, q_bias, v_bias),
        o_weight, q_weight, k_weight, v_weight, picture_ids[None, :], devices, parts,
    )
    q, k, v = (item.reshape(LEN, width) for item in (q, k, v))
    attended, log_total = attend(q, k, v, span, id_row)
    heads_first = attended.reshape(devices, own_count, width)
    output, grad_residual, grad_attended, fc_sum, small = middle(
        heads_first, o_all, fc1_weight, fc2_weight, tokens, out_grad,
        own_ids, vectors, parts,
    )
    dqkv, grad_fc1, grad_fc2, output = attend_back(
        q, k, v, span, id_row, attended, log_total, grad_attended.reshape(LEN, width),
        fc_sum.reshape(-1, depth), output, hidden_local,
    )
    grad_tokens, grad_w, grad_o, sums = close(
        dqkv.reshape(devices, own_count, 3 * width), q_weight, k_weight, v_weight, norm1_all,
        heads_first, tokens, vectors, grad_residual, small, parts,
    )
    (
        grad_tokens, grad_q, grad_k, grad_v, grad_o, grad_g1, grad_b1, grad_g2, grad_b2, grad_bo,
        grad_bf2, grad_bq, grad_bv, grad_bf1,
    ) = settle(
        grad_tokens, grad_w.reshape(-1, depth), grad_o.reshape(-1, depth), sums, width, hidden_local
    )
    return (
        output, grad_tokens, grad_g1, grad_b1, grad_q.T, grad_bq, grad_k.T, grad_v.T, grad_bv,
        grad_o, grad_bo, grad_g2, grad_b2, grad_fc1.T, grad_bf1, grad_fc2, grad_bf2,
    )


def solution(mesh):
    rows, whole = P(("dp", "tensor"), None), P()
    columns, down, along = P(None, "tensor"), P("tensor", None), P("tensor")
    return jax.shard_map(
        functools.partial(on_device, mesh.shape["tensor"], mesh.shape["dp"]),
        mesh=mesh,
        in_specs=(
            rows, P("dp"), whole, whole, columns, along, columns, columns, along, down, whole,
            whole, whole, columns, along, down, whole, rows,
        ),
        out_specs=(
            rows, rows, whole, whole, columns, along, columns, columns, along, down, whole,
            whole, whole, columns, along, down, whole,
        ),
        check_vma=False,
    )
```

```python
import functools

import jax
import jax.numpy as jnp
from jax import lax
from jax.experimental import pallas as pl
from jax.experimental.pallas import tpu as pltpu
from jax.sharding import PartitionSpec as P

HD = 72
LEN = 2048
BLOCK = 256
NORM_EPS = 1e-06
NEG_FILL = -1e30
LOG2E = 1.4426950408889634
VMEM_ALL = 67043328
BF16 = jnp.bfloat16
F32 = jnp.float32
MESH = pl.DeviceIdType.MESH
VMEM = pltpu.VMEM
DMA = pltpu.SemaphoreType.DMA
VSPEC = pl.BlockSpec(memory_space=pltpu.VMEM)
SSPEC = pl.BlockSpec(memory_space=pltpu.SMEM)
HBM = pl.BlockSpec(memory_space=pltpu.HBM)


def nn(left, right):
    return lax.dot_general(left, right, (((1,), (0,)), ((), ())), preferred_element_type=F32)


def nt(left, right):
    return lax.dot_general(left, right, (((1,), (1,)), ((), ())), preferred_element_type=F32)


def tn(left, right):
    return lax.dot_general(left, right, (((0,), (0,)), ((), ())), preferred_element_type=F32)


def remote(src, dst, send_sem, recv_sem, **where):
    return pltpu.make_async_remote_copy(
        src_ref=src, dst_ref=dst, send_sem=send_sem, recv_sem=recv_sem,
        device_id=where, device_id_type=MESH,
    )


def loading(sems, pairs):
    copies = [
        pltpu.make_async_copy(src, dst, sems.at[index]) for index, (src, dst) in enumerate(pairs)
    ]
    for copy in copies:
        copy.start()
    return copies


def place():
    me = lax.axis_index("tensor")
    core = lax.rem(me, 2)
    return me, core, lax.div(me, 2)


def greet_peers(axes):
    barrier = pltpu.get_barrier_semaphore()
    for axis, size in axes:
        me = lax.axis_index(axis)

        def greet(step, carry):
            pl.semaphore_signal(
                barrier, inc=1, device_id={axis: lax.rem(me + step, size)}, device_id_type=MESH
            )
            return carry

        lax.fori_loop(1, size, greet, 0)
    pl.semaphore_wait(barrier, sum(size - 1 for _, size in axes))


def normalize(values):
    average = jnp.mean(values, axis=-1, keepdims=True)
    centred = values - average
    variance = jnp.mean(centred * centred, axis=-1, keepdims=True)
    scale = lax.rsqrt(variance + NORM_EPS)
    return centred * scale, scale


class LineGather:
    def __init__(self, stages, buffer, send_sem, recv_sem):
        self.stages, self.buffer, self.send_sem, self.recv_sem = stages, buffer, send_sem, recv_sem
        self.me, self.core, self.stage = place()
        self.partner = self.me + 1 - 2 * self.core

    def copy(self, block, way, target):
        return remote(
            self.buffer.at[block], self.buffer.at[block],
            self.send_sem.at[block, way], self.recv_sem.at[block], tensor=target,
        )

    def each_copy(self, block, right, left, act):
        pl.when(right)(lambda: act(self.copy(block, 0, self.me + 2)))
        pl.when(left)(lambda: act(self.copy(block, 1, self.me - 2)))
        act(self.copy(block, 2, self.partner))

    def start(self):
        self.each_copy(
            self.me, self.stage < self.stages - 1, self.stage > 0, lambda copy: copy.start()
        )

    def start_inward(self):
        low = self.stage < self.stages // 2
        self.each_copy(self.me, low, jnp.logical_not(low), lambda copy: copy.start())

    def start_outward(self):
        low = self.stage < self.stages // 2
        pl.when(jnp.logical_not(low) & (self.stage < self.stages - 1))(
            lambda: self.copy(self.me, 0, self.me + 2).start()
        )
        pl.when(low & (self.stage > 0))(lambda: self.copy(self.me, 1, self.me - 2).start())

    def incoming(self, reach, side, core):
        far = jnp.where(side == 0, self.stage - reach, self.stage + reach)
        return (far >= 0) & (far < self.stages), 2 * far + core

    def arrive(self, block):
        self.copy(block, 2, self.partner).wait_recv()

    def ways(self, side):
        return (side == 0) & (self.stage < self.stages - 1), (side == 1) & (self.stage > 0)

    def relay(self, reach):
        for side in range(2):
            valid, block = self.incoming(reach, side, self.core)

            @pl.when(valid)
            def _():
                self.arrive(block)
                self.each_copy(block, *self.ways(jnp.int32(side)), lambda copy: copy.start())

    def use_own(self, compute):
        compute(self.me)
        self.arrive(self.partner)
        compute(self.partner)

    def use(self, reach, compute):
        def body(index, carry):
            side, other = lax.rem(index, 2), lax.div(index, 2)
            valid, block = self.incoming(
                reach, side, jnp.where(other == 0, self.core, 1 - self.core)
            )

            @pl.when(valid)
            def _():
                pl.when(other == 1)(lambda: self.arrive(block))
                compute(block)

            return carry

        lax.fori_loop(0, 4, body, 0)

    def run(self, compute, after_first=lambda: None, before_last=lambda: None):
        def body(reach, carry):
            pl.when(reach == self.stages - 1)(before_last)
            self.relay(reach)
            pl.when(reach == 1)(after_first)
            self.use(reach, compute)
            return carry

        self.use_own(compute)
        lax.fori_loop(1, self.stages, body, 0)

    def at_end(self):
        return (self.stage == 0) | (self.stage == self.stages - 1)

    def finish(self):
        self.each_copy(
            self.me, self.stage < self.stages - 1, self.stage > 0, lambda copy: copy.wait_send()
        )

        def body(index, carry):
            reach, side = lax.div(index, 2) + 1, lax.rem(index, 2)
            valid, block = self.incoming(reach, side, self.core)

            @pl.when(valid)
            def _():
                self.each_copy(block, *self.ways(side), lambda copy: copy.wait_send())

            return carry

        lax.fori_loop(0, 2 * (self.stages - 1), body, 0)


class LineScatter:
    def __init__(self, stages, partial, cross, lane, sems):
        self.stages, self.partial, self.cross, self.lane = stages, partial, cross, lane
        self.cross_send, self.cross_recv, self.lane_send, self.lane_recv = sems
        self.me, self.core, self.stage = place()
        self.partner = self.me + 1 - 2 * self.core

    def cross_copy(self, far):
        return remote(
            self.partial.at[2 * far + 1 - self.core], self.cross.at[far],
            self.cross_send.at[far], self.cross_recv.at[far], tensor=self.partner,
        )

    def slot(self, way, far, holder):
        return far if way == 0 else jnp.where(far == holder, self.stages, far)

    def lane_copy(self, way, far, holder):
        target = self.me + 2 if way == 0 else self.me - 2
        slot = self.slot(way, far, holder)
        return remote(
            self.partial.at[2 * far + self.core], self.lane.at[slot],
            self.lane_send.at[far], self.lane_recv.at[slot], tensor=target,
        )

    def sent(self, way, far):
        return self.lane_copy(way, far, self.stage + (1 if way == 0 else -1))

    def received(self, way, far):
        self.lane_copy(way, far, self.stage).wait_recv()
        return self.lane[self.slot(way, far, self.stage)].astype(F32)

    def put(self, block, value):
        self.partial[block] = value.astype(BF16)

        @pl.when(lax.rem(block, 2) != self.core)
        def _():
            self.cross_copy(lax.div(block, 2)).start()

    def produce(self, compute):
        def body(index, carry):
            reach = self.stages - 1 - lax.div(index, 4)
            side, other = lax.rem(lax.div(index, 2), 2), lax.rem(index, 2)
            far = jnp.where(side == 0, self.stage + reach, self.stage - reach)

            @pl.when((far >= 0) & (far < self.stages) & ((reach > 0) | (side == 0)))
            def _():
                block = 2 * far + jnp.where(other == 0, 1 - self.core, self.core)
                self.put(block, compute(block))

            return carry

        lax.fori_loop(0, 4 * self.stages, body, 0)

    def chip_sum(self, far):
        return self.partial[2 * far + self.core].astype(F32) + self.cross[far].astype(F32)

    def send_sum(self, way, far, incoming):
        self.cross_copy(far).wait_recv()
        block = 2 * far + self.core

        @pl.when(incoming)
        def _():
            self.partial[block] = (self.chip_sum(far) + self.received(way, far)).astype(BF16)

        @pl.when(jnp.logical_not(incoming))
        def _():
            self.partial[block] = self.chip_sum(far).astype(BF16)

        self.sent(way, far).start()

    def step(self, reach):
        right, left = self.stage + reach, self.stage - reach
        pl.when(right < self.stages)(lambda: self.send_sum(0, right, self.stage > 0))
        pl.when(left >= 0)(lambda: self.send_sum(1, left, self.stage < self.stages - 1))

    def steps(self, first, last):
        lax.fori_loop(first, last, lambda index, carry: (self.step(self.stages - 1 - index), carry)[1], 0)

    def own(self, total_ref):
        self.cross_copy(self.stage).wait_recv()
        total_ref[...] = self.chip_sum(self.stage)

        @pl.when(self.stage > 0)
        def _():
            total_ref[...] += self.received(0, self.stage)

        @pl.when(self.stage < self.stages - 1)
        def _():
            total_ref[...] += self.received(1, self.stage)

    def finish(self):
        def body(far, carry):
            self.cross_copy(far).wait_send()
            pl.when(far > self.stage)(lambda: self.sent(0, far).wait_send())
            pl.when(far < self.stage)(lambda: self.sent(1, far).wait_send())
            return carry

        lax.fori_loop(0, self.stages, body, 0)


def scatter_shapes(stages, rows, depth):
    return [
        VMEM((2 * stages, rows, depth), BF16), VMEM((stages, rows, depth), BF16),
        VMEM((stages + 1, rows, depth), BF16),
        DMA((stages,)), DMA((stages,)), DMA((stages,)), DMA((stages + 1,)),
    ]


def exchange(axis, size, slots, send_sem, recv_sem):
    me = lax.axis_index(axis)

    def copy_to(other, slot):
        return remote(
            slots.at[slot], slots.at[slot], send_sem.at[other], recv_sem.at[slot], **{axis: other}
        )

    def start(step, carry):
        copy_to(lax.rem(me + step, size), me).start()
        return carry

    def wait(step, carry):
        other = lax.rem(me + step, size)
        copy_to(other, other).wait_recv()
        copy_to(other, me).wait_send()
        return carry

    lax.fori_loop(1, size, start, 0)
    return lambda: lax.fori_loop(1, size, wait, 0)


def piece_height(height, parts):
    return -(-height // (16 * parts)) * 16


class RowSum:
    def __init__(self, parts, piece, arrive, send_sem, recv_sem):
        self.parts, self.piece, self.arrive = parts, piece, arrive
        self.send_sem, self.recv_sem = send_sem, recv_sem
        self.row = lax.axis_index("dp")

    def copy(self, other, source):
        return remote(
            self.piece.at[other], self.arrive.at[source],
            self.send_sem.at[other], self.recv_sem.at[source], dp=other,
        )

    def others(self, act, start):
        return lax.fori_loop(
            1, self.parts, lambda step, carry: act(lax.rem(self.row + step, self.parts), carry), start
        )

    def start(self, total):
        high = self.piece.shape[1]
        for part in range(self.parts):
            self.piece[part] = total[part * high : (part + 1) * high, :].astype(BF16)

        def send(other, carry):
            self.copy(other, self.row).start()
            return carry

        self.others(send, 0)

    def reduce(self):
        def add(other, so_far):
            self.copy(other, other).wait_recv()
            self.copy(other, self.row).wait_send()
            return so_far + self.arrive[other].astype(F32)

        return self.others(add, self.piece[self.row].astype(F32)).astype(BF16)


def rowsum_shapes(parts, high, depth):
    return [
        VMEM((parts, high, depth), BF16), VMEM((parts, high, depth), BF16), DMA((parts,)), DMA((parts,)),
    ]


def column(row):
    return jnp.broadcast_to(row, (128, row.shape[1])).T[:, :1]


def piece_rows(width, parts):
    return min(rows for rows in range(8, width + 1, 8) if width % rows == 0 and width // rows <= parts)


class WeightSpread:
    def __init__(self, stages, parts, buffer, sems):
        self.stages, self.parts, self.buffer = stages, parts, buffer
        self.line_send, self.line_recv, self.row_send, self.row_recv, self.core_send, self.core_recv = sems
        self.count = buffer.shape[0]
        self.me, self.core, self.stage = place()
        self.partner = self.me + 1 - 2 * self.core
        self.row = lax.axis_index("dp")
        self.here = self.row < self.count
        self.slot = jnp.minimum(self.row, self.count - 1)

    def copy(self, source, block, send_sem, recv_sem, **where):
        ref = self.buffer.at[source, block]
        return remote(ref, ref, send_sem, recv_sem, **where)

    def line_copy(self, other, far):
        return self.copy(
            self.slot, 2 * far + self.core, self.line_send.at[other], self.line_recv.at[far],
            tensor=2 * other + self.core,
        )

    def row_copy(self, other, source, far):
        return self.copy(
            source, 2 * far + self.core, self.row_send.at[other, far], self.row_recv.at[source, far],
            dp=other,
        )

    def core_copy(self, source, far, core):
        return self.copy(
            source, 2 * far + core, self.core_send.at[source, far], self.core_recv.at[source, far],
            tensor=self.partner,
        )

    def other_stages(self, act):
        def body(step, carry):
            act(lax.rem(self.stage + step, self.stages))
            return carry

        lax.fori_loop(1, self.stages, body, 0)

    def other_rows(self, act):
        def body(index, carry):
            step = lax.div(index, self.stages) + 1
            act(lax.rem(self.row + step, self.parts), lax.rem(index, self.stages))
            return carry

        lax.fori_loop(0, (self.parts - 1) * self.stages, body, 0)

    def pieces(self, act):
        def body(index, carry):
            act(lax.div(index, self.stages), lax.rem(index, self.stages))
            return carry

        lax.fori_loop(0, self.count * self.stages, body, 0)

    def start(self):
        self.other_stages(lambda other: self.line_copy(other, self.stage).start())

    def to_rows(self):
        self.other_stages(lambda other: self.line_copy(other, other).wait_recv())
        self.other_rows(lambda other, far: self.row_copy(other, self.slot, far).start())

    def pass_on(self):
        def act(source, far):
            pl.when(source != self.row)(lambda: self.row_copy(self.row, source, far).wait_recv())
            self.core_copy(source, far, self.core).start()

        self.pieces(act)

    def finish(self):
        @pl.when(self.here)
        def _():
            self.other_stages(lambda other: self.line_copy(other, self.stage).wait_send())
            self.other_rows(lambda other, far: self.row_copy(other, self.slot, far).wait_send())

        def act(source, far):
            self.core_copy(source, far, 1 - self.core).wait_recv()
            self.core_copy(source, far, self.core).wait_send()

        self.pieces(act)


def project_kernel(
    stages, parts, tok_hbm, g1_ref, b1_ref, bo_ref, g2_ref, b2_ref, bf2_ref, bf1_ref, bq_ref, bv_ref, wo_hbm, wq_hbm, wk_hbm, wv_hbm, ids_ref,
    norm_hbm, q_hbm, k_hbm, v_hbm, wo_out, vec_ref, span_ref, idr_ref, ido_ref,
    wo_all, line_send, line_recv, row_send, row_recv, core_send, core_recv, tok, norm, q_ref, k_ref, v_ref, weight, send_sem, recv_sem, out_sem, load_sem,
):
    me, _, _ = place()
    width, rows = wq_hbm.shape[0], tok.shape[0]
    loads = loading(
        load_sem,
        ((tok_hbm, tok), (wq_hbm, weight.at[0]), (wk_hbm, weight.at[1]), (wv_hbm, weight.at[2])),
    )
    spread = WeightSpread(
        stages, parts, wo_all, (line_send, line_recv, row_send, row_recv, core_send, core_recv)
    )
    high = wo_all.shape[2]
    own_piece = pltpu.make_async_copy(
        wo_hbm.at[pl.ds(pl.multiple_of(spread.slot * high, high), high)],
        wo_all.at[spread.slot, me], load_sem.at[4],
    )
    pl.when(spread.here)(own_piece.start)
    vec_ref[...] = jnp.zeros_like(vec_ref)
    for index, ref in enumerate(
        (g1_ref, b1_ref, bo_ref, g2_ref, b2_ref, bf2_ref, bf1_ref, bq_ref, bv_ref)
    ):
        vec_ref[index : index + 1, 0 : ref.shape[0]] = ref[...].astype(F32)[None, :]
    greet_peers((("tensor", 2 * stages), ("dp", parts)))

    @pl.when(spread.here)
    def _():
        own_piece.wait()
        spread.start()

    loads[0].wait()
    normed, _ = normalize(tok[...].astype(F32))
    norm[me] = (normed * vec_ref[0:1, :] + vec_ref[1:2, :]).astype(BF16)
    gather = LineGather(stages, norm, send_sem, recv_sem)
    gather.start()
    ids = ids_ref[...].astype(F32)
    idr_ref[...] = ids
    ido_ref[...] = idr_ref[:, pl.ds(pl.multiple_of(me * rows, rows), rows)]
    for block in range(ids.shape[1] // BLOCK):
        first = ids[:, block * BLOCK : block * BLOCK + 1]
        last = ids[:, (block + 1) * BLOCK - 1 : (block + 1) * BLOCK]
        begin = jnp.sum(jnp.where(ids > first, 1.0, 0.0))
        end = jnp.sum(jnp.where(ids >= jnp.maximum(last, 1.0), 1.0, 0.0))
        span_ref[0, block] = lax.div(begin.astype(jnp.int32), BLOCK)
        span_ref[1, block] = lax.div(end.astype(jnp.int32) + (BLOCK - 1), BLOCK)
    for load in loads[1:]:
        load.wait()

    def keep(block):
        return [
            pltpu.make_async_copy(src.at[block], dst.at[block], out_sem.at[index, block])
            for index, (src, dst) in enumerate(
                ((norm, norm_hbm), (q_ref, q_hbm), (k_ref, k_hbm), (v_ref, v_hbm))
            )
        ]

    def compute(block):
        q_ref[block] = (nt(norm[block], weight[0]) + vec_ref[7:8, :width]).astype(BF16)
        k_ref[block] = nt(norm[block], weight[1]).astype(BF16)
        v_ref[block] = (nt(norm[block], weight[2]) + vec_ref[8:9, :width]).astype(BF16)
        for copy in keep(block):
            copy.start()

    gather.run(compute, lambda: pl.when(spread.here)(spread.to_rows), spread.pass_on)
    spread.finish()
    out_copy = pltpu.make_async_copy(wo_all, wo_out, load_sem.at[5])
    out_copy.start()
    gather.finish()

    def kept(block, carry):
        for copy in keep(block):
            copy.wait()
        return carry

    lax.fori_loop(0, 2 * stages, kept, 0)
    out_copy.wait()


def project(tokens, vectors, wo, wq, wk, wv, ids, devices, parts):
    rows, depth = tokens.shape
    width, length = wq.shape[1], ids.shape[1]
    stages = devices // 2
    high = piece_rows(width, parts)
    head = jax.ShapeDtypeStruct((devices, rows, width), BF16)
    pieces = (width // high, devices, high, depth)
    return pl.pallas_call(
        functools.partial(project_kernel, stages, parts),
        name="project",
        out_shape=(
            jax.ShapeDtypeStruct((devices, rows, depth), BF16), head, head, head,
            jax.ShapeDtypeStruct(pieces, BF16), jax.ShapeDtypeStruct((16, depth), F32),
            jax.ShapeDtypeStruct((2, length // BLOCK), jnp.int32),
            jax.ShapeDtypeStruct((1, length), F32), jax.ShapeDtypeStruct((1, rows), F32),
        ),
        in_specs=[HBM] + [VSPEC] * 9 + [HBM, HBM, HBM, HBM, VSPEC],
        out_specs=(HBM, HBM, HBM, HBM, HBM, VSPEC, SSPEC, VSPEC, VSPEC),
        scratch_shapes=[
            VMEM(pieces, BF16), DMA((stages,)), DMA((stages,)),
            *[DMA((parts, stages))] * 4,
            VMEM((rows, depth), BF16), VMEM((devices, rows, depth), BF16),
            *[VMEM((devices, rows, width), BF16)] * 3, VMEM((3, width, depth), BF16),
            DMA((devices, 3)), DMA((devices,)), DMA((4, devices)), DMA((6,)),
        ],
        compiler_params=pltpu.CompilerParams(
            collective_id=0, has_side_effects=True, vmem_limit_bytes=VMEM_ALL
        ),
    )(tokens, *vectors, wo, wq.T, wk.T, wv.T, ids)


def lanes_of(head, width):
    lane = lax.broadcasted_iota(jnp.int32, (1, width), 1)
    return (lane >= head * HD) & (lane < (head + 1) * HD)


def fill_columns(row_ref, column_ref):
    for block in range(row_ref.shape[1] // BLOCK):
        at = pl.ds(block * BLOCK, BLOCK)
        column_ref[at, :] = column(row_ref[:, at])


def head_rows(head, width):
    row = lax.broadcasted_iota(jnp.int32, (width, 1), 0)
    return (row >= head * HD) & (row < (head + 1) * HD)


def side_by_side(block_t, heads):
    width = block_t.shape[0]
    zero = jnp.zeros_like(block_t)
    return jnp.concatenate([jnp.where(head_rows(h, width), block_t, zero) for h in range(heads)], axis=1)


def stacked(block, heads):
    width = block.shape[1]
    zero = jnp.zeros_like(block)
    return jnp.concatenate([jnp.where(lanes_of(h, width), block, zero) for h in range(heads)], axis=0)


def repeat_lanes(row, heads):
    return jnp.concatenate([row] * heads, axis=1)


def attend_kernel(
    heads, span_ref, q_hbm, k_hbm, v_hbm, idr_ref, o_ref, log_ref,
    q_ref, k_ref, v_ref, load_sem, idc_ref, vt_ref, acc_ref,
):
    length, width = q_ref.shape
    scale = HD ** (-0.5) * LOG2E
    loads = loading(load_sem, ((v_hbm, v_ref), (q_hbm, q_ref), (k_hbm, k_ref)))
    fill_columns(idr_ref, idc_ref)
    for load in loads:
        load.wait()

    def turn(block, total):
        at = pl.ds(pl.multiple_of(block * BLOCK, BLOCK), BLOCK)
        value = v_ref[at, :].astype(F32)
        vt_ref[block] = value.T.astype(BF16)
        return total + jnp.sum(value, axis=0, keepdims=True)

    mean_value = column(
        lax.fori_loop(0, length // BLOCK, turn, jnp.zeros((1, width), F32)) * (1.0 / length)
    )
    rows = o_ref.shape[2]

    def per_block(block, carry):
        at = pl.ds(pl.multiple_of(block * BLOCK, BLOCK), BLOCK)
        query = side_by_side(q_ref[at, :].astype(F32).T.astype(BF16), heads)
        id_row = idr_ref[:, at]
        id_rows = repeat_lanes(id_row, heads)
        acc_ref[...] = jnp.zeros_like(acc_ref)

        def per_key(other, state):
            top, total = state
            keys_at = pl.ds(pl.multiple_of(other * BLOCK, BLOCK), BLOCK)
            id_col = idc_ref[keys_at, :]
            allowed = (id_col == id_rows) & (id_col > 0)
            scores = jnp.where(allowed, nn(k_ref[keys_at, :], query) * scale, NEG_FILL)
            new_top = jnp.maximum(top, jnp.max(scores, axis=0, keepdims=True))
            weight = jnp.exp2(scores - new_top)
            shrink = jnp.exp2(top - new_top)
            total = total * shrink + jnp.sum(weight, axis=0, keepdims=True)
            acc_ref[...] = acc_ref[...] * shrink + nn(vt_ref[other], weight.astype(BF16))
            return new_top, total

        top, total = lax.fori_loop(
            span_ref[0, block], span_ref[1, block], per_key,
            (jnp.full((1, heads * BLOCK), NEG_FILL, F32), jnp.zeros((1, heads * BLOCK), F32)),
        )
        scaled = acc_ref[...] / total
        logs = jnp.where(id_rows == 0, 0.0, top + jnp.log2(total))
        result = jnp.zeros((width, BLOCK), F32)
        for h in range(heads):
            here = slice(h * BLOCK, (h + 1) * BLOCK)
            result = jnp.where(head_rows(h, width), scaled[:, here], result)
            log_ref[h : h + 1, at] = logs[:, here]
        result = jnp.where(id_row == 0, mean_value, result).astype(BF16)
        for part in range(BLOCK // rows):
            o_ref[block * (BLOCK // rows) + part] = result[:, part * rows : (part + 1) * rows]
        return carry

    lax.fori_loop(0, length // BLOCK, per_block, 0)


def attend(q, k, v, span, id_row, devices):
    length, width = q.shape
    heads = width // HD
    return pl.pallas_call(
        functools.partial(attend_kernel, heads),
        name="attend",
        out_shape=(
            jax.ShapeDtypeStruct((devices, width, length // devices), BF16),
            jax.ShapeDtypeStruct((heads, length), F32),
        ),
        in_specs=[SSPEC, HBM, HBM, HBM, VSPEC],
        out_specs=(VSPEC,) * 2,
        scratch_shapes=[
            *[VMEM((length, width), BF16)] * 3, DMA((3,)),
            VMEM((length, 1), F32), VMEM((length // BLOCK, width, BLOCK), BF16),
            VMEM((width, heads * BLOCK), F32),
        ],
        compiler_params=pltpu.CompilerParams(vmem_limit_bytes=VMEM_ALL),
    )(span, q, k, v, id_row)


def attend_back_kernel(
    heads, span_ref, q_hbm, k_hbm, v_hbm, idr_ref, o_hbm, log_ref, g_hbm, fc_hbm, layer_hbm,
    out_ref, fc1_hbm, fc2_hbm, layer_out, fc, fc1, fc2, layer, side_sem, q_ref, k_ref, v_ref, o_ref, g_ref, load_sem,
    idc_ref, dq_ref, dk_ref, dv_ref, q_side, q_stack, g_side, g_stack, row_ref, log_side,
):
    length, width = q_ref.shape
    score_scale = HD ** (-0.5)
    loads = loading(
        load_sem, ((q_hbm, q_ref), (g_hbm, g_ref), (o_hbm, o_ref), (k_hbm, k_ref), (v_hbm, v_ref))
    )
    layer_in = pltpu.make_async_copy(layer_hbm, layer, side_sem.at[0])
    fc_in = pltpu.make_async_copy(fc_hbm, fc, side_sem.at[1])
    layer_in.start()
    fc_in.start()
    dq_ref[...] = jnp.zeros_like(dq_ref)
    fill_columns(idr_ref, idc_ref)
    for load in loads:
        load.wait()

    def prepare(block, pad):
        at = pl.ds(pl.multiple_of(block * BLOCK, BLOCK), BLOCK)
        query = q_ref[at, :]
        many = BLOCK // g_ref.shape[2]
        grad_t = jnp.concatenate([g_ref[block * many + part] for part in range(many)], axis=1)
        out_t = jnp.concatenate([o_ref[block * many + part] for part in range(many)], axis=1)
        wide_t = grad_t.astype(F32)
        wide = wide_t.T
        product = wide_t * out_t.astype(F32)
        q_side[block] = side_by_side(query.astype(F32).T.astype(BF16), heads)
        g_side[block] = side_by_side(grad_t, heads)
        q_stack[block] = stacked(query, heads)
        g_stack[block] = stacked(wide.astype(BF16), heads)
        for h in range(heads):
            here = slice(h * BLOCK, (h + 1) * BLOCK)
            row_ref[block, :, here] = jnp.sum(
                jnp.where(head_rows(h, width), product, 0.0), axis=0, keepdims=True
            )
            log_side[block, :, here] = log_ref[h : h + 1, at]
        return pad + jnp.sum(jnp.where(idc_ref[at, :] == 0, wide, 0.0), axis=0, keepdims=True)

    pad = lax.fori_loop(0, length // BLOCK, prepare, jnp.zeros((1, width), F32)) * (1.0 / length)
    units = fc1.shape[0]
    second = -(-units // 16) * 16
    layer_in.wait()
    fc_in.wait()
    fc1[...] = fc[0:units, :].astype(F32)
    fc2[...] = fc[second : second + units, :].astype(F32)
    outs = [
        pltpu.make_async_copy(src, dst, side_sem.at[2 + index])
        for index, (src, dst) in enumerate(((layer, layer_out), (fc1, fc1_hbm), (fc2, fc2_hbm)))
    ]
    for out in outs:
        out.start()

    def per_key(block, carry):
        at = pl.ds(pl.multiple_of(block * BLOCK, BLOCK), BLOCK)
        key, value, id_col = k_ref[at, :], v_ref[at, :], idc_ref[at, :]
        key_side = side_by_side(key.astype(F32).T.astype(BF16), heads)
        real = id_col > 0
        dk_ref[...] = jnp.zeros_like(dk_ref)
        dv_ref[...] = jnp.zeros_like(dv_ref)

        def per_query(other, inner):
            query_at = pl.ds(pl.multiple_of(other * BLOCK, BLOCK), BLOCK)
            allowed = (id_col == repeat_lanes(idr_ref[:, query_at], heads)) & real
            scores = nn(key, q_side[other]) * (score_scale * LOG2E) - log_side[other]
            prob = jnp.exp2(jnp.where(allowed, scores, NEG_FILL))
            dv_ref[...] += nn(prob.astype(BF16), g_stack[other])
            back = (prob * (nn(value, g_side[other]) - row_ref[other])).astype(BF16)
            dk_ref[...] += nn(back, q_stack[other])
            back_rows = jnp.concatenate(
                [back[:, h * BLOCK : (h + 1) * BLOCK] for h in range(heads)], axis=0
            )
            dq_ref[other] += nn(key_side, back_rows)
            return inner

        lax.fori_loop(span_ref[0, block], span_ref[1, block], per_query, 0)
        out_ref[at, width : 2 * width] = (dk_ref[...] * score_scale).astype(BF16)
        out_ref[at, 2 * width :] = (dv_ref[...] + pad).astype(BF16)
        return carry

    lax.fori_loop(0, length // BLOCK, per_key, 0)

    def settle(block, carry):
        at = pl.ds(pl.multiple_of(block * BLOCK, BLOCK), BLOCK)
        out_ref[at, :width] = (dq_ref[block].T * score_scale).astype(BF16)
        return carry

    lax.fori_loop(0, length // BLOCK, settle, 0)
    for out in outs:
        out.wait()


def attend_back(q, k, v, span, id_row, o, log_total, grad, fc, layer, units):
    length, width = q.shape
    heads = width // HD
    blocks, depth = length // BLOCK, layer.shape[1]
    whole = VMEM((length, width), BF16)
    side, stack = VMEM((blocks, width, heads * BLOCK), BF16), VMEM((blocks, heads * BLOCK, width), BF16)
    line = VMEM((blocks, 1, heads * BLOCK), F32)
    return pl.pallas_call(
        functools.partial(attend_back_kernel, heads),
        name="attend_back",
        out_shape=(
            jax.ShapeDtypeStruct((length, 3 * width), BF16), jax.ShapeDtypeStruct((units, depth), F32),
            jax.ShapeDtypeStruct((units, depth), F32), jax.ShapeDtypeStruct(layer.shape, BF16),
        ),
        in_specs=[SSPEC, HBM, HBM, HBM, VSPEC, HBM, VSPEC, HBM, HBM, HBM],
        out_specs=(VSPEC, HBM, HBM, HBM),
        scratch_shapes=[
            VMEM(fc.shape, BF16), VMEM((units, depth), F32), VMEM((units, depth), F32),
            VMEM(layer.shape, BF16), DMA((5,)),
            whole, whole, whole, VMEM(o.shape, BF16), VMEM(grad.shape, BF16), DMA((5,)),
            VMEM((length, 1), F32), VMEM((blocks, width, BLOCK), F32), VMEM((BLOCK, width), F32),
            VMEM((BLOCK, width), F32), side, stack, side, stack, line, line,
        ],
        compiler_params=pltpu.CompilerParams(vmem_limit_bytes=VMEM_ALL),
    )(span, q, k, v, id_row, o, log_total, grad, fc, layer)


def gelu_pair(u):
    slope = (2.0 / jnp.pi) ** 0.5
    bent = jnp.tanh(slope * (u + 0.044715 * u * u * u))
    half = 0.5 * (1.0 + bent)
    return u * half, half + 0.5 * u * (1.0 - bent * bent) * slope * (1.0 + 3 * 0.044715 * u * u)


def middle_kernel(
    stages, parts, att_hbm, wo_hbm, fc1_hbm, fc2_hbm, tok_hbm, top_hbm, ids_ref, vec_ref,
    out_ref, gres_ref, gatt_ref, fc_hbm, small_ref,
    wo, fc1, fc2, tok, top, load_sem,
    held, held_send, held_recv, norm_all, norm_send, norm_recv, top_all, top_send, top_recv,
    hidden, slope, grad_pre,
    br_part, br_cross, br_lane, br_s0, br_s1, br_s2, br_s3,
    gn_part, gn_cross, gn_lane, gn_s0, gn_s1, gn_s2, gn_s3,
    resid, total, acc, piece, arrive, piece_send, piece_recv, fa_send, fa_recv, free_sem, out_sem,
    back, back_send, back_recv,
):
    me, _, _ = place()
    devices = 2 * stages
    rows, depth = tok_hbm.shape
    high = wo_hbm.shape[2]
    units = fc1_hbm.shape[0]
    second = -(-units // 16) * 16
    loads = loading(
        load_sem,
        ((tok_hbm, tok), (top_hbm, top), (fc1_hbm, fc1), (fc2_hbm, fc2), (att_hbm.at[me], held.at[me]),
         *((wo_hbm.at[index], wo.at[:, pl.ds(index * high, high)]) for index in range(wo_hbm.shape[0]))),
    )
    greet_peers((("tensor", devices), ("dp", parts)))

    def held_copy(other, source):
        return remote(
            att_hbm.at[other], held.at[source], held_send.at[other], held_recv.at[source], tensor=other
        )

    def send_held(step, carry):
        held_copy(lax.rem(me + step, devices), me).start()
        return carry

    lax.fori_loop(1, devices, send_held, 0)
    gather2 = LineGather(stages, norm_all, norm_send, norm_recv)
    gather3 = LineGather(stages, top_all, top_send, top_recv)
    branch = LineScatter(stages, br_part, br_cross, br_lane, (br_s0, br_s1, br_s2, br_s3))
    gnorm = LineScatter(stages, gn_part, gn_cross, gn_lane, (gn_s0, gn_s1, gn_s2, gn_s3))

    mask = column(jnp.where(ids_ref[...] > 0, 1.0, 0.0))
    acc[...] = jnp.zeros_like(acc)
    small_ref[...] = jnp.zeros_like(small_ref)
    loads[0].wait()
    loads[1].wait()
    top_own = top[...].astype(F32) * mask
    top_all[me] = top_own.astype(BF16)
    small_ref[5:6, :] = jnp.sum(top_own, axis=0, keepdims=True)
    resid[...] = tok[...].astype(F32) + vec_ref[2:3, :]
    for load in loads[4:]:
        load.wait()
    resid[...] += tn(held[me], wo[me])

    def add_held(step, carry):
        other = lax.rem(me + devices - step, devices)
        held_copy(other, other).wait_recv()
        resid[...] += tn(held[other], wo[other])
        return carry

    lax.fori_loop(1, devices, add_held, 0)
    normed, _ = normalize(resid[...])
    norm_all[me] = (normed * vec_ref[3:4, :] + vec_ref[4:5, :]).astype(BF16)
    gather2.start()
    loads[2].wait()
    loads[3].wait()

    def forward(block):
        pre_act = nt(norm_all[block], fc1[...]) + vec_ref[6:7, 0:units]
        value, slope_now = gelu_pair(pre_act)
        hidden[block] = value.astype(BF16)
        slope[block] = slope_now.astype(BF16)
        branch.put(block, nn(hidden[block], fc2[...]))

    at_end = gather2.at_end()
    gather2.run(forward, lambda: pl.when(at_end)(gather3.start_inward))
    pl.when(jnp.logical_not(at_end))(gather3.start_inward)
    gather3.start_outward()
    pl.when(at_end)(lambda: branch.steps(0, stages - 1))

    def backward(block):
        grad = nt(top_all[block], fc2[...]) * slope[block].astype(F32)
        low = grad.astype(BF16)
        grad_pre[block] = low
        small_ref[7:8, 0:units] += jnp.sum(low.astype(F32), axis=0, keepdims=True)
        gnorm.put(block, nn(grad_pre[block], fc1[...]))
        acc[0:units, :] += tn(grad_pre[block], norm_all[block])
        acc[second : second + units, :] += tn(hidden[block], top_all[block])

    gather3.run(backward)
    gnorm.step(stages - 1)
    sums = RowSum(parts, piece, arrive, piece_send, piece_recv)
    sums.start(acc)

    pl.when(jnp.logical_not(at_end))(lambda: branch.steps(1, stages - 1))
    gnorm.steps(1, stages - 1)
    fc_sum = sums.reduce()

    def to_rows(act):
        lax.fori_loop(
            1, parts, lambda step, carry: (act(lax.rem(sums.row + step, parts)), carry)[1], 0
        )

    to_rows(
        lambda other: pl.semaphore_signal(
            free_sem, inc=1, device_id={"dp": other}, device_id_type=MESH
        )
    )
    pl.semaphore_wait(free_sem, parts - 1)
    arrive[sums.row] = fc_sum
    wait_fc = exchange("dp", parts, arrive, fa_send, fa_recv)
    branch.own(total)
    out_ref[...] = (mask * (resid[...] + total[...] + vec_ref[5:6, :])).astype(BF16)

    gnorm.own(total)
    grad = total[...]
    normed, scale = normalize(resid[...])
    small_ref[2:3, :] = jnp.sum(grad * normed, axis=0, keepdims=True)
    small_ref[3:4, :] = jnp.sum(grad, axis=0, keepdims=True)
    inner = grad * vec_ref[3:4, :]
    inner_mean = jnp.mean(inner, axis=-1, keepdims=True)
    inner_proj = jnp.mean(inner * normed, axis=-1, keepdims=True)
    grad_resid = top[...].astype(F32) * mask + scale * (inner - inner_mean - normed * inner_proj)
    gres_ref[...] = grad_resid
    tok[...] = grad_resid.astype(BF16)
    small_ref[4:5, :] = jnp.sum(grad_resid, axis=0, keepdims=True)

    def back_copy(other, source):
        return remote(
            back.at[other], gatt_ref.at[source], back_send.at[other], back_recv.at[source], tensor=other
        )

    def send_back(step, carry):
        other = lax.rem(me + step, devices)
        back[other] = nt(wo[other], tok[...]).astype(BF16)
        back_copy(other, me).start()
        return carry

    lax.fori_loop(1, devices, send_back, 0)
    gatt_ref[me] = nt(wo[me], tok[...]).astype(BF16)

    wait_fc()
    out_fc = pltpu.make_async_copy(arrive, fc_hbm, out_sem)
    out_fc.start()

    def settle(step, carry):
        other = lax.rem(me + devices - step, devices)
        back_copy(other, other).wait_recv()
        back_copy(other, me).wait_send()
        held_copy(other, me).wait_send()
        return carry

    lax.fori_loop(1, devices, settle, 0)
    gather2.finish()
    gather3.finish()
    branch.finish()
    gnorm.finish()
    out_fc.wait()


def middle(att, wo, fc1, fc2, tokens, out_grad, ids, vectors, parts):
    devices, width, rows = att.shape
    depth, units = fc1.shape
    stages = devices // 2
    high = piece_height(2 * (-(-units // 16) * 16), parts)
    return pl.pallas_call(
        functools.partial(middle_kernel, stages, parts),
        name="middle",
        out_shape=(
            jax.ShapeDtypeStruct((rows, depth), BF16),
            jax.ShapeDtypeStruct((rows, depth), F32),
            jax.ShapeDtypeStruct((devices, width, rows), BF16),
            jax.ShapeDtypeStruct((parts, high, depth), BF16),
            jax.ShapeDtypeStruct((8, depth), F32),
        ),
        in_specs=[HBM] * 6 + [VSPEC] * 2,
        out_specs=(VSPEC, VSPEC, VSPEC, HBM, VSPEC),
        scratch_shapes=[
            VMEM((devices, width, depth), BF16), VMEM((units, depth), BF16), VMEM((units, depth), BF16),
            VMEM((rows, depth), BF16), VMEM((rows, depth), BF16), DMA((5 + wo.shape[0],)),
            VMEM((devices, width, rows), BF16), DMA((devices,)), DMA((devices,)),
            VMEM((devices, rows, depth), BF16), DMA((devices, 3)), DMA((devices,)),
            VMEM((devices, rows, depth), BF16), DMA((devices, 3)), DMA((devices,)),
            VMEM((devices, rows, units), BF16), VMEM((devices, rows, units), BF16),
            VMEM((devices, rows, units), BF16),
            *scatter_shapes(stages, rows, depth), *scatter_shapes(stages, rows, depth),
            VMEM((rows, depth), F32), VMEM((rows, depth), F32),
            VMEM((parts * high, depth), F32), *rowsum_shapes(parts, high, depth),
            DMA((parts,)), DMA((parts,)), pltpu.SemaphoreType.REGULAR, DMA,
            VMEM((devices, width, rows), BF16), DMA((devices,)), DMA((devices,)),
        ],
        compiler_params=pltpu.CompilerParams(
            collective_id=2, has_side_effects=True, vmem_limit_bytes=VMEM_ALL
        ),
    )(
        att, wo, fc1.T, fc2, tokens, out_grad, ids, vectors,
    )


def add_slots(slots):
    return lax.fori_loop(
        1, slots.shape[0], lambda slot, so_far: so_far + slots[slot], slots[0]
    )


def close_kernel(
    stages, parts, dx_hbm, wq_hbm, wk_hbm, wv_hbm, norm_hbm, att_hbm, tok_hbm, vec_ref, resid_hbm,
    small_ref,
    gtok_ref, gw_hbm, go_hbm, gsmall_ref,
    dx_ref, weight, norm, att_ref, tok_ref, resid_ref, load_sem, gatt_all, gatt_send, gatt_recv,
    partial, cross, lane, cross_send, cross_recv, lane_send, lane_recv,
    total, acc, acc_o, w_piece, w_arrive, w_send, w_recv, o_piece, o_arrive, o_send, o_recv,
    w_all, o_all, wa_send, wa_recv, oa_send, oa_recv, out_sem,
    slots_t, slots_d, st_send, st_recv, sd_send, sd_recv,
    late_t, late_d, lt_send, lt_recv, ld_send, ld_recv,
):
    me, _, _ = place()
    row = lax.axis_index("dp")
    devices = 2 * stages
    wide, width = dx_ref.shape[2], att_ref.shape[1]
    loads = loading(
        load_sem,
        ((resid_hbm, resid_ref), (dx_hbm, dx_ref),
         *((src, weight.at[pl.ds(index * width, width)]) for index, src in enumerate((wq_hbm, wk_hbm, wv_hbm))),
         (norm_hbm, norm), (att_hbm, att_ref), (tok_hbm, tok_ref)),
    )
    greet_peers((("tensor", devices), ("dp", parts)))
    slots_t[me] = small_ref[...]
    wait_small = exchange("tensor", devices, slots_t, st_send, st_recv)
    loads[0].wait()
    gatt_all[me] = resid_ref[...].astype(BF16)
    gather = LineGather(stages, gatt_all, gatt_send, gatt_recv)
    gather.start()
    for load in loads[1:5]:
        load.wait()
    scatter = LineScatter(
        stages, partial, cross, lane, (cross_send, cross_recv, lane_send, lane_recv)
    )
    scatter.produce(lambda block: nn(dx_ref[block], weight[...]))
    scatter.step(stages - 1)

    acc[...] = jnp.zeros_like(acc)
    acc_o[...] = jnp.zeros_like(acc_o)
    for load in loads[5:]:
        load.wait()

    def weight_block(block, bias):
        grad = dx_ref[block]
        acc[0:wide, :] += tn(grad, norm[block])
        return bias + jnp.sum(grad.astype(F32), axis=0, keepdims=True)

    bias = lax.fori_loop(0, devices, weight_block, jnp.zeros((1, wide), F32))
    w_sum = RowSum(parts, w_piece, w_arrive, w_send, w_recv)
    w_sum.start(acc)

    def weight_o(block):
        acc_o[0:width, :] += nn(att_ref[block], gatt_all[block])

    gather.use_own(weight_o)

    def both(reach, carry):
        gather.relay(reach)
        pl.when(reach < stages - 1)(lambda: scatter.step(stages - 1 - reach))
        gather.use(reach, weight_o)
        return carry

    lax.fori_loop(1, min(2, stages), both, 0)
    w_all[row] = w_sum.reduce()
    wait_w = exchange("dp", parts, w_all, wa_send, wa_recv)
    wait_small()
    line = lax.broadcasted_iota(jnp.int32, small_ref.shape, 0)
    sums = add_slots(slots_t)
    slots_d[row] = jnp.where(line < 6, sums, small_ref[...])
    slots_d[row, 6:7, 0:wide] = bias
    wait_rows = exchange("dp", parts, slots_d, sd_send, sd_recv)
    lax.fori_loop(min(2, stages), stages, both, 0)
    o_sum = RowSum(parts, o_piece, o_arrive, o_send, o_recv)
    o_sum.start(acc_o)
    o_all[row] = o_sum.reduce()
    wait_o = exchange("dp", parts, o_all, oa_send, oa_recv)

    scatter.own(total)
    grad = total[...]
    normed, scale = normalize(tok_ref[...].astype(F32))
    quarter = late_t.shape[2]
    for index, value in enumerate((grad * normed, grad)):
        line_sum = jnp.sum(value, axis=0, keepdims=True)
        for part in range(4):
            late_t[me, 4 * index + part : 4 * index + part + 1, :] = line_sum[
                :, part * quarter : (part + 1) * quarter
            ]
    wait_late = exchange("tensor", devices, late_t, lt_send, lt_recv)
    inner = grad * vec_ref[0:1, :]
    inner_mean = jnp.mean(inner, axis=-1, keepdims=True)
    inner_proj = jnp.mean(inner * normed, axis=-1, keepdims=True)
    gtok_ref[...] = resid_ref[...] + scale * (inner - inner_mean - normed * inner_proj)
    wait_late()
    late_d[row] = add_slots(late_t)
    wait_last = exchange("dp", parts, late_d, ld_send, ld_recv)
    outs = []
    for index, (wait, src, dst) in enumerate(
        ((wait_w, w_all, gw_hbm), (wait_o, o_all, go_hbm))
    ):
        wait()
        out = pltpu.make_async_copy(src, dst, out_sem.at[index])
        out.start()
        outs.append(out)
    wait_rows()
    gsmall_ref[...] = add_slots(slots_d)
    wait_last()
    late = add_slots(late_d)
    for index in range(2):
        for part in range(4):
            gsmall_ref[index : index + 1, part * quarter : (part + 1) * quarter] = late[
                4 * index + part : 4 * index + part + 1, :
            ]
    gather.finish()
    scatter.finish()
    for out in outs:
        out.wait()


def close(dx, wq, wk, wv, norm, att, tokens, vectors, resid, small, parts):
    devices, rows, wide = dx.shape
    depth = tokens.shape[1]
    stages = devices // 2
    width = wide // 3
    w_high, o_high = piece_height(wide, parts), piece_height(width, parts)
    pieces = [(parts, high, depth) for high in (w_high, o_high)]
    return pl.pallas_call(
        functools.partial(close_kernel, stages, parts),
        name="close",
        out_shape=(
            jax.ShapeDtypeStruct((rows, depth), F32),
            *(jax.ShapeDtypeStruct(shape, BF16) for shape in pieces),
            jax.ShapeDtypeStruct(small.shape, F32),
        ),
        in_specs=[HBM] * 7 + [VSPEC, HBM, VSPEC],
        out_specs=(VSPEC, HBM, HBM, VSPEC),
        scratch_shapes=[
            VMEM((devices, rows, wide), BF16), VMEM((wide, depth), BF16),
            VMEM((devices, rows, depth), BF16), VMEM((devices, width, rows), BF16),
            VMEM((rows, depth), BF16), VMEM((rows, depth), F32), DMA((8,)),
            VMEM((devices, rows, depth), BF16), DMA((devices, 3)), DMA((devices,)),
            *scatter_shapes(stages, rows, depth),
            VMEM((rows, depth), F32), VMEM((parts * w_high, depth), F32),
            VMEM((parts * o_high, depth), F32),
            *rowsum_shapes(parts, w_high, depth), *rowsum_shapes(parts, o_high, depth),
            *(VMEM(shape, BF16) for shape in pieces), *[DMA((parts,))] * 4, DMA((2,)),
            VMEM((devices,) + small.shape, F32), VMEM((parts,) + small.shape, F32),
            DMA((devices,)), DMA((devices,)), DMA((parts,)), DMA((parts,)),
            VMEM((devices, 8, depth // 4), F32), VMEM((parts, 8, depth // 4), F32),
            DMA((devices,)), DMA((devices,)), DMA((parts,)), DMA((parts,)),
        ],
        compiler_params=pltpu.CompilerParams(
            collective_id=1, has_side_effects=True, vmem_limit_bytes=VMEM_ALL
        ),
    )(dx, wq.T, wk.T, wv.T, norm, att, tokens, vectors, resid, small)


def settle_kernel(
    gtok_hbm, gw_hbm, go_hbm, sums_ref,
    gtok_out, wq_ref, wk_ref, wv_ref, wo_ref,
    g1_ref, b1_ref, g2_ref, b2_ref, bo_ref, bf2_ref, bq_ref, bv_ref, bf1_ref,
    gtok, gw, go, sems,
):
    width, units = wq_ref.shape[0], bf1_ref.shape[0]
    loads = loading(sems, ((gtok_hbm, gtok), (gw_hbm, gw), (go_hbm, go)))
    for row, ref in enumerate((g1_ref, b1_ref, g2_ref, b2_ref, bo_ref, bf2_ref)):
        ref[...] = sums_ref[row, :]
    bq_ref[...] = sums_ref[6:7, 0:width].reshape(width)
    bv_ref[...] = sums_ref[6:7, 2 * width : 3 * width].reshape(width)
    bf1_ref[...] = sums_ref[7:8, 0:units].reshape(units)
    loads[0].wait()
    out = pltpu.make_async_copy(gtok, gtok_out, sems.at[3])
    out.start()
    loads[1].wait()
    loads[2].wait()
    wq_ref[...] = gw[0:width, :].astype(F32)
    wk_ref[...] = gw[width : 2 * width, :].astype(F32)
    wv_ref[...] = gw[2 * width : 3 * width, :].astype(F32)
    wo_ref[...] = go[0:width, :].astype(F32)
    out.wait()


def settle(gtok, gw, go, sums, width, units):
    depth = gtok.shape[1]
    weight = jax.ShapeDtypeStruct((width, depth), F32)
    return pl.pallas_call(
        settle_kernel,
        name="settle",
        out_shape=(
            jax.ShapeDtypeStruct(gtok.shape, F32), weight, weight, weight, weight,
            *(jax.ShapeDtypeStruct((size,), F32) for size in (depth,) * 6 + (width, width, units)),
        ),
        in_specs=[HBM, HBM, HBM, VSPEC],
        out_specs=(HBM,) + (VSPEC,) * 13,
        scratch_shapes=[
            VMEM(gtok.shape, F32), VMEM(gw.shape, BF16), VMEM(go.shape, BF16), DMA((4,)),
        ],
        compiler_params=pltpu.CompilerParams(vmem_limit_bytes=VMEM_ALL),
    )(gtok, gw, go, sums)


def on_device(
    devices, parts, tokens, picture_ids, ln1_gain, ln1_bias, q_weight, q_bias, k_weight, v_weight, v_bias,
    o_weight, o_bias, ln2_gain, ln2_bias, fc1_weight, fc1_bias, fc2_weight, fc2_bias, out_grad,
):
    own_count, depth = tokens.shape
    hidden_local = fc1_weight.shape[1]
    width = q_weight.shape[1]
    norm1_all, q, k, v, o_all, vectors, span, id_row, own_ids = project(
        tokens,
        (ln1_gain, ln1_bias, o_bias, ln2_gain, ln2_bias, fc2_bias, fc1_bias, q_bias, v_bias),
        o_weight, q_weight, k_weight, v_weight, picture_ids[None, :], devices, parts,
    )
    q, k, v = (item.reshape(LEN, width) for item in (q, k, v))
    attended, log_total = attend(q, k, v, span, id_row, devices)
    output, grad_residual, grad_attended, fc_sum, small = middle(
        attended, o_all, fc1_weight, fc2_weight, tokens, out_grad,
        own_ids, vectors, parts,
    )
    dqkv, grad_fc1, grad_fc2, output = attend_back(
        q, k, v, span, id_row, attended, log_total, grad_attended,
        fc_sum.reshape(-1, depth), output, hidden_local,
    )
    grad_tokens, grad_w, grad_o, sums = close(
        dqkv.reshape(devices, own_count, 3 * width), q_weight, k_weight, v_weight, norm1_all,
        attended, tokens, vectors, grad_residual, small, parts,
    )
    (
        grad_tokens, grad_q, grad_k, grad_v, grad_o, grad_g1, grad_b1, grad_g2, grad_b2, grad_bo,
        grad_bf2, grad_bq, grad_bv, grad_bf1,
    ) = settle(
        grad_tokens, grad_w.reshape(-1, depth), grad_o.reshape(-1, depth), sums, width, hidden_local
    )
    return (
        output, grad_tokens, grad_g1, grad_b1, grad_q.T, grad_bq, grad_k.T, grad_v.T, grad_bv,
        grad_o, grad_bo, grad_g2, grad_b2, grad_fc1.T, grad_bf1, grad_fc2, grad_bf2,
    )


def solution(mesh):
    rows, whole = P(("dp", "tensor"), None), P()
    columns, down, along = P(None, "tensor"), P("tensor", None), P("tensor")
    return jax.shard_map(
        functools.partial(on_device, mesh.shape["tensor"], mesh.shape["dp"]),
        mesh=mesh,
        in_specs=(
            rows, P("dp"), whole, whole, columns, along, columns, columns, along, down, whole,
            whole, whole, columns, along, down, whole, rows,
        ),
        out_specs=(
            rows, rows, whole, whole, columns, along, columns, columns, along, down, whole,
            whole, whole, columns, along, down, whole,
        ),
        check_vma=False,
    )
```
